32 devices in a mesh: dp: 8 (over z, y), seq: 4 (over x, core).
Axes of the slice: x: 2, y: 2, z: 4, core: 2. Of those that a mesh axis runs over, the one named last changes fastest.
Arguments:
- residual: float32 [8192, 768], P(('dp', 'seq')), may hold values from -6 to 6
- cotangent: float32 [8192, 768], P(('dp', 'seq')), may hold values from -6 to 6
- segments: int32 [8192], P('dp'), may hold values from 0 to 15, as said below
- triple_weight: float32 [2, 768, 2304], P(None, 'dp', 'seq'), may hold values from -0.21875 to 0.21875
- triple_moment: float32 [2, 768, 2304], P(None, 'dp', 'seq'), may hold values from -0.33 to 0.33
- triple_square: float32 [2, 768, 2304], P(None, 'dp', 'seq'), may hold values from 0.00025 to 0.001
- triple_shadow: float32 [2, 768, 2304], P(None, 'dp', 'seq'), may hold values from -0.21875 to 0.21875
- output_weight: float32 [2, 768, 768], P(None, 'dp', 'seq'), may hold values from -0.875 to 0.875
- output_moment: float32 [2, 768, 768], P(None, 'dp', 'seq'), may hold values from -0.33 to 0.33
- output_square: float32 [2, 768, 768], P(None, 'dp', 'seq'), may hold values from 0.00025 to 0.001
- output_shadow: float32 [2, 768, 768], P(None, 'dp', 'seq'), may hold values from -0.875 to 0.875
- expand_weight: float32 [2, 768, 3072], P(None, 'dp', 'seq'), may hold values from -0.21875 to 0.21875
- expand_moment: float32 [2, 768, 3072], P(None, 'dp', 'seq'), may hold values from -0.33 to 0.33
- expand_square: float32 [2, 768, 3072], P(None, 'dp', 'seq'), may hold values from 0.00025 to 0.001
- expand_shadow: float32 [2, 768, 3072], P(None, 'dp', 'seq'), may hold values from -0.21875 to 0.21875
- shrink_weight: float32 [2, 3072, 768], P(None, 'dp', 'seq'), may hold values from -0.109375 to 0.109375
- shrink_moment: float32 [2, 3072, 768], P(None, 'dp', 'seq'), may hold values from -0.33 to 0.33
- shrink_square: float32 [2, 3072, 768], P(None, 'dp', 'seq'), may hold values from 0.00025 to 0.001
- shrink_shadow: float32 [2, 3072, 768], P(None, 'dp', 'seq'), may hold values from -0.109375 to 0.109375
- scales_weight: float32 [2, 4, 768], P(None, 'seq', 'dp'), may hold values from -0.5 to 2.3
- scales_moment: float32 [2, 4, 768], P(None, 'seq', 'dp'), may hold values from -0.33 to 0.33
- scales_square: float32 [2, 4, 768], P(None, 'seq', 'dp'), may hold values from 0.00025 to 0.32
- scales_shadow: float32 [2, 4, 768], P(None, 'seq', 'dp'), may hold values from -0.5 to 2.3
Outputs:
- block_out: float32 [8192, 768], P(('dp', 'seq'))
- input_grad: float32 [8192, 768], P(('dp', 'seq'))
- grad_norm: float32 [], replicated
- triple_updated: float32 [2, 768, 2304], P(None, 'dp', 'seq')
- triple_momentum: float32 [2, 768, 2304], P(None, 'dp', 'seq')
- triple_variance: float32 [2, 768, 2304], P(None, 'dp', 'seq')
- triple_average: float32 [2, 768, 2304], P(None, 'dp', 'seq')
- output_updated: float32 [2, 768, 768], P(None, 'dp', 'seq')
- output_momentum: float32 [2, 768, 768], P(None, 'dp', 'seq')
- output_variance: float32 [2, 768, 768], P(None, 'dp', 'seq')
- output_average: float32 [2, 768, 768], P(None, 'dp', 'seq')
- expand_updated: float32 [2, 768, 3072], P(None, 'dp', 'seq')
- expand_momentum: float32 [2, 768, 3072], P(None, 'dp', 'seq')
- expand_variance: float32 [2, 768, 3072], P(None, 'dp', 'seq')
- expand_average: float32 [2, 768, 3072], P(None, 'dp', 'seq')
- shrink_updated: float32 [2, 3072, 768], P(None, 'dp', 'seq')
- shrink_momentum: float32 [2, 3072, 768], P(None, 'dp', 'seq')
- shrink_variance: float32 [2, 3072, 768], P(None, 'dp', 'seq')
- shrink_average: float32 [2, 3072, 768], P(None, 'dp', 'seq')
- scales_updated: float32 [2, 4, 768], P(None, 'seq', 'dp')
- scales_momentum: float32 [2, 4, 768], P(None, 'seq', 'dp')
- scales_variance: float32 [2, 4, 768], P(None, 'seq', 'dp')
- scales_average: float32 [2, 4, 768], P(None, 'seq', 'dp')
The draws below stay inside these ranges and needn't reach their ends.
Inputs may be any that keep to these rules, and one draw needn't show every extreme that they name: Ids never fall along the tokens; each aligned block of 1024 tokens holds whole segments only, and ids of different blocks differ; every segment has 1024 or half of 1024 tokens and starts at a multiple of half of 1024 within its block; ids need not be consecutive.
All inputs are finite; a program needn't handle non-finite values.
Results may differ from the reference program's by a relative error of at most 0.02.
Values may be sent and summed in bfloat16 or wider, within the bound.
A program may use at most 192 MiB of HBM per device.

```python
import math
import jax
import jax.numpy as jnp
from jax import lax

D = 768
FF = 3072
H = 12
HD = 64
LAYERS = 2
SEQ_LEN = 1024
STEP = 2
GROUP = 1024
TOKENS = 8192


def draw_segments(key, part):
    units = GROUP // SEQ_LEN
    groups = TOKENS // GROUP
    whole = jax.random.randint(jax.random.fold_in(key, 5), (groups, units), 0, 2).astype(jnp.int32)
    place = jnp.arange(GROUP, dtype=jnp.int32)
    unit_of = place // SEQ_LEN
    second = (place % SEQ_LEN >= SEQ_LEN // 2).astype(jnp.int32)
    global_unit = jnp.arange(groups, dtype=jnp.int32)[:, None] * units + unit_of[None, :]
    whole_at = whole[:, unit_of]
    whole_id = jnp.where(global_unit == 0, 0, 2 * global_unit + 1)
    split_id = 2 * global_unit + second[None, :]
    ids = jnp.where(whole_at == 1, whole_id, split_id)
    return ids.reshape(TOKENS).astype(jnp.int32)


def scale_rows_draw(key):
    ramp = jnp.arange(D, dtype=jnp.float32) / float(D - 1)
    base = 0.4 + ramp
    rough = 1.0 + jax.random.uniform(jax.random.fold_in(key, 1), (LAYERS, 4, D), jnp.float32, -0.4, 0.4)
    gains = base[None, None, :] * rough
    shifts = jnp.clip(0.1 * jax.random.normal(jax.random.fold_in(key, 2), (LAYERS, 4, D), jnp.float32), -0.5, 0.5)
    picked = (jnp.arange(4) % 2 == 0)[None, :, None]
    return jnp.where(picked, gains, shifts).astype(jnp.float32)


def draw_scales_weight(key, part):
    return scale_rows_draw(jax.random.fold_in(key, 11))


def draw_scales_shadow(key, part):
    return scale_rows_draw(jax.random.fold_in(key, 23))


def draw_scales_square(key, part):
    low_end = 0.00025
    high_end = 0.001
    share = jax.random.uniform(jax.random.fold_in(key, 37), (LAYERS, 4, D), jnp.float32, 0.0, 1.0)
    return jnp.exp(jnp.log(low_end) + share * (jnp.log(high_end) - jnp.log(low_end))).astype(jnp.float32)


def block_scale(stream_key, dims, pieces, least, largest):
    gain = 1.0
    for axis_at, blocks in pieces:
        heights = jax.random.uniform(jax.random.fold_in(jax.random.fold_in(stream_key, 6), axis_at), (blocks,), jnp.float32, least / len(pieces), largest / len(pieces))
        gain = gain * jnp.repeat(jnp.exp(heights), dims[axis_at] // blocks).reshape((-1,) + (1,) * (len(dims) - 1 - axis_at))
    return gain


def scatter_about(own_key, extent, deviation, bound, shards=(), kind=jnp.bfloat16):
    factor_of = block_scale(own_key, extent, shards, -0.22, 0.18) if shards else 1.0
    drawn = jax.random.normal(own_key, extent, jnp.float32) * deviation * factor_of
    return jnp.minimum(jnp.maximum(drawn, -bound), bound).astype(kind)


def setup_inputs(seed: int = 0) -> dict:
    key_of = jax.random.split(jax.random.key(seed), 24)
    residual = scatter_about(key_of[0], (TOKENS, D), 1.0, 6.0, ((0, 32),), jnp.float32)
    cotangent = scatter_about(key_of[1], (TOKENS, D), 1.0, 6.0, ((0, 32),), jnp.float32)
    segments = draw_segments(jax.random.fold_in(key_of[23], 71), 0)
    triple_weight = scatter_about(key_of[3], (LAYERS, D, 3 * D), D ** -0.5, 0.21875, ((1, 8), (2, 4)), jnp.float32)
    triple_moment = scatter_about(key_of[4], (LAYERS, D, 3 * D), 0.055, 0.33, ((1, 8), (2, 4)), jnp.float32)
    triple_square = jnp.clip(jnp.exp(math.log(0.001) - 1.3862944 * jax.random.uniform(key_of[5], (LAYERS, D, 3 * D), jnp.float32) ** block_scale(key_of[5], (LAYERS, D, 3 * D), ((1, 8), (2, 4)), -0.2, 0.2)), 0.00025, 0.001)
    triple_shadow = scatter_about(key_of[6], (LAYERS, D, 3 * D), D ** -0.5, 0.21875, ((1, 8), (2, 4)), jnp.float32)
    output_weight = scatter_about(key_of[7], (LAYERS, D, D), (D // 16) ** -0.5, 0.875, ((1, 8), (2, 4)), jnp.float32)
    output_moment = scatter_about(key_of[8], (LAYERS, D, D), 0.055, 0.33, ((1, 8), (2, 4)), jnp.float32)
    output_square = jnp.clip(jnp.exp(math.log(0.001) - 1.3862944 * jax.random.uniform(key_of[9], (LAYERS, D, D), jnp.float32) ** block_scale(key_of[9], (LAYERS, D, D), ((1, 8), (2, 4)), -0.2, 0.2)), 0.00025, 0.001)
    output_shadow = scatter_about(key_of[10], (LAYERS, D, D), (D // 16) ** -0.5, 0.875, ((1, 8), (2, 4)), jnp.float32)
    expand_weight = scatter_about(key_of[11], (LAYERS, D, FF), D ** -0.5, 0.21875, ((1, 8), (2, 4)), jnp.float32)
    expand_moment = scatter_about(key_of[12], (LAYERS, D, FF), 0.055, 0.33, ((1, 8), (2, 4)), jnp.float32)
    expand_square = jnp.clip(jnp.exp(math.log(0.001) - 1.3862944 * jax.random.uniform(key_of[13], (LAYERS, D, FF), jnp.float32) ** block_scale(key_of[13], (LAYERS, D, FF), ((1, 8), (2, 4)), -0.2, 0.2)), 0.00025, 0.001)
    expand_shadow = scatter_about(key_of[14], (LAYERS, D, FF), D ** -0.5, 0.21875, ((1, 8), (2, 4)), jnp.float32)
    shrink_weight = scatter_about(key_of[15], (LAYERS, FF, D), FF ** -0.5, 0.109375, ((1, 8), (2, 4)), jnp.float32)
    shrink_moment = scatter_about(key_of[16], (LAYERS, FF, D), 0.055, 0.33, ((1, 8), (2, 4)), jnp.float32)
    shrink_square = jnp.clip(jnp.exp(math.log(0.001) - 1.3862944 * jax.random.uniform(key_of[17], (LAYERS, FF, D), jnp.float32) ** block_scale(key_of[17], (LAYERS, FF, D), ((1, 8), (2, 4)), -0.2, 0.2)), 0.00025, 0.001)
    shrink_shadow = scatter_about(key_of[18], (LAYERS, FF, D), FF ** -0.5, 0.109375, ((1, 8), (2, 4)), jnp.float32)
    scales_weight = draw_scales_weight(jax.random.fold_in(key_of[23], 71), 0)
    scales_moment = scatter_about(key_of[20], (LAYERS, 4, D), 0.055, 0.33, ((1, 4), (2, 8)), jnp.float32)
    scales_square = draw_scales_square(jax.random.fold_in(key_of[23], 71), 0)
    scales_shadow = draw_scales_shadow(jax.random.fold_in(key_of[23], 71), 0)
    return {"residual": residual, "cotangent": cotangent, "segments": segments, "triple_weight": triple_weight, "triple_moment": triple_moment, "triple_square": triple_square, "triple_shadow": triple_shadow, "output_weight": output_weight, "output_moment": output_moment, "output_square": output_square, "output_shadow": output_shadow, "expand_weight": expand_weight, "expand_moment": expand_moment, "expand_square": expand_square, "expand_shadow": expand_shadow, "shrink_weight": shrink_weight, "shrink_moment": shrink_moment, "shrink_square": shrink_square, "shrink_shadow": shrink_shadow, "scales_weight": scales_weight, "scales_moment": scales_moment, "scales_square": scales_square, "scales_shadow": scales_shadow}


EPSILON = 1e-05
ROTARY_BASE = 10000.0
BETA_ONE = 0.9
BETA_TWO = 0.999
ADAM_EPSILON = 1e-08
DECAY_RATE = 0.01
SHADOW_RATE = 0.99
CLIP_RATIO = 0.5
RATE_FACTOR = 1.5
SCALES_RATE = 0.6
MASKED = -1000000000.0
HIGHEST = lax.Precision.HIGHEST

@jax.custom_vjp
def low(v):
    return lax.optimization_barrier(v.astype(jnp.bfloat16)).astype(jnp.float32)

@jax.custom_vjp
def low_back(v):
    return v

def low_keep(v):
    return (low(v), None)

def low_pass(kept, grad):
    return (grad,)

def back_keep(v):
    return (v, None)

def back_low(kept, grad):
    return (low(grad),)
low.defvjp(low_keep, low_pass)
low_back.defvjp(back_keep, back_low)

def both_round(values):
    return low(low_back(values))

def layer_norm(values, gain_row, shift_row):
    center = values - lax.optimization_barrier(jnp.mean(values, axis=-1, keepdims=True))
    spread = lax.optimization_barrier(jnp.mean(center * center, axis=-1, keepdims=True))
    return center * lax.rsqrt(spread + EPSILON) * gain_row + shift_row

def rotary(values, positions):
    row_count = values.shape[0]
    shaped = values.reshape(row_count, -1, HD)
    half_width = HD // 2
    inverse = 1.0 / ROTARY_BASE ** (jnp.arange(half_width, dtype=jnp.float32) * (2.0 / HD))
    angles = positions.astype(jnp.float32)[:, None] * inverse[None, :]
    cosine = jnp.cos(angles)[:, None, :]
    sine_table = jnp.sin(angles)[:, None, :]
    first_half = shaped[:, :, :half_width]
    second_half = shaped[:, :, half_width:]
    turned = jnp.concatenate([first_half * cosine - second_half * sine_table, second_half * cosine + first_half * sine_table], axis=-1)
    return turned.reshape(row_count, -1)

def start_positions(segment_block):
    earlier = (segment_block[None, :] < segment_block[:, None]).astype(jnp.int32)
    return jnp.arange(segment_block.shape[0], dtype=jnp.int32) - lax.optimization_barrier(jnp.sum(earlier, axis=1)).astype(jnp.int32)

def attend_group(packed):
    queries, keys, values, segment_block = packed
    group_rows = queries.shape[0]
    query_heads = queries.reshape(group_rows, H, HD)
    key_heads = keys.reshape(group_rows, H, HD)
    value_heads = values.reshape(group_rows, H, HD)
    scores = jnp.einsum('qhd,khd->hqk', query_heads, key_heads, precision=HIGHEST) * HD ** (-0.5)
    scores = low_back(scores)
    same_doc = segment_block[:, None] == segment_block[None, :]
    scores = jnp.where(same_doc[None], scores, MASKED)
    weights = low(jax.nn.softmax(scores, axis=-1))
    context = jnp.einsum('hqk,khd->qhd', weights, value_heads, precision=HIGHEST)
    return context.reshape(group_rows, D)

def forward(params, residual, segments):
    triple, output, expand, shrink, scales = params
    segment_groups = segments.reshape(-1, GROUP)
    positions = lax.map(start_positions, segment_groups).reshape(-1)
    attend = jax.checkpoint(attend_group)
    stream = residual
    for layer_index in range(LAYERS):
        scale_rows = low(scales[layer_index])
        normed = low(layer_norm(stream, scale_rows[0], scale_rows[1]))
        projected = low_back(jnp.dot(normed, low(triple[layer_index]), precision=HIGHEST))
        queries = both_round(rotary(projected[:, :D], positions))
        keys = both_round(rotary(projected[:, D:2 * D], positions))
        values = both_round(projected[:, 2 * D:])
        context = lax.map(attend, (queries.reshape(-1, GROUP, D), keys.reshape(-1, GROUP, D), values.reshape(-1, GROUP, D), segment_groups))
        context = both_round(context.reshape(-1, D))
        stream = stream + low_back(jnp.dot(context, low(output[layer_index]), precision=HIGHEST))
        normed = low(layer_norm(stream, scale_rows[2], scale_rows[3]))
        hidden = low_back(jnp.dot(normed, low(expand[layer_index]), precision=HIGHEST))
        active = low(jax.nn.gelu(hidden, approximate=False))
        stream = stream + low_back(jnp.dot(active, low(shrink[layer_index]), precision=HIGHEST))
    return stream

def adam_step(weight, moment, square, shadow, gradient, step_rate):
    shadow_decay = min(SHADOW_RATE, (1.0 + STEP) / (10.0 + STEP))
    momentum = BETA_ONE * moment + (1.0 - BETA_ONE) * gradient
    variance = BETA_TWO * square + (1.0 - BETA_TWO) * gradient * gradient
    corrected = momentum / (1.0 - BETA_ONE ** STEP) / (jnp.sqrt(variance / (1.0 - BETA_TWO ** STEP)) + ADAM_EPSILON)
    updated = weight - step_rate * (corrected + DECAY_RATE * weight)
    average = shadow_decay * shadow + (1.0 - shadow_decay) * updated
    return (updated, momentum, variance, average)

def reference(residual, cotangent, segments, triple_weight, triple_moment, triple_square, triple_shadow, output_weight, output_moment, output_square, output_shadow, expand_weight, expand_moment, expand_square, expand_shadow, shrink_weight, shrink_moment, shrink_square, shrink_shadow, scales_weight, scales_moment, scales_square, scales_shadow):
    params = (triple_weight, output_weight, expand_weight, shrink_weight, scales_weight)
    block_out, pullback = jax.vjp(lambda weights, inputs: forward(weights, inputs, segments), params, residual)
    weight_grads, input_grad = pullback(cotangent)
    squares = jnp.float32(0.0)
    for grad_array in weight_grads:
        squares = squares + jnp.sum(grad_array * grad_array)
    grad_norm = jnp.sqrt(squares)
    limit = CLIP_RATIO * math.sqrt(float(LAYERS * (4 * D * D + 2 * D * FF + 4 * D)))
    factor = limit / (grad_norm + 1e-06)
    triple_updated, triple_momentum, triple_variance, triple_average = adam_step(triple_weight, triple_moment, triple_square, triple_shadow, weight_grads[0] * factor, RATE_FACTOR / math.sqrt(D))
    output_updated, output_momentum, output_variance, output_average = adam_step(output_weight, output_moment, output_square, output_shadow, weight_grads[1] * factor, RATE_FACTOR / math.sqrt(D // 16))
    expand_updated, expand_momentum, expand_variance, expand_average = adam_step(expand_weight, expand_moment, expand_square, expand_shadow, weight_grads[2] * factor, RATE_FACTOR / math.sqrt(D))
    shrink_updated, shrink_momentum, shrink_variance, shrink_average = adam_step(shrink_weight, shrink_moment, shrink_square, shrink_shadow, weight_grads[3] * factor, RATE_FACTOR / math.sqrt(FF))
    scales_updated, scales_momentum, scales_variance, scales_average = adam_step(scales_weight, scales_moment, scales_square, scales_shadow, weight_grads[4] * factor, SCALES_RATE)
    return (block_out, input_grad, grad_norm, triple_updated, triple_momentum, triple_variance, triple_average, output_updated, output_momentum, output_variance, output_average, expand_updated, expand_momentum, expand_variance, expand_average, shrink_updated, shrink_momentum, shrink_variance, shrink_average, scales_updated, scales_momentum, scales_variance, scales_average)
```

```python
import functools
import math

import jax
import jax.numpy as jnp
from jax import lax
from jax.experimental import pallas as pl
from jax.experimental.pallas import tpu as pltpu
from jax.sharding import PartitionSpec as P

D = 768
FF = 3072
HD = 64
LAYERS = 2
STEP = 2
SEQ = 4

EPSILON = 1e-05
ROTARY_BASE = 10000.0
BETA_ONE = 0.9
BETA_TWO = 0.999
ADAM_EPSILON = 1e-08
DECAY_RATE = 0.01
SHADOW_RATE = 0.99
CLIP_RATIO = 0.5
RATE_FACTOR = 1.5
SCALES_RATE = 0.6
MASKED = -1000000000.0

HALF = D // 2
TRI = 3 * HALF
HID = FF // 2
BF = jnp.bfloat16
F32 = jnp.float32
MESH = pl.DeviceIdType.MESH
VMEM_BYTES = 60 << 20


def adam_step(weight, moment, square, shadow, gradient, step_rate):
    shadow_decay = min(SHADOW_RATE, (1.0 + STEP) / (10.0 + STEP))
    momentum = BETA_ONE * moment + (1.0 - BETA_ONE) * gradient
    variance = BETA_TWO * square + (1.0 - BETA_TWO) * gradient * gradient
    corrected = (
        momentum
        / (1.0 - BETA_ONE**STEP)
        / (jnp.sqrt(variance / (1.0 - BETA_TWO**STEP)) + ADAM_EPSILON)
    )
    updated = weight - step_rate * (corrected + DECAY_RATE * weight)
    average = shadow_decay * shadow + (1.0 - shadow_decay) * updated
    return (updated, momentum, variance, average)


def nn(a, b):
    return lax.dot_general(a, b, (((1,), (0,)), ((), ())), preferred_element_type=F32)


def nt(a, b):
    return lax.dot_general(a, b, (((1,), (1,)), ((), ())), preferred_element_type=F32)


def tn(a, b):
    return lax.dot_general(a, b, (((0,), (0,)), ((), ())), preferred_element_type=F32)


def place():
    s = lax.axis_index("seq")
    x = lax.div(s, 2)
    c = lax.rem(s, 2)
    return lax.axis_index("dp"), x, c, lax.rem(s + 2, SEQ), s + 1 - 2 * c


def greet(d, peer, sib):
    barrier = pltpu.get_barrier_semaphore()
    for other in (peer, sib):
        pl.semaphore_signal(barrier, inc=1, device_id=(d, other), device_id_type=MESH)
    pl.semaphore_wait(barrier, 2)


def rows_of(c, n):
    return pl.ds(pl.multiple_of(c * n, n), n)


class Copies:
    def __init__(self, lsem, ssem, rsem, d):
        self.lsem, self.ssem, self.rsem, self.d = lsem, ssem, rsem, d
        self.n_local = 0
        self.n_remote = 0

    def local(self, src, dst):
        copy = pltpu.make_async_copy(src, dst, self.lsem.at[self.n_local])
        self.n_local += 1
        copy.start()
        return copy

    def push(self, src, dst, to):
        copy = pltpu.make_async_remote_copy(
            src_ref=src,
            dst_ref=dst,
            send_sem=self.ssem.at[self.n_remote],
            recv_sem=self.rsem.at[self.n_remote],
            device_id=(self.d, to),
            device_id_type=MESH,
        )
        self.n_remote += 1
        copy.start()
        return copy


def norm_stats(values):
    center = values - jnp.mean(values, axis=-1, keepdims=True)
    spread = jnp.mean(center * center, axis=-1, keepdims=True)
    scale = lax.rsqrt(spread + EPSILON)
    return center * scale, scale


def norm_back(values, gain, dy):
    xhat, scale = norm_stats(values)
    u = gain * dy
    du = u - jnp.mean(u, axis=-1, keepdims=True)
    back = scale * (du - xhat * jnp.mean(u * xhat, axis=-1, keepdims=True))
    rows = jnp.concatenate(
        [jnp.sum(xhat * dy, axis=0, keepdims=True), jnp.sum(dy, axis=0, keepdims=True)], axis=0
    )
    return back, rows


def turn(chunk, cosine, sine):
    lane = lax.broadcasted_iota(jnp.int32, chunk.shape, 1)
    swapped = jnp.where(
        lax.rem(lane, HD) < HD // 2, pltpu.roll(chunk, 128 - HD // 2, 1), pltpu.roll(chunk, HD // 2, 1)
    )
    return chunk * cosine + swapped * sine


def half_of(pair, which):
    lane = lax.broadcasted_iota(jnp.int32, pair.shape, 1)
    keep = (lane < HD) if which == 0 else (lane >= HD)
    return jnp.where(keep, pair, jnp.zeros_like(pair))


def attend_fwd_kernel(
    h, wa, sc, cs, bias, mid, na_o, q_o, k_o, v_o, ctx_o, lse_o,
    wt, wo, na, q, k, v, ctxt, ctx, lse, psend, precv, lsem, ssem, rsem,
):
    d, x, c, peer, sib = place()
    y = 1 - x
    rows = h.shape[0]
    copies = Copies(lsem, ssem, rsem, d)
    greet(d, peer, sib)
    wt_own, wo_own = wt.at[rows_of(c, HALF), :], wo.at[:, rows_of(c, HALF)]
    tri_part, out_part = wa.at[:, pl.ds(0, TRI)], wa.at[:, pl.ds(TRI, HALF)]
    tri_sent = copies.push(tri_part, wt_own, sib)
    tri_local = copies.local(tri_part, wt_own)
    out_sent = copies.push(out_part, wo_own, sib)
    out_local = copies.local(out_part, wo_own)
    xhat, _ = norm_stats(h[...])
    na[x] = (xhat * sc[0:1, :] + sc[1:2, :]).astype(BF)
    na_sent = copies.push(na.at[x], na.at[x], peer)
    tri_local.wait()
    tri_sent.wait()

    def project(block):
        cosine, sine = cs[block, :, 0:128], cs[block, :, 128:256]
        for j in range(9):
            part = nn(na[block], wt[:, 128 * j : 128 * j + 128])
            lanes = pl.ds(128 * (j % 3), 128)
            if j < 3:
                q[block, :, lanes] = (turn(part, cosine, sine) * HD**-0.5).astype(BF)
            elif j < 6:
                k[block, rows_of(c, rows), lanes] = turn(part, cosine, sine).astype(BF)
            else:
                v[block, rows_of(c, rows), lanes] = part.astype(BF)

    def share(block):
        mine = (block, rows_of(c, rows))
        return [copies.push(k.at[mine], k.at[mine], sib), copies.push(v.at[mine], v.at[mine], sib)]

    project(x)
    shared = share(x)
    na_sent.wait()
    project(y)
    shared += share(y)
    out_local.wait()
    out_sent.wait()
    for copy in shared:
        copy.wait()

    def attend(block):
        other = 1 - block

        def pair_step(p, carry):
            lanes = pl.ds(pl.multiple_of(p * 128, 128), 128)
            q_pair = q[block, :, lanes]
            k_same, k_cross = k[block, :, lanes], k[other, :, lanes]
            v_same, v_cross = v[block, :, lanes], v[other, :, lanes]
            for which in range(2):
                q_head = half_of(q_pair, which)
                s_same = nt(k_same, q_head)
                s_cross = nt(k_cross, q_head) + bias[0]
                top = jnp.maximum(
                    jnp.max(s_same, axis=0, keepdims=True), jnp.max(s_cross, axis=0, keepdims=True)
                )
                e_same = jnp.exp(s_same - top)
                e_cross = jnp.exp(s_cross - top)
                total = jnp.sum(e_same, axis=0, keepdims=True) + jnp.sum(
                    e_cross, axis=0, keepdims=True
                )
                mixed = tn(v_same, e_same.astype(BF)) + tn(v_cross, e_cross.astype(BF))
                head = pl.ds(pl.multiple_of(p * 128 + which * HD, HD), HD)
                ctxt[head, :] = mixed[which * HD : which * HD + HD, :] / total
                lse[block, pl.ds(2 * p + which, 1), :] = top + jnp.log(total)
            return carry

        lax.fori_loop(0, HALF // 128, pair_step, 0)
        ctx[block] = ctxt[...].T.astype(BF)
        return nn(ctx[block], wo[...])

    psend[...] = attend(y).astype(BF)
    part_sent = copies.push(psend, precv, peer)
    mid[...] = h[...] + attend(x)
    saves = [
        copies.local(a, b)
        for a, b in ((na, na_o), (q, q_o), (k, k_o), (v, v_o), (ctx, ctx_o), (lse, lse_o))
    ]
    part_sent.wait()
    mid[...] = mid[...] + precv[...].astype(F32)
    for copy in saves:
        copy.wait()


def hbm():
    return pl.BlockSpec(memory_space=pl.ANY)


def vmem():
    return pl.BlockSpec(memory_space=pltpu.VMEM)


def call(kernel, name, number, ins, outs, out_shape, scratch, n_local, n_remote, flops, args):
    return pl.pallas_call(
        kernel,
        name=name,
        out_shape=out_shape,
        in_specs=ins,
        out_specs=outs,
        scratch_shapes=[
            *scratch,
            pltpu.SemaphoreType.DMA((n_local,)),
            pltpu.SemaphoreType.DMA((n_remote,)),
            pltpu.SemaphoreType.DMA((n_remote,)),
        ],
        cost_estimate=pl.CostEstimate(flops=flops, bytes_accessed=16 << 20, transcendentals=0),
        compiler_params=pltpu.CompilerParams(
            collective_id=number, has_side_effects=True, vmem_limit_bytes=VMEM_BYTES
        ),
    )(*args)


def sds(shape, dtype):
    return jax.ShapeDtypeStruct(shape, dtype)


def attend_fwd(h, wa, scales, tables, bias):
    t = h.shape[0]
    return call(
        attend_fwd_kernel, "attend_fwd", 0,
        [vmem(), hbm(), vmem(), vmem(), pl.BlockSpec(memory_space=pltpu.SMEM)],
        [vmem()] + [hbm()] * 6,
        [
            sds((t, D), F32), sds((2, t, D), BF), sds((2, t, HALF), BF), sds((2, 2 * t, HALF), BF),
            sds((2, 2 * t, HALF), BF), sds((2, t, HALF), BF), sds((2, 8, t), F32),
        ],
        [
            pltpu.VMEM((D, TRI), BF), pltpu.VMEM((HALF, D), BF), pltpu.VMEM((2, t, D), BF),
            pltpu.VMEM((2, t, HALF), BF), pltpu.VMEM((2, 2 * t, HALF), BF),
            pltpu.VMEM((2, 2 * t, HALF), BF), pltpu.VMEM((HALF, t), F32),
            pltpu.VMEM((2, t, HALF), BF), pltpu.VMEM((2, 8, t), F32),
            pltpu.VMEM((t, D), BF), pltpu.VMEM((t, D), BF),
        ],
        8, 8, 6 << 30, (h, wa, scales, tables, bias),
    )


def gelu_parts(hidden):
    phi_cap = 0.5 * (1.0 + lax.erf(hidden * math.sqrt(0.5)))
    density = jnp.exp(-0.5 * hidden * hidden) * (1.0 / math.sqrt(2.0 * math.pi))
    return hidden * phi_cap, phi_cap + hidden * density


def feed_fwd_kernel(
    mid, wf, sc, h_next, nb_o, act_o, slope_o,
    we, ws, nb, act, slope, psend, precv, lsem, ssem, rsem,
):
    d, x, c, peer, sib = place()
    y = 1 - x
    copies = Copies(lsem, ssem, rsem, d)
    greet(d, peer, sib)
    xhat, _ = norm_stats(mid[...])
    nb[x] = (xhat * sc[2:3, :] + sc[3:4, :]).astype(BF)
    nb_sent = copies.push(nb.at[x], nb.at[x], peer)
    we_own, ws_own = we.at[:, rows_of(c, D)], ws.at[rows_of(c, D), :]
    exp_part, shr_part = wf.at[:, pl.ds(0, D)], wf.at[:, pl.ds(D, D)]
    weights = [
        copies.local(exp_part, we_own),
        copies.push(exp_part, we_own, sib),
        copies.local(shr_part, ws_own),
        copies.push(shr_part, ws_own, sib),
    ]
    for copy in weights:
        copy.wait()

    def feed(block):
        def step(i, carry):
            lanes = pl.ds(pl.multiple_of(i * 256, 256), 256)
            value, rate = gelu_parts(nn(nb[block], we[:, lanes]))
            act[block, :, lanes] = value.astype(BF)
            slope[block, :, lanes] = rate.astype(BF)
            return carry

        lax.fori_loop(0, HID // 256, step, 0)
        return nn(act[block], ws[...])

    h_next[...] = mid[...] + feed(x)
    nb_sent.wait()
    psend[...] = feed(y).astype(BF)
    part_sent = copies.push(psend, precv, peer)
    saves = [copies.local(a, b) for a, b in ((nb, nb_o), (act, act_o), (slope, slope_o))]
    part_sent.wait()
    h_next[...] = h_next[...] + precv[...].astype(F32)
    for copy in saves:
        copy.wait()


def feed_fwd(mid, wf, scales):
    t = mid.shape[0]
    return call(
        feed_fwd_kernel, "feed_fwd", 1,
        [vmem(), hbm(), vmem()],
        [vmem()] + [hbm()] * 3,
        [sds((t, D), F32), sds((2, t, D), BF), sds((2, t, HID), BF), sds((2, t, HID), BF)],
        [
            pltpu.VMEM((D, HID), BF), pltpu.VMEM((HID, D), BF), pltpu.VMEM((2, t, D), BF),
            pltpu.VMEM((2, t, HID), BF), pltpu.VMEM((2, t, HID), BF),
            pltpu.VMEM((t, D), BF), pltpu.VMEM((t, D), BF),
        ],
        5, 4, 5 << 30, (mid, wf, scales),
    )


def feed_bwd_kernel(
    g, mid, wf, sc, nb_h, act_h, slope_h, mid_grad, wg_o, rows_o,
    we, ws, nb, act, slope, gl, hg, part, psend, precv, gown, gsend, grecv, lsem, ssem, rsem,
):
    d, x, c, peer, sib = place()
    y = 1 - x
    t = g.shape[0]
    copies = Copies(lsem, ssem, rsem, d)
    greet(d, peer, sib)
    gl[x] = g[...].astype(BF)
    g_sent = copies.push(gl.at[x], gl.at[x], peer)
    we_own, ws_own = we.at[:, rows_of(c, D)], ws.at[rows_of(c, D), :]
    exp_part, shr_part = wf.at[:, pl.ds(0, D)], wf.at[:, pl.ds(D, D)]
    weights = [
        copies.local(shr_part, ws_own),
        copies.push(shr_part, ws_own, sib),
        copies.local(exp_part, we_own),
        copies.push(exp_part, we_own, sib),
        copies.local(slope_h, slope),
        copies.local(act_h, act),
        copies.local(nb_h, nb),
    ]
    for copy in weights:
        copy.wait()

    def back(block):
        def step(i, carry):
            lanes = pl.ds(pl.multiple_of(i * 256, 256), 256)
            pulled = nt(gl[block], ws[lanes, :])
            hg[block, :, lanes] = (pulled * slope[block, :, lanes].astype(F32)).astype(BF)
            return carry

        lax.fori_loop(0, HID // 256, step, 0)
        return nt(hg[block], we[...])

    part[...] = back(x)
    g_sent.wait()
    psend[...] = back(y).astype(BF)
    part_sent = copies.push(psend, precv, peer)

    gl_all = gl[...].reshape(2 * t, D)
    nb_all = nb[...].reshape(2 * t, D)

    def grads(which, store):
        def step(i, carry):
            at = pl.ds(pl.multiple_of(i * 256, 256), 256)
            off = pl.ds(pl.multiple_of(which * D + i * 256, 256), 256)
            hg_part = hg[:, :, off].reshape(2 * t, 256)
            act_part = act[:, :, off].reshape(2 * t, 256)
            store(0, at, tn(nb_all, hg_part))
            store(1, at, tn(act_part, gl_all))
            return carry

        lax.fori_loop(0, D // 256, step, 0)

    def to_send(kind, at, value):
        if kind == 0:
            gsend[:, at] = value.astype(BF)
        else:
            gsend[at, pl.ds(D, D)] = value.astype(BF)

    def to_keep(kind, at, value):
        if kind == 0:
            gown[:, at] = value
        else:
            gown[at, pl.ds(D, D)] = value

    grads(1 - c, to_send)
    grad_sent = copies.push(gsend, grecv, sib)
    grads(c, to_keep)
    part_sent.wait()
    dy = part[...] + precv[...].astype(F32)
    back_mid, rows = norm_back(mid[...], sc[2:3, :], dy)
    mid_grad[...] = g[...] + back_mid
    rows_o[...] = rows
    grad_sent.wait()
    gsend[...] = (gown[...] + grecv[...].astype(F32)).astype(BF)
    copies.local(gsend, wg_o).wait()


def feed_bwd(g, mid, wf, scales, nb, act, slope):
    t = g.shape[0]
    return call(
        feed_bwd_kernel, "feed_bwd", 2,
        [vmem(), vmem(), hbm(), vmem(), hbm(), hbm(), hbm()],
        [vmem(), hbm(), vmem()],
        [sds((t, D), F32), sds((D, 2 * D), BF), sds((2, D), F32)],
        [
            pltpu.VMEM((D, HID), BF), pltpu.VMEM((HID, D), BF), pltpu.VMEM((2, t, D), BF),
            pltpu.VMEM((2, t, HID), BF), pltpu.VMEM((2, t, HID), BF), pltpu.VMEM((2, t, D), BF),
            pltpu.VMEM((2, t, HID), BF), pltpu.VMEM((t, D), F32), pltpu.VMEM((t, D), BF),
            pltpu.VMEM((t, D), BF), pltpu.VMEM((D, 2 * D), F32), pltpu.VMEM((D, 2 * D), BF),
            pltpu.VMEM((D, 2 * D), BF),
        ],
        6, 5, 10 << 30, (g, mid, wf, scales, nb, act, slope),
    )


def attend_bwd_kernel(
    mg, h, wa, sc, cs, bias, na, q, k, v, ctx, lse, g_prev, wg_o, rows_o,
    wt, wo, ml, cg, delta, dqt, dk, dv, kvsend, kvrecv, pg, part, psend, precv,
    gown, gsend, grecv, lsem, ssem, rsem,
):
    d, x, c, peer, sib = place()
    y = 1 - x
    t = mg.shape[0]
    copies = Copies(lsem, ssem, rsem, d)
    greet(d, peer, sib)
    ml[x] = mg[...].astype(BF)
    ml_sent = copies.push(ml.at[x], ml.at[x], peer)
    wt_own, wo_own = wt.at[rows_of(c, HALF), :], wo.at[:, rows_of(c, HALF)]
    tri_part, out_part = wa.at[:, pl.ds(0, TRI)], wa.at[:, pl.ds(TRI, HALF)]
    out_moves = [copies.local(out_part, wo_own), copies.push(out_part, wo_own, sib)]
    tri_moves = [copies.local(tri_part, wt_own), copies.push(tri_part, wt_own, sib)]
    dk[...] = jnp.zeros_like(dk)
    dv[...] = jnp.zeros_like(dv)
    for copy in out_moves:
        copy.wait()

    def attend(block):
        other = 1 - block
        pulled = nt(ml[block], wo[...])
        cg[block] = pulled.astype(BF)
        weighed = (cg[block].astype(F32) * ctx[block].astype(F32)).T
        for head in range(HALF // HD):
            delta[head : head + 1, :] = jnp.sum(
                weighed[head * HD : head * HD + HD, :], axis=0, keepdims=True
            )

        def pair_step(p, carry):
            lanes = pl.ds(pl.multiple_of(p * 128, 128), 128)
            q_pair, cg_pair = q[block, :, lanes], cg[block, :, lanes]
            for which in range(2):
                q_head, cg_head = half_of(q_pair, which), half_of(cg_pair, which)
                row = pl.ds(2 * p + which, 1)
                total, dots = lse[block, row, :], delta[row, :]
                turned = None
                for side in (block, other):
                    k_pair, v_pair = k[side, :, lanes], v[side, :, lanes]
                    scores = nt(k_pair, q_head)
                    if side is other:
                        scores = scores + bias[0]
                    probs = jnp.exp(scores - total)
                    score_grad = (probs * (nt(v_pair, cg_head) - dots)).astype(BF)
                    dv[side, :, lanes] += nn(probs.astype(BF), cg_head)
                    dk[side, :, lanes] += nn(score_grad, q_head)
                    piece = tn(k_pair, score_grad)
                    turned = piece if turned is None else turned + piece
                head = pl.ds(pl.multiple_of(p * 128 + which * HD, HD), HD)
                dqt[block, head, :] = turned[which * HD : which * HD + HD, :] * HD**-0.5
            return carry

        lax.fori_loop(0, HALF // 128, pair_step, 0)

    attend(x)
    ml_sent.wait()
    attend(y)
    theirs, mine = rows_of(1 - c, t), rows_of(c, t)
    for side in range(2):
        kvsend[side, :, pl.ds(0, HALF)] = dk[side, theirs, :].astype(BF)
        kvsend[side, :, pl.ds(HALF, HALF)] = dv[side, theirs, :].astype(BF)
    kv_sent = copies.push(kvsend, kvrecv, sib)

    def unturn(block, j, value):
        cosine, sine = cs[block, :, 0:128], cs[block, :, 128:256]
        rounded = value.astype(BF).astype(F32)
        pg[block, :, pl.ds(128 * j, 128)] = turn(rounded, cosine, -sine).astype(BF)

    for side in range(2):
        for j in range(3):
            unturn(side, j, dqt[side, 128 * j : 128 * j + 128, :].T)
    kv_sent.wait()
    for side in range(2):
        for j in range(3):
            at = pl.ds(128 * j, 128)
            unturn(side, 3 + j, dk[side, mine, at] + kvrecv[side, :, at].astype(F32))
            pg[side, :, pl.ds(D + 128 * j, 128)] = (
                dv[side, mine, at] + kvrecv[side, :, pl.ds(HALF + 128 * j, 128)].astype(F32)
            ).astype(BF)
    for copy in tri_moves:
        copy.wait()
    psend[...] = nt(pg[y], wt[...]).astype(BF)
    part_sent = copies.push(psend, precv, peer)
    part[...] = nt(pg[x], wt[...])

    ml_all = ml[...].reshape(2 * t, D)
    na_all = na[...].reshape(2 * t, D)
    ctx_all = ctx[...].reshape(2 * t, HALF)

    def grads(which, store):
        def step(i, carry):
            off = pl.ds(pl.multiple_of(which * HALF + i * 128, 128), 128)
            at = pl.ds(pl.multiple_of(i * 128, 128), 128)
            store(0, at, tn(na[:, :, off].reshape(2 * t, 128), pg[...].reshape(2 * t, TRI)))
            store(1, at, tn(ctx_all, ml[:, :, off].reshape(2 * t, 128)))
            return carry

        lax.fori_loop(0, HALF // 128, step, 0)

    def to_send(kind, at, value):
        if kind == 0:
            gsend[at, pl.ds(0, TRI)] = value.astype(BF)
        else:
            gsend[:, pl.ds(pl.multiple_of(TRI + at.start, 128), 128)] = value.astype(BF)

    def to_keep(kind, at, value):
        if kind == 0:
            gown[at, pl.ds(0, TRI)] = value
        else:
            gown[:, pl.ds(pl.multiple_of(TRI + at.start, 128), 128)] = value

    grads(1 - c, to_send)
    grad_sent = copies.push(gsend, grecv, sib)
    grads(c, to_keep)
    part_sent.wait()
    dy = part[...] + precv[...].astype(F32)
    back, rows = norm_back(h[...], sc[0:1, :], dy)
    g_prev[...] = mg[...] + back
    rows_o[...] = rows
    grad_sent.wait()
    gsend[...] = (gown[...] + grecv[...].astype(F32)).astype(BF)
    copies.local(gsend, wg_o).wait()


def attend_bwd(mg, h, wa, scales, tables, bias, saved):
    t = mg.shape[0]
    return call(
        attend_bwd_kernel, "attend_bwd", 3,
        [vmem(), vmem(), hbm(), vmem(), vmem(), pl.BlockSpec(memory_space=pltpu.SMEM)] + [vmem()] * 6,
        [vmem(), hbm(), vmem()],
        [sds((t, D), F32), sds((HALF, 2 * D), BF), sds((2, D), F32)],
        [
            pltpu.VMEM((D, TRI), BF), pltpu.VMEM((HALF, D), BF), pltpu.VMEM((2, t, D), BF),
            pltpu.VMEM((2, t, HALF), BF), pltpu.VMEM((8, t), F32), pltpu.VMEM((2, HALF, t), F32),
            pltpu.VMEM((2, 2 * t, HALF), F32), pltpu.VMEM((2, 2 * t, HALF), F32),
            pltpu.VMEM((2, t, D), BF), pltpu.VMEM((2, t, D), BF), pltpu.VMEM((2, t, TRI), BF),
            pltpu.VMEM((t, D), F32), pltpu.VMEM((t, D), BF), pltpu.VMEM((t, D), BF),
            pltpu.VMEM((HALF, 2 * D), F32), pltpu.VMEM((HALF, 2 * D), BF),
            pltpu.VMEM((HALF, 2 * D), BF),
        ],
        3, 6, 10 << 30, (mg, h, wa, scales, tables, bias, *saved),
    )


class Moves:
    def __init__(self, dp):
        self.dp = dp
        self.d = lax.axis_index("dp")
        s = lax.axis_index("seq")
        self.s, self.x, self.c = s, s // 2, s % 2
        half = dp // 2
        ids = [(d, s) for d in range(dp) for s in range(SEQ)]
        self.tri = []
        for r in range(2):
            for j in range(3):
                perm = []
                for d, s in ids:
                    b = (3 * s + j) % 4
                    to = (2 * (d % half) + (r ^ (b % 2)), 2 * (b // 2) + d // half)
                    perm.append((d * SEQ + s, to[0] * SEQ + to[1]))
                self.tri.append(perm)
        self.out = []
        for r in range(2):
            perm = []
            for d, s in ids:
                to = (2 * (d % half) + (r ^ (s % 2)), 2 * (d // half) + s // 2)
                perm.append((d * SEQ + s, to[0] * SEQ + to[1]))
            self.out.append(perm)
        self.shr = []
        for k in range(4):
            perm = []
            for d, s in ids:
                to = (4 * (d % (dp // 4)) + (k + s) % 4, d // (dp // 4))
                perm.append((d * SEQ + s, to[0] * SEQ + to[1]))
            self.shr.append(perm)

    def send(self, piece, perm, back):
        if back:
            perm = [(b, a) for a, b in perm]
        return lax.ppermute(piece, ("dp", "seq"), perm)

    @staticmethod
    def pick(pieces, index):
        return lax.dynamic_index_in_dim(jnp.stack(pieces), index, 0, keepdims=False)

    def tri_out(self, low):
        n, rows, _ = low.shape
        halves = low.reshape(n, 2, rows // 2, 3, 192)
        got = []
        for r in range(2):
            for j in range(3):
                which = r ^ (((3 * self.s + j) % 4) % 2)
                piece = lax.dynamic_index_in_dim(halves[:, :, :, j], which, 1, keepdims=False)
                got.append(self.send(piece, self.tri[3 * r + j], False))
        parts = []
        for t in range(3):
            for bb in range(2):
                r, j = bb ^ (self.d % 2), (t + 2 * self.x + bb) % 3
                parts.append(self.pick(got, 3 * r + j))
        return jnp.concatenate(parts, axis=-1)

    def tri_back(self, grad):
        n, rows, _ = grad.shape
        got = []
        for r in range(2):
            for j in range(3):
                bb = (self.d % 2) ^ r
                t = (j - (2 * self.x + bb)) % 3
                piece = lax.dynamic_slice_in_dim(grad, (2 * t + bb) * 192, 192, 2)
                got.append(self.send(piece, self.tri[3 * r + j], True))
        cols = []
        for j in range(3):
            two = []
            for hh in range(2):
                r = hh ^ (((3 * self.s + j) % 4) % 2)
                two.append(self.pick([got[j], got[3 + j]], r))
            cols.append(jnp.concatenate(two, axis=1))
        return jnp.concatenate(cols, axis=-1)

    def out_out(self, low):
        n, rows, _ = low.shape
        halves = low.reshape(n, 2, rows // 2, 192)
        got = [
            self.send(
                lax.dynamic_index_in_dim(halves, r ^ (self.s % 2), 1, keepdims=False), self.out[r], False
            )
            for r in range(2)
        ]
        return jnp.concatenate([self.pick(got, u ^ (self.d % 2)) for u in range(2)], axis=-1)

    def out_back(self, grad):
        got = []
        for r in range(2):
            u = r ^ (self.d % 2)
            got.append(self.send(lax.dynamic_slice_in_dim(grad, u * 192, 192, 2), self.out[r], True))
        return jnp.concatenate([self.pick(got, hh ^ (self.s % 2)) for hh in range(2)], axis=1)

    def shr_out(self, low):
        n, rows, _ = low.shape
        subs = low.reshape(n, 4, rows // 4, 192)
        got = [
            self.send(
                lax.dynamic_index_in_dim(subs, (k + self.s) % 4, 1, keepdims=False), self.shr[k], False
            )
            for k in range(4)
        ]
        return jnp.concatenate([self.pick(got, (self.d - s) % 4) for s in range(4)], axis=-1)

    def shr_back(self, grad):
        got = []
        for k in range(4):
            piece = lax.dynamic_slice_in_dim(grad, ((self.d - k) % 4) * 192, 192, 2)
            got.append(self.send(piece, self.shr[k], True))
        return jnp.concatenate([self.pick(got, (sub - self.s) % 4) for sub in range(4)], axis=1)


def tables_here(segments, t, x, c):
    group = segments.shape[0]
    whole = segments[0] == segments[group - 1]
    place_in_half = c * t + jnp.arange(t, dtype=jnp.int32)
    second = jnp.where(whole, group // 2, 0).astype(jnp.int32)
    positions = jnp.stack([place_in_half, place_in_half + second]).astype(F32)
    lane = jnp.arange(128, dtype=jnp.int32)
    inverse = 1.0 / ROTARY_BASE ** ((lane % (HD // 2)).astype(F32) * (2.0 / HD))
    angles = positions[:, :, None] * inverse[None, None, :]
    sign = jnp.where(lane % HD < HD // 2, -1.0, 1.0).astype(F32)
    tables = jnp.concatenate([jnp.cos(angles), jnp.sin(angles) * sign], axis=-1)
    bias = jnp.where(whole, 0.0, MASKED).astype(F32).reshape(1)
    return tables, bias


def local(dp, *args):
    (residual, cotangent, segments) = args[:3]
    (
        triple_weight, triple_moment, triple_square, triple_shadow,
        output_weight, output_moment, output_square, output_shadow,
        expand_weight, expand_moment, expand_square, expand_shadow,
        shrink_weight, shrink_moment, shrink_square, shrink_shadow,
        scales_weight, scales_moment, scales_square, scales_shadow,
    ) = args[3:]
    moves = Moves(dp)
    t = residual.shape[0]
    d, s = lax.axis_index("dp"), lax.axis_index("seq")
    tables, bias = tables_here(segments, t, moves.x, moves.c)

    scales_all = lax.psum(
        lax.dynamic_update_slice(
            jnp.zeros((LAYERS, 4, D), F32), scales_weight.astype(BF).astype(F32), (0, s, d * (D // dp))
        ),
        ("dp", "seq"),
    )
    tri = moves.tri_out(triple_weight.astype(BF))
    out = moves.out_out(output_weight.astype(BF))
    shr = moves.shr_out(shrink_weight.astype(BF))
    attend_parts = jnp.concatenate([tri, out], axis=-1)
    feed_parts = jnp.concatenate([expand_weight.astype(BF), shr], axis=-1)
    gather = functools.partial(lax.all_gather, axis_name="dp", axis=0, tiled=True)
    wa, wf = [], []
    for layer in range(LAYERS):
        wa.append(gather(attend_parts[layer]))
        wf.append(gather(feed_parts[layer]))

    stream = residual
    kept = []
    for layer in range(LAYERS):
        scales = scales_all[layer]
        middle, *attend_saved = attend_fwd(stream, wa[layer], scales, tables, bias)
        following, *feed_saved = feed_fwd(middle, wf[layer], scales)
        kept.append((stream, middle, attend_saved, feed_saved))
        stream = following

    g = cotangent
    attend_grads, feed_grads, scale_grads = [None] * LAYERS, [None] * LAYERS, [None] * LAYERS
    scatter = functools.partial(lax.psum_scatter, axis_name="dp", scatter_dimension=0, tiled=True)
    for layer in reversed(range(LAYERS)):
        scales = scales_all[layer]
        h, middle, attend_saved, feed_saved = kept[layer]
        mg, feed_grad, rows_b = feed_bwd(g, middle, wf[layer], scales, *feed_saved)
        feed_grads[layer] = scatter(feed_grad).astype(F32)
        g, attend_grad, rows_a = attend_bwd(mg, h, wa[layer], scales, tables, bias, attend_saved)
        attend_grads[layer] = scatter(attend_grad).astype(F32)
        scale_grads[layer] = jnp.concatenate([rows_a, rows_b], axis=0)

    scale_grad = lax.psum(jnp.stack(scale_grads), ("dp", "seq"))
    own_scale = lax.dynamic_slice(scale_grad, (0, s, d * (D // dp)), (LAYERS, 1, D // dp))
    squares = jnp.sum(own_scale * own_scale)
    for part in (*attend_grads, *feed_grads):
        squares = squares + jnp.sum(part * part)
    grad_norm = jnp.sqrt(lax.psum(squares, ("dp", "seq")))
    limit = CLIP_RATIO * math.sqrt(float(LAYERS * (4 * D * D + 2 * D * FF + 4 * D)))
    factor = limit / (grad_norm + 1e-06)

    attend_grad, feed_grad = jnp.stack(attend_grads).astype(BF), jnp.stack(feed_grads).astype(BF)
    triple_grad = moves.tri_back(attend_grad[:, :, :TRI]).astype(F32)
    output_grad = moves.out_back(attend_grad[:, :, TRI:]).astype(F32)
    expand_grad = feed_grad[:, :, :D].astype(F32)
    shrink_grad = moves.shr_back(feed_grad[:, :, D:]).astype(F32)

    results = [stream, g, grad_norm]
    for weight, moment, square, shadow, grad, rate in (
        (triple_weight, triple_moment, triple_square, triple_shadow, triple_grad, RATE_FACTOR / math.sqrt(D)),
        (output_weight, output_moment, output_square, output_shadow, output_grad, RATE_FACTOR / math.sqrt(D // 16)),
        (expand_weight, expand_moment, expand_square, expand_shadow, expand_grad, RATE_FACTOR / math.sqrt(D)),
        (shrink_weight, shrink_moment, shrink_square, shrink_shadow, shrink_grad, RATE_FACTOR / math.sqrt(FF)),
        (scales_weight, scales_moment, scales_square, scales_shadow, own_scale, SCALES_RATE),
    ):
        results.extend(adam_step(weight, moment, square, shadow, grad * factor, rate))
    return tuple(results)


def solution(mesh):
    token = P(("dp", "seq"), None)
    weight = P(None, "dp", "seq")
    scale = P(None, "seq", "dp")
    return jax.shard_map(
        functools.partial(local, mesh.shape["dp"]),
        mesh=mesh,
        in_specs=(token, token, P("dp"), *([weight] * 16), *([scale] * 4)),
        out_specs=(token, token, P(), *([weight] * 16), *([scale] * 4)),
        check_vma=False,
    )
```

```python
import functools
import math

import jax
import jax.numpy as jnp
from jax import lax
from jax.experimental import pallas as pl
from jax.experimental.pallas import tpu as pltpu
from jax.sharding import PartitionSpec as P

D = 768
FF = 3072
HD = 64
LAYERS = 2
STEP = 2
SEQ = 4

EPSILON = 1e-05
ROTARY_BASE = 10000.0
BETA_ONE = 0.9
BETA_TWO = 0.999
ADAM_EPSILON = 1e-08
DECAY_RATE = 0.01
SHADOW_RATE = 0.99
CLIP_RATIO = 0.5
RATE_FACTOR = 1.5
SCALES_RATE = 0.6
MASKED = -1000000000.0

HALF = D // 2
TRI = 3 * HALF
HID = FF // 2
BF = jnp.bfloat16
F32 = jnp.float32
MESH = pl.DeviceIdType.MESH
VMEM_BYTES = 60 << 20


def adam_step(weight, moment, square, shadow, gradient, step_rate):
    shadow_decay = min(SHADOW_RATE, (1.0 + STEP) / (10.0 + STEP))
    momentum = BETA_ONE * moment + (1.0 - BETA_ONE) * gradient
    variance = BETA_TWO * square + (1.0 - BETA_TWO) * gradient * gradient
    corrected = (
        momentum
        / (1.0 - BETA_ONE**STEP)
        / (jnp.sqrt(variance / (1.0 - BETA_TWO**STEP)) + ADAM_EPSILON)
    )
    updated = weight - step_rate * (corrected + DECAY_RATE * weight)
    average = shadow_decay * shadow + (1.0 - shadow_decay) * updated
    return (updated, momentum, variance, average)


def nn(a, b):
    return lax.dot_general(a, b, (((1,), (0,)), ((), ())), preferred_element_type=F32)


def nt(a, b):
    return lax.dot_general(a, b, (((1,), (1,)), ((), ())), preferred_element_type=F32)


def tn(a, b):
    return lax.dot_general(a, b, (((0,), (0,)), ((), ())), preferred_element_type=F32)


def place():
    s = lax.axis_index("seq")
    x = lax.div(s, 2)
    c = lax.rem(s, 2)
    return lax.axis_index("dp"), x, c, lax.rem(s + 2, SEQ), s + 1 - 2 * c


def greet(d, peer, sib):
    barrier = pltpu.get_barrier_semaphore()
    for other in (peer, sib):
        pl.semaphore_signal(barrier, inc=1, device_id=(d, other), device_id_type=MESH)
    pl.semaphore_wait(barrier, 2)


def rows_of(c, n):
    return pl.ds(pl.multiple_of(c * n, n), n)


class Copies:
    def __init__(self, lsem, ssem, rsem, d):
        self.lsem, self.ssem, self.rsem, self.d = lsem, ssem, rsem, d
        self.n_local = 0
        self.n_remote = 0

    def local(self, src, dst):
        copy = pltpu.make_async_copy(src, dst, self.lsem.at[self.n_local])
        self.n_local += 1
        copy.start()
        return copy

    def push(self, src, dst, to):
        copy = pltpu.make_async_remote_copy(
            src_ref=src,
            dst_ref=dst,
            send_sem=self.ssem.at[self.n_remote],
            recv_sem=self.rsem.at[self.n_remote],
            device_id=(self.d, to),
            device_id_type=MESH,
        )
        self.n_remote += 1
        copy.start()
        return copy


def norm_stats(values):
    center = values - jnp.mean(values, axis=-1, keepdims=True)
    spread = jnp.mean(center * center, axis=-1, keepdims=True)
    scale = lax.rsqrt(spread + EPSILON)
    return center * scale, scale


def norm_back(values, gain, dy):
    xhat, scale = norm_stats(values)
    u = gain * dy
    du = u - jnp.mean(u, axis=-1, keepdims=True)
    back = scale * (du - xhat * jnp.mean(u * xhat, axis=-1, keepdims=True))
    rows = jnp.concatenate(
        [jnp.sum(xhat * dy, axis=0, keepdims=True), jnp.sum(dy, axis=0, keepdims=True)], axis=0
    )
    return back, rows


def turn(chunk, cosine, sine):
    lane = lax.broadcasted_iota(jnp.int32, chunk.shape, 1)
    swapped = jnp.where(
        lax.rem(lane, HD) < HD // 2, pltpu.roll(chunk, 128 - HD // 2, 1), pltpu.roll(chunk, HD // 2, 1)
    )
    return chunk * cosine + swapped * sine


def half_of(pair, which):
    lane = lax.broadcasted_iota(jnp.int32, pair.shape, 1)
    keep = (lane < HD) if which == 0 else (lane >= HD)
    return jnp.where(keep, pair, jnp.zeros_like(pair))


def attend_fwd_kernel(
    h, wa, sc, cs, bias, mid, na_o, q_o, k_o, v_o, ctx_o, lse_o,
    wt, wo, na, q, k, v, ctxt, ctx, lse, psend, precv, lsem, ssem, rsem,
):
    d, x, c, peer, sib = place()
    y = 1 - x
    rows = h.shape[0]
    copies = Copies(lsem, ssem, rsem, d)
    greet(d, peer, sib)
    wt_own, wo_own = wt.at[rows_of(c, HALF), :], wo.at[:, rows_of(c, HALF)]
    tri_part, out_part = wa.at[:, pl.ds(0, TRI)], wa.at[:, pl.ds(TRI, HALF)]
    tri_sent = copies.push(tri_part, wt_own, sib)
    tri_local = copies.local(tri_part, wt_own)
    out_sent = copies.push(out_part, wo_own, sib)
    out_local = copies.local(out_part, wo_own)
    xhat, _ = norm_stats(h[...])
    na[x] = (xhat * sc[0:1, :] + sc[1:2, :]).astype(BF)
    na_sent = copies.push(na.at[x], na.at[x], peer)
    tri_local.wait()
    tri_sent.wait()

    def project(block):
        cosine, sine = cs[block, :, 0:128], cs[block, :, 128:256]
        for j in range(9):
            part = nn(na[block], wt[:, 128 * j : 128 * j + 128])
            lanes = pl.ds(128 * (j % 3), 128)
            if j < 3:
                q[block, :, lanes] = (turn(part, cosine, sine) * HD**-0.5).astype(BF)
            elif j < 6:
                k[block, rows_of(c, rows), lanes] = turn(part, cosine, sine).astype(BF)
            else:
                v[block, rows_of(c, rows), lanes] = part.astype(BF)

    def share(block):
        mine = (block, rows_of(c, rows))
        return [copies.push(k.at[mine], k.at[mine], sib), copies.push(v.at[mine], v.at[mine], sib)]

    project(x)
    shared = share(x)
    na_sent.wait()
    project(y)
    shared += share(y)
    out_local.wait()
    out_sent.wait()
    for copy in shared:
        copy.wait()

    def attend(block):
        other = 1 - block

        def pair_step(p, carry):
            lanes = pl.ds(pl.multiple_of(p * 128, 128), 128)
            q_pair = q[block, :, lanes]
            k_same, k_cross = k[block, :, lanes], k[other, :, lanes]
            v_same, v_cross = v[block, :, lanes], v[other, :, lanes]
            for which in range(2):
                q_head = half_of(q_pair, which)
                s_same = nt(k_same, q_head)
                s_cross = nt(k_cross, q_head) + bias[0]
                top = jnp.maximum(
                    jnp.max(s_same, axis=0, keepdims=True), jnp.max(s_cross, axis=0, keepdims=True)
                )
                e_same = jnp.exp(s_same - top)
                e_cross = jnp.exp(s_cross - top)
                total = jnp.sum(e_same, axis=0, keepdims=True) + jnp.sum(
                    e_cross, axis=0, keepdims=True
                )
                mixed = tn(v_same, e_same.astype(BF)) + tn(v_cross, e_cross.astype(BF))
                head = pl.ds(pl.multiple_of(p * 128 + which * HD, HD), HD)
                ctxt[head, :] = mixed[which * HD : which * HD + HD, :] / total
                lse[block, pl.ds(2 * p + which, 1), :] = top + jnp.log(total)
            return carry

        lax.fori_loop(0, HALF // 128, pair_step, 0)
        ctx[block] = ctxt[...].T.astype(BF)
        return nn(ctx[block], wo[...])

    psend[...] = attend(y).astype(BF)
    part_sent = copies.push(psend, precv, peer)
    mid[...] = h[...] + attend(x)
    saves = [
        copies.local(a, b)
        for a, b in ((na, na_o), (q, q_o), (k, k_o), (v, v_o), (ctx, ctx_o), (lse, lse_o))
    ]
    part_sent.wait()
    mid[...] = mid[...] + precv[...].astype(F32)
    for copy in saves:
        copy.wait()


def hbm():
    return pl.BlockSpec(memory_space=pl.ANY)


def vmem():
    return pl.BlockSpec(memory_space=pltpu.VMEM)


def call(kernel, name, number, ins, outs, out_shape, scratch, n_local, n_remote, flops, args):
    return pl.pallas_call(
        kernel,
        name=name,
        out_shape=out_shape,
        in_specs=ins,
        out_specs=outs,
        scratch_shapes=[
            *scratch,
            pltpu.SemaphoreType.DMA((n_local,)),
            pltpu.SemaphoreType.DMA((n_remote,)),
            pltpu.SemaphoreType.DMA((n_remote,)),
        ],
        cost_estimate=pl.CostEstimate(flops=flops, bytes_accessed=16 << 20, transcendentals=0),
        compiler_params=pltpu.CompilerParams(
            collective_id=number, has_side_effects=True, vmem_limit_bytes=VMEM_BYTES
        ),
    )(*args)


def sds(shape, dtype):
    return jax.ShapeDtypeStruct(shape, dtype)


def attend_fwd(h, wa, scales, tables, bias):
    t = h.shape[0]
    return call(
        attend_fwd_kernel, "attend_fwd", 0,
        [vmem(), hbm(), vmem(), vmem(), pl.BlockSpec(memory_space=pltpu.SMEM)],
        [vmem()] + [hbm()] * 6,
        [
            sds((t, D), F32), sds((2, t, D), BF), sds((2, t, HALF), BF), sds((2, 2 * t, HALF), BF),
            sds((2, 2 * t, HALF), BF), sds((2, t, HALF), BF), sds((2, 8, t), F32),
        ],
        [
            pltpu.VMEM((D, TRI), BF), pltpu.VMEM((HALF, D), BF), pltpu.VMEM((2, t, D), BF),
            pltpu.VMEM((2, t, HALF), BF), pltpu.VMEM((2, 2 * t, HALF), BF),
            pltpu.VMEM((2, 2 * t, HALF), BF), pltpu.VMEM((HALF, t), F32),
            pltpu.VMEM((2, t, HALF), BF), pltpu.VMEM((2, 8, t), F32),
            pltpu.VMEM((t, D), BF), pltpu.VMEM((t, D), BF),
        ],
        8, 8, 6 << 30, (h, wa, scales, tables, bias),
    )


def gelu_parts(hidden):
    phi_cap = 0.5 * (1.0 + lax.erf(hidden * math.sqrt(0.5)))
    density = jnp.exp(-0.5 * hidden * hidden) * (1.0 / math.sqrt(2.0 * math.pi))
    return hidden * phi_cap, phi_cap + hidden * density


def feed_fwd_kernel(
    mid, wf, sc, h_next, nb_o, act_o, slope_o,
    we, ws, nb, act, slope, psend, precv, lsem, ssem, rsem,
):
    d, x, c, peer, sib = place()
    y = 1 - x
    copies = Copies(lsem, ssem, rsem, d)
    greet(d, peer, sib)
    xhat, _ = norm_stats(mid[...])
    nb[x] = (xhat * sc[2:3, :] + sc[3:4, :]).astype(BF)
    nb_sent = copies.push(nb.at[x], nb.at[x], peer)
    we_own, ws_own = we.at[:, rows_of(c, D)], ws.at[rows_of(c, D), :]
    exp_part, shr_part = wf.at[:, pl.ds(0, D)], wf.at[:, pl.ds(D, D)]
    weights = [
        copies.local(exp_part, we_own),
        copies.push(exp_part, we_own, sib),
        copies.local(shr_part, ws_own),
        copies.push(shr_part, ws_own, sib),
    ]
    for copy in weights:
        copy.wait()

    def feed(block):
        def step(i, carry):
            lanes = pl.ds(pl.multiple_of(i * 256, 256), 256)
            value, rate = gelu_parts(nn(nb[block], we[:, lanes]))
            act[block, :, lanes] = value.astype(BF)
            slope[block, :, lanes] = rate.astype(BF)
            return carry

        lax.fori_loop(0, HID // 256, step, 0)
        return nn(act[block], ws[...])

    h_next[...] = mid[...] + feed(x)
    nb_sent.wait()
    psend[...] = feed(y).astype(BF)
    part_sent = copies.push(psend, precv, peer)
    saves = [copies.local(a, b) for a, b in ((nb, nb_o), (act, act_o), (slope, slope_o))]
    part_sent.wait()
    h_next[...] = h_next[...] + precv[...].astype(F32)
    for copy in saves:
        copy.wait()


def feed_fwd(mid, wf, scales):
    t = mid.shape[0]
    return call(
        feed_fwd_kernel, "feed_fwd", 1,
        [vmem(), hbm(), vmem()],
        [vmem()] + [hbm()] * 3,
        [sds((t, D), F32), sds((2, t, D), BF), sds((2, t, HID), BF), sds((2, t, HID), BF)],
        [
            pltpu.VMEM((D, HID), BF), pltpu.VMEM((HID, D), BF), pltpu.VMEM((2, t, D), BF),
            pltpu.VMEM((2, t, HID), BF), pltpu.VMEM((2, t, HID), BF),
            pltpu.VMEM((t, D), BF), pltpu.VMEM((t, D), BF),
        ],
        5, 4, 5 << 30, (mid, wf, scales),
    )


def feed_bwd_kernel(
    g, mid, wf, sc, nb_h, act_h, slope_h, mid_grad, wg_o, rows_o,
    we, ws, nb, act, slope, gl, hg, part, psend, precv, gown, gsend, grecv, lsem, ssem, rsem,
):
    d, x, c, peer, sib = place()
    y = 1 - x
    t = g.shape[0]
    copies = Copies(lsem, ssem, rsem, d)
    greet(d, peer, sib)
    gl[x] = g[...].astype(BF)
    g_sent = copies.push(gl.at[x], gl.at[x], peer)
    we_own, ws_own = we.at[:, rows_of(c, D)], ws.at[rows_of(c, D), :]
    exp_part, shr_part = wf.at[:, pl.ds(0, D)], wf.at[:, pl.ds(D, D)]
    weights = [
        copies.local(shr_part, ws_own),
        copies.push(shr_part, ws_own, sib),
        copies.local(exp_part, we_own),
        copies.push(exp_part, we_own, sib),
        copies.local(slope_h, slope),
        copies.local(act_h, act),
        copies.local(nb_h, nb),
    ]
    for copy in weights:
        copy.wait()

    def back(block):
        def step(i, carry):
            lanes = pl.ds(pl.multiple_of(i * 256, 256), 256)
            pulled = nt(gl[block], ws[lanes, :])
            hg[block, :, lanes] = (pulled * slope[block, :, lanes].astype(F32)).astype(BF)
            return carry

        lax.fori_loop(0, HID // 256, step, 0)
        return nt(hg[block], we[...])

    part[...] = back(x)
    g_sent.wait()
    psend[...] = back(y).astype(BF)
    part_sent = copies.push(psend, precv, peer)

    gl_all = gl[...].reshape(2 * t, D)
    nb_all = nb[...].reshape(2 * t, D)

    def grads(which, store):
        def step(i, carry):
            at = pl.ds(pl.multiple_of(i * 256, 256), 256)
            off = pl.ds(pl.multiple_of(which * D + i * 256, 256), 256)
            hg_part = hg[:, :, off].reshape(2 * t, 256)
            act_part = act[:, :, off].reshape(2 * t, 256)
            store(0, at, tn(nb_all, hg_part))
            store(1, at, tn(act_part, gl_all))
            return carry

        lax.fori_loop(0, D // 256, step, 0)

    def to_send(kind, at, value):
        if kind == 0:
            gsend[:, at] = value.astype(BF)
        else:
            gsend[at, pl.ds(D, D)] = value.astype(BF)

    def to_keep(kind, at, value):
        if kind == 0:
            gown[:, at] = value
        else:
            gown[at, pl.ds(D, D)] = value

    grads(1 - c, to_send)
    grad_sent = copies.push(gsend, grecv, sib)
    grads(c, to_keep)
    part_sent.wait()
    dy = part[...] + precv[...].astype(F32)
    back_mid, rows = norm_back(mid[...], sc[2:3, :], dy)
    mid_grad[...] = g[...] + back_mid
    rows_o[...] = rows
    grad_sent.wait()
    gsend[...] = (gown[...] + grecv[...].astype(F32)).astype(BF)
    copies.local(gsend, wg_o).wait()


def feed_bwd(g, mid, wf, scales, nb, act, slope):
    t = g.shape[0]
    return call(
        feed_bwd_kernel, "feed_bwd", 2,
        [vmem(), vmem(), hbm(), vmem(), hbm(), hbm(), hbm()],
        [vmem(), hbm(), vmem()],
        [sds((t, D), F32), sds((D, 2 * D), BF), sds((2, D), F32)],
        [
            pltpu.VMEM((D, HID), BF), pltpu.VMEM((HID, D), BF), pltpu.VMEM((2, t, D), BF),
            pltpu.VMEM((2, t, HID), BF), pltpu.VMEM((2, t, HID), BF), pltpu.VMEM((2, t, D), BF),
            pltpu.VMEM((2, t, HID), BF), pltpu.VMEM((t, D), F32), pltpu.VMEM((t, D), BF),
            pltpu.VMEM((t, D), BF), pltpu.VMEM((D, 2 * D), F32), pltpu.VMEM((D, 2 * D), BF),
            pltpu.VMEM((D, 2 * D), BF),
        ],
        6, 5, 10 << 30, (g, mid, wf, scales, nb, act, slope),
    )


def attend_bwd_kernel(
    mg, h, wa, sc, cs, bias, na, q, k, v, ctx, lse, g_prev, wg_o, rows_o,
    wt, wo, ml, cg, delta, dqt, dk, dv, kvsend, kvrecv, pg, part, psend, precv,
    gown, gsend, grecv, lsem, ssem, rsem,
):
    d, x, c, peer, sib = place()
    y = 1 - x
    t = mg.shape[0]
    copies = Copies(lsem, ssem, rsem, d)
    greet(d, peer, sib)
    ml[x] = mg[...].astype(BF)
    ml_sent = copies.push(ml.at[x], ml.at[x], peer)
    wt_own, wo_own = wt.at[rows_of(c, HALF), :], wo.at[:, rows_of(c, HALF)]
    tri_part, out_part = wa.at[:, pl.ds(0, TRI)], wa.at[:, pl.ds(TRI, HALF)]
    out_moves = [copies.local(out_part, wo_own), copies.push(out_part, wo_own, sib)]
    tri_moves = [copies.local(tri_part, wt_own), copies.push(tri_part, wt_own, sib)]
    dk[...] = jnp.zeros_like(dk)
    dv[...] = jnp.zeros_like(dv)
    for copy in out_moves:
        copy.wait()

    def attend(block):
        other = 1 - block
        pulled = nt(ml[block], wo[...])
        cg[block] = pulled.astype(BF)
        weighed = (cg[block].astype(F32) * ctx[block].astype(F32)).T
        for head in range(HALF // HD):
            delta[head : head + 1, :] = jnp.sum(
                weighed[head * HD : head * HD + HD, :], axis=0, keepdims=True
            )

        def pair_step(p, carry):
            lanes = pl.ds(pl.multiple_of(p * 128, 128), 128)
            q_pair, cg_pair = q[block, :, lanes], cg[block, :, lanes]
            for which in range(2):
                q_head, cg_head = half_of(q_pair, which), half_of(cg_pair, which)
                row = pl.ds(2 * p + which, 1)
                total, dots = lse[block, row, :], delta[row, :]
                turned = None
                for side in (block, other):
                    k_pair, v_pair = k[side, :, lanes], v[side, :, lanes]
                    scores = nt(k_pair, q_head)
                    if side is other:
                        scores = scores + bias[0]
                    probs = jnp.exp(scores - total)
                    score_grad = (probs * (nt(v_pair, cg_head) - dots)).astype(BF)
                    dv[side, :, lanes] += nn(probs.astype(BF), cg_head)
                    dk[side, :, lanes] += nn(score_grad, q_head)
                    piece = tn(k_pair, score_grad)
                    turned = piece if turned is None else turned + piece
                head = pl.ds(pl.multiple_of(p * 128 + which * HD, HD), HD)
                dqt[block, head, :] = turned[which * HD : which * HD + HD, :] * HD**-0.5
            return carry

        lax.fori_loop(0, HALF // 128, pair_step, 0)

    attend(x)
    ml_sent.wait()
    attend(y)
    theirs, mine = rows_of(1 - c, t), rows_of(c, t)
    for side in range(2):
        kvsend[side, :, pl.ds(0, HALF)] = dk[side, theirs, :].astype(BF)
        kvsend[side, :, pl.ds(HALF, HALF)] = dv[side, theirs, :].astype(BF)
    kv_sent = copies.push(kvsend, kvrecv, sib)

    def unturn(block, j, value):
        cosine, sine = cs[block, :, 0:128], cs[block, :, 128:256]
        rounded = value.astype(BF).astype(F32)
        pg[block, :, pl.ds(128 * j, 128)] = turn(rounded, cosine, -sine).astype(BF)

    for side in range(2):
        for j in range(3):
            unturn(side, j, dqt[side, 128 * j : 128 * j + 128, :].T)
    kv_sent.wait()
    for side in range(2):
        for j in range(3):
            at = pl.ds(128 * j, 128)
            unturn(side, 3 + j, dk[side, mine, at] + kvrecv[side, :, at].astype(F32))
            pg[side, :, pl.ds(D + 128 * j, 128)] = (
                dv[side, mine, at] + kvrecv[side, :, pl.ds(HALF + 128 * j, 128)].astype(F32)
            ).astype(BF)
    for copy in tri_moves:
        copy.wait()
    psend[...] = nt(pg[y], wt[...]).astype(BF)
    part_sent = copies.push(psend, precv, peer)
    part[...] = nt(pg[x], wt[...])

    ml_all = ml[...].reshape(2 * t, D)
    na_all = na[...].reshape(2 * t, D)
    ctx_all = ctx[...].reshape(2 * t, HALF)

    def grads(which, store):
        def step(i, carry):
            off = pl.ds(pl.multiple_of(which * HALF + i * 128, 128), 128)
            at = pl.ds(pl.multiple_of(i * 128, 128), 128)
            store(0, at, tn(na[:, :, off].reshape(2 * t, 128), pg[...].reshape(2 * t, TRI)))
            store(1, at, tn(ctx_all, ml[:, :, off].reshape(2 * t, 128)))
            return carry

        lax.fori_loop(0, HALF // 128, step, 0)

    def to_send(kind, at, value):
        if kind == 0:
            gsend[at, pl.ds(0, TRI)] = value.astype(BF)
        else:
            gsend[:, pl.ds(pl.multiple_of(TRI + at.start, 128), 128)] = value.astype(BF)

    def to_keep(kind, at, value):
        if kind == 0:
            gown[at, pl.ds(0, TRI)] = value
        else:
            gown[:, pl.ds(pl.multiple_of(TRI + at.start, 128), 128)] = value

    grads(1 - c, to_send)
    grad_sent = copies.push(gsend, grecv, sib)
    grads(c, to_keep)
    part_sent.wait()
    dy = part[...] + precv[...].astype(F32)
    back, rows = norm_back(h[...], sc[0:1, :], dy)
    g_prev[...] = mg[...] + back
    rows_o[...] = rows
    grad_sent.wait()
    gsend[...] = (gown[...] + grecv[...].astype(F32)).astype(BF)
    copies.local(gsend, wg_o).wait()


def attend_bwd(mg, h, wa, scales, tables, bias, saved):
    t = mg.shape[0]
    return call(
        attend_bwd_kernel, "attend_bwd", 3,
        [vmem(), vmem(), hbm(), vmem(), vmem(), pl.BlockSpec(memory_space=pltpu.SMEM)] + [vmem()] * 6,
        [vmem(), hbm(), vmem()],
        [sds((t, D), F32), sds((HALF, 2 * D), BF), sds((2, D), F32)],
        [
            pltpu.VMEM((D, TRI), BF), pltpu.VMEM((HALF, D), BF), pltpu.VMEM((2, t, D), BF),
            pltpu.VMEM((2, t, HALF), BF), pltpu.VMEM((8, t), F32), pltpu.VMEM((2, HALF, t), F32),
            pltpu.VMEM((2, 2 * t, HALF), F32), pltpu.VMEM((2, 2 * t, HALF), F32),
            pltpu.VMEM((2, t, D), BF), pltpu.VMEM((2, t, D), BF), pltpu.VMEM((2, t, TRI), BF),
            pltpu.VMEM((t, D), F32), pltpu.VMEM((t, D), BF), pltpu.VMEM((t, D), BF),
            pltpu.VMEM((HALF, 2 * D), F32), pltpu.VMEM((HALF, 2 * D), BF),
            pltpu.VMEM((HALF, 2 * D), BF),
        ],
        3, 6, 10 << 30, (mg, h, wa, scales, tables, bias, *saved),
    )


def feed_back_kernel(
    g, mid, we_h, ws_h, sc, nb_h, act_h, slope_h, mid_grad, wg_o, rows_o,
    we, ws, nb, act, slope, gl, hg, part, psend, precv, gown, gsend, grecv, lsem, ssem, rsem,
):
    d, x, c, peer, sib = place()
    y = 1 - x
    t = g.shape[0]
    copies = Copies(lsem, ssem, rsem, d)
    greet(d, peer, sib)
    gl[x] = g[...].astype(BF)
    g_sent = copies.push(gl.at[x], gl.at[x], peer)
    we_own, ws_own = we.at[:, rows_of(c, D)], ws.at[rows_of(c, D), :]
    weights = [
        copies.local(ws_h, ws),
        copies.local(we_h, we),
        copies.local(slope_h, slope),
        copies.local(act_h, act),
        copies.local(nb_h, nb),
    ]
    for copy in weights:
        copy.wait()

    def back(block):
        def step(i, carry):
            lanes = pl.ds(pl.multiple_of(i * 256, 256), 256)
            pulled = nt(gl[block], ws[lanes, :])
            hg[block, :, lanes] = (pulled * slope[block, :, lanes].astype(F32)).astype(BF)
            return carry

        lax.fori_loop(0, HID // 256, step, 0)
        return nt(hg[block], we[...])

    part[...] = back(x)
    g_sent.wait()
    psend[...] = back(y).astype(BF)
    part_sent = copies.push(psend, precv, peer)

    gl_all = gl[...].reshape(2 * t, D)
    nb_all = nb[...].reshape(2 * t, D)

    def grads(which, store):
        def step(i, carry):
            at = pl.ds(pl.multiple_of(i * 256, 256), 256)
            off = pl.ds(pl.multiple_of(which * D + i * 256, 256), 256)
            hg_part = hg[:, :, off].reshape(2 * t, 256)
            act_part = act[:, :, off].reshape(2 * t, 256)
            store(0, at, tn(nb_all, hg_part))
            store(1, at, tn(act_part, gl_all))
            return carry

        lax.fori_loop(0, D // 256, step, 0)

    def to_send(kind, at, value):
        if kind == 0:
            gsend[:, at] = value.astype(BF)
        else:
            gsend[at, pl.ds(D, D)] = value.astype(BF)

    def to_keep(kind, at, value):
        if kind == 0:
            gown[:, at] = value
        else:
            gown[at, pl.ds(D, D)] = value

    grads(1 - c, to_send)
    grad_sent = copies.push(gsend, grecv, sib)
    grads(c, to_keep)
    part_sent.wait()
    dy = part[...] + precv[...].astype(F32)
    back_mid, rows = norm_back(mid[...], sc[2:3, :], dy)
    mid_grad[...] = g[...] + back_mid
    rows_o[...] = rows
    grad_sent.wait()
    gsend[...] = (gown[...] + grecv[...].astype(F32)).astype(BF)
    copies.local(gsend, wg_o).wait()


def feed_back(g, mid, we, ws, scales, nb, act, slope):
    t = g.shape[0]
    return call(
        feed_back_kernel, "feed_back", 5,
        [vmem(), vmem(), hbm(), hbm(), vmem(), hbm(), hbm(), hbm()],
        [vmem(), hbm(), vmem()],
        [sds((t, D), F32), sds((D, 2 * D), BF), sds((2, D), F32)],
        [
            pltpu.VMEM((D, HID), BF), pltpu.VMEM((HID, D), BF), pltpu.VMEM((2, t, D), BF),
            pltpu.VMEM((2, t, HID), BF), pltpu.VMEM((2, t, HID), BF), pltpu.VMEM((2, t, D), BF),
            pltpu.VMEM((2, t, HID), BF), pltpu.VMEM((t, D), F32), pltpu.VMEM((t, D), BF),
            pltpu.VMEM((t, D), BF), pltpu.VMEM((D, 2 * D), F32), pltpu.VMEM((D, 2 * D), BF),
            pltpu.VMEM((D, 2 * D), BF),
        ],
        6, 3, 10 << 30, (g, mid, we, ws, scales, nb, act, slope),
    )


def attend_back_kernel(
    mg, h, wt_h, wo_h, sc, cs, bias, na, q, k, v, ctx, lse, g_prev, wg_o, rows_o,
    wt, wo, ml, cg, delta, dqt, dk, dv, kvsend, kvrecv, pg, part, psend, precv,
    gown, gsend, grecv, lsem, ssem, rsem,
):
    d, x, c, peer, sib = place()
    y = 1 - x
    t = mg.shape[0]
    copies = Copies(lsem, ssem, rsem, d)
    greet(d, peer, sib)
    ml[x] = mg[...].astype(BF)
    ml_sent = copies.push(ml.at[x], ml.at[x], peer)
    wt_own, wo_own = wt.at[rows_of(c, HALF), :], wo.at[:, rows_of(c, HALF)]
    out_moves = [copies.local(wo_h, wo)]
    tri_moves = [copies.local(wt_h, wt)]
    dk[...] = jnp.zeros_like(dk)
    dv[...] = jnp.zeros_like(dv)
    for copy in out_moves:
        copy.wait()

    def attend(block):
        other = 1 - block
        pulled = nt(ml[block], wo[...])
        cg[block] = pulled.astype(BF)
        weighed = (cg[block].astype(F32) * ctx[block].astype(F32)).T
        for head in range(HALF // HD):
            delta[head : head + 1, :] = jnp.sum(
                weighed[head * HD : head * HD + HD, :], axis=0, keepdims=True
            )

        def pair_step(p, carry):
            lanes = pl.ds(pl.multiple_of(p * 128, 128), 128)
            q_pair, cg_pair = q[block, :, lanes], cg[block, :, lanes]
            for which in range(2):
                q_head, cg_head = half_of(q_pair, which), half_of(cg_pair, which)
                row = pl.ds(2 * p + which, 1)
                total, dots = lse[block, row, :], delta[row, :]
                turned = None
                for side in (block, other):
                    k_pair, v_pair = k[side, :, lanes], v[side, :, lanes]
                    scores = nt(k_pair, q_head)
                    if side is other:
                        scores = scores + bias[0]
                    probs = jnp.exp(scores - total)
                    score_grad = (probs * (nt(v_pair, cg_head) - dots)).astype(BF)
                    dv[side, :, lanes] += nn(probs.astype(BF), cg_head)
                    dk[side, :, lanes] += nn(score_grad, q_head)
                    piece = tn(k_pair, score_grad)
                    turned = piece if turned is None else turned + piece
                head = pl.ds(pl.multiple_of(p * 128 + which * HD, HD), HD)
                dqt[block, head, :] = turned[which * HD : which * HD + HD, :] * HD**-0.5
            return carry

        lax.fori_loop(0, HALF // 128, pair_step, 0)

    attend(x)
    ml_sent.wait()
    attend(y)
    theirs, mine = rows_of(1 - c, t), rows_of(c, t)
    for side in range(2):
        kvsend[side, :, pl.ds(0, HALF)] = dk[side, theirs, :].astype(BF)
        kvsend[side, :, pl.ds(HALF, HALF)] = dv[side, theirs, :].astype(BF)
    kv_sent = copies.push(kvsend, kvrecv, sib)

    def unturn(block, j, value):
        cosine, sine = cs[block, :, 0:128], cs[block, :, 128:256]
        rounded = value.astype(BF).astype(F32)
        pg[block, :, pl.ds(128 * j, 128)] = turn(rounded, cosine, -sine).astype(BF)

    for side in range(2):
        for j in range(3):
            unturn(side, j, dqt[side, 128 * j : 128 * j + 128, :].T)
    kv_sent.wait()
    for side in range(2):
        for j in range(3):
            at = pl.ds(128 * j, 128)
            unturn(side, 3 + j, dk[side, mine, at] + kvrecv[side, :, at].astype(F32))
            pg[side, :, pl.ds(D + 128 * j, 128)] = (
                dv[side, mine, at] + kvrecv[side, :, pl.ds(HALF + 128 * j, 128)].astype(F32)
            ).astype(BF)
    for copy in tri_moves:
        copy.wait()
    psend[...] = nt(pg[y], wt[...]).astype(BF)
    part_sent = copies.push(psend, precv, peer)
    part[...] = nt(pg[x], wt[...])

    ml_all = ml[...].reshape(2 * t, D)
    na_all = na[...].reshape(2 * t, D)
    ctx_all = ctx[...].reshape(2 * t, HALF)

    def grads(which, store):
        def step(i, carry):
            off = pl.ds(pl.multiple_of(which * HALF + i * 128, 128), 128)
            at = pl.ds(pl.multiple_of(i * 128, 128), 128)
            store(0, at, tn(na[:, :, off].reshape(2 * t, 128), pg[...].reshape(2 * t, TRI)))
            store(1, at, tn(ctx_all, ml[:, :, off].reshape(2 * t, 128)))
            return carry

        lax.fori_loop(0, HALF // 128, step, 0)

    def to_send(kind, at, value):
        if kind == 0:
            gsend[at, pl.ds(0, TRI)] = value.astype(BF)
        else:
            gsend[:, pl.ds(pl.multiple_of(TRI + at.start, 128), 128)] = value.astype(BF)

    def to_keep(kind, at, value):
        if kind == 0:
            gown[at, pl.ds(0, TRI)] = value
        else:
            gown[:, pl.ds(pl.multiple_of(TRI + at.start, 128), 128)] = value

    grads(1 - c, to_send)
    grad_sent = copies.push(gsend, grecv, sib)
    grads(c, to_keep)
    part_sent.wait()
    dy = part[...] + precv[...].astype(F32)
    back, rows = norm_back(h[...], sc[0:1, :], dy)
    g_prev[...] = mg[...] + back
    rows_o[...] = rows
    grad_sent.wait()
    gsend[...] = (gown[...] + grecv[...].astype(F32)).astype(BF)
    copies.local(gsend, wg_o).wait()


def attend_back(mg, h, wt, wo, scales, tables, bias, saved):
    t = mg.shape[0]
    return call(
        attend_back_kernel, "attend_back", 6,
        [vmem(), vmem(), hbm(), hbm(), vmem(), vmem(), pl.BlockSpec(memory_space=pltpu.SMEM)] + [vmem()] * 6,
        [vmem(), hbm(), vmem()],
        [sds((t, D), F32), sds((HALF, 2 * D), BF), sds((2, D), F32)],
        [
            pltpu.VMEM((D, TRI), BF), pltpu.VMEM((HALF, D), BF), pltpu.VMEM((2, t, D), BF),
            pltpu.VMEM((2, t, HALF), BF), pltpu.VMEM((8, t), F32), pltpu.VMEM((2, HALF, t), F32),
            pltpu.VMEM((2, 2 * t, HALF), F32), pltpu.VMEM((2, 2 * t, HALF), F32),
            pltpu.VMEM((2, t, D), BF), pltpu.VMEM((2, t, D), BF), pltpu.VMEM((2, t, TRI), BF),
            pltpu.VMEM((t, D), F32), pltpu.VMEM((t, D), BF), pltpu.VMEM((t, D), BF),
            pltpu.VMEM((HALF, 2 * D), F32), pltpu.VMEM((HALF, 2 * D), BF),
            pltpu.VMEM((HALF, 2 * D), BF),
        ],
        3, 4, 10 << 30, (mg, h, wt, wo, scales, tables, bias, *saved),
    )


KINDS = ("whole", "half", "out", "exp", "shr")


class Refs:
    def __init__(self, names, refs):
        assert len(names) == len(refs)
        for name, ref in zip(names, refs):
            setattr(self, name, ref)


def hold(ref):
    return ref


class Weights:
    def __init__(self, n, dp, rows):
        self.n = n
        self.zs = dp // 2
        self.rows = rows
        s = lax.axis_index("seq")
        self.s = s
        self.x, self.c = lax.div(s, 2), lax.rem(s, 2)
        self.d = lax.axis_index("dp")
        self.z, self.y = lax.div(self.d, 2), lax.rem(self.d, 2)
        self.sib, self.peer = s + 1 - 2 * self.c, lax.rem(s + 2, SEQ)
        self.across = self.d + 1 - 2 * self.y
        self.upper = lax.div(self.z, self.zs // 2)
        self.source = {"whole": n.p_whole, "half": n.p_half, "out": n.p_out, "exp": n.p_exp, "shr": n.p_shr}

    def slot(self, kind):
        return self.z if kind == "exp" else 2 * lax.rem(self.z, self.zs // 2) + self.c

    def target(self, kind):
        if kind == "exp":
            return self.s
        if kind == "whole":
            return 2 * self.x + self.upper
        if kind == "half":
            return 2 * (1 - self.x) + self.upper
        return 2 * self.upper + self.x

    def view(self, kind, layer, y, j, x, c):
        n, r = self.n, self.rows
        if kind == "exp":
            return n.we.at[layer, rows_of(2 * j + y, r), rows_of(c, D)]
        core = lax.rem(j, 2)
        at = 2 * lax.div(j, 2) + y
        if kind == "whole":
            start = pl.multiple_of(HALF * c + r * at, r)
            return n.wt.at[layer, pl.ds(start, r), rows_of(x + core, HALF)]
        if kind == "half":
            return n.hb.at[layer, core, rows_of(at, r), :]
        if kind == "out":
            return n.ob.at[layer, core, rows_of(at, r), :]
        return n.sb.at[layer, core, rows_of(at, 4 * r), :]

    def remote(self, src, dst, kind, layer, stage, sent, slot, to):
        number = KINDS.index(kind)
        return pltpu.make_async_remote_copy(
            src_ref=src,
            dst_ref=dst,
            send_sem=self.n.ssem.at[layer, number, stage, sent],
            recv_sem=self.n.rsem.at[layer, number, stage, slot],
            device_id=to,
            device_id_type=MESH,
        )

    def first(self, kind, layer, act):
        number = KINDS.index(kind)
        slot, to = self.slot(kind), self.target(kind)
        src = self.source[kind].at[layer]
        dst = self.view(kind, layer, self.y, slot, lax.div(to, 2), lax.rem(to, 2))

        def one(k):
            other = lax.rem(self.z + k, self.zs)
            copy = self.remote(src, dst, kind, layer, 0, k, slot, (2 * other + self.y, to))
            copy.start() if act == "start" else copy.wait_send()

        def here():
            if act == "start":
                pltpu.make_async_copy(src, dst, self.n.rsem.at[layer, number, 0, slot]).start()

        if kind == "exp":
            here()
        elif kind == "half":
            one(0)
        else:
            pl.when(to == self.s)(here)
            pl.when(to != self.s)(lambda: one(0))

        def step(k, carry):
            one(k)
            return carry

        lax.fori_loop(1, self.zs, step, 0)

    def onward(self, kind, layer, j):
        ref = self.view(kind, layer, self.y, j, self.x, self.c)
        copy = self.remote(ref, ref, kind, layer, 0, j, j, (self.across, self.s))
        copy.wait_recv()
        self.remote(ref, ref, kind, layer, 1, j, j, (self.across, self.s)).start()

    def onward_all(self, kind, layer):
        def step(j, carry):
            self.onward(kind, layer, j)
            return carry

        lax.fori_loop(0, self.zs, step, 0)

    def arrive(self, kind, layer):
        def step(j, carry):
            ref = self.view(kind, layer, 1 - self.y, j, self.x, self.c)
            self.remote(ref, ref, kind, layer, 1, j, j, (self.across, self.s)).wait_recv()
            return carry

        lax.fori_loop(0, self.zs, step, 0)

    def finish(self, kind, layer):
        self.first(kind, layer, "wait")

        def step(j, carry):
            ref = self.view(kind, layer, self.y, j, self.x, self.c)
            self.remote(ref, ref, kind, layer, 1, j, j, (self.across, self.s)).wait_send()
            return carry

        lax.fori_loop(0, self.zs, step, 0)


def greet_all(w):
    barrier = pltpu.get_barrier_semaphore()

    def one(i, carry):
        z, s = lax.div(i, SEQ), lax.rem(i, SEQ)
        away = jnp.logical_or(z != w.z, s != w.s)

        @pl.when(away)
        def _():
            pl.semaphore_signal(barrier, inc=1, device_id=(2 * z + w.y, s), device_id_type=MESH)

        return carry

    lax.fori_loop(0, w.zs * SEQ, one, 0)
    pl.semaphore_signal(barrier, inc=1, device_id=(w.across, w.s), device_id_type=MESH)
    pl.semaphore_wait(barrier, w.zs * SEQ)


def gather_scales_start(w):
    n = w.n
    mine = n.scl.at[w.y, w.z, w.s]
    mine[...] = n.sc_own[...]

    def one(i, carry):
        z, s = lax.div(i, SEQ), lax.rem(i, SEQ)

        @pl.when(jnp.logical_or(z != w.z, s != w.s))
        def _():
            pltpu.make_async_remote_copy(
                src_ref=mine, dst_ref=mine, send_sem=n.sc_ssem.at[i],
                recv_sem=n.sc_rsem.at[w.z * SEQ + w.s], device_id=(2 * z + w.y, s), device_id_type=MESH,
            ).start()

        return carry

    lax.fori_loop(0, w.zs * SEQ, one, 0)


def gather_scales_end(w):
    n = w.n

    def one(i, carry):
        z, s = lax.div(i, SEQ), lax.rem(i, SEQ)

        @pl.when(jnp.logical_or(z != w.z, s != w.s))
        def _():
            slot = n.scl.at[w.y, z, s]
            copy = pltpu.make_async_remote_copy(
                src_ref=slot, dst_ref=slot, send_sem=n.sc_ssem.at[i], recv_sem=n.sc_rsem.at[i],
                device_id=(2 * z + w.y, s), device_id_type=MESH,
            )
            copy.wait_recv()
            copy.wait_send()

        return carry

    lax.fori_loop(0, w.zs * SEQ, one, 0)
    count = w.zs * SEQ
    plane = n.scl.at[w.y]
    copy = pltpu.make_async_remote_copy(
        src_ref=plane, dst_ref=plane, send_sem=n.sc_ssem.at[count], recv_sem=n.sc_rsem.at[count],
        device_id=(w.across, w.s), device_id_type=MESH,
    )
    copy.start()
    copy.wait()
    wide = n.sc.shape[-1] // (2 * w.zs)
    for s in range(SEQ):
        both = [n.scl[d % 2, d // 2, s][:, :wide] for d in range(2 * w.zs)]
        rows = jnp.concatenate(both, axis=1)
        for layer in range(LAYERS):
            n.sc[layer, s : s + 1, :] = rows[layer : layer + 1, :]


FWD_OUT = (
    "h_out", "h_mid", "mid_o0", "mid_o1", "sc_o",
    "na_o0", "q_o0", "k_o0", "v_o0", "ctx_o0", "lse_o0", "nb_o0", "act_o0", "slope_o0", "wt_o0", "wo_o0", "we_o0", "ws_o0",
    "na_o1", "q_o1", "k_o1", "v_o1", "ctx_o1", "lse_o1", "nb_o1", "act_o1", "slope_o1", "wt_o1", "wo_o1", "we_o1", "ws_o1",
)
FWD_IN = ("h0", "sc_own", "cs", "bias", "p_whole", "p_half", "p_out", "p_exp", "p_shr")
FWD_SCRATCH = (
    "wt", "wo", "we", "ws", "hb", "ob", "sb", "scl", "sc", "na", "q", "k", "v", "ctxt", "ctx", "lse", "nb", "act",
    "slope", "psend", "precv", "hs", "mid", "ssem", "rsem", "sc_ssem", "sc_rsem", "xs", "xr", "lsem",
)


def fwd_kernel(dp, *refs):
    n = Refs((*FWD_IN, *FWD_OUT, *FWD_SCRATCH), refs)
    rows = n.p_exp.shape[1]
    t = n.h0.shape[0]
    w = Weights(n, dp, rows)
    x, c, peer, sib = w.x, w.c, w.peer, w.sib
    y = 1 - x
    copies = Copies(n.lsem, n.xs, n.xr, w.d)
    waits = []

    def save(src, dst):
        waits.append(copies.local(src, dst))

    greet_all(w)
    w.first("whole", 0, "start")
    w.first("half", 0, "start")
    gather_scales_start(w)
    w.first("out", 0, "start")
    n.hs[0] = n.h0[...]
    xhat, _ = norm_stats(n.hs[0])
    gather_scales_end(w)

    def share_tri(layer):
        own = n.wt.at[layer, rows_of(c, HALF), :]
        n.wt[layer, rows_of(c, HALF), rows_of(2 * (1 - x), HALF)] = jnp.concatenate(
            [n.hb[layer, 0], n.hb[layer, 1]], axis=1
        )
        return copies.push(own, own, sib)

    def share_cols(into, parts, layer):
        own = into.at[layer, :, rows_of(c, HALF)]
        into[layer, :, rows_of(c, HALF)] = jnp.concatenate([parts[layer, 0], parts[layer, 1]], axis=1)
        return copies.push(own, own, sib)

    def share_exp(layer):
        own = n.we.at[layer, :, rows_of(c, D)]
        return copies.push(own, own, sib)

    for layer in range(LAYERS):
        last = layer == LAYERS - 1
        if layer:
            xhat, _ = norm_stats(n.hs[layer])
        n.na[layer, x] = (xhat * n.sc[layer, 0:1, :] + n.sc[layer, 1:2, :]).astype(BF)
        na_sent = copies.push(n.na.at[layer, x], n.na.at[layer, x], peer)
        if layer == 0:
            w.onward_all("whole", 0)
            w.onward_all("half", 0)
            w.first("exp", 0, "start")
            w.onward_all("out", 0)
            w.first("shr", 0, "start")
            w.arrive("whole", 0)
            w.arrive("half", 0)
            tri_sent = share_tri(0)
        tri_sent.wait()

        def project(block):
            cosine, sine = n.cs[block, :, 0:128], n.cs[block, :, 128:256]
            for j in range(9):
                part = nn(n.na[layer, block], n.wt[layer, :, 128 * j : 128 * j + 128])
                lanes = pl.ds(128 * (j % 3), 128)
                if j < 3:
                    n.q[layer, block, :, lanes] = (turn(part, cosine, sine) * HD**-0.5).astype(BF)
                elif j < 6:
                    n.k[layer, block, rows_of(c, t), lanes] = turn(part, cosine, sine).astype(BF)
                else:
                    n.v[layer, block, rows_of(c, t), lanes] = part.astype(BF)

        def share(block):
            at = (layer, block, rows_of(c, t))
            return [
                copies.push(n.k.at[at], n.k.at[at], sib),
                copies.push(n.v.at[at], n.v.at[at], sib),
            ]

        project(x)
        shared = share(x)
        na_sent.wait()
        project(y)
        shared += share(y)
        w.arrive("out", layer)
        out_sent = share_cols(n.wo, n.ob, layer)
        for copy in shared:
            copy.wait()
        save(n.na.at[layer], getattr(n, f"na_o{layer}"))
        save(n.q.at[layer], getattr(n, f"q_o{layer}"))
        save(n.k.at[layer], getattr(n, f"k_o{layer}"))
        save(n.v.at[layer], getattr(n, f"v_o{layer}"))

        def attend(block, pump):
            other = 1 - block

            def pair_step(p, carry):
                pump(p)
                lanes = pl.ds(pl.multiple_of(p * 128, 128), 128)
                q_pair = n.q[layer, block, :, lanes]
                k_same, k_cross = n.k[layer, block, :, lanes], n.k[layer, other, :, lanes]
                v_same, v_cross = n.v[layer, block, :, lanes], n.v[layer, other, :, lanes]
                for which in range(2):
                    q_head = half_of(q_pair, which)
                    s_same = nt(k_same, q_head)
                    s_cross = nt(k_cross, q_head) + n.bias[0]
                    top = jnp.maximum(
                        jnp.max(s_same, axis=0, keepdims=True), jnp.max(s_cross, axis=0, keepdims=True)
                    )
                    e_same = jnp.exp(s_same - top)
                    e_cross = jnp.exp(s_cross - top)
                    total = jnp.sum(e_same, axis=0, keepdims=True) + jnp.sum(
                        e_cross, axis=0, keepdims=True
                    )
                    mixed = tn(v_same, e_same.astype(BF)) + tn(v_cross, e_cross.astype(BF))
                    head = pl.ds(pl.multiple_of(p * 128 + which * HD, HD), HD)
                    n.ctxt[head, :] = mixed[which * HD : which * HD + HD, :] / total
                    n.lse[layer, block, pl.ds(2 * p + which, 1), :] = top + jnp.log(total)
                return carry

            lax.fori_loop(0, HALF // 128, pair_step, 0)
            n.ctx[layer, block] = n.ctxt[...].T.astype(BF)

        attend(y, lambda p: w.onward("exp", layer, p))
        out_sent.wait()
        use = 2 * layer
        n.psend[use] = nn(n.ctx[layer, y], n.wo[layer]).astype(BF)
        part_sent = copies.push(n.psend.at[use], n.precv.at[use], peer)

        def rest(p):
            w.onward("shr", layer, p)

        w.onward("exp", layer, w.zs - 1)
        attend(x, rest)
        w.onward("shr", layer, w.zs - 1)
        if not last:
            w.first("whole", layer + 1, "start")
            w.first("half", layer + 1, "start")
            w.first("out", layer + 1, "start")
        n.mid[layer] = n.hs[layer] + nn(n.ctx[layer, x], n.wo[layer])
        save(n.ctx.at[layer], getattr(n, f"ctx_o{layer}"))
        save(n.lse.at[layer], getattr(n, f"lse_o{layer}"))
        save(n.wt.at[layer], getattr(n, f"wt_o{layer}"))
        save(n.wo.at[layer], getattr(n, f"wo_o{layer}"))
        part_sent.wait()
        n.mid[layer] = n.mid[layer] + n.precv[use].astype(F32)
        save(n.mid.at[layer], getattr(n, f"mid_o{layer}"))

        xhat, _ = norm_stats(n.mid[layer])
        n.nb[layer, x] = (xhat * n.sc[layer, 2:3, :] + n.sc[layer, 3:4, :]).astype(BF)
        nb_sent = copies.push(n.nb.at[layer, x], n.nb.at[layer, x], peer)
        w.arrive("exp", layer)
        exp_sent = share_exp(layer)
        w.arrive("shr", layer)
        shr_sent = share_cols(n.ws, n.sb, layer)
        exp_sent.wait()

        def feed(block, pump):
            def step(i, carry):
                pump(i)
                lanes = pl.ds(pl.multiple_of(i * 256, 256), 256)
                value, rate = gelu_parts(nn(n.nb[layer, block], n.we[layer, :, lanes]))
                n.act[layer, block, :, lanes] = value.astype(BF)
                n.slope[layer, block, :, lanes] = rate.astype(BF)
                return carry

            lax.fori_loop(0, HID // 256, step, 0)

        def pump_tri(i):
            if not last:

                @pl.when(i < w.zs)
                def _():
                    w.onward("whole", layer + 1, i)
                    w.onward("half", layer + 1, i)

        def pump_out(i):
            if not last:

                @pl.when(i < w.zs)
                def _():
                    w.onward("out", layer + 1, i)

        feed(x, pump_tri)
        shr_sent.wait()
        n.hs[layer + 1] = n.mid[layer] + nn(n.act[layer, x], n.ws[layer])
        nb_sent.wait()
        feed(y, pump_out)
        use = 2 * layer + 1
        n.psend[use] = nn(n.act[layer, y], n.ws[layer]).astype(BF)
        part_sent = copies.push(n.psend.at[use], n.precv.at[use], peer)
        save(n.nb.at[layer], getattr(n, f"nb_o{layer}"))
        save(n.act.at[layer], getattr(n, f"act_o{layer}"))
        save(n.slope.at[layer], getattr(n, f"slope_o{layer}"))
        save(n.we.at[layer], getattr(n, f"we_o{layer}"))
        save(n.ws.at[layer], getattr(n, f"ws_o{layer}"))
        if not last:
            w.first("exp", layer + 1, "start")
            w.first("shr", layer + 1, "start")
            w.arrive("whole", layer + 1)
            w.arrive("half", layer + 1)
            tri_sent = share_tri(layer + 1)
        part_sent.wait()
        n.hs[layer + 1] = n.hs[layer + 1] + n.precv[use].astype(F32)

    n.h_out[...] = n.hs[LAYERS]
    n.sc_o[...] = n.sc[...]
    save(n.hs.at[1], n.h_mid)
    for copy in waits:
        copy.wait()
    for layer in range(LAYERS):
        for kind in KINDS:
            w.finish(kind, layer)


def forward_all(dp, h, sc_own, tables, bias, pieces):
    t = h.shape[0]
    zs = dp // 2
    per_layer = [
        sds((2, t, D), BF), sds((2, t, HALF), BF), sds((2, 2 * t, HALF), BF), sds((2, 2 * t, HALF), BF),
        sds((2, t, HALF), BF), sds((2, 8, t), F32), sds((2, t, D), BF), sds((2, t, HID), BF), sds((2, t, HID), BF),
        sds((D, TRI), BF), sds((HALF, D), BF), sds((D, HID), BF), sds((HID, D), BF),
    ]
    token = sds((t, D), F32)
    outs = [token, token, token, token, sds((LAYERS, 4, D), F32), *per_layer, *per_layer]
    specs = [vmem(), hbm(), hbm(), hbm(), vmem(), *([hbm()] * (2 * len(per_layer)))]
    n_layers = LAYERS
    scratch = [
        pltpu.VMEM((n_layers, D, TRI), BF), pltpu.VMEM((n_layers, HALF, D), BF),
        pltpu.VMEM((n_layers, D, HID), BF), pltpu.VMEM((n_layers, HID, D), BF),
        pltpu.VMEM((n_layers, 2, HALF, 192), BF), pltpu.VMEM((n_layers, 2, HALF, 192), BF),
        pltpu.VMEM((n_layers, 2, HID, 192), BF), pltpu.VMEM((2, zs, SEQ, 8, 128), F32),
        pltpu.VMEM((n_layers, 4, D), F32), pltpu.VMEM((n_layers, 2, t, D), BF),
        pltpu.VMEM((n_layers, 2, t, HALF), BF), pltpu.VMEM((n_layers, 2, 2 * t, HALF), BF),
        pltpu.VMEM((n_layers, 2, 2 * t, HALF), BF), pltpu.VMEM((HALF, t), F32),
        pltpu.VMEM((n_layers, 2, t, HALF), BF), pltpu.VMEM((n_layers, 2, 8, t), F32),
        pltpu.VMEM((n_layers, 2, t, D), BF), pltpu.VMEM((n_layers, 2, t, HID), BF),
        pltpu.VMEM((n_layers, 2, t, HID), BF), pltpu.VMEM((2 * n_layers, t, D), BF),
        pltpu.VMEM((2 * n_layers, t, D), BF), pltpu.VMEM((n_layers + 1, t, D), F32),
        pltpu.VMEM((n_layers, t, D), F32),
        pltpu.SemaphoreType.DMA((n_layers, len(KINDS), 2, zs)),
        pltpu.SemaphoreType.DMA((n_layers, len(KINDS), 2, zs)),
        pltpu.SemaphoreType.DMA((zs * SEQ + 1,)), pltpu.SemaphoreType.DMA((zs * SEQ + 1,)),
        pltpu.SemaphoreType.DMA((24,)), pltpu.SemaphoreType.DMA((24,)), pltpu.SemaphoreType.DMA((32,)),
    ]
    results = pl.pallas_call(
        functools.partial(fwd_kernel, dp),
        name="forward",
        out_shape=outs,
        in_specs=[vmem(), vmem(), vmem(), pl.BlockSpec(memory_space=pltpu.SMEM), *([hbm()] * 5)],
        out_specs=specs,
        scratch_shapes=scratch,
        cost_estimate=pl.CostEstimate(flops=22 << 30, bytes_accessed=32 << 20, transcendentals=0),
        compiler_params=pltpu.CompilerParams(
            collective_id=4, has_side_effects=True, vmem_limit_bytes=VMEM_BYTES
        ),
    )(h, sc_own, tables, bias, *pieces)
    return Refs(FWD_OUT, results)


def pieces_of(triple_weight, output_weight, expand_weight, shrink_weight, c):
    tri = triple_weight.astype(BF)
    whole = jnp.where(c == 0, tri[:, :, :HALF], tri[:, :, 192:])
    half = jnp.where(c == 0, tri[:, :, HALF:], tri[:, :, :192])
    return whole, half, output_weight.astype(BF), expand_weight.astype(BF), shrink_weight.astype(BF)


class Moves:
    def __init__(self, dp):
        self.dp = dp
        self.d = lax.axis_index("dp")
        s = lax.axis_index("seq")
        self.s, self.x, self.c = s, s // 2, s % 2
        half = dp // 2
        ids = [(d, s) for d in range(dp) for s in range(SEQ)]
        self.tri = []
        for r in range(2):
            for j in range(3):
                perm = []
                for d, s in ids:
                    b = (3 * s + j) % 4
                    to = (2 * (d % half) + (r ^ (b % 2)), 2 * (b // 2) + d // half)
                    perm.append((d * SEQ + s, to[0] * SEQ + to[1]))
                self.tri.append(perm)
        self.out = []
        for r in range(2):
            perm = []
            for d, s in ids:
                to = (2 * (d % half) + (r ^ (s % 2)), 2 * (d // half) + s // 2)
                perm.append((d * SEQ + s, to[0] * SEQ + to[1]))
            self.out.append(perm)
        self.shr = []
        for k in range(4):
            perm = []
            for d, s in ids:
                to = (4 * (d % (dp // 4)) + (k + s) % 4, d // (dp // 4))
                perm.append((d * SEQ + s, to[0] * SEQ + to[1]))
            self.shr.append(perm)

    def send(self, piece, perm, back):
        if back:
            perm = [(b, a) for a, b in perm]
        return lax.ppermute(piece, ("dp", "seq"), perm)

    @staticmethod
    def pick(pieces, index):
        return lax.dynamic_index_in_dim(jnp.stack(pieces), index, 0, keepdims=False)

    def tri_out(self, low):
        n, rows, _ = low.shape
        halves = low.reshape(n, 2, rows // 2, 3, 192)
        got = []
        for r in range(2):
            for j in range(3):
                which = r ^ (((3 * self.s + j) % 4) % 2)
                piece = lax.dynamic_index_in_dim(halves[:, :, :, j], which, 1, keepdims=False)
                got.append(self.send(piece, self.tri[3 * r + j], False))
        parts = []
        for t in range(3):
            for bb in range(2):
                r, j = bb ^ (self.d % 2), (t + 2 * self.x + bb) % 3
                parts.append(self.pick(got, 3 * r + j))
        return jnp.concatenate(parts, axis=-1)

    def tri_back(self, grad):
        n, rows, _ = grad.shape
        got = []
        for r in range(2):
            for j in range(3):
                bb = (self.d % 2) ^ r
                t = (j - (2 * self.x + bb)) % 3
                piece = lax.dynamic_slice_in_dim(grad, (2 * t + bb) * 192, 192, 2)
                got.append(self.send(piece, self.tri[3 * r + j], True))
        cols = []
        for j in range(3):
            two = []
            for hh in range(2):
                r = hh ^ (((3 * self.s + j) % 4) % 2)
                two.append(self.pick([got[j], got[3 + j]], r))
            cols.append(jnp.concatenate(two, axis=1))
        return jnp.concatenate(cols, axis=-1)

    def out_out(self, low):
        n, rows, _ = low.shape
        halves = low.reshape(n, 2, rows // 2, 192)
        got = [
            self.send(
                lax.dynamic_index_in_dim(halves, r ^ (self.s % 2), 1, keepdims=False), self.out[r], False
            )
            for r in range(2)
        ]
        return jnp.concatenate([self.pick(got, u ^ (self.d % 2)) for u in range(2)], axis=-1)

    def out_back(self, grad):
        got = []
        for r in range(2):
            u = r ^ (self.d % 2)
            got.append(self.send(lax.dynamic_slice_in_dim(grad, u * 192, 192, 2), self.out[r], True))
        return jnp.concatenate([self.pick(got, hh ^ (self.s % 2)) for hh in range(2)], axis=1)

    def shr_out(self, low):
        n, rows, _ = low.shape
        subs = low.reshape(n, 4, rows // 4, 192)
        got = [
            self.send(
                lax.dynamic_index_in_dim(subs, (k + self.s) % 4, 1, keepdims=False), self.shr[k], False
            )
            for k in range(4)
        ]
        return jnp.concatenate([self.pick(got, (self.d - s) % 4) for s in range(4)], axis=-1)

    def shr_back(self, grad):
        got = []
        for k in range(4):
            piece = lax.dynamic_slice_in_dim(grad, ((self.d - k) % 4) * 192, 192, 2)
            got.append(self.send(piece, self.shr[k], True))
        return jnp.concatenate([self.pick(got, (sub - self.s) % 4) for sub in range(4)], axis=1)


def tables_here(segments, t, x, c):
    group = segments.shape[0]
    whole = segments[0] == segments[group - 1]
    place_in_half = c * t + jnp.arange(t, dtype=jnp.int32)
    second = jnp.where(whole, group // 2, 0).astype(jnp.int32)
    positions = jnp.stack([place_in_half, place_in_half + second]).astype(F32)
    lane = jnp.arange(128, dtype=jnp.int32)
    inverse = 1.0 / ROTARY_BASE ** ((lane % (HD // 2)).astype(F32) * (2.0 / HD))
    angles = positions[:, :, None] * inverse[None, None, :]
    sign = jnp.where(lane % HD < HD // 2, -1.0, 1.0).astype(F32)
    tables = jnp.concatenate([jnp.cos(angles), jnp.sin(angles) * sign], axis=-1)
    bias = jnp.where(whole, 0.0, MASKED).astype(F32).reshape(1)
    return tables, bias


def layers_narrow(
    dp, moves, residual, cotangent, scales_weight, tables, bias,
    triple_weight, output_weight, expand_weight, shrink_weight,
):
    d, s = lax.axis_index("dp"), lax.axis_index("seq")
    scales_all = lax.psum(
        lax.dynamic_update_slice(
            jnp.zeros((LAYERS, 4, D), F32), scales_weight.astype(BF).astype(F32), (0, s, d * (D // dp))
        ),
        ("dp", "seq"),
    )
    tri = moves.tri_out(triple_weight.astype(BF))
    out = moves.out_out(output_weight.astype(BF))
    shr = moves.shr_out(shrink_weight.astype(BF))
    attend_parts = jnp.concatenate([tri, out], axis=-1)
    feed_parts = jnp.concatenate([expand_weight.astype(BF), shr], axis=-1)
    gather = functools.partial(lax.all_gather, axis_name="dp", axis=0, tiled=True)
    wa, wf = [], []
    for layer in range(LAYERS):
        wa.append(gather(attend_parts[layer]))
        wf.append(gather(feed_parts[layer]))

    stream = residual
    kept = []
    for layer in range(LAYERS):
        scales = scales_all[layer]
        middle, *attend_saved = attend_fwd(stream, wa[layer], scales, tables, bias)
        following, *feed_saved = feed_fwd(middle, wf[layer], scales)
        kept.append((stream, middle, attend_saved, feed_saved))
        stream = following

    g = cotangent
    attend_grads, feed_grads, scale_grads = [None] * LAYERS, [None] * LAYERS, [None] * LAYERS
    scatter = functools.partial(lax.psum_scatter, axis_name="dp", scatter_dimension=0, tiled=True)
    for layer in reversed(range(LAYERS)):
        scales = scales_all[layer]
        h, middle, attend_saved, feed_saved = kept[layer]
        mg, feed_grad, rows_b = feed_bwd(g, middle, wf[layer], scales, *feed_saved)
        feed_grads[layer] = scatter(feed_grad).astype(F32)
        g, attend_grad, rows_a = attend_bwd(mg, h, wa[layer], scales, tables, bias, attend_saved)
        attend_grads[layer] = scatter(attend_grad).astype(F32)
        scale_grads[layer] = jnp.concatenate([rows_a, rows_b], axis=0)

    return stream, g, attend_grads, feed_grads, scale_grads


def layers_wide(dp, residual, cotangent, sc_own, tables, bias, pieces):
    f = forward_all(dp, residual, sc_own, tables, bias, pieces)
    stream, scales_all = f.h_out, f.sc_o
    g = cotangent
    attend_grads, feed_grads, scale_grads = [None] * LAYERS, [None] * LAYERS, [None] * LAYERS
    scatter = functools.partial(lax.psum_scatter, axis_name="dp", scatter_dimension=0, tiled=True)
    for layer in reversed(range(LAYERS)):
        scales = scales_all[layer]
        h, middle = (f.h_mid, f.mid_o1) if layer else (residual, f.mid_o0)
        feed_saved = [getattr(f, f"{k}_o{layer}") for k in ("nb", "act", "slope")]
        attend_saved = [getattr(f, f"{k}_o{layer}") for k in ("na", "q", "k", "v", "ctx", "lse")]
        wt, wo, we, ws = (getattr(f, f"{k}_o{layer}") for k in ("wt", "wo", "we", "ws"))
        mg, feed_grad, rows_b = feed_back(g, middle, we, ws, scales, *feed_saved)
        feed_grads[layer] = scatter(feed_grad).astype(F32)
        g, attend_grad, rows_a = attend_back(mg, h, wt, wo, scales, tables, bias, attend_saved)
        attend_grads[layer] = scatter(attend_grad).astype(F32)
        scale_grads[layer] = jnp.concatenate([rows_a, rows_b], axis=0)
    return stream, g, attend_grads, feed_grads, scale_grads


def local(dp, *args):
    (residual, cotangent, segments) = args[:3]
    (
        triple_weight, triple_moment, triple_square, triple_shadow,
        output_weight, output_moment, output_square, output_shadow,
        expand_weight, expand_moment, expand_square, expand_shadow,
        shrink_weight, shrink_moment, shrink_square, shrink_shadow,
        scales_weight, scales_moment, scales_square, scales_shadow,
    ) = args[3:]
    moves = Moves(dp)
    t = residual.shape[0]
    d, s = lax.axis_index("dp"), lax.axis_index("seq")
    tables, bias = tables_here(segments, t, moves.x, moves.c)

    if (D // dp) % 16 == 0:
        sc_own = jnp.zeros((8, 128), F32)
        sc_own = sc_own.at[:LAYERS, : D // dp].set(scales_weight[:, 0].astype(BF).astype(F32))
        pieces = pieces_of(triple_weight, output_weight, expand_weight, shrink_weight, moves.c)
        stream, g, attend_grads, feed_grads, scale_grads = layers_wide(
            dp, residual, cotangent, sc_own, tables, bias, pieces
        )
    else:
        stream, g, attend_grads, feed_grads, scale_grads = layers_narrow(
            dp, moves, residual, cotangent, scales_weight, tables, bias,
            triple_weight, output_weight, expand_weight, shrink_weight,
        )

    scale_grad = lax.psum(jnp.stack(scale_grads), ("dp", "seq"))
    own_scale = lax.dynamic_slice(scale_grad, (0, s, d * (D // dp)), (LAYERS, 1, D // dp))
    squares = jnp.sum(own_scale * own_scale)
    for part in (*attend_grads, *feed_grads):
        squares = squares + jnp.sum(part * part)
    grad_norm = jnp.sqrt(lax.psum(squares, ("dp", "seq")))
    limit = CLIP_RATIO * math.sqrt(float(LAYERS * (4 * D * D + 2 * D * FF + 4 * D)))
    factor = limit / (grad_norm + 1e-06)

    attend_grad, feed_grad = jnp.stack(attend_grads).astype(BF), jnp.stack(feed_grads).astype(BF)
    triple_grad = moves.tri_back(attend_grad[:, :, :TRI]).astype(F32)
    output_grad = moves.out_back(attend_grad[:, :, TRI:]).astype(F32)
    expand_grad = feed_grad[:, :, :D].astype(F32)
    shrink_grad = moves.shr_back(feed_grad[:, :, D:]).astype(F32)

    results = [stream, g, grad_norm]
    for weight, moment, square, shadow, grad, rate in (
        (triple_weight, triple_moment, triple_square, triple_shadow, triple_grad, RATE_FACTOR / math.sqrt(D)),
        (output_weight, output_moment, output_square, output_shadow, output_grad, RATE_FACTOR / math.sqrt(D // 16)),
        (expand_weight, expand_moment, expand_square, expand_shadow, expand_grad, RATE_FACTOR / math.sqrt(D)),
        (shrink_weight, shrink_moment, shrink_square, shrink_shadow, shrink_grad, RATE_FACTOR / math.sqrt(FF)),
        (scales_weight, scales_moment, scales_square, scales_shadow, own_scale, SCALES_RATE),
    ):
        results.extend(adam_step(weight, moment, square, shadow, grad * factor, rate))
    return tuple(results)


def solution(mesh):
    token = P(("dp", "seq"), None)
    weight = P(None, "dp", "seq")
    scale = P(None, "seq", "dp")
    return jax.shard_map(
        functools.partial(local, mesh.shape["dp"]),
        mesh=mesh,
        in_specs=(token, token, P("dp"), *([weight] * 16), *([scale] * 4)),
        out_specs=(token, token, P(), *([weight] * 16), *([scale] * 4)),
        check_vma=False,
    )
```

```python
import functools
import math
from typing import Any, NamedTuple

import jax
import jax.numpy as jnp
from jax import lax
from jax.experimental import pallas as pl
from jax.experimental.pallas import tpu as pltpu
from jax.sharding import PartitionSpec as P

D = 768
FF = 3072
HD = 64
LAYERS = 2
STEP = 2
SEQ = 4

EPSILON = 1e-05
ROTARY_BASE = 10000.0
BETA_ONE = 0.9
BETA_TWO = 0.999
ADAM_EPSILON = 1e-08
DECAY_RATE = 0.01
SHADOW_RATE = 0.99
CLIP_RATIO = 0.5
RATE_FACTOR = 1.5
SCALES_RATE = 0.6
MASKED = -1000000000.0

HALF = D // 2
TRI = 3 * HALF
HID = FF // 2
BF = jnp.bfloat16
F32 = jnp.float32
MESH = pl.DeviceIdType.MESH
VMEM_BYTES = 60 << 20


def adam_step(weight, moment, square, shadow, gradient, step_rate):
    shadow_decay = min(SHADOW_RATE, (1.0 + STEP) / (10.0 + STEP))
    momentum = BETA_ONE * moment + (1.0 - BETA_ONE) * gradient
    variance = BETA_TWO * square + (1.0 - BETA_TWO) * gradient * gradient
    corrected = (
        momentum
        / (1.0 - BETA_ONE**STEP)
        / (jnp.sqrt(variance / (1.0 - BETA_TWO**STEP)) + ADAM_EPSILON)
    )
    updated = weight - step_rate * (corrected + DECAY_RATE * weight)
    average = shadow_decay * shadow + (1.0 - shadow_decay) * updated
    return (updated, momentum, variance, average)


def nn(a, b):
    return lax.dot_general(a, b, (((1,), (0,)), ((), ())), preferred_element_type=F32)


def nt(a, b):
    return lax.dot_general(a, b, (((1,), (1,)), ((), ())), preferred_element_type=F32)


def tn(a, b):
    return lax.dot_general(a, b, (((0,), (0,)), ((), ())), preferred_element_type=F32)


def place():
    s = lax.axis_index("seq")
    x = lax.div(s, 2)
    c = lax.rem(s, 2)
    return lax.axis_index("dp"), x, c, lax.rem(s + 2, SEQ), s + 1 - 2 * c


def greet(d, peer, sib):
    barrier = pltpu.get_barrier_semaphore()
    for other in (peer, sib):
        pl.semaphore_signal(barrier, inc=1, device_id=(d, other), device_id_type=MESH)
    pl.semaphore_wait(barrier, 2)


def rows_of(c, n):
    return pl.ds(pl.multiple_of(c * n, n), n)


class Copies:
    def __init__(self, lsem, ssem, rsem, d):
        self.lsem, self.ssem, self.rsem, self.d = lsem, ssem, rsem, d
        self.n_local = 0
        self.n_remote = 0

    def local(self, src, dst):
        copy = pltpu.make_async_copy(src, dst, self.lsem.at[self.n_local])
        self.n_local += 1
        copy.start()
        return copy

    def push(self, src, dst, to):
        copy = pltpu.make_async_remote_copy(
            src_ref=src,
            dst_ref=dst,
            send_sem=self.ssem.at[self.n_remote],
            recv_sem=self.rsem.at[self.n_remote],
            device_id=(self.d, to),
            device_id_type=MESH,
        )
        self.n_remote += 1
        copy.start()
        return copy


def norm_stats(values):
    center = values - jnp.mean(values, axis=-1, keepdims=True)
    spread = jnp.mean(center * center, axis=-1, keepdims=True)
    scale = lax.rsqrt(spread + EPSILON)
    return center * scale, scale


def norm_back(values, gain, dy):
    xhat, scale = norm_stats(values)
    u = gain * dy
    du = u - jnp.mean(u, axis=-1, keepdims=True)
    back = scale * (du - xhat * jnp.mean(u * xhat, axis=-1, keepdims=True))
    rows = jnp.concatenate(
        [jnp.sum(xhat * dy, axis=0, keepdims=True), jnp.sum(dy, axis=0, keepdims=True)], axis=0
    )
    return back, rows


def turn(chunk, cosine, sine):
    lane = lax.broadcasted_iota(jnp.int32, chunk.shape, 1)
    swapped = jnp.where(
        lax.rem(lane, HD) < HD // 2, pltpu.roll(chunk, 128 - HD // 2, 1), pltpu.roll(chunk, HD // 2, 1)
    )
    return chunk * cosine + swapped * sine


def half_of(pair, which):
    lane = lax.broadcasted_iota(jnp.int32, pair.shape, 1)
    keep = (lane < HD) if which == 0 else (lane >= HD)
    return jnp.where(keep, pair, jnp.zeros_like(pair))


def attend_fwd_kernel(
    h, wa, sc, cs, bias, mid, na_o, q_o, k_o, v_o, ctx_o, lse_o,
    wt, wo, na, q, k, v, ctxt, ctx, lse, psend, precv, lsem, ssem, rsem,
):
    d, x, c, peer, sib = place()
    y = 1 - x
    rows = h.shape[0]
    copies = Copies(lsem, ssem, rsem, d)
    greet(d, peer, sib)
    wt_own, wo_own = wt.at[rows_of(c, HALF), :], wo.at[:, rows_of(c, HALF)]
    tri_part, out_part = wa.at[:, pl.ds(0, TRI)], wa.at[:, pl.ds(TRI, HALF)]
    tri_sent = copies.push(tri_part, wt_own, sib)
    tri_local = copies.local(tri_part, wt_own)
    out_sent = copies.push(out_part, wo_own, sib)
    out_local = copies.local(out_part, wo_own)
    xhat, _ = norm_stats(h[...])
    na[x] = (xhat * sc[0:1, :] + sc[1:2, :]).astype(BF)
    na_sent = copies.push(na.at[x], na.at[x], peer)
    tri_local.wait()
    tri_sent.wait()

    def project(block):
        cosine, sine = cs[block, :, 0:128], cs[block, :, 128:256]
        for j in range(9):
            part = nn(na[block], wt[:, 128 * j : 128 * j + 128])
            lanes = pl.ds(128 * (j % 3), 128)
            if j < 3:
                q[block, :, lanes] = (turn(part, cosine, sine) * HD**-0.5).astype(BF)
            elif j < 6:
                k[block, rows_of(c, rows), lanes] = turn(part, cosine, sine).astype(BF)
            else:
                v[block, rows_of(c, rows), lanes] = part.astype(BF)

    def share(block):
        mine = (block, rows_of(c, rows))
        return [copies.push(k.at[mine], k.at[mine], sib), copies.push(v.at[mine], v.at[mine], sib)]

    project(x)
    shared = share(x)
    na_sent.wait()
    project(y)
    shared += share(y)
    out_local.wait()
    out_sent.wait()
    for copy in shared:
        copy.wait()

    def attend(block):
        other = 1 - block

        def pair_step(p, carry):
            lanes = pl.ds(pl.multiple_of(p * 128, 128), 128)
            q_pair = q[block, :, lanes]
            k_same, k_cross = k[block, :, lanes], k[other, :, lanes]
            v_same, v_cross = v[block, :, lanes], v[other, :, lanes]
            for which in range(2):
                q_head = half_of(q_pair, which)
                s_same = nt(k_same, q_head)
                s_cross = nt(k_cross, q_head) + bias[0]
                top = jnp.maximum(
                    jnp.max(s_same, axis=0, keepdims=True), jnp.max(s_cross, axis=0, keepdims=True)
                )
                e_same = jnp.exp(s_same - top)
                e_cross = jnp.exp(s_cross - top)
                total = jnp.sum(e_same, axis=0, keepdims=True) + jnp.sum(
                    e_cross, axis=0, keepdims=True
                )
                mixed = tn(v_same, e_same.astype(BF)) + tn(v_cross, e_cross.astype(BF))
                head = pl.ds(pl.multiple_of(p * 128 + which * HD, HD), HD)
                ctxt[head, :] = mixed[which * HD : which * HD + HD, :] / total
                lse[block, pl.ds(2 * p + which, 1), :] = top + jnp.log(total)
            return carry

        lax.fori_loop(0, HALF // 128, pair_step, 0)
        ctx[block] = ctxt[...].T.astype(BF)
        return nn(ctx[block], wo[...])

    psend[...] = attend(y).astype(BF)
    part_sent = copies.push(psend, precv, peer)
    mid[...] = h[...] + attend(x)
    saves = [
        copies.local(a, b)
        for a, b in ((na, na_o), (q, q_o), (k, k_o), (v, v_o), (ctx, ctx_o), (lse, lse_o))
    ]
    part_sent.wait()
    mid[...] = mid[...] + precv[...].astype(F32)
    for copy in saves:
        copy.wait()


def hbm():
    return pl.BlockSpec(memory_space=pl.ANY)


def vmem():
    return pl.BlockSpec(memory_space=pltpu.VMEM)


def call(kernel, name, number, ins, outs, out_shape, scratch, n_local, n_remote, flops, args):
    return pl.pallas_call(
        kernel,
        name=name,
        out_shape=out_shape,
        in_specs=ins,
        out_specs=outs,
        scratch_shapes=[
            *scratch,
            pltpu.SemaphoreType.DMA((n_local,)),
            pltpu.SemaphoreType.DMA((n_remote,)),
            pltpu.SemaphoreType.DMA((n_remote,)),
        ],
        cost_estimate=pl.CostEstimate(flops=flops, bytes_accessed=16 << 20, transcendentals=0),
        compiler_params=pltpu.CompilerParams(
            collective_id=number, has_side_effects=True, vmem_limit_bytes=VMEM_BYTES
        ),
    )(*args)


def sds(shape, dtype):
    return jax.ShapeDtypeStruct(shape, dtype)


def attend_fwd(h, wa, scales, tables, bias):
    t = h.shape[0]
    return call(
        attend_fwd_kernel, "attend_fwd", 0,
        [vmem(), hbm(), vmem(), vmem(), pl.BlockSpec(memory_space=pltpu.SMEM)],
        [vmem()] + [hbm()] * 6,
        [
            sds((t, D), F32), sds((2, t, D), BF), sds((2, t, HALF), BF), sds((2, 2 * t, HALF), BF),
            sds((2, 2 * t, HALF), BF), sds((2, t, HALF), BF), sds((2, 8, t), F32),
        ],
        [
            pltpu.VMEM((D, TRI), BF), pltpu.VMEM((HALF, D), BF), pltpu.VMEM((2, t, D), BF),
            pltpu.VMEM((2, t, HALF), BF), pltpu.VMEM((2, 2 * t, HALF), BF),
            pltpu.VMEM((2, 2 * t, HALF), BF), pltpu.VMEM((HALF, t), F32),
            pltpu.VMEM((2, t, HALF), BF), pltpu.VMEM((2, 8, t), F32),
            pltpu.VMEM((t, D), BF), pltpu.VMEM((t, D), BF),
        ],
        8, 8, 6 << 30, (h, wa, scales, tables, bias),
    )


def gelu_parts(hidden):
    phi_cap = 0.5 * (1.0 + lax.erf(hidden * math.sqrt(0.5)))
    density = jnp.exp(-0.5 * hidden * hidden) * (1.0 / math.sqrt(2.0 * math.pi))
    return hidden * phi_cap, phi_cap + hidden * density


def feed_fwd_kernel(
    mid, wf, sc, h_next, nb_o, act_o, slope_o,
    we, ws, nb, act, slope, psend, precv, lsem, ssem, rsem,
):
    d, x, c, peer, sib = place()
    y = 1 - x
    copies = Copies(lsem, ssem, rsem, d)
    greet(d, peer, sib)
    xhat, _ = norm_stats(mid[...])
    nb[x] = (xhat * sc[2:3, :] + sc[3:4, :]).astype(BF)
    nb_sent = copies.push(nb.at[x], nb.at[x], peer)
    we_own, ws_own = we.at[:, rows_of(c, D)], ws.at[rows_of(c, D), :]
    exp_part, shr_part = wf.at[:, pl.ds(0, D)], wf.at[:, pl.ds(D, D)]
    weights = [
        copies.local(exp_part, we_own),
        copies.push(exp_part, we_own, sib),
        copies.local(shr_part, ws_own),
        copies.push(shr_part, ws_own, sib),
    ]
    for copy in weights:
        copy.wait()

    def feed(block):
        def step(i, carry):
            lanes = pl.ds(pl.multiple_of(i * 256, 256), 256)
            value, rate = gelu_parts(nn(nb[block], we[:, lanes]))
            act[block, :, lanes] = value.astype(BF)
            slope[block, :, lanes] = rate.astype(BF)
            return carry

        lax.fori_loop(0, HID // 256, step, 0)
        return nn(act[block], ws[...])

    h_next[...] = mid[...] + feed(x)
    nb_sent.wait()
    psend[...] = feed(y).astype(BF)
    part_sent = copies.push(psend, precv, peer)
    saves = [copies.local(a, b) for a, b in ((nb, nb_o), (act, act_o), (slope, slope_o))]
    part_sent.wait()
    h_next[...] = h_next[...] + precv[...].astype(F32)
    for copy in saves:
        copy.wait()


def feed_fwd(mid, wf, scales):
    t = mid.shape[0]
    return call(
        feed_fwd_kernel, "feed_fwd", 1,
        [vmem(), hbm(), vmem()],
        [vmem()] + [hbm()] * 3,
        [sds((t, D), F32), sds((2, t, D), BF), sds((2, t, HID), BF), sds((2, t, HID), BF)],
        [
            pltpu.VMEM((D, HID), BF), pltpu.VMEM((HID, D), BF), pltpu.VMEM((2, t, D), BF),
            pltpu.VMEM((2, t, HID), BF), pltpu.VMEM((2, t, HID), BF),
            pltpu.VMEM((t, D), BF), pltpu.VMEM((t, D), BF),
        ],
        5, 4, 5 << 30, (mid, wf, scales),
    )


def feed_bwd_kernel(
    g, mid, wf, sc, nb_h, act_h, slope_h, mid_grad, wg_o, rows_o,
    we, ws, nb, act, slope, gl, hg, part, psend, precv, gown, gsend, grecv, lsem, ssem, rsem,
):
    d, x, c, peer, sib = place()
    y = 1 - x
    t = g.shape[0]
    copies = Copies(lsem, ssem, rsem, d)
    greet(d, peer, sib)
    gl[x] = g[...].astype(BF)
    g_sent = copies.push(gl.at[x], gl.at[x], peer)
    we_own, ws_own = we.at[:, rows_of(c, D)], ws.at[rows_of(c, D), :]
    exp_part, shr_part = wf.at[:, pl.ds(0, D)], wf.at[:, pl.ds(D, D)]
    weights = [
        copies.local(shr_part, ws_own),
        copies.push(shr_part, ws_own, sib),
        copies.local(exp_part, we_own),
        copies.push(exp_part, we_own, sib),
        copies.local(slope_h, slope),
        copies.local(act_h, act),
        copies.local(nb_h, nb),
    ]
    for copy in weights:
        copy.wait()

    def back(block):
        def step(i, carry):
            lanes = pl.ds(pl.multiple_of(i * 256, 256), 256)
            pulled = nt(gl[block], ws[lanes, :])
            hg[block, :, lanes] = (pulled * slope[block, :, lanes].astype(F32)).astype(BF)
            return carry

        lax.fori_loop(0, HID // 256, step, 0)
        return nt(hg[block], we[...])

    part[...] = back(x)
    g_sent.wait()
    psend[...] = back(y).astype(BF)
    part_sent = copies.push(psend, precv, peer)

    gl_all = gl[...].reshape(2 * t, D)
    nb_all = nb[...].reshape(2 * t, D)

    def grads(which, store):
        def step(i, carry):
            at = pl.ds(pl.multiple_of(i * 256, 256), 256)
            off = pl.ds(pl.multiple_of(which * D + i * 256, 256), 256)
            hg_part = hg[:, :, off].reshape(2 * t, 256)
            act_part = act[:, :, off].reshape(2 * t, 256)
            store(0, at, tn(nb_all, hg_part))
            store(1, at, tn(act_part, gl_all))
            return carry

        lax.fori_loop(0, D // 256, step, 0)

    def to_send(kind, at, value):
        if kind == 0:
            gsend[:, at] = value.astype(BF)
        else:
            gsend[at, pl.ds(D, D)] = value.astype(BF)

    def to_keep(kind, at, value):
        if kind == 0:
            gown[:, at] = value
        else:
            gown[at, pl.ds(D, D)] = value

    grads(1 - c, to_send)
    grad_sent = copies.push(gsend, grecv, sib)
    grads(c, to_keep)
    part_sent.wait()
    dy = part[...] + precv[...].astype(F32)
    back_mid, rows = norm_back(mid[...], sc[2:3, :], dy)
    mid_grad[...] = g[...] + back_mid
    rows_o[...] = rows
    grad_sent.wait()
    gsend[...] = (gown[...] + grecv[...].astype(F32)).astype(BF)
    copies.local(gsend, wg_o).wait()


def feed_bwd(g, mid, wf, scales, nb, act, slope):
    t = g.shape[0]
    return call(
        feed_bwd_kernel, "feed_bwd", 2,
        [vmem(), vmem(), hbm(), vmem(), hbm(), hbm(), hbm()],
        [vmem(), hbm(), vmem()],
        [sds((t, D), F32), sds((D, 2 * D), BF), sds((2, D), F32)],
        [
            pltpu.VMEM((D, HID), BF), pltpu.VMEM((HID, D), BF), pltpu.VMEM((2, t, D), BF),
            pltpu.VMEM((2, t, HID), BF), pltpu.VMEM((2, t, HID), BF), pltpu.VMEM((2, t, D), BF),
            pltpu.VMEM((2, t, HID), BF), pltpu.VMEM((t, D), F32), pltpu.VMEM((t, D), BF),
            pltpu.VMEM((t, D), BF), pltpu.VMEM((D, 2 * D), F32), pltpu.VMEM((D, 2 * D), BF),
            pltpu.VMEM((D, 2 * D), BF),
        ],
        6, 5, 10 << 30, (g, mid, wf, scales, nb, act, slope),
    )


def attend_bwd_kernel(
    mg, h, wa, sc, cs, bias, na, q, k, v, ctx, lse, g_prev, wg_o, rows_o,
    wt, wo, ml, cg, delta, dqt, dk, dv, kvsend, kvrecv, pg, part, psend, precv,
    gown, gsend, grecv, lsem, ssem, rsem,
):
    d, x, c, peer, sib = place()
    y = 1 - x
    t = mg.shape[0]
    copies = Copies(lsem, ssem, rsem, d)
    greet(d, peer, sib)
    ml[x] = mg[...].astype(BF)
    ml_sent = copies.push(ml.at[x], ml.at[x], peer)
    wt_own, wo_own = wt.at[rows_of(c, HALF), :], wo.at[:, rows_of(c, HALF)]
    tri_part, out_part = wa.at[:, pl.ds(0, TRI)], wa.at[:, pl.ds(TRI, HALF)]
    out_moves = [copies.local(out_part, wo_own), copies.push(out_part, wo_own, sib)]
    tri_moves = [copies.local(tri_part, wt_own), copies.push(tri_part, wt_own, sib)]
    dk[...] = jnp.zeros_like(dk)
    dv[...] = jnp.zeros_like(dv)
    for copy in out_moves:
        copy.wait()

    def attend(block):
        other = 1 - block
        pulled = nt(ml[block], wo[...])
        cg[block] = pulled.astype(BF)
        weighed = (cg[block].astype(F32) * ctx[block].astype(F32)).T
        for head in range(HALF // HD):
            delta[head : head + 1, :] = jnp.sum(
                weighed[head * HD : head * HD + HD, :], axis=0, keepdims=True
            )

        def pair_step(p, carry):
            lanes = pl.ds(pl.multiple_of(p * 128, 128), 128)
            q_pair, cg_pair = q[block, :, lanes], cg[block, :, lanes]
            for which in range(2):
                q_head, cg_head = half_of(q_pair, which), half_of(cg_pair, which)
                row = pl.ds(2 * p + which, 1)
                total, dots = lse[block, row, :], delta[row, :]
                turned = None
                for side in (block, other):
                    k_pair, v_pair = k[side, :, lanes], v[side, :, lanes]
                    scores = nt(k_pair, q_head)
                    if side is other:
                        scores = scores + bias[0]
                    probs = jnp.exp(scores - total)
                    score_grad = (probs * (nt(v_pair, cg_head) - dots)).astype(BF)
                    dv[side, :, lanes] += nn(probs.astype(BF), cg_head)
                    dk[side, :, lanes] += nn(score_grad, q_head)
                    piece = tn(k_pair, score_grad)
                    turned = piece if turned is None else turned + piece
                head = pl.ds(pl.multiple_of(p * 128 + which * HD, HD), HD)
                dqt[block, head, :] = turned[which * HD : which * HD + HD, :] * HD**-0.5
            return carry

        lax.fori_loop(0, HALF // 128, pair_step, 0)

    attend(x)
    ml_sent.wait()
    attend(y)
    theirs, mine = rows_of(1 - c, t), rows_of(c, t)
    for side in range(2):
        kvsend[side, :, pl.ds(0, HALF)] = dk[side, theirs, :].astype(BF)
        kvsend[side, :, pl.ds(HALF, HALF)] = dv[side, theirs, :].astype(BF)
    kv_sent = copies.push(kvsend, kvrecv, sib)

    def unturn(block, j, value):
        cosine, sine = cs[block, :, 0:128], cs[block, :, 128:256]
        rounded = value.astype(BF).astype(F32)
        pg[block, :, pl.ds(128 * j, 128)] = turn(rounded, cosine, -sine).astype(BF)

    for side in range(2):
        for j in range(3):
            unturn(side, j, dqt[side, 128 * j : 128 * j + 128, :].T)
    kv_sent.wait()
    for side in range(2):
        for j in range(3):
            at = pl.ds(128 * j, 128)
            unturn(side, 3 + j, dk[side, mine, at] + kvrecv[side, :, at].astype(F32))
            pg[side, :, pl.ds(D + 128 * j, 128)] = (
                dv[side, mine, at] + kvrecv[side, :, pl.ds(HALF + 128 * j, 128)].astype(F32)
            ).astype(BF)
    for copy in tri_moves:
        copy.wait()
    psend[...] = nt(pg[y], wt[...]).astype(BF)
    part_sent = copies.push(psend, precv, peer)
    part[...] = nt(pg[x], wt[...])

    ml_all = ml[...].reshape(2 * t, D)
    na_all = na[...].reshape(2 * t, D)
    ctx_all = ctx[...].reshape(2 * t, HALF)

    def grads(which, store):
        def step(i, carry):
            off = pl.ds(pl.multiple_of(which * HALF + i * 128, 128), 128)
            at = pl.ds(pl.multiple_of(i * 128, 128), 128)
            store(0, at, tn(na[:, :, off].reshape(2 * t, 128), pg[...].reshape(2 * t, TRI)))
            store(1, at, tn(ctx_all, ml[:, :, off].reshape(2 * t, 128)))
            return carry

        lax.fori_loop(0, HALF // 128, step, 0)

    def to_send(kind, at, value):
        if kind == 0:
            gsend[at, pl.ds(0, TRI)] = value.astype(BF)
        else:
            gsend[:, pl.ds(pl.multiple_of(TRI + at.start, 128), 128)] = value.astype(BF)

    def to_keep(kind, at, value):
        if kind == 0:
            gown[at, pl.ds(0, TRI)] = value
        else:
            gown[:, pl.ds(pl.multiple_of(TRI + at.start, 128), 128)] = value

    grads(1 - c, to_send)
    grad_sent = copies.push(gsend, grecv, sib)
    grads(c, to_keep)
    part_sent.wait()
    dy = part[...] + precv[...].astype(F32)
    back, rows = norm_back(h[...], sc[0:1, :], dy)
    g_prev[...] = mg[...] + back
    rows_o[...] = rows
    grad_sent.wait()
    gsend[...] = (gown[...] + grecv[...].astype(F32)).astype(BF)
    copies.local(gsend, wg_o).wait()


def attend_bwd(mg, h, wa, scales, tables, bias, saved):
    t = mg.shape[0]
    return call(
        attend_bwd_kernel, "attend_bwd", 3,
        [vmem(), vmem(), hbm(), vmem(), vmem(), pl.BlockSpec(memory_space=pltpu.SMEM)] + [vmem()] * 6,
        [vmem(), hbm(), vmem()],
        [sds((t, D), F32), sds((HALF, 2 * D), BF), sds((2, D), F32)],
        [
            pltpu.VMEM((D, TRI), BF), pltpu.VMEM((HALF, D), BF), pltpu.VMEM((2, t, D), BF),
            pltpu.VMEM((2, t, HALF), BF), pltpu.VMEM((8, t), F32), pltpu.VMEM((2, HALF, t), F32),
            pltpu.VMEM((2, 2 * t, HALF), F32), pltpu.VMEM((2, 2 * t, HALF), F32),
            pltpu.VMEM((2, t, D), BF), pltpu.VMEM((2, t, D), BF), pltpu.VMEM((2, t, TRI), BF),
            pltpu.VMEM((t, D), F32), pltpu.VMEM((t, D), BF), pltpu.VMEM((t, D), BF),
            pltpu.VMEM((HALF, 2 * D), F32), pltpu.VMEM((HALF, 2 * D), BF),
            pltpu.VMEM((HALF, 2 * D), BF),
        ],
        3, 6, 10 << 30, (mg, h, wa, scales, tables, bias, *saved),
    )


K_WHOLE, K_HALF, K_OUT, K_EXP, K_SHR = range(5)
KINDS = (K_WHOLE, K_HALF, K_OUT, K_EXP, K_SHR)


class Saved(NamedTuple):
    na: Any
    q: Any
    k: Any
    v: Any
    ctx: Any
    lse: Any
    nb: Any
    act: Any
    slope: Any
    wt: Any
    wo: Any
    we: Any
    ws: Any


class ForwardIn(NamedTuple):
    h0: Any
    sc_own: Any
    cs: Any
    bias: Any
    p_whole: Any
    p_half: Any
    p_out: Any
    p_exp: Any
    p_shr: Any


class ForwardHead(NamedTuple):
    h_out: Any
    h_mid: Any
    mid_o0: Any
    mid_o1: Any
    sc_o: Any


class ForwardScratch(NamedTuple):
    wt: Any
    wo: Any
    we: Any
    ws: Any
    hb: Any
    ob: Any
    sb: Any
    scl: Any
    sc: Any
    na: Any
    q: Any
    k: Any
    v: Any
    ctxt: Any
    ctx: Any
    lse: Any
    nb: Any
    act: Any
    slope: Any
    psend: Any
    precv: Any
    hs: Any
    mid: Any
    ssem: Any
    rsem: Any
    sc_ssem: Any
    sc_rsem: Any
    xs: Any
    xr: Any
    lsem: Any


class Refs:
    def __init__(self, *groups):
        for group in groups:
            for name, ref in zip(group._fields, group):
                setattr(self, name, ref)


def split(refs, *kinds):
    out, at = [], 0
    for kind in kinds:
        size = len(kind._fields)
        out.append(kind(*refs[at : at + size]))
        at += size
    return out


class Weights:
    def __init__(self, n, dp, rows):
        self.n = n
        self.zs = dp // 2
        self.rows = rows
        s = lax.axis_index("seq")
        self.s = s
        self.x, self.c = lax.div(s, 2), lax.rem(s, 2)
        self.d = lax.axis_index("dp")
        self.z, self.y = lax.div(self.d, 2), lax.rem(self.d, 2)
        self.sib, self.peer = s + 1 - 2 * self.c, lax.rem(s + 2, SEQ)
        self.across = self.d + 1 - 2 * self.y
        self.upper = lax.div(self.z, self.zs // 2)
        self.source = {K_WHOLE: n.p_whole, K_HALF: n.p_half, K_OUT: n.p_out, K_EXP: n.p_exp, K_SHR: n.p_shr}

    def slot(self, kind):
        return self.z if kind == K_EXP else 2 * lax.rem(self.z, self.zs // 2) + self.c

    def target(self, kind):
        if kind == K_EXP:
            return self.s
        if kind == K_WHOLE:
            return 2 * self.x + self.upper
        if kind == K_HALF:
            return 2 * (1 - self.x) + self.upper
        return 2 * self.upper + self.x

    def view(self, kind, layer, y, j, x, c):
        n, r = self.n, self.rows
        if kind == K_EXP:
            return n.we.at[layer, rows_of(2 * j + y, r), rows_of(c, D)]
        core = lax.rem(j, 2)
        at = 2 * lax.div(j, 2) + y
        if kind == K_WHOLE:
            start = pl.multiple_of(HALF * c + r * at, r)
            return n.wt.at[layer, pl.ds(start, r), rows_of(x + core, HALF)]
        if kind == K_HALF:
            return n.hb.at[layer, core, rows_of(at, r), :]
        if kind == K_OUT:
            return n.ob.at[layer, core, rows_of(at, r), :]
        return n.sb.at[layer, core, rows_of(at, 4 * r), :]

    def remote(self, src, dst, kind, layer, stage, sent, slot, to):
        number = kind
        return pltpu.make_async_remote_copy(
            src_ref=src,
            dst_ref=dst,
            send_sem=self.n.ssem.at[layer, number, stage, sent],
            recv_sem=self.n.rsem.at[layer, number, stage, slot],
            device_id=to,
            device_id_type=MESH,
        )

    def first(self, kind, layer, act):
        number = kind
        slot, to = self.slot(kind), self.target(kind)
        src = self.source[kind].at[layer]
        dst = self.view(kind, layer, self.y, slot, lax.div(to, 2), lax.rem(to, 2))

        def one(k):
            other = lax.rem(self.z + k, self.zs)
            copy = self.remote(src, dst, kind, layer, 0, k, slot, (2 * other + self.y, to))
            copy.start() if act == "start" else copy.wait_send()

        def here():
            if act == "start":
                pltpu.make_async_copy(src, dst, self.n.rsem.at[layer, number, 0, slot]).start()

        if kind == K_EXP:
            here()
        elif kind == K_HALF:
            one(0)
        else:
            pl.when(to == self.s)(here)
            pl.when(to != self.s)(lambda: one(0))

        def step(k, carry):
            one(k)
            return carry

        lax.fori_loop(1, self.zs, step, 0)

    def onward(self, kind, layer, j):
        ref = self.view(kind, layer, self.y, j, self.x, self.c)
        copy = self.remote(ref, ref, kind, layer, 0, j, j, (self.across, self.s))
        copy.wait_recv()
        self.remote(ref, ref, kind, layer, 1, j, j, (self.across, self.s)).start()

    def onward_all(self, kind, layer):
        def step(j, carry):
            self.onward(kind, layer, j)
            return carry

        lax.fori_loop(0, self.zs, step, 0)

    def arrive(self, kind, layer):
        def step(j, carry):
            ref = self.view(kind, layer, 1 - self.y, j, self.x, self.c)
            self.remote(ref, ref, kind, layer, 1, j, j, (self.across, self.s)).wait_recv()
            return carry

        lax.fori_loop(0, self.zs, step, 0)

    def finish(self, kind, layer):
        self.first(kind, layer, "wait")

        def step(j, carry):
            ref = self.view(kind, layer, self.y, j, self.x, self.c)
            self.remote(ref, ref, kind, layer, 1, j, j, (self.across, self.s)).wait_send()
            return carry

        lax.fori_loop(0, self.zs, step, 0)


def greet_all(w):
    barrier = pltpu.get_barrier_semaphore()

    def one(i, carry):
        z, s = lax.div(i, SEQ), lax.rem(i, SEQ)
        away = jnp.logical_or(z != w.z, s != w.s)

        @pl.when(away)
        def _():
            pl.semaphore_signal(barrier, inc=1, device_id=(2 * z + w.y, s), device_id_type=MESH)

        return carry

    lax.fori_loop(0, w.zs * SEQ, one, 0)
    pl.semaphore_signal(barrier, inc=1, device_id=(w.across, w.s), device_id_type=MESH)
    pl.semaphore_wait(barrier, w.zs * SEQ)


def gather_scales_start(w):
    n = w.n
    mine = n.scl.at[w.y, w.z, w.s]
    mine[...] = n.sc_own[...]

    def one(i, carry):
        z, s = lax.div(i, SEQ), lax.rem(i, SEQ)

        @pl.when(jnp.logical_or(z != w.z, s != w.s))
        def _():
            pltpu.make_async_remote_copy(
                src_ref=mine, dst_ref=mine, send_sem=n.sc_ssem.at[i],
                recv_sem=n.sc_rsem.at[w.z * SEQ + w.s], device_id=(2 * z + w.y, s), device_id_type=MESH,
            ).start()

        return carry

    lax.fori_loop(0, w.zs * SEQ, one, 0)


def gather_scales_end(w):
    n = w.n

    def one(i, carry):
        z, s = lax.div(i, SEQ), lax.rem(i, SEQ)

        @pl.when(jnp.logical_or(z != w.z, s != w.s))
        def _():
            slot = n.scl.at[w.y, z, s]
            copy = pltpu.make_async_remote_copy(
                src_ref=slot, dst_ref=slot, send_sem=n.sc_ssem.at[i], recv_sem=n.sc_rsem.at[i],
                device_id=(2 * z + w.y, s), device_id_type=MESH,
            )
            copy.wait_recv()
            copy.wait_send()

        return carry

    lax.fori_loop(0, w.zs * SEQ, one, 0)
    count = w.zs * SEQ
    plane = n.scl.at[w.y]
    copy = pltpu.make_async_remote_copy(
        src_ref=plane, dst_ref=plane, send_sem=n.sc_ssem.at[count], recv_sem=n.sc_rsem.at[count],
        device_id=(w.across, w.s), device_id_type=MESH,
    )
    copy.start()
    copy.wait()
    wide = n.sc.shape[-1] // (2 * w.zs)
    for s in range(SEQ):
        both = [n.scl[d % 2, d // 2, s][:, :wide] for d in range(2 * w.zs)]
        rows = jnp.concatenate(both, axis=1)
        for layer in range(LAYERS):
            n.sc[layer, s : s + 1, :] = rows[layer : layer + 1, :]


def fwd_kernel(dp, *refs):
    ins, outs, saved0, saved1, scratch = split(refs, ForwardIn, ForwardHead, Saved, Saved, ForwardScratch)
    n = Refs(ins, outs, scratch)
    saved = (saved0, saved1)
    rows = n.p_exp.shape[1]
    t = n.h0.shape[0]
    w = Weights(n, dp, rows)
    x, c, peer, sib = w.x, w.c, w.peer, w.sib
    y = 1 - x
    copies = Copies(n.lsem, n.xs, n.xr, w.d)
    waits = []

    def save(src, dst):
        waits.append(copies.local(src, dst))

    greet_all(w)
    w.first(K_WHOLE, 0, "start")
    w.first(K_HALF, 0, "start")
    gather_scales_start(w)
    w.first(K_OUT, 0, "start")
    n.hs[0] = n.h0[...]
    xhat, _ = norm_stats(n.hs[0])
    gather_scales_end(w)

    def share_tri(layer):
        own = n.wt.at[layer, rows_of(c, HALF), :]
        n.wt[layer, rows_of(c, HALF), rows_of(2 * (1 - x), HALF)] = jnp.concatenate(
            [n.hb[layer, 0], n.hb[layer, 1]], axis=1
        )
        return copies.push(own, own, sib)

    def share_cols(into, parts, layer):
        own = into.at[layer, :, rows_of(c, HALF)]
        into[layer, :, rows_of(c, HALF)] = jnp.concatenate([parts[layer, 0], parts[layer, 1]], axis=1)
        return copies.push(own, own, sib)

    def share_exp(layer):
        own = n.we.at[layer, :, rows_of(c, D)]
        return copies.push(own, own, sib)

    for layer in range(LAYERS):
        last = layer == LAYERS - 1
        if layer:
            xhat, _ = norm_stats(n.hs[layer])
        n.na[layer, x] = (xhat * n.sc[layer, 0:1, :] + n.sc[layer, 1:2, :]).astype(BF)
        na_sent = copies.push(n.na.at[layer, x], n.na.at[layer, x], peer)
        if layer == 0:
            w.onward_all(K_WHOLE, 0)
            w.onward_all(K_HALF, 0)
            w.first(K_EXP, 0, "start")
            w.onward_all(K_OUT, 0)
            w.first(K_SHR, 0, "start")
            w.arrive(K_WHOLE, 0)
            w.arrive(K_HALF, 0)
            tri_sent = share_tri(0)
        tri_sent.wait()

        def project(block):
            cosine, sine = n.cs[block, :, 0:128], n.cs[block, :, 128:256]
            for j in range(9):
                part = nn(n.na[layer, block], n.wt[layer, :, 128 * j : 128 * j + 128])
                lanes = pl.ds(128 * (j % 3), 128)
                if j < 3:
                    n.q[layer, block, :, lanes] = (turn(part, cosine, sine) * HD**-0.5).astype(BF)
                elif j < 6:
                    n.k[layer, block, rows_of(c, t), lanes] = turn(part, cosine, sine).astype(BF)
                else:
                    n.v[layer, block, rows_of(c, t), lanes] = part.astype(BF)

        def share(block):
            at = (layer, block, rows_of(c, t))
            return [
                copies.push(n.k.at[at], n.k.at[at], sib),
                copies.push(n.v.at[at], n.v.at[at], sib),
            ]

        project(x)
        shared = share(x)
        na_sent.wait()
        project(y)
        shared += share(y)
        w.arrive(K_OUT, layer)
        out_sent = share_cols(n.wo, n.ob, layer)
        for copy in shared:
            copy.wait()
        save(n.na.at[layer], saved[layer].na)
        save(n.q.at[layer], saved[layer].q)
        save(n.k.at[layer], saved[layer].k)
        save(n.v.at[layer], saved[layer].v)

        def attend(block, pump):
            other = 1 - block

            def pair_step(p, carry):
                pump(p)
                lanes = pl.ds(pl.multiple_of(p * 128, 128), 128)
                q_pair = n.q[layer, block, :, lanes]
                k_same, k_cross = n.k[layer, block, :, lanes], n.k[layer, other, :, lanes]
                v_same, v_cross = n.v[layer, block, :, lanes], n.v[layer, other, :, lanes]
                for which in range(2):
                    q_head = half_of(q_pair, which)
                    s_same = nt(k_same, q_head)
                    s_cross = nt(k_cross, q_head) + n.bias[0]
                    top = jnp.maximum(
                        jnp.max(s_same, axis=0, keepdims=True), jnp.max(s_cross, axis=0, keepdims=True)
                    )
                    e_same = jnp.exp(s_same - top)
                    e_cross = jnp.exp(s_cross - top)
                    total = jnp.sum(e_same, axis=0, keepdims=True) + jnp.sum(
                        e_cross, axis=0, keepdims=True
                    )
                    mixed = tn(v_same, e_same.astype(BF)) + tn(v_cross, e_cross.astype(BF))
                    head = pl.ds(pl.multiple_of(p * 128 + which * HD, HD), HD)
                    n.ctxt[head, :] = mixed[which * HD : which * HD + HD, :] / total
                    n.lse[layer, block, pl.ds(2 * p + which, 1), :] = top + jnp.log(total)
                return carry

            lax.fori_loop(0, HALF // 128, pair_step, 0)
            n.ctx[layer, block] = n.ctxt[...].T.astype(BF)

        attend(y, lambda p: w.onward(K_EXP, layer, p))
        out_sent.wait()
        use = 2 * layer
        n.psend[use] = nn(n.ctx[layer, y], n.wo[layer]).astype(BF)
        part_sent = copies.push(n.psend.at[use], n.precv.at[use], peer)

        def rest(p):
            w.onward(K_SHR, layer, p)

        w.onward(K_EXP, layer, w.zs - 1)
        attend(x, rest)
        w.onward(K_SHR, layer, w.zs - 1)
        if not last:
            w.first(K_WHOLE, layer + 1, "start")
            w.first(K_HALF, layer + 1, "start")
            w.first(K_OUT, layer + 1, "start")
        n.mid[layer] = n.hs[layer] + nn(n.ctx[layer, x], n.wo[layer])
        save(n.ctx.at[layer], saved[layer].ctx)
        save(n.lse.at[layer], saved[layer].lse)
        save(n.wt.at[layer], saved[layer].wt)
        save(n.wo.at[layer], saved[layer].wo)
        part_sent.wait()
        n.mid[layer] = n.mid[layer] + n.precv[use].astype(F32)
        save(n.mid.at[layer], (n.mid_o0, n.mid_o1)[layer])

        xhat, _ = norm_stats(n.mid[layer])
        n.nb[layer, x] = (xhat * n.sc[layer, 2:3, :] + n.sc[layer, 3:4, :]).astype(BF)
        nb_sent = copies.push(n.nb.at[layer, x], n.nb.at[layer, x], peer)
        w.arrive(K_EXP, layer)
        exp_sent = share_exp(layer)
        w.arrive(K_SHR, layer)
        shr_sent = share_cols(n.ws, n.sb, layer)
        exp_sent.wait()

        def feed(block, pump):
            def step(i, carry):
                pump(i)
                lanes = pl.ds(pl.multiple_of(i * 256, 256), 256)
                value, rate = gelu_parts(nn(n.nb[layer, block], n.we[layer, :, lanes]))
                n.act[layer, block, :, lanes] = value.astype(BF)
                n.slope[layer, block, :, lanes] = rate.astype(BF)
                return carry

            lax.fori_loop(0, HID // 256, step, 0)

        def pump_tri(i):
            if not last:

                @pl.when(i < w.zs)
                def _():
                    w.onward(K_WHOLE, layer + 1, i)
                    w.onward(K_HALF, layer + 1, i)

        def pump_out(i):
            if not last:

                @pl.when(i < w.zs)
                def _():
                    w.onward(K_OUT, layer + 1, i)

        feed(x, pump_tri)
        shr_sent.wait()
        n.hs[layer + 1] = n.mid[layer] + nn(n.act[layer, x], n.ws[layer])
        nb_sent.wait()
        feed(y, pump_out)
        use = 2 * layer + 1
        n.psend[use] = nn(n.act[layer, y], n.ws[layer]).astype(BF)
        part_sent = copies.push(n.psend.at[use], n.precv.at[use], peer)
        save(n.nb.at[layer], saved[layer].nb)
        save(n.act.at[layer], saved[layer].act)
        save(n.slope.at[layer], saved[layer].slope)
        save(n.we.at[layer], saved[layer].we)
        save(n.ws.at[layer], saved[layer].ws)
        if not last:
            w.first(K_EXP, layer + 1, "start")
            w.first(K_SHR, layer + 1, "start")
            w.arrive(K_WHOLE, layer + 1)
            w.arrive(K_HALF, layer + 1)
            tri_sent = share_tri(layer + 1)
        part_sent.wait()
        n.hs[layer + 1] = n.hs[layer + 1] + n.precv[use].astype(F32)

    n.h_out[...] = n.hs[LAYERS]
    n.sc_o[...] = n.sc[...]
    save(n.hs.at[1], n.h_mid)
    for copy in waits:
        copy.wait()
    for layer in range(LAYERS):
        for kind in KINDS:
            w.finish(kind, layer)


def forward_all(dp, h, sc_own, tables, bias, pieces):
    t = h.shape[0]
    zs = dp // 2
    per_layer = [
        sds((2, t, D), BF), sds((2, t, HALF), BF), sds((2, 2 * t, HALF), BF), sds((2, 2 * t, HALF), BF),
        sds((2, t, HALF), BF), sds((2, 8, t), F32), sds((2, t, D), BF), sds((2, t, HID), BF), sds((2, t, HID), BF),
        sds((D, TRI), BF), sds((HALF, D), BF), sds((D, HID), BF), sds((HID, D), BF),
    ]
    token = sds((t, D), F32)
    outs = [token, token, token, token, sds((LAYERS, 4, D), F32), *per_layer, *per_layer]
    specs = [vmem(), hbm(), hbm(), hbm(), vmem(), *([hbm()] * (2 * len(per_layer)))]
    n_layers = LAYERS
    scratch = [
        pltpu.VMEM((n_layers, D, TRI), BF), pltpu.VMEM((n_layers, HALF, D), BF),
        pltpu.VMEM((n_layers, D, HID), BF), pltpu.VMEM((n_layers, HID, D), BF),
        pltpu.VMEM((n_layers, 2, HALF, 192), BF), pltpu.VMEM((n_layers, 2, HALF, 192), BF),
        pltpu.VMEM((n_layers, 2, HID, 192), BF), pltpu.VMEM((2, zs, SEQ, 8, 128), F32),
        pltpu.VMEM((n_layers, 4, D), F32), pltpu.VMEM((n_layers, 2, t, D), BF),
        pltpu.VMEM((n_layers, 2, t, HALF), BF), pltpu.VMEM((n_layers, 2, 2 * t, HALF), BF),
        pltpu.VMEM((n_layers, 2, 2 * t, HALF), BF), pltpu.VMEM((HALF, t), F32),
        pltpu.VMEM((n_layers, 2, t, HALF), BF), pltpu.VMEM((n_layers, 2, 8, t), F32),
        pltpu.VMEM((n_layers, 2, t, D), BF), pltpu.VMEM((n_layers, 2, t, HID), BF),
        pltpu.VMEM((n_layers, 2, t, HID), BF), pltpu.VMEM((2 * n_layers, t, D), BF),
        pltpu.VMEM((2 * n_layers, t, D), BF), pltpu.VMEM((n_layers + 1, t, D), F32),
        pltpu.VMEM((n_layers, t, D), F32),
        pltpu.SemaphoreType.DMA((n_layers, len(KINDS), 2, zs)),
        pltpu.SemaphoreType.DMA((n_layers, len(KINDS), 2, zs)),
        pltpu.SemaphoreType.DMA((zs * SEQ + 1,)), pltpu.SemaphoreType.DMA((zs * SEQ + 1,)),
        pltpu.SemaphoreType.DMA((24,)), pltpu.SemaphoreType.DMA((24,)), pltpu.SemaphoreType.DMA((32,)),
    ]
    results = pl.pallas_call(
        functools.partial(fwd_kernel, dp),
        name="forward",
        out_shape=outs,
        in_specs=[vmem(), vmem(), vmem(), pl.BlockSpec(memory_space=pltpu.SMEM), *([hbm()] * 5)],
        out_specs=specs,
        scratch_shapes=scratch,
        cost_estimate=pl.CostEstimate(flops=22 << 30, bytes_accessed=32 << 20, transcendentals=0),
        compiler_params=pltpu.CompilerParams(
            collective_id=4, has_side_effects=True, vmem_limit_bytes=VMEM_BYTES
        ),
    )(h, sc_own, tables, bias, *pieces)
    return split(results, ForwardHead, Saved, Saved)


def pieces_of(triple_weight, output_weight, expand_weight, shrink_weight, c):
    tri = triple_weight.astype(BF)
    whole = jnp.where(c == 0, tri[:, :, :HALF], tri[:, :, 192:])
    half = jnp.where(c == 0, tri[:, :, HALF:], tri[:, :, :192])
    return whole, half, output_weight.astype(BF), expand_weight.astype(BF), shrink_weight.astype(BF)


class Sums:
    def __init__(self, n, dp, rows):
        self.n = n
        self.zs = dp // 2
        self.rows = rows
        s = lax.axis_index("seq")
        self.s = s
        self.x, self.c = lax.div(s, 2), lax.rem(s, 2)
        self.d = lax.axis_index("dp")
        self.z, self.y = lax.div(self.d, 2), lax.rem(self.d, 2)
        self.sib, self.peer = s + 1 - 2 * self.c, lax.rem(s + 2, SEQ)
        self.across = self.d + 1 - 2 * self.y
        self.staged = {K_WHOLE: n.gw, K_HALF: n.gh, K_OUT: n.go, K_EXP: n.ge, K_SHR: n.gs}
        self.landed = {K_WHOLE: n.yw, K_HALF: n.yh, K_OUT: n.yo, K_EXP: n.ye, K_SHR: n.ys}
        self.owned = {K_WHOLE: n.zw, K_HALF: n.zh, K_OUT: n.zo, K_EXP: n.ze, K_SHR: n.zr}

    def view(self, kind, layer, y, j):
        r = self.rows
        if kind == K_EXP:
            return self.staged[kind].at[layer, rows_of(2 * j + y, r), :]
        tall = 4 * r if kind == K_SHR else r
        return self.staged[kind].at[layer, lax.rem(j, 2), rows_of(2 * lax.div(j, 2) + y, tall), :]

    def owner(self, kind, j):
        if kind == K_EXP:
            return j, self.s
        zz, core, half = lax.div(j, 2), lax.rem(j, 2), self.zs // 2
        if kind == K_WHOLE:
            return self.c * half + zz, 2 * self.x + core
        if kind == K_HALF:
            return self.c * half + zz, 2 * (1 - self.x) + core
        return self.x * half + zz, 2 * self.c + core

    def remote(self, src, dst, kind, layer, stage, sent, slot, to):
        number = kind
        return pltpu.make_async_remote_copy(
            src_ref=src,
            dst_ref=dst,
            send_sem=self.n.ssem.at[layer, number, stage, sent],
            recv_sem=self.n.rsem.at[layer, number, stage, slot],
            device_id=to,
            device_id_type=MESH,
        )

    def over(self, fn):
        def step(j, carry):
            fn(j)
            return carry

        lax.fori_loop(0, self.zs, step, 0)

    def across_copy(self, kind, layer, j):
        return self.remote(
            self.view(kind, layer, 1 - self.y, j), self.landed[kind].at[layer, j],
            kind, layer, 0, j, j, (self.across, self.s),
        )

    def across_all(self, kind, layer):
        self.over(lambda j: self.across_copy(kind, layer, j).start())

    def along_copy(self, kind, layer, j):
        z, s = self.owner(kind, j)
        src, dst = self.view(kind, layer, self.y, j), self.owned[kind].at[layer, self.z]
        away = jnp.logical_or(z != self.z, s != self.s)
        far = self.remote(src, dst, kind, layer, 1, j, self.z, (2 * z + self.y, s))
        number = kind
        return away, far, src, dst, self.n.rsem.at[layer, number, 1, self.z]

    def along(self, kind, layer, j):
        self.across_copy(kind, layer, j).wait_recv()
        mine = self.view(kind, layer, self.y, j)
        mine[...] = (mine[...].astype(F32) + self.landed[kind][layer, j].astype(F32)).astype(BF)
        away, far, src, dst, sem = self.along_copy(kind, layer, j)
        pl.when(away)(lambda: far.start())
        pl.when(jnp.logical_not(away))(lambda: pltpu.make_async_copy(src, dst, sem).start())

    def total(self, kind, layer):
        def wait(z):
            ref = self.owned[kind].at[layer, z]
            self.remote(ref, ref, kind, layer, 1, z, z, (self.across, self.s)).wait_recv()

        self.over(wait)
        value = self.owned[kind][layer, 0].astype(F32)
        for z in range(1, self.zs):
            value = value + self.owned[kind][layer, z].astype(F32)
        return value

    def finish(self, kind, layer):
        def step(j):
            self.across_copy(kind, layer, j).wait_send()
            away, far, _, _, _ = self.along_copy(kind, layer, j)
            pl.when(away)(lambda: far.wait_send())

        self.over(step)


def everywhere_start(w, use, buf):
    n = w.n
    mine = buf.at[w.y, w.z, w.s]

    def one(i, carry):
        z, s = lax.div(i, SEQ), lax.rem(i, SEQ)

        @pl.when(jnp.logical_or(z != w.z, s != w.s))
        def _():
            pltpu.make_async_remote_copy(
                src_ref=mine, dst_ref=mine, send_sem=n.ev_ssem.at[use, i],
                recv_sem=n.ev_rsem.at[use, w.z * SEQ + w.s], device_id=(2 * z + w.y, s), device_id_type=MESH,
            ).start()

        return carry

    lax.fori_loop(0, w.zs * SEQ, one, 0)


def everywhere_end(w, use, buf, pair):
    n = w.n

    def one(i, carry):
        z, s = lax.div(i, SEQ), lax.rem(i, SEQ)

        @pl.when(jnp.logical_or(z != w.z, s != w.s))
        def _():
            slot = buf.at[w.y, z, s]
            copy = pltpu.make_async_remote_copy(
                src_ref=slot, dst_ref=slot, send_sem=n.ev_ssem.at[use, i], recv_sem=n.ev_rsem.at[use, i],
                device_id=(2 * z + w.y, s), device_id_type=MESH,
            )
            copy.wait_recv()
            copy.wait_send()

        return carry

    lax.fori_loop(0, w.zs * SEQ, one, 0)

    def add(i, total):
        return total + buf[w.y, lax.div(i, SEQ), lax.rem(i, SEQ)]

    pair[w.y] = lax.fori_loop(1, w.zs * SEQ, add, buf[w.y, 0, 0])
    count = w.zs * SEQ
    copy = pltpu.make_async_remote_copy(
        src_ref=pair.at[w.y], dst_ref=pair.at[w.y], send_sem=n.ev_ssem.at[use, count],
        recv_sem=n.ev_rsem.at[use, count], device_id=(w.across, w.s), device_id_type=MESH,
    )
    copy.start()
    copy.wait()
    return pair[0] + pair[1]


class Loaded(NamedTuple):
    na: Any
    q: Any
    k: Any
    v: Any
    ctx: Any
    lse: Any
    nb: Any
    act: Any
    slope: Any
    wt: Any
    wo: Any
    we: Any
    ws: Any
    h: Any
    mid: Any


class BackwardIn(NamedTuple):
    g0: Any
    sc: Any
    cs: Any
    bias: Any


class BackwardOut(NamedTuple):
    g_out: Any
    scale_o: Any
    norm_o: Any
    whole_g: Any
    half_g: Any
    out_g: Any
    exp_g: Any
    shr_g: Any


class BackwardScratch(NamedTuple):
    gl: Any
    hg: Any
    ml: Any
    cg: Any
    delta: Any
    dqt: Any
    dk: Any
    dv: Any
    kvsend: Any
    kvrecv: Any
    pg: Any
    part: Any
    psend: Any
    precv: Any
    gs_exp: Any
    gr_exp: Any
    gs_shr: Any
    gr_shr: Any
    gr_att: Any
    gw: Any
    gh: Any
    go: Any
    ge: Any
    gs: Any
    yw: Any
    yh: Any
    yo: Any
    ye: Any
    ys: Any
    zw: Any
    zh: Any
    zo: Any
    ze: Any
    zr: Any
    early: Any
    early_pair: Any
    late: Any
    late_pair: Any
    sq: Any
    sq_pair: Any
    ssem: Any
    rsem: Any
    ev_ssem: Any
    ev_rsem: Any
    xs: Any
    xr: Any
    lsem: Any


def bwd_kernel(dp, *refs):
    ins, saved0, saved1, outs, loaded, scratch = split(
        refs, BackwardIn, Loaded, Loaded, BackwardOut, Loaded, BackwardScratch
    )
    n = Refs(ins, outs, loaded, scratch)
    saved = (saved0, saved1)
    t = n.g0.shape[0]
    w = Sums(n, dp, D // dp)
    x, c, peer, sib = w.x, w.c, w.peer, w.sib
    y = 1 - x
    copies = Copies(n.lsem, n.xs, n.xr, w.d)
    loading = {}

    def load(layer, *wanted):
        for place in wanted:
            loading[place] = copies.local(saved[layer][place], loaded[place])

    def ready(*wanted):
        for place in wanted:
            loading[place].wait()

    na, q, k, v, ctx, lse, nb, act, slope, wt, wo, we, ws, h, mid = range(len(Loaded._fields))
    feed_places = (ws, slope, we, act, nb, mid)
    attend_places = (wo, ctx, q, k, v, lse, wt, na, h)
    load(LAYERS - 1, *feed_places, *attend_places)
    greet_all(w)
    n.g_out[...] = n.g0[...]

    for layer in reversed(range(LAYERS)):
        top = layer == LAYERS - 1

        n.gl[layer, x] = n.g_out[...].astype(BF)
        g_sent = copies.push(n.gl.at[layer, x], n.gl.at[layer, x], peer)
        ready(ws, slope, we)

        def back(block, pump):
            def step(i, carry):
                pump(i)
                lanes = pl.ds(pl.multiple_of(i * 256, 256), 256)
                pulled = nt(n.gl[layer, block], n.ws[lanes, :])
                n.hg[block, :, lanes] = (pulled * n.slope[block, :, lanes].astype(F32)).astype(BF)
                return carry

            lax.fori_loop(0, HID // 256, step, 0)
            return nt(n.hg[block], n.we[...])

        def pump_tri(i):
            if not top:

                @pl.when(i < w.zs)
                def _():
                    w.along(K_WHOLE, layer + 1, i)
                    w.along(K_HALF, layer + 1, i)
                    w.along(K_OUT, layer + 1, i)

        n.part[...] = back(x, lambda i: None)
        g_sent.wait()
        use = 2 * layer
        n.psend[...] = back(y, lambda i: None).astype(BF)
        part_sent = copies.push(n.psend, n.precv.at[use], peer)
        ready(act, nb, mid)
        gl_all = n.gl[layer].reshape(2 * t, D)
        nb_all = n.nb[...].reshape(2 * t, D)

        def exp_tile(which, i):
            off = pl.ds(pl.multiple_of(which * D + i * 256, 256), 256)
            return tn(nb_all, n.hg[:, :, off].reshape(2 * t, 256))

        def shr_tile(which, i):
            off = pl.ds(pl.multiple_of(i * 256, 256), 256)
            cols = n.gl[layer, :, :, rows_of(which, HALF)].reshape(2 * t, HALF)
            return tn(n.act[:, :, off].reshape(2 * t, 256), cols)

        def send_exp(i, carry):
            at = pl.ds(pl.multiple_of(i * 256, 256), 256)
            n.gs_exp[:, at] = exp_tile(1 - c, i).astype(BF)
            return carry

        def send_shr(i, carry):
            at = pl.ds(pl.multiple_of(i * 256, 256), 256)
            n.gs_shr[at, :] = shr_tile(1 - c, i).astype(BF)
            return carry

        lax.fori_loop(0, D // 256, send_exp, 0)
        exp_sent = copies.push(n.gs_exp, n.gr_exp, sib)
        lax.fori_loop(0, HID // 256, send_shr, 0)
        shr_sent = copies.push(n.gs_shr, n.gr_shr, sib)

        def keep_exp(i, carry):
            at = pl.ds(pl.multiple_of(i * 256, 256), 256)
            n.ge[layer, :, at] = (exp_tile(c, i) + n.gr_exp[:, at].astype(F32)).astype(BF)
            return carry

        def keep_shr(i, carry):
            pump_tri(i)
            at = pl.ds(pl.multiple_of(i * 256, 256), 256)
            value = (shr_tile(c, i) + n.gr_shr[at, :].astype(F32)).astype(BF)
            n.gs[layer, 0, at, :] = value[:, :192]
            n.gs[layer, 1, at, :] = value[:, 192:]
            return carry

        exp_sent.wait()
        lax.fori_loop(0, D // 256, keep_exp, 0)
        w.across_all(K_EXP, layer)
        shr_sent.wait()
        lax.fori_loop(0, HID // 256, keep_shr, 0)
        w.across_all(K_SHR, layer)
        part_sent.wait()
        dy = n.part[...] + n.precv[use].astype(F32)
        back_mid, rows_b = norm_back(n.mid[...], n.sc[layer, 2:3, :], dy)
        n.g_out[...] = n.g_out[...] + back_mid

        n.ml[layer, x] = n.g_out[...].astype(BF)
        ml_sent = copies.push(n.ml.at[layer, x], n.ml.at[layer, x], peer)
        if layer:
            load(layer - 1, *feed_places)
        n.dk[...] = jnp.zeros_like(n.dk)
        n.dv[...] = jnp.zeros_like(n.dv)
        ready(wo, ctx, q, k, v, lse)

        def attend(block, pump):
            other = 1 - block
            n.cg[block] = nt(n.ml[layer, block], n.wo[...]).astype(BF)
            weighed = (n.cg[block].astype(F32) * n.ctx[block].astype(F32)).T
            for head in range(HALF // HD):
                n.delta[head : head + 1, :] = jnp.sum(
                    weighed[head * HD : head * HD + HD, :], axis=0, keepdims=True
                )

            def pair_step(p, carry):
                pump(p)
                lanes = pl.ds(pl.multiple_of(p * 128, 128), 128)
                q_pair, cg_pair = n.q[block, :, lanes], n.cg[block, :, lanes]
                for which in range(2):
                    q_head, cg_head = half_of(q_pair, which), half_of(cg_pair, which)
                    row = pl.ds(2 * p + which, 1)
                    total, dots = n.lse[block, row, :], n.delta[row, :]
                    turned = None
                    for side in (block, other):
                        k_pair, v_pair = n.k[side, :, lanes], n.v[side, :, lanes]
                        scores = nt(k_pair, q_head)
                        if side is other:
                            scores = scores + n.bias[0]
                        probs = jnp.exp(scores - total)
                        score_grad = (probs * (nt(v_pair, cg_head) - dots)).astype(BF)
                        n.dv[side, :, lanes] += nn(probs.astype(BF), cg_head)
                        n.dk[side, :, lanes] += nn(score_grad, q_head)
                        piece = tn(k_pair, score_grad)
                        turned = piece if turned is None else turned + piece
                    head = pl.ds(pl.multiple_of(p * 128 + which * HD, HD), HD)
                    n.dqt[block, head, :] = turned[which * HD : which * HD + HD, :] * HD**-0.5
                return carry

            lax.fori_loop(0, HALF // 128, pair_step, 0)

        attend(x, lambda p: w.along(K_EXP, layer, p))
        ml_sent.wait()

        def pump_y(p):
            w.along(K_SHR, layer, p)

        w.along(K_EXP, layer, w.zs - 1)
        attend(y, pump_y)
        theirs, mine = rows_of(1 - c, t), rows_of(c, t)
        for side in range(2):
            n.kvsend[side, :, pl.ds(0, HALF)] = n.dk[side, theirs, :].astype(BF)
            n.kvsend[side, :, pl.ds(HALF, HALF)] = n.dv[side, theirs, :].astype(BF)
        kv_sent = copies.push(n.kvsend, n.kvrecv.at[layer], sib)
        w.along(K_SHR, layer, w.zs - 1)

        def unturn(block, j, value):
            cosine, sine = n.cs[block, :, 0:128], n.cs[block, :, 128:256]
            rounded = value.astype(BF).astype(F32)
            n.pg[block, :, pl.ds(128 * j, 128)] = turn(rounded, cosine, -sine).astype(BF)

        for side in range(2):
            for j in range(3):
                unturn(side, j, n.dqt[side, 128 * j : 128 * j + 128, :].T)
        kv_sent.wait()
        for side in range(2):
            for j in range(3):
                at = pl.ds(128 * j, 128)
                unturn(side, 3 + j, n.dk[side, mine, at] + n.kvrecv[layer, side, :, at].astype(F32))
                n.pg[side, :, pl.ds(D + 128 * j, 128)] = (
                    n.dv[side, mine, at] + n.kvrecv[layer, side, :, pl.ds(HALF + 128 * j, 128)].astype(F32)
                ).astype(BF)
        ready(wt, na, h)
        use = 2 * layer + 1
        n.psend[...] = nt(n.pg[y], n.wt[...]).astype(BF)
        part_sent = copies.push(n.psend, n.precv.at[use], peer)
        ctx_all = n.ctx[...].reshape(2 * t, HALF)

        def na_cols(which, i):
            off = pl.ds(pl.multiple_of(which * HALF + i * 128, 128), 128)
            return n.na[:, :, off].reshape(2 * t, 128)

        def send_tri(i, carry):
            at = pl.ds(pl.multiple_of(i * 128, 128), 128)
            value = tn(na_cols(1 - c, i), n.pg[...].reshape(2 * t, TRI)).astype(BF)
            for third in range(3):
                to = pl.ds(pl.multiple_of(third * HALF + i * 128, 128), 128)
                n.gs_shr[to, :] = value[:, third * HALF : third * HALF + HALF]
            return carry

        lax.fori_loop(0, HALF // 128, send_tri, 0)
        tri_rows, out_rows = pl.ds(0, TRI), pl.ds(TRI, HALF)
        tri_sent = copies.push(n.gs_shr.at[tri_rows], n.gr_att.at[tri_rows], sib)
        theirs_too = n.ml[layer, :, :, rows_of(1 - c, HALF)].reshape(2 * t, HALF)
        n.gs_shr[out_rows, :] = tn(ctx_all, theirs_too).astype(BF)
        out_sent = copies.push(n.gs_shr.at[out_rows], n.gr_att.at[out_rows], sib)
        n.part[...] = nt(n.pg[x], n.wt[...])
        tri_sent.wait()

        def keep_tri(i, carry):
            at = pl.ds(pl.multiple_of(i * 128, 128), 128)
            rows = na_cols(c, i)
            for part, third in enumerate((x, x + 1, 2 * (1 - x))):
                cols = rows_of(third, HALF)
                value = tn(rows, n.pg[:, :, cols].reshape(2 * t, HALF))
                got = n.gr_att[pl.ds(pl.multiple_of(third * HALF + i * 128, 128), 128), :]
                value = (value + got.astype(F32)).astype(BF)
                if part < 2:
                    n.gw[layer, part, at, :] = value
                else:
                    n.gh[layer, 0, at, :] = value[:, :192]
                    n.gh[layer, 1, at, :] = value[:, 192:]
            return carry

        lax.fori_loop(0, HALF // 128, keep_tri, 0)
        w.across_all(K_WHOLE, layer)
        w.across_all(K_HALF, layer)
        out_sent.wait()
        value = tn(ctx_all, n.ml[layer, :, :, rows_of(c, HALF)].reshape(2 * t, HALF))
        value = (value + n.gr_att[out_rows, :].astype(F32)).astype(BF)
        n.go[layer, 0] = value[:, :192]
        n.go[layer, 1] = value[:, 192:]
        w.across_all(K_OUT, layer)
        part_sent.wait()
        dy = n.part[...] + n.precv[use].astype(F32)
        back_h, rows_a = norm_back(n.h[...], n.sc[layer, 0:1, :], dy)
        n.g_out[...] = n.g_out[...] + back_h
        mine_at = (w.y, w.z, w.s)
        if layer:
            load(layer - 1, *attend_places)
            n.early[(*mine_at, pl.ds(0, 2))] = rows_a
            n.early[(*mine_at, pl.ds(2, 2))] = rows_b
        else:
            n.early[(*mine_at, pl.ds(4, 2))] = rows_b
            n.late[mine_at] = rows_a

    everywhere_start(w, 0, n.early)
    everywhere_start(w, 1, n.late)
    for kind in (K_WHOLE, K_HALF, K_OUT):
        w.over(lambda j: w.along(kind, 0, j))
    squares = jnp.zeros((1, 1), F32)

    def squared(value):
        return jnp.sum(jnp.sum(value * value, axis=1, keepdims=True), axis=0, keepdims=True)

    results = (n.whole_g, n.half_g, n.out_g, n.exp_g, n.shr_g)
    order = [(kind, layer) for layer in (1, 0) for kind in (K_EXP, K_SHR, K_WHOLE, K_HALF, K_OUT)]
    for kind, layer in order[:5]:
        value = w.total(kind, layer)
        squares = squares + squared(value)
        results[kind][layer] = value
    first = everywhere_end(w, 0, n.early, n.early_pair)
    second = everywhere_end(w, 1, n.late, n.late_pair)
    n.scale_o[1, pl.ds(0, 2)] = first[0:2]
    n.scale_o[1, pl.ds(2, 2)] = first[2:4]
    n.scale_o[0, pl.ds(0, 2)] = second
    n.scale_o[0, pl.ds(2, 2)] = first[4:6]
    for kind, layer in order[5:]:
        value = w.total(kind, layer)
        squares = squares + squared(value)
        results[kind][layer] = value
    n.sq[w.y, w.z, w.s] = jnp.broadcast_to(squares, (8, 128))
    everywhere_start(w, 2, n.sq)
    total = everywhere_end(w, 2, n.sq, n.sq_pair)
    n.norm_o[...] = total + squared(first[0:6]) + squared(second)
    for layer in range(LAYERS):
        for kind in KINDS:
            w.finish(kind, layer)


def backward_all(dp, g, f, residual, tables, bias):
    t = g.shape[0]
    zs = dp // 2
    r = D // dp
    head, saved0, saved1 = f
    saved = (*saved0, residual, head.mid_o0, *saved1, head.h_mid, head.mid_o1)
    outs = [
        sds((t, D), F32), sds((LAYERS, 4, D), F32), sds((8, 128), F32), sds((LAYERS, r, HALF), F32),
        sds((LAYERS, r, 192), F32), sds((LAYERS, r, 192), F32), sds((LAYERS, r, D), F32), sds((LAYERS, 4 * r, 192), F32),
    ]
    v = pltpu.VMEM
    ll = LAYERS
    scratch = [
        *(v(array.shape, array.dtype) for array in saved[: len(Loaded._fields)]),
        v((ll, 2, t, D), BF), v((2, t, HID), BF), v((ll, 2, t, D), BF), v((2, t, HALF), BF), v((8, t), F32),
        v((2, HALF, t), F32), v((2, 2 * t, HALF), F32), v((2, 2 * t, HALF), F32), v((2, t, D), BF),
        v((ll, 2, t, D), BF), v((2, t, TRI), BF), v((t, D), F32), v((t, D), BF), v((2 * ll, t, D), BF),
        v((D, D), BF), v((D, D), BF), v((HID, HALF), BF), v((HID, HALF), BF), v((HID, HALF), BF),
        v((ll, 2, HALF, HALF), BF), v((ll, 2, HALF, 192), BF), v((ll, 2, HALF, 192), BF), v((ll, D, D), BF),
        v((ll, 2, HID, 192), BF),
        *([v((ll, zs, r, HALF), BF), v((ll, zs, r, 192), BF), v((ll, zs, r, 192), BF), v((ll, zs, r, D), BF),
           v((ll, zs, 4 * r, 192), BF)] * 2),
        v((2, zs, SEQ, 8, D), F32), v((2, 8, D), F32), v((2, zs, SEQ, 2, D), F32), v((2, 2, D), F32),
        v((2, zs, SEQ, 8, 128), F32), v((2, 8, 128), F32),
        pltpu.SemaphoreType.DMA((ll, len(KINDS), 2, zs)), pltpu.SemaphoreType.DMA((ll, len(KINDS), 2, zs)),
        pltpu.SemaphoreType.DMA((3, zs * SEQ + 1)), pltpu.SemaphoreType.DMA((3, zs * SEQ + 1)),
        pltpu.SemaphoreType.DMA((20,)), pltpu.SemaphoreType.DMA((20,)), pltpu.SemaphoreType.DMA((32,)),
    ]
    results = pl.pallas_call(
        functools.partial(bwd_kernel, dp),
        name="backward",
        out_shape=outs,
        in_specs=[vmem(), vmem(), vmem(), pl.BlockSpec(memory_space=pltpu.SMEM), *([hbm()] * len(saved))],
        out_specs=[vmem()] * len(outs),
        scratch_shapes=scratch,
        cost_estimate=pl.CostEstimate(flops=44 << 30, bytes_accessed=48 << 20, transcendentals=0),
        compiler_params=pltpu.CompilerParams(
            collective_id=5, has_side_effects=True, vmem_limit_bytes=VMEM_BYTES
        ),
    )(g, head.sc_o, tables, bias, *saved)
    return BackwardOut(*results)


class Moves:
    def __init__(self, dp):
        self.dp = dp
        self.d = lax.axis_index("dp")
        s = lax.axis_index("seq")
        self.s, self.x, self.c = s, s // 2, s % 2
        half = dp // 2
        ids = [(d, s) for d in range(dp) for s in range(SEQ)]
        self.tri = []
        for r in range(2):
            for j in range(3):
                perm = []
                for d, s in ids:
                    b = (3 * s + j) % 4
                    to = (2 * (d % half) + (r ^ (b % 2)), 2 * (b // 2) + d // half)
                    perm.append((d * SEQ + s, to[0] * SEQ + to[1]))
                self.tri.append(perm)
        self.out = []
        for r in range(2):
            perm = []
            for d, s in ids:
                to = (2 * (d % half) + (r ^ (s % 2)), 2 * (d // half) + s // 2)
                perm.append((d * SEQ + s, to[0] * SEQ + to[1]))
            self.out.append(perm)
        self.shr = []
        for k in range(4):
            perm = []
            for d, s in ids:
                to = (4 * (d % (dp // 4)) + (k + s) % 4, d // (dp // 4))
                perm.append((d * SEQ + s, to[0] * SEQ + to[1]))
            self.shr.append(perm)

    def send(self, piece, perm, back):
        if back:
            perm = [(b, a) for a, b in perm]
        return lax.ppermute(piece, ("dp", "seq"), perm)

    @staticmethod
    def pick(pieces, index):
        return lax.dynamic_index_in_dim(jnp.stack(pieces), index, 0, keepdims=False)

    def tri_out(self, low):
        n, rows, _ = low.shape
        halves = low.reshape(n, 2, rows // 2, 3, 192)
        got = []
        for r in range(2):
            for j in range(3):
                which = r ^ (((3 * self.s + j) % 4) % 2)
                piece = lax.dynamic_index_in_dim(halves[:, :, :, j], which, 1, keepdims=False)
                got.append(self.send(piece, self.tri[3 * r + j], False))
        parts = []
        for t in range(3):
            for bb in range(2):
                r, j = bb ^ (self.d % 2), (t + 2 * self.x + bb) % 3
                parts.append(self.pick(got, 3 * r + j))
        return jnp.concatenate(parts, axis=-1)

    def tri_back(self, grad):
        n, rows, _ = grad.shape
        got = []
        for r in range(2):
            for j in range(3):
                bb = (self.d % 2) ^ r
                t = (j - (2 * self.x + bb)) % 3
                piece = lax.dynamic_slice_in_dim(grad, (2 * t + bb) * 192, 192, 2)
                got.append(self.send(piece, self.tri[3 * r + j], True))
        cols = []
        for j in range(3):
            two = []
            for hh in range(2):
                r = hh ^ (((3 * self.s + j) % 4) % 2)
                two.append(self.pick([got[j], got[3 + j]], r))
            cols.append(jnp.concatenate(two, axis=1))
        return jnp.concatenate(cols, axis=-1)

    def out_out(self, low):
        n, rows, _ = low.shape
        halves = low.reshape(n, 2, rows // 2, 192)
        got = [
            self.send(
                lax.dynamic_index_in_dim(halves, r ^ (self.s % 2), 1, keepdims=False), self.out[r], False
            )
            for r in range(2)
        ]
        return jnp.concatenate([self.pick(got, u ^ (self.d % 2)) for u in range(2)], axis=-1)

    def out_back(self, grad):
        got = []
        for r in range(2):
            u = r ^ (self.d % 2)
            got.append(self.send(lax.dynamic_slice_in_dim(grad, u * 192, 192, 2), self.out[r], True))
        return jnp.concatenate([self.pick(got, hh ^ (self.s % 2)) for hh in range(2)], axis=1)

    def shr_out(self, low):
        n, rows, _ = low.shape
        subs = low.reshape(n, 4, rows // 4, 192)
        got = [
            self.send(
                lax.dynamic_index_in_dim(subs, (k + self.s) % 4, 1, keepdims=False), self.shr[k], False
            )
            for k in range(4)
        ]
        return jnp.concatenate([self.pick(got, (self.d - s) % 4) for s in range(4)], axis=-1)

    def shr_back(self, grad):
        got = []
        for k in range(4):
            piece = lax.dynamic_slice_in_dim(grad, ((self.d - k) % 4) * 192, 192, 2)
            got.append(self.send(piece, self.shr[k], True))
        return jnp.concatenate([self.pick(got, (sub - self.s) % 4) for sub in range(4)], axis=1)


def tables_here(segments, t, x, c):
    group = segments.shape[0]
    whole = segments[0] == segments[group - 1]
    place_in_half = c * t + jnp.arange(t, dtype=jnp.int32)
    second = jnp.where(whole, group // 2, 0).astype(jnp.int32)
    positions = jnp.stack([place_in_half, place_in_half + second]).astype(F32)
    lane = jnp.arange(128, dtype=jnp.int32)
    inverse = 1.0 / ROTARY_BASE ** ((lane % (HD // 2)).astype(F32) * (2.0 / HD))
    angles = positions[:, :, None] * inverse[None, None, :]
    sign = jnp.where(lane % HD < HD // 2, -1.0, 1.0).astype(F32)
    tables = jnp.concatenate([jnp.cos(angles), jnp.sin(angles) * sign], axis=-1)
    bias = jnp.where(whole, 0.0, MASKED).astype(F32).reshape(1)
    return tables, bias


def layers_narrow(
    dp, moves, residual, cotangent, scales_weight, tables, bias,
    triple_weight, output_weight, expand_weight, shrink_weight,
):
    d, s = lax.axis_index("dp"), lax.axis_index("seq")
    scales_all = lax.psum(
        lax.dynamic_update_slice(
            jnp.zeros((LAYERS, 4, D), F32), scales_weight.astype(BF).astype(F32), (0, s, d * (D // dp))
        ),
        ("dp", "seq"),
    )
    tri = moves.tri_out(triple_weight.astype(BF))
    out = moves.out_out(output_weight.astype(BF))
    shr = moves.shr_out(shrink_weight.astype(BF))
    attend_parts = jnp.concatenate([tri, out], axis=-1)
    feed_parts = jnp.concatenate([expand_weight.astype(BF), shr], axis=-1)
    gather = functools.partial(lax.all_gather, axis_name="dp", axis=0, tiled=True)
    wa, wf = [], []
    for layer in range(LAYERS):
        wa.append(gather(attend_parts[layer]))
        wf.append(gather(feed_parts[layer]))

    stream = residual
    kept = []
    for layer in range(LAYERS):
        scales = scales_all[layer]
        middle, *attend_saved = attend_fwd(stream, wa[layer], scales, tables, bias)
        following, *feed_saved = feed_fwd(middle, wf[layer], scales)
        kept.append((stream, middle, attend_saved, feed_saved))
        stream = following

    g = cotangent
    attend_grads, feed_grads, scale_grads = [None] * LAYERS, [None] * LAYERS, [None] * LAYERS
    scatter = functools.partial(lax.psum_scatter, axis_name="dp", scatter_dimension=0, tiled=True)
    for layer in reversed(range(LAYERS)):
        scales = scales_all[layer]
        h, middle, attend_saved, feed_saved = kept[layer]
        mg, feed_grad, rows_b = feed_bwd(g, middle, wf[layer], scales, *feed_saved)
        feed_grads[layer] = scatter(feed_grad).astype(F32)
        g, attend_grad, rows_a = attend_bwd(mg, h, wa[layer], scales, tables, bias, attend_saved)
        attend_grads[layer] = scatter(attend_grad).astype(F32)
        scale_grads[layer] = jnp.concatenate([rows_a, rows_b], axis=0)

    scale_grad = lax.psum(jnp.stack(scale_grads), ("dp", "seq"))
    own_scale = lax.dynamic_slice(scale_grad, (0, s, d * (D // dp)), (LAYERS, 1, D // dp))
    squares = jnp.sum(own_scale * own_scale)
    for part in (*attend_grads, *feed_grads):
        squares = squares + jnp.sum(part * part)
    grad_norm = jnp.sqrt(lax.psum(squares, ("dp", "seq")))

    attend_grad, feed_grad = jnp.stack(attend_grads).astype(BF), jnp.stack(feed_grads).astype(BF)
    triple_grad = moves.tri_back(attend_grad[:, :, :TRI]).astype(F32)
    output_grad = moves.out_back(attend_grad[:, :, TRI:]).astype(F32)
    expand_grad = feed_grad[:, :, :D].astype(F32)
    shrink_grad = moves.shr_back(feed_grad[:, :, D:]).astype(F32)
    return stream, g, grad_norm, (triple_grad, output_grad, expand_grad, shrink_grad, own_scale)


def layers_wide(
    dp, moves, residual, cotangent, scales_weight, tables, bias,
    triple_weight, output_weight, expand_weight, shrink_weight,
):
    d, s, c = lax.axis_index("dp"), lax.axis_index("seq"), moves.c
    sc_own = jnp.zeros((8, 128), F32)
    sc_own = sc_own.at[:LAYERS, : D // dp].set(scales_weight[:, 0].astype(BF).astype(F32))
    pieces = pieces_of(triple_weight, output_weight, expand_weight, shrink_weight, c)
    f = forward_all(dp, residual, sc_own, tables, bias, pieces)
    b = backward_all(dp, cotangent, f, residual, tables, bias)
    triple_grad = jnp.where(
        c == 0,
        jnp.concatenate([b.whole_g, b.half_g], axis=-1),
        jnp.concatenate([b.half_g, b.whole_g], axis=-1),
    )
    own_scale = lax.dynamic_slice(b.scale_o, (0, s, d * (D // dp)), (LAYERS, 1, D // dp))
    grad_norm = jnp.sqrt(b.norm_o[0, 0])
    return f[0].h_out, b.g_out, grad_norm, (triple_grad, b.out_g, b.exp_g, b.shr_g, own_scale)


def local(dp, *args):
    (residual, cotangent, segments) = args[:3]
    (
        triple_weight, triple_moment, triple_square, triple_shadow,
        output_weight, output_moment, output_square, output_shadow,
        expand_weight, expand_moment, expand_square, expand_shadow,
        shrink_weight, shrink_moment, shrink_square, shrink_shadow,
        scales_weight, scales_moment, scales_square, scales_shadow,
    ) = args[3:]
    moves = Moves(dp)
    t = residual.shape[0]
    d, s = lax.axis_index("dp"), lax.axis_index("seq")
    tables, bias = tables_here(segments, t, moves.x, moves.c)

    if (D // dp) % 16 == 0:
        stream, g, grad_norm, grads = layers_wide(
            dp, moves, residual, cotangent, scales_weight, tables, bias,
            triple_weight, output_weight, expand_weight, shrink_weight,
        )
    else:
        stream, g, grad_norm, grads = layers_narrow(
            dp, moves, residual, cotangent, scales_weight, tables, bias,
            triple_weight, output_weight, expand_weight, shrink_weight,
        )
    triple_grad, output_grad, expand_grad, shrink_grad, own_scale = grads
    limit = CLIP_RATIO * math.sqrt(float(LAYERS * (4 * D * D + 2 * D * FF + 4 * D)))
    factor = limit / (grad_norm + 1e-06)

    results = [stream, g, grad_norm]
    for weight, moment, square, shadow, grad, rate in (
        (triple_weight, triple_moment, triple_square, triple_shadow, triple_grad, RATE_FACTOR / math.sqrt(D)),
        (output_weight, output_moment, output_square, output_shadow, output_grad, RATE_FACTOR / math.sqrt(D // 16)),
        (expand_weight, expand_moment, expand_square, expand_shadow, expand_grad, RATE_FACTOR / math.sqrt(D)),
        (shrink_weight, shrink_moment, shrink_square, shrink_shadow, shrink_grad, RATE_FACTOR / math.sqrt(FF)),
        (scales_weight, scales_moment, scales_square, scales_shadow, own_scale, SCALES_RATE),
    ):
        results.extend(adam_step(weight, moment, square, shadow, grad * factor, rate))
    return tuple(results)


def solution(mesh):
    token = P(("dp", "seq"), None)
    weight = P(None, "dp", "seq")
    scale = P(None, "seq", "dp")
    return jax.shard_map(
        functools.partial(local, mesh.shape["dp"]),
        mesh=mesh,
        in_specs=(token, token, P("dp"), *([weight] * 16), *([scale] * 4)),
        out_specs=(token, token, P(), *([weight] * 16), *([scale] * 4)),
        check_vma=False,
    )
```

```python
import functools
import math
from typing import Any, NamedTuple

import jax
import jax.numpy as jnp
from jax import lax
from jax.experimental import pallas as pl
from jax.experimental.pallas import tpu as pltpu
from jax.sharding import PartitionSpec as P

D = 768
FF = 3072
HD = 64
LAYERS = 2
STEP = 2
SEQ = 4

EPSILON = 1e-05
ROTARY_BASE = 10000.0
BETA_ONE = 0.9
BETA_TWO = 0.999
ADAM_EPSILON = 1e-08
DECAY_RATE = 0.01
SHADOW_RATE = 0.99
CLIP_RATIO = 0.5
RATE_FACTOR = 1.5
SCALES_RATE = 0.6
MASKED = -1000000000.0

HALF = D // 2
TRI = 3 * HALF
HID = FF // 2
BF = jnp.bfloat16
F32 = jnp.float32
MESH = pl.DeviceIdType.MESH
VMEM_BYTES = 60 << 20


def adam_step(weight, moment, square, shadow, gradient, step_rate):
    shadow_decay = min(SHADOW_RATE, (1.0 + STEP) / (10.0 + STEP))
    momentum = BETA_ONE * moment + (1.0 - BETA_ONE) * gradient
    variance = BETA_TWO * square + (1.0 - BETA_TWO) * gradient * gradient
    corrected = (
        momentum
        / (1.0 - BETA_ONE**STEP)
        / (jnp.sqrt(variance / (1.0 - BETA_TWO**STEP)) + ADAM_EPSILON)
    )
    updated = weight - step_rate * (corrected + DECAY_RATE * weight)
    average = shadow_decay * shadow + (1.0 - shadow_decay) * updated
    return (updated, momentum, variance, average)


def nn(a, b):
    return lax.dot_general(a, b, (((1,), (0,)), ((), ())), preferred_element_type=F32)


def nt(a, b):
    return lax.dot_general(a, b, (((1,), (1,)), ((), ())), preferred_element_type=F32)


def tn(a, b):
    return lax.dot_general(a, b, (((0,), (0,)), ((), ())), preferred_element_type=F32)


def place():
    s = lax.axis_index("seq")
    x = lax.div(s, 2)
    c = lax.rem(s, 2)
    return lax.axis_index("dp"), x, c, lax.rem(s + 2, SEQ), s + 1 - 2 * c


def greet(d, peer, sib):
    barrier = pltpu.get_barrier_semaphore()
    for other in (peer, sib):
        pl.semaphore_signal(barrier, inc=1, device_id=(d, other), device_id_type=MESH)
    pl.semaphore_wait(barrier, 2)


def rows_of(c, n):
    return pl.ds(pl.multiple_of(c * n, n), n)


class Copies:
    def __init__(self, lsem, ssem, rsem, d):
        self.lsem, self.ssem, self.rsem, self.d = lsem, ssem, rsem, d
        self.n_local = 0
        self.n_remote = 0

    def local(self, src, dst):
        copy = pltpu.make_async_copy(src, dst, self.lsem.at[self.n_local])
        self.n_local += 1
        copy.start()
        return copy

    def push(self, src, dst, to):
        copy = pltpu.make_async_remote_copy(
            src_ref=src,
            dst_ref=dst,
            send_sem=self.ssem.at[self.n_remote],
            recv_sem=self.rsem.at[self.n_remote],
            device_id=(self.d, to),
            device_id_type=MESH,
        )
        self.n_remote += 1
        copy.start()
        return copy


def norm_stats(values):
    center = values - jnp.mean(values, axis=-1, keepdims=True)
    spread = jnp.mean(center * center, axis=-1, keepdims=True)
    scale = lax.rsqrt(spread + EPSILON)
    return center * scale, scale


def norm_back(values, gain, dy):
    xhat, scale = norm_stats(values)
    u = gain * dy
    du = u - jnp.mean(u, axis=-1, keepdims=True)
    back = scale * (du - xhat * jnp.mean(u * xhat, axis=-1, keepdims=True))
    rows = jnp.concatenate(
        [jnp.sum(xhat * dy, axis=0, keepdims=True), jnp.sum(dy, axis=0, keepdims=True)], axis=0
    )
    return back, rows


def turn(chunk, cosine, sine):
    lane = lax.broadcasted_iota(jnp.int32, chunk.shape, 1)
    swapped = jnp.where(
        lax.rem(lane, HD) < HD // 2, pltpu.roll(chunk, 128 - HD // 2, 1), pltpu.roll(chunk, HD // 2, 1)
    )
    return chunk * cosine + swapped * sine


def half_of(pair, which):
    lane = lax.broadcasted_iota(jnp.int32, pair.shape, 1)
    keep = (lane < HD) if which == 0 else (lane >= HD)
    return jnp.where(keep, pair, jnp.zeros_like(pair))


def attend_fwd_kernel(
    h, wa, sc, cs, bias, mid, na_o, q_o, k_o, v_o, ctx_o, lse_o,
    wt, wo, na, q, k, v, ctxt, ctx, lse, psend, precv, lsem, ssem, rsem,
):
    d, x, c, peer, sib = place()
    y = 1 - x
    rows = h.shape[0]
    copies = Copies(lsem, ssem, rsem, d)
    greet(d, peer, sib)
    wt_own, wo_own = wt.at[rows_of(c, HALF), :], wo.at[:, rows_of(c, HALF)]
    tri_part, out_part = wa.at[:, pl.ds(0, TRI)], wa.at[:, pl.ds(TRI, HALF)]
    tri_sent = copies.push(tri_part, wt_own, sib)
    tri_local = copies.local(tri_part, wt_own)
    out_sent = copies.push(out_part, wo_own, sib)
    out_local = copies.local(out_part, wo_own)
    xhat, _ = norm_stats(h[...])
    na[x] = (xhat * sc[0:1, :] + sc[1:2, :]).astype(BF)
    na_sent = copies.push(na.at[x], na.at[x], peer)
    tri_local.wait()
    tri_sent.wait()

    def project(block):
        cosine, sine = cs[block, :, 0:128], cs[block, :, 128:256]
        for j in range(9):
            part = nn(na[block], wt[:, 128 * j : 128 * j + 128])
            lanes = pl.ds(128 * (j % 3), 128)
            if j < 3:
                q[block, :, lanes] = (turn(part, cosine, sine) * HD**-0.5).astype(BF)
            elif j < 6:
                k[block, rows_of(c, rows), lanes] = turn(part, cosine, sine).astype(BF)
            else:
                v[block, rows_of(c, rows), lanes] = part.astype(BF)

    def share(block):
        mine = (block, rows_of(c, rows))
        return [copies.push(k.at[mine], k.at[mine], sib), copies.push(v.at[mine], v.at[mine], sib)]

    project(x)
    shared = share(x)
    na_sent.wait()
    project(y)
    shared += share(y)
    out_local.wait()
    out_sent.wait()
    for copy in shared:
        copy.wait()

    def attend(block):
        other = 1 - block

        def pair_step(p, carry):
            lanes = pl.ds(pl.multiple_of(p * 128, 128), 128)
            q_pair = q[block, :, lanes]
            k_same, k_cross = k[block, :, lanes], k[other, :, lanes]
            v_same, v_cross = v[block, :, lanes], v[other, :, lanes]
            for which in range(2):
                q_head = half_of(q_pair, which)
                s_same = nt(k_same, q_head)
                s_cross = nt(k_cross, q_head) + bias[0]
                top = jnp.maximum(
                    jnp.max(s_same, axis=0, keepdims=True), jnp.max(s_cross, axis=0, keepdims=True)
                )
                e_same = jnp.exp(s_same - top)
                e_cross = jnp.exp(s_cross - top)
                total = jnp.sum(e_same, axis=0, keepdims=True) + jnp.sum(
                    e_cross, axis=0, keepdims=True
                )
                mixed = tn(v_same, e_same.astype(BF)) + tn(v_cross, e_cross.astype(BF))
                head = pl.ds(pl.multiple_of(p * 128 + which * HD, HD), HD)
                ctxt[head, :] = mixed[which * HD : which * HD + HD, :] / total
                lse[block, pl.ds(2 * p + which, 1), :] = top + jnp.log(total)
            return carry

        lax.fori_loop(0, HALF // 128, pair_step, 0)
        ctx[block] = ctxt[...].T.astype(BF)
        return nn(ctx[block], wo[...])

    psend[...] = attend(y).astype(BF)
    part_sent = copies.push(psend, precv, peer)
    mid[...] = h[...] + attend(x)
    saves = [
        copies.local(a, b)
        for a, b in ((na, na_o), (q, q_o), (k, k_o), (v, v_o), (ctx, ctx_o), (lse, lse_o))
    ]
    part_sent.wait()
    mid[...] = mid[...] + precv[...].astype(F32)
    for copy in saves:
        copy.wait()


def hbm():
    return pl.BlockSpec(memory_space=pl.ANY)


def vmem():
    return pl.BlockSpec(memory_space=pltpu.VMEM)


def call(kernel, name, number, ins, outs, out_shape, scratch, n_local, n_remote, flops, args):
    return pl.pallas_call(
        kernel,
        name=name,
        out_shape=out_shape,
        in_specs=ins,
        out_specs=outs,
        scratch_shapes=[
            *scratch,
            pltpu.SemaphoreType.DMA((n_local,)),
            pltpu.SemaphoreType.DMA((n_remote,)),
            pltpu.SemaphoreType.DMA((n_remote,)),
        ],
        cost_estimate=pl.CostEstimate(flops=flops, bytes_accessed=16 << 20, transcendentals=0),
        compiler_params=pltpu.CompilerParams(
            collective_id=number, has_side_effects=True, vmem_limit_bytes=VMEM_BYTES
        ),
    )(*args)


def sds(shape, dtype):
    return jax.ShapeDtypeStruct(shape, dtype)


def attend_fwd(h, wa, scales, tables, bias):
    t = h.shape[0]
    return call(
        attend_fwd_kernel, "attend_fwd", 0,
        [vmem(), hbm(), vmem(), vmem(), pl.BlockSpec(memory_space=pltpu.SMEM)],
        [vmem()] + [hbm()] * 6,
        [
            sds((t, D), F32), sds((2, t, D), BF), sds((2, t, HALF), BF), sds((2, 2 * t, HALF), BF),
            sds((2, 2 * t, HALF), BF), sds((2, t, HALF), BF), sds((2, 8, t), F32),
        ],
        [
            pltpu.VMEM((D, TRI), BF), pltpu.VMEM((HALF, D), BF), pltpu.VMEM((2, t, D), BF),
            pltpu.VMEM((2, t, HALF), BF), pltpu.VMEM((2, 2 * t, HALF), BF),
            pltpu.VMEM((2, 2 * t, HALF), BF), pltpu.VMEM((HALF, t), F32),
            pltpu.VMEM((2, t, HALF), BF), pltpu.VMEM((2, 8, t), F32),
            pltpu.VMEM((t, D), BF), pltpu.VMEM((t, D), BF),
        ],
        8, 8, 6 << 30, (h, wa, scales, tables, bias),
    )


def gelu_parts(hidden):
    phi_cap = 0.5 * (1.0 + lax.erf(hidden * math.sqrt(0.5)))
    density = jnp.exp(-0.5 * hidden * hidden) * (1.0 / math.sqrt(2.0 * math.pi))
    return hidden * phi_cap, phi_cap + hidden * density


def feed_fwd_kernel(
    mid, wf, sc, h_next, nb_o, act_o, slope_o,
    we, ws, nb, act, slope, psend, precv, lsem, ssem, rsem,
):
    d, x, c, peer, sib = place()
    y = 1 - x
    copies = Copies(lsem, ssem, rsem, d)
    greet(d, peer, sib)
    xhat, _ = norm_stats(mid[...])
    nb[x] = (xhat * sc[2:3, :] + sc[3:4, :]).astype(BF)
    nb_sent = copies.push(nb.at[x], nb.at[x], peer)
    we_own, ws_own = we.at[:, rows_of(c, D)], ws.at[rows_of(c, D), :]
    exp_part, shr_part = wf.at[:, pl.ds(0, D)], wf.at[:, pl.ds(D, D)]
    weights = [
        copies.local(exp_part, we_own),
        copies.push(exp_part, we_own, sib),
        copies.local(shr_part, ws_own),
        copies.push(shr_part, ws_own, sib),
    ]
    for copy in weights:
        copy.wait()

    def feed(block):
        def step(i, carry):
            lanes = pl.ds(pl.multiple_of(i * 256, 256), 256)
            value, rate = gelu_parts(nn(nb[block], we[:, lanes]))
            act[block, :, lanes] = value.astype(BF)
            slope[block, :, lanes] = rate.astype(BF)
            return carry

        lax.fori_loop(0, HID // 256, step, 0)
        return nn(act[block], ws[...])

    h_next[...] = mid[...] + feed(x)
    nb_sent.wait()
    psend[...] = feed(y).astype(BF)
    part_sent = copies.push(psend, precv, peer)
    saves = [copies.local(a, b) for a, b in ((nb, nb_o), (act, act_o), (slope, slope_o))]
    part_sent.wait()
    h_next[...] = h_next[...] + precv[...].astype(F32)
    for copy in saves:
        copy.wait()


def feed_fwd(mid, wf, scales):
    t = mid.shape[0]
    return call(
        feed_fwd_kernel, "feed_fwd", 1,
        [vmem(), hbm(), vmem()],
        [vmem()] + [hbm()] * 3,
        [sds((t, D), F32), sds((2, t, D), BF), sds((2, t, HID), BF), sds((2, t, HID), BF)],
        [
            pltpu.VMEM((D, HID), BF), pltpu.VMEM((HID, D), BF), pltpu.VMEM((2, t, D), BF),
            pltpu.VMEM((2, t, HID), BF), pltpu.VMEM((2, t, HID), BF),
            pltpu.VMEM((t, D), BF), pltpu.VMEM((t, D), BF),
        ],
        5, 4, 5 << 30, (mid, wf, scales),
    )


def feed_bwd_kernel(
    g, mid, wf, sc, nb_h, act_h, slope_h, mid_grad, wg_o, rows_o,
    we, ws, nb, act, slope, gl, hg, part, psend, precv, gown, gsend, grecv, lsem, ssem, rsem,
):
    d, x, c, peer, sib = place()
    y = 1 - x
    t = g.shape[0]
    copies = Copies(lsem, ssem, rsem, d)
    greet(d, peer, sib)
    gl[x] = g[...].astype(BF)
    g_sent = copies.push(gl.at[x], gl.at[x], peer)
    we_own, ws_own = we.at[:, rows_of(c, D)], ws.at[rows_of(c, D), :]
    exp_part, shr_part = wf.at[:, pl.ds(0, D)], wf.at[:, pl.ds(D, D)]
    weights = [
        copies.local(shr_part, ws_own),
        copies.push(shr_part, ws_own, sib),
        copies.local(exp_part, we_own),
        copies.push(exp_part, we_own, sib),
        copies.local(slope_h, slope),
        copies.local(act_h, act),
        copies.local(nb_h, nb),
    ]
    for copy in weights:
        copy.wait()

    def back(block):
        def step(i, carry):
            lanes = pl.ds(pl.multiple_of(i * 256, 256), 256)
            pulled = nt(gl[block], ws[lanes, :])
            hg[block, :, lanes] = (pulled * slope[block, :, lanes].astype(F32)).astype(BF)
            return carry

        lax.fori_loop(0, HID // 256, step, 0)
        return nt(hg[block], we[...])

    part[...] = back(x)
    g_sent.wait()
    psend[...] = back(y).astype(BF)
    part_sent = copies.push(psend, precv, peer)

    gl_all = gl[...].reshape(2 * t, D)
    nb_all = nb[...].reshape(2 * t, D)

    def grads(which, store):
        def step(i, carry):
            at = pl.ds(pl.multiple_of(i * 256, 256), 256)
            off = pl.ds(pl.multiple_of(which * D + i * 256, 256), 256)
            hg_part = hg[:, :, off].reshape(2 * t, 256)
            act_part = act[:, :, off].reshape(2 * t, 256)
            store(0, at, tn(nb_all, hg_part))
            store(1, at, tn(act_part, gl_all))
            return carry

        lax.fori_loop(0, D // 256, step, 0)

    def to_send(kind, at, value):
        if kind == 0:
            gsend[:, at] = value.astype(BF)
        else:
            gsend[at, pl.ds(D, D)] = value.astype(BF)

    def to_keep(kind, at, value):
        if kind == 0:
            gown[:, at] = value
        else:
            gown[at, pl.ds(D, D)] = value

    grads(1 - c, to_send)
    grad_sent = copies.push(gsend, grecv, sib)
    grads(c, to_keep)
    part_sent.wait()
    dy = part[...] + precv[...].astype(F32)
    back_mid, rows = norm_back(mid[...], sc[2:3, :], dy)
    mid_grad[...] = g[...] + back_mid
    rows_o[...] = rows
    grad_sent.wait()
    gsend[...] = (gown[...] + grecv[...].astype(F32)).astype(BF)
    copies.local(gsend, wg_o).wait()


def feed_bwd(g, mid, wf, scales, nb, act, slope):
    t = g.shape[0]
    return call(
        feed_bwd_kernel, "feed_bwd", 2,
        [vmem(), vmem(), hbm(), vmem(), hbm(), hbm(), hbm()],
        [vmem(), hbm(), vmem()],
        [sds((t, D), F32), sds((D, 2 * D), BF), sds((2, D), F32)],
        [
            pltpu.VMEM((D, HID), BF), pltpu.VMEM((HID, D), BF), pltpu.VMEM((2, t, D), BF),
            pltpu.VMEM((2, t, HID), BF), pltpu.VMEM((2, t, HID), BF), pltpu.VMEM((2, t, D), BF),
            pltpu.VMEM((2, t, HID), BF), pltpu.VMEM((t, D), F32), pltpu.VMEM((t, D), BF),
            pltpu.VMEM((t, D), BF), pltpu.VMEM((D, 2 * D), F32), pltpu.VMEM((D, 2 * D), BF),
            pltpu.VMEM((D, 2 * D), BF),
        ],
        6, 5, 10 << 30, (g, mid, wf, scales, nb, act, slope),
    )


def attend_bwd_kernel(
    mg, h, wa, sc, cs, bias, na, q, k, v, ctx, lse, g_prev, wg_o, rows_o,
    wt, wo, ml, cg, delta, dqt, dk, dv, kvsend, kvrecv, pg, part, psend, precv,
    gown, gsend, grecv, lsem, ssem, rsem,
):
    d, x, c, peer, sib = place()
    y = 1 - x
    t = mg.shape[0]
    copies = Copies(lsem, ssem, rsem, d)
    greet(d, peer, sib)
    ml[x] = mg[...].astype(BF)
    ml_sent = copies.push(ml.at[x], ml.at[x], peer)
    wt_own, wo_own = wt.at[rows_of(c, HALF), :], wo.at[:, rows_of(c, HALF)]
    tri_part, out_part = wa.at[:, pl.ds(0, TRI)], wa.at[:, pl.ds(TRI, HALF)]
    out_moves = [copies.local(out_part, wo_own), copies.push(out_part, wo_own, sib)]
    tri_moves = [copies.local(tri_part, wt_own), copies.push(tri_part, wt_own, sib)]
    dk[...] = jnp.zeros_like(dk)
    dv[...] = jnp.zeros_like(dv)
    for copy in out_moves:
        copy.wait()

    def attend(block):
        other = 1 - block
        pulled = nt(ml[block], wo[...])
        cg[block] = pulled.astype(BF)
        weighed = (cg[block].astype(F32) * ctx[block].astype(F32)).T
        for head in range(HALF // HD):
            delta[head : head + 1, :] = jnp.sum(
                weighed[head * HD : head * HD + HD, :], axis=0, keepdims=True
            )

        def pair_step(p, carry):
            lanes = pl.ds(pl.multiple_of(p * 128, 128), 128)
            q_pair, cg_pair = q[block, :, lanes], cg[block, :, lanes]
            for which in range(2):
                q_head, cg_head = half_of(q_pair, which), half_of(cg_pair, which)
                row = pl.ds(2 * p + which, 1)
                total, dots = lse[block, row, :], delta[row, :]
                turned = None
                for side in (block, other):
                    k_pair, v_pair = k[side, :, lanes], v[side, :, lanes]
                    scores = nt(k_pair, q_head)
                    if side is other:
                        scores = scores + bias[0]
                    probs = jnp.exp(scores - total)
                    score_grad = (probs * (nt(v_pair, cg_head) - dots)).astype(BF)
                    dv[side, :, lanes] += nn(probs.astype(BF), cg_head)
                    dk[side, :, lanes] += nn(score_grad, q_head)
                    piece = tn(k_pair, score_grad)
                    turned = piece if turned is None else turned + piece
                head = pl.ds(pl.multiple_of(p * 128 + which * HD, HD), HD)
                dqt[block, head, :] = turned[which * HD : which * HD + HD, :] * HD**-0.5
            return carry

        lax.fori_loop(0, HALF // 128, pair_step, 0)

    attend(x)
    ml_sent.wait()
    attend(y)
    theirs, mine = rows_of(1 - c, t), rows_of(c, t)
    for side in range(2):
        kvsend[side, :, pl.ds(0, HALF)] = dk[side, theirs, :].astype(BF)
        kvsend[side, :, pl.ds(HALF, HALF)] = dv[side, theirs, :].astype(BF)
    kv_sent = copies.push(kvsend, kvrecv, sib)

    def unturn(block, j, value):
        cosine, sine = cs[block, :, 0:128], cs[block, :, 128:256]
        rounded = value.astype(BF).astype(F32)
        pg[block, :, pl.ds(128 * j, 128)] = turn(rounded, cosine, -sine).astype(BF)

    for side in range(2):
        for j in range(3):
            unturn(side, j, dqt[side, 128 * j : 128 * j + 128, :].T)
    kv_sent.wait()
    for side in range(2):
        for j in range(3):
            at = pl.ds(128 * j, 128)
            unturn(side, 3 + j, dk[side, mine, at] + kvrecv[side, :, at].astype(F32))
            pg[side, :, pl.ds(D + 128 * j, 128)] = (
                dv[side, mine, at] + kvrecv[side, :, pl.ds(HALF + 128 * j, 128)].astype(F32)
            ).astype(BF)
    for copy in tri_moves:
        copy.wait()
    psend[...] = nt(pg[y], wt[...]).astype(BF)
    part_sent = copies.push(psend, precv, peer)
    part[...] = nt(pg[x], wt[...])

    ml_all = ml[...].reshape(2 * t, D)
    na_all = na[...].reshape(2 * t, D)
    ctx_all = ctx[...].reshape(2 * t, HALF)

    def grads(which, store):
        def step(i, carry):
            off = pl.ds(pl.multiple_of(which * HALF + i * 128, 128), 128)
            at = pl.ds(pl.multiple_of(i * 128, 128), 128)
            store(0, at, tn(na[:, :, off].reshape(2 * t, 128), pg[...].reshape(2 * t, TRI)))
            store(1, at, tn(ctx_all, ml[:, :, off].reshape(2 * t, 128)))
            return carry

        lax.fori_loop(0, HALF // 128, step, 0)

    def to_send(kind, at, value):
        if kind == 0:
            gsend[at, pl.ds(0, TRI)] = value.astype(BF)
        else:
            gsend[:, pl.ds(pl.multiple_of(TRI + at.start, 128), 128)] = value.astype(BF)

    def to_keep(kind, at, value):
        if kind == 0:
            gown[at, pl.ds(0, TRI)] = value
        else:
            gown[:, pl.ds(pl.multiple_of(TRI + at.start, 128), 128)] = value

    grads(1 - c, to_send)
    grad_sent = copies.push(gsend, grecv, sib)
    grads(c, to_keep)
    part_sent.wait()
    dy = part[...] + precv[...].astype(F32)
    back, rows = norm_back(h[...], sc[0:1, :], dy)
    g_prev[...] = mg[...] + back
    rows_o[...] = rows
    grad_sent.wait()
    gsend[...] = (gown[...] + grecv[...].astype(F32)).astype(BF)
    copies.local(gsend, wg_o).wait()


def attend_bwd(mg, h, wa, scales, tables, bias, saved):
    t = mg.shape[0]
    return call(
        attend_bwd_kernel, "attend_bwd", 3,
        [vmem(), vmem(), hbm(), vmem(), vmem(), pl.BlockSpec(memory_space=pltpu.SMEM)] + [vmem()] * 6,
        [vmem(), hbm(), vmem()],
        [sds((t, D), F32), sds((HALF, 2 * D), BF), sds((2, D), F32)],
        [
            pltpu.VMEM((D, TRI), BF), pltpu.VMEM((HALF, D), BF), pltpu.VMEM((2, t, D), BF),
            pltpu.VMEM((2, t, HALF), BF), pltpu.VMEM((8, t), F32), pltpu.VMEM((2, HALF, t), F32),
            pltpu.VMEM((2, 2 * t, HALF), F32), pltpu.VMEM((2, 2 * t, HALF), F32),
            pltpu.VMEM((2, t, D), BF), pltpu.VMEM((2, t, D), BF), pltpu.VMEM((2, t, TRI), BF),
            pltpu.VMEM((t, D), F32), pltpu.VMEM((t, D), BF), pltpu.VMEM((t, D), BF),
            pltpu.VMEM((HALF, 2 * D), F32), pltpu.VMEM((HALF, 2 * D), BF),
            pltpu.VMEM((HALF, 2 * D), BF),
        ],
        3, 6, 10 << 30, (mg, h, wa, scales, tables, bias, *saved),
    )


TRIPLE, OUTPUT, EXPAND, SHRINK = range(4)
KINDS = (TRIPLE, OUTPUT, EXPAND, SHRINK)
ZS = 4


class Spot:
    def __init__(self):
        s = lax.axis_index("seq")
        self.s = s
        self.x, self.c = lax.div(s, 2), lax.rem(s, 2)
        self.d = lax.axis_index("dp")
        self.z, self.y = lax.div(self.d, 2), lax.rem(self.d, 2)
        self.upper, self.odd = lax.div(self.z, 2), lax.rem(self.z, 2)
        self.sib, self.peer = s + 1 - 2 * self.c, lax.rem(s + 2, SEQ)
        self.across = self.d + 1 - 2 * self.y
        self.zs = ZS

    def count(self, kind):
        return ZS if kind == EXPAND else ZS // 2

    def origin(self, kind, j):
        if kind == TRIPLE:
            return 2 * self.c + j
        if kind == OUTPUT:
            return 2 * self.x + j
        return j if kind == EXPAND else 2 * j + self.x

    def own_slot(self, kind):
        return {TRIPLE: self.odd, OUTPUT: self.odd, EXPAND: self.z, SHRINK: self.upper}[kind]

    def if_owner(self, kind, act):
        if kind == EXPAND:
            act()
        elif kind == TRIPLE:
            pl.when(self.c == self.upper)(act)
        elif kind == OUTPUT:
            pl.when(self.x == self.upper)(act)
        else:
            pl.when(self.x == self.odd)(act)

    def naturals(self, kind):
        x, c = self.x, self.c
        if kind == TRIPLE:
            return ((0, 2 * x), (1, 2 * x + 1), (2, 2 * (1 - x)), (3, 2 * (1 - x) + 1))
        if kind == EXPAND:
            return ((0, 2 * c + x),)
        return ((0, 2 * c), (1, 2 * c + 1))

    def targets(self, kind):
        x, c = self.x, self.c
        if kind == TRIPLE:
            return ((c, 0, 2 * x + self.upper), (2 + c, 1, 2 * (1 - x) + self.upper))
        if kind == OUTPUT:
            return ((c, 0, 2 * self.upper + x),)
        if kind == EXPAND:
            return ((0, 0, 2 * c + x),)
        return ((c, 0, 2 * self.odd + x),)


class Saved(NamedTuple):
    na: Any
    q: Any
    k: Any
    v: Any
    ctx: Any
    ctx_t: Any
    lse: Any
    nb: Any
    act: Any
    slope: Any
    wt: Any
    wo: Any
    we: Any
    ws: Any


class ForwardIn(NamedTuple):
    h0: Any
    sc_own: Any
    cs: Any
    bias: Any
    p_whole: Any
    p_half: Any
    p_out: Any
    p_exp: Any
    p_shr: Any


class ForwardHead(NamedTuple):
    h_out: Any
    h_mid: Any
    mid_o0: Any
    mid_o1: Any
    sc_o: Any


class ForwardScratch(NamedTuple):
    wt: Any
    wo: Any
    we: Any
    ws: Any
    hb: Any
    ob: Any
    scl: Any
    sc: Any
    na: Any
    q: Any
    k: Any
    v: Any
    ctxt: Any
    ctx: Any
    ctx_t: Any
    lse: Any
    nb: Any
    na_t: Any
    nb_t: Any
    act: Any
    slope: Any
    psend: Any
    precv: Any
    hs: Any
    mid: Any
    ssem: Any
    rsem: Any
    zero_ssem: Any
    zero_rsem: Any
    sc_ssem: Any
    sc_rsem: Any
    xs: Any
    xr: Any
    lsem: Any


class Refs:
    def __init__(self, *groups):
        for group in groups:
            for name, ref in zip(group._fields, group):
                setattr(self, name, ref)


def split(refs, *kinds):
    out, at = [], 0
    for kind in kinds:
        size = len(kind._fields)
        out.append(kind(*refs[at : at + size]))
        at += size
    return out


class Weights(Spot):
    def __init__(self, n, rows):
        super().__init__()
        self.n = n
        self.rows = rows
        self.source = {
            TRIPLE: (n.p_whole, n.p_half), OUTPUT: (n.p_out,), EXPAND: (n.p_exp,), SHRINK: (n.p_shr,)
        }

    def view(self, kind, layer, y, z, c):
        n, r = self.n, self.rows
        if kind == EXPAND:
            return n.we.at[layer, rows_of(2 * z + y, r), rows_of(c, D)]
        at = 2 * lax.rem(z, 2) + y
        if kind == TRIPLE:
            return n.wt.at[layer, pl.ds(pl.multiple_of(HALF * c + r * at, r), r), :]
        if kind == OUTPUT:
            return n.wo.at[layer, rows_of(at, r), rows_of(c, HALF)]
        return n.ws.at[layer, rows_of(c, HALF), rows_of(2 * lax.div(z, 2) + y, 4 * r)]

    def piece(self, kind, layer, number, to):
        n, r = self.n, self.rows
        x, c = lax.div(to, 2), lax.rem(to, 2)
        if kind == TRIPLE:
            start = pl.ds(pl.multiple_of(HALF * c + r * (2 * self.odd + self.y), r), r)
            return (n.wt.at[layer, start, rows_of(x + self.core_of(number), HALF)], n.hb.at[layer, self.core_of(number)])
        if kind == OUTPUT:
            return n.ob.at[layer, number]
        if kind == EXPAND:
            return self.view(kind, layer, self.y, self.z, c)
        rows = pl.ds(pl.multiple_of(HALF * c + 192 * number, 192), 192)
        return n.ws.at[layer, rows, rows_of(2 * self.upper + self.y, 4 * r)]

    @staticmethod
    def core_of(number):
        return lax.rem(number, 2)

    def landing(self, kind, layer, number, part, to):
        spot = self.piece(kind, layer, number, to)
        return spot[part] if kind == TRIPLE else spot

    def zero_copy(self, kind, layer, number, part, to):
        return pltpu.make_async_remote_copy(
            src_ref=self.source[kind][part].at[layer],
            dst_ref=self.landing(kind, layer, number, part, to),
            send_sem=self.n.zero_ssem.at[layer, kind, part],
            recv_sem=self.n.zero_rsem.at[layer, kind, number],
            device_id=(self.d, to),
            device_id_type=MESH,
        )

    def zero_here(self, kind, layer, number, part, to):
        return pltpu.make_async_copy(
            self.source[kind][part].at[layer], self.landing(kind, layer, number, part, to),
            self.n.zero_rsem.at[layer, kind, number],
        )

    def zero(self, kind, layer):
        for number, part, to in self.targets(kind):
            away = to != self.s
            place = (kind, layer, number, part, to)
            pl.when(away)(lambda place=place: self.zero_copy(*place).start())
            pl.when(jnp.logical_not(away))(lambda place=place: self.zero_here(*place).start())

    def remote(self, ref, kind, layer, stage, sent, slot, to):
        return pltpu.make_async_remote_copy(
            src_ref=ref,
            dst_ref=ref,
            send_sem=self.n.ssem.at[layer, kind, stage, sent],
            recv_sem=self.n.rsem.at[layer, kind, stage, slot],
            device_id=to,
            device_id_type=MESH,
        )

    def spread(self, kind, layer):
        def act():
            for number, _ in self.naturals(kind):
                part = 1 if kind == TRIPLE and number >= 2 else 0
                ref = self.landing(kind, layer, number, part, self.s)
                pltpu.make_async_remote_copy(
                    src_ref=ref, dst_ref=ref, send_sem=self.n.zero_ssem.at[layer, kind, part],
                    recv_sem=self.n.zero_rsem.at[layer, kind, number], device_id=(self.d, self.peer),
                    device_id_type=MESH,
                ).wait_recv()
            n, r = self.n, self.rows
            if kind == TRIPLE:
                start = HALF * self.c + r * (2 * self.odd + self.y)
                join(n.hb[layer, 0], n.hb[layer, 1], n.wt, layer, start, 2 * (1 - self.x) * HALF, r)
            elif kind == OUTPUT:
                join(n.ob[layer, 0], n.ob[layer, 1], n.wo, layer, r * (2 * self.odd + self.y), HALF * self.c, r)
            ref = self.view(kind, layer, self.y, self.z, self.c)
            slot = self.own_slot(kind)
            for k in range(1, ZS):
                other = lax.rem(self.z + k, ZS)
                self.remote(ref, kind, layer, 0, k, slot, (2 * other + self.y, self.s)).start()
            self.remote(ref, kind, layer, 1, slot, slot, (self.across, self.s)).start()

        self.if_owner(kind, act)

    def onward(self, kind, layer, j):
        z = self.origin(kind, j)

        @pl.when(z != self.z)
        def _():
            ref = self.view(kind, layer, self.y, z, self.c)
            self.remote(ref, kind, layer, 0, 0, j, (self.across, self.s)).wait_recv()
            self.remote(ref, kind, layer, 1, j, j, (self.across, self.s)).start()

    def onward_all(self, kind, layer):
        for j in range(self.count(kind)):
            self.onward(kind, layer, j)

    def arrive(self, kind, layer):
        for j in range(self.count(kind)):
            ref = self.view(kind, layer, 1 - self.y, self.origin(kind, j), self.c)
            self.remote(ref, kind, layer, 1, j, j, (self.across, self.s)).wait_recv()

    def finish(self, kind, layer):
        for number, part, to in self.targets(kind):
            place = (kind, layer, number, part, to)
            pl.when(to != self.s)(lambda place=place: self.zero_copy(*place).wait_send())

        def act():
            ref = self.view(kind, layer, self.y, self.z, self.c)
            for k in range(1, ZS):
                self.remote(ref, kind, layer, 0, k, 0, (self.across, self.s)).wait_send()

        self.if_owner(kind, act)
        for j in range(self.count(kind)):
            ref = self.view(kind, layer, self.y, self.origin(kind, j), self.c)
            self.remote(ref, kind, layer, 1, j, j, (self.across, self.s)).wait_send()


def join(first, second, into, layer, row, col, rows):
    half = rows // 2
    top, bottom = join_packed(first[rows:], second[rows:])
    all_rows = pl.ds(pl.multiple_of(row, half), rows)
    into[layer, all_rows, pl.ds(pl.multiple_of(col, 128), 128)] = first[:rows]
    middle = pl.ds(pl.multiple_of(col + 128, 128), 128)
    into[layer, pl.ds(pl.multiple_of(row, half), half), middle] = top
    into[layer, pl.ds(pl.multiple_of(row + half, half), half), middle] = bottom
    into[layer, all_rows, pl.ds(pl.multiple_of(col + 256, 128), 128)] = second[:rows]


def greet_all(w):
    barrier = pltpu.get_barrier_semaphore()

    def one(i, carry):
        z, s = lax.div(i, SEQ), lax.rem(i, SEQ)
        away = jnp.logical_or(z != w.z, s != w.s)

        @pl.when(away)
        def _():
            pl.semaphore_signal(barrier, inc=1, device_id=(2 * z + w.y, s), device_id_type=MESH)

        return carry

    lax.fori_loop(0, w.zs * SEQ, one, 0)
    pl.semaphore_signal(barrier, inc=1, device_id=(w.across, w.s), device_id_type=MESH)
    pl.semaphore_wait(barrier, w.zs * SEQ)


def left_half(shape):
    return lax.broadcasted_iota(jnp.int32, shape, 1) < HD


def join_packed(first, second):
    first, second = first.astype(F32), second.astype(F32)
    left = left_half(first.shape)
    top = jnp.where(left, first, second)
    bottom = pltpu.roll(jnp.where(left, second, first), HD, 1)
    return top.astype(BF), bottom.astype(BF)


def pack_wide(value):
    half = value.shape[0] // 2
    top, bottom = value[:half, 128:256], pltpu.roll(value[half:, 128:256], HD, 1)
    left = left_half(top.shape)
    first, second = jnp.where(left, top, bottom), jnp.where(left, bottom, top)
    return (
        jnp.concatenate([value[:, :128], first], axis=0),
        jnp.concatenate([value[:, 256:], second], axis=0),
    )


def gather_scales_start(w):
    n = w.n
    mine = n.scl.at[w.y, w.z, w.s]
    mine[...] = n.sc_own[...]

    def one(i, carry):
        z, s = lax.div(i, SEQ), lax.rem(i, SEQ)

        @pl.when(jnp.logical_or(z != w.z, s != w.s))
        def _():
            pltpu.make_async_remote_copy(
                src_ref=mine, dst_ref=mine, send_sem=n.sc_ssem.at[i],
                recv_sem=n.sc_rsem.at[w.z * SEQ + w.s], device_id=(2 * z + w.y, s), device_id_type=MESH,
            ).start()

        return carry

    lax.fori_loop(0, w.zs * SEQ, one, 0)


def gather_scales_end(w):
    n = w.n

    def one(i, carry):
        z, s = lax.div(i, SEQ), lax.rem(i, SEQ)

        @pl.when(jnp.logical_or(z != w.z, s != w.s))
        def _():
            slot = n.scl.at[w.y, z, s]
            copy = pltpu.make_async_remote_copy(
                src_ref=slot, dst_ref=slot, send_sem=n.sc_ssem.at[i], recv_sem=n.sc_rsem.at[i],
                device_id=(2 * z + w.y, s), device_id_type=MESH,
            )
            copy.wait_recv()
            copy.wait_send()

        return carry

    lax.fori_loop(0, w.zs * SEQ, one, 0)
    count = w.zs * SEQ
    plane = n.scl.at[w.y]
    copy = pltpu.make_async_remote_copy(
        src_ref=plane, dst_ref=plane, send_sem=n.sc_ssem.at[count], recv_sem=n.sc_rsem.at[count],
        device_id=(w.across, w.s), device_id_type=MESH,
    )
    copy.start()
    copy.wait()
    wide = n.sc.shape[-1] // (2 * w.zs)
    for s in range(SEQ):
        both = [n.scl[d % 2, d // 2, s][:, :wide] for d in range(2 * w.zs)]
        rows = jnp.concatenate(both, axis=1)
        for layer in range(LAYERS):
            n.sc[layer, s : s + 1, :] = rows[layer : layer + 1, :]


def fwd_kernel(dp, *refs):
    ins, outs, saved0, saved1, scratch = split(refs, ForwardIn, ForwardHead, Saved, Saved, ForwardScratch)
    n = Refs(ins, outs, scratch)
    saved = (saved0, saved1)
    rows = n.p_exp.shape[1]
    t = n.h0.shape[0]
    w = Weights(n, rows)
    x, c, peer, sib = w.x, w.c, w.peer, w.sib
    y = 1 - x
    copies = Copies(n.lsem, n.xs, n.xr, w.d)
    waits = []

    def save(src, dst):
        waits.append(copies.local(src, dst))

    greet_all(w)
    w.zero(TRIPLE, 0)
    gather_scales_start(w)
    for kind in (OUTPUT, EXPAND, SHRINK):
        w.zero(kind, 0)
    w.spread(TRIPLE, 0)
    w.spread(OUTPUT, 0)
    n.hs[0] = n.h0[...]
    xhat, _ = norm_stats(n.hs[0])
    gather_scales_end(w)

    def share_tri(layer):
        own = n.wt.at[layer, rows_of(c, HALF), :]
        return copies.push(own, own, sib)

    def share_out(layer):
        own = n.wo.at[layer, :, rows_of(c, HALF)]
        return copies.push(own, own, sib)

    def share_shr(layer):
        own = n.ws.at[layer, rows_of(c, HALF), :]
        return copies.push(own, own, sib)

    def share_exp(layer):
        own = n.we.at[layer, :, rows_of(c, D)]
        return copies.push(own, own, sib)

    for layer in range(LAYERS):
        last = layer == LAYERS - 1
        if layer:
            xhat, _ = norm_stats(n.hs[layer])
        n.na[layer, x] = (xhat * n.sc[layer, 0:1, :] + n.sc[layer, 1:2, :]).astype(BF)
        na_sent = copies.push(n.na.at[layer, x], n.na.at[layer, x], peer)
        if layer == 0:
            w.onward_all(TRIPLE, 0)
            w.spread(EXPAND, 0)
            w.spread(SHRINK, 0)
            w.onward_all(OUTPUT, 0)
            for kind in KINDS:
                w.zero(kind, 1)
            w.arrive(TRIPLE, 0)
            tri_sent = share_tri(0)
        tri_sent.wait()

        def project(block):
            cosine, sine = n.cs[block, :, 0:128], n.cs[block, :, 128:256]
            for j in range(9):
                part = nn(n.na[layer, block], n.wt[layer, :, 128 * j : 128 * j + 128])
                lanes = pl.ds(128 * (j % 3), 128)
                if j < 3:
                    n.q[layer, block, :, lanes] = (turn(part, cosine, sine) * HD**-0.5).astype(BF)
                elif j < 6:
                    n.k[layer, block, rows_of(c, t), lanes] = turn(part, cosine, sine).astype(BF)
                else:
                    n.v[layer, block, rows_of(c, t), lanes] = part.astype(BF)

        def share(block):
            at = (layer, block, rows_of(c, t))
            return [
                copies.push(n.k.at[at], n.k.at[at], sib),
                copies.push(n.v.at[at], n.v.at[at], sib),
            ]

        project(x)
        shared = share(x)
        na_sent.wait()
        project(y)
        shared += share(y)
        w.arrive(OUTPUT, layer)
        out_sent = share_out(layer)
        for copy in shared:
            copy.wait()
        save(n.q.at[layer], saved[layer].q)
        save(n.k.at[layer], saved[layer].k)
        save(n.v.at[layer], saved[layer].v)

        def attend(block, pump):
            other = 1 - block

            def pair_step(p, carry):
                pump(p)
                lanes = pl.ds(pl.multiple_of(p * 128, 128), 128)
                q_pair = n.q[layer, block, :, lanes]
                k_same, k_cross = n.k[layer, block, :, lanes], n.k[layer, other, :, lanes]
                v_same, v_cross = n.v[layer, block, :, lanes], n.v[layer, other, :, lanes]
                for which in range(2):
                    q_head = half_of(q_pair, which)
                    s_same = nt(k_same, q_head)
                    s_cross = nt(k_cross, q_head) + n.bias[0]
                    top = jnp.maximum(
                        jnp.max(s_same, axis=0, keepdims=True), jnp.max(s_cross, axis=0, keepdims=True)
                    )
                    e_same = jnp.exp(s_same - top)
                    e_cross = jnp.exp(s_cross - top)
                    total = jnp.sum(e_same, axis=0, keepdims=True) + jnp.sum(
                        e_cross, axis=0, keepdims=True
                    )
                    mixed = tn(v_same, e_same.astype(BF)) + tn(v_cross, e_cross.astype(BF))
                    head = pl.ds(pl.multiple_of(p * 128 + which * HD, HD), HD)
                    n.ctxt[head, :] = mixed[which * HD : which * HD + HD, :] / total
                    n.lse[layer, block, pl.ds(2 * p + which, 1), :] = top + jnp.log(total)
                return carry

            lax.fori_loop(0, HALF // 128, pair_step, 0)
            n.ctx_t[layer, :, rows_of(block, t)] = n.ctxt[...].astype(BF)
            n.ctx[layer, block] = n.ctxt[...].T.astype(BF)

        def early(p):
            kind = SHRINK if layer else EXPAND
            pl.when(p > 0)(lambda: w.onward(kind, layer, p - 1))

        attend(y, early)
        out_sent.wait()
        use = 2 * layer
        n.psend[use] = nn(n.ctx[layer, y], n.wo[layer]).astype(BF)
        part_sent = copies.push(n.psend.at[use], n.precv.at[use], peer)

        if not last:
            w.spread(TRIPLE, layer + 1)
            w.spread(OUTPUT, layer + 1)

        def late(p):
            if layer == 0:
                pl.when(p == 0)(lambda: w.onward(EXPAND, layer, 2))
                pl.when(p == 0)(lambda: w.onward(EXPAND, layer, 3))
                pl.when(p > 0)(lambda: w.onward(SHRINK, layer, p - 1))

        attend(x, late)
        if not last:
            w.spread(EXPAND, layer + 1)
            w.spread(SHRINK, layer + 1)
        n.mid[layer] = n.hs[layer] + nn(n.ctx[layer, x], n.wo[layer])
        save(n.ctx.at[layer], saved[layer].ctx)
        save(n.lse.at[layer], saved[layer].lse)
        save(n.wt.at[layer], saved[layer].wt)
        save(n.wo.at[layer], saved[layer].wo)
        save(n.ctx_t.at[layer], saved[layer].ctx_t)
        for block in range(2):
            n.na_t[layer, :, block * t : block * t + t] = n.na[layer, block].T
        save(n.na_t.at[layer], saved[layer].na)
        part_sent.wait()
        n.mid[layer] = n.mid[layer] + n.precv[use].astype(F32)
        save(n.mid.at[layer], (n.mid_o0, n.mid_o1)[layer])

        xhat, _ = norm_stats(n.mid[layer])
        n.nb[layer, x] = (xhat * n.sc[layer, 2:3, :] + n.sc[layer, 3:4, :]).astype(BF)
        nb_sent = copies.push(n.nb.at[layer, x], n.nb.at[layer, x], peer)
        w.arrive(EXPAND, layer)
        exp_sent = share_exp(layer)
        w.arrive(SHRINK, layer)
        shr_sent = share_shr(layer)
        exp_sent.wait()

        def feed(block, pump):
            def step(i, carry):
                pump(i)
                lanes = pl.ds(pl.multiple_of(i * 256, 256), 256)
                value, rate = gelu_parts(nn(n.nb[layer, block], n.we[layer, :, lanes]))
                n.act[layer, block, :, lanes] = value.astype(BF)
                n.slope[layer, block, :, lanes] = rate.astype(BF)
                return carry

            lax.fori_loop(0, HID // 256, step, 0)

        def pump(i):
            if not last:

                @pl.when(i < 2)
                def _():
                    w.onward(TRIPLE, layer + 1, i)
                    w.onward(OUTPUT, layer + 1, i)

        feed(x, lambda i: None)
        shr_sent.wait()
        n.hs[layer + 1] = n.mid[layer] + nt(n.act[layer, x], n.ws[layer])
        nb_sent.wait()
        feed(y, pump)
        use = 2 * layer + 1
        n.psend[use] = nt(n.act[layer, y], n.ws[layer]).astype(BF)
        part_sent = copies.push(n.psend.at[use], n.precv.at[use], peer)
        for block in range(2):
            n.nb_t[layer, :, block * t : block * t + t] = n.nb[layer, block].T
        save(n.nb_t.at[layer], saved[layer].nb)
        save(n.act.at[layer], saved[layer].act)
        save(n.slope.at[layer], saved[layer].slope)
        save(n.we.at[layer], saved[layer].we)
        save(n.ws.at[layer], saved[layer].ws)
        if not last:
            w.onward_all(EXPAND, layer + 1)
            w.arrive(TRIPLE, layer + 1)
            tri_sent = share_tri(layer + 1)
        part_sent.wait()
        n.hs[layer + 1] = n.hs[layer + 1] + n.precv[use].astype(F32)

    n.h_out[...] = n.hs[LAYERS]
    n.sc_o[...] = n.sc[...]
    save(n.hs.at[1], n.h_mid)
    for copy in waits:
        copy.wait()
    for layer in range(LAYERS):
        for kind in KINDS:
            w.finish(kind, layer)


def forward_all(dp, h, sc_own, tables, bias, pieces):
    t = h.shape[0]
    zs, packed = dp // 2, 3 * (D // dp) // 2
    per_layer = [
        sds((D, 2 * t), BF), sds((2, t, HALF), BF), sds((2, 2 * t, HALF), BF), sds((2, 2 * t, HALF), BF),
        sds((2, t, HALF), BF), sds((HALF, 2 * t), BF), sds((2, 8, t), F32), sds((D, 2 * t), BF), sds((2, t, HID), BF),
        sds((2, t, HID), BF), sds((D, TRI), BF), sds((HALF, D), BF), sds((D, HID), BF), sds((D, HID), BF),
    ]
    token = sds((t, D), F32)
    outs = [token, token, token, token, sds((LAYERS, 4, D), F32), *per_layer, *per_layer]
    specs = [vmem(), hbm(), hbm(), hbm(), vmem(), *([hbm()] * (2 * len(per_layer)))]
    n_layers = LAYERS
    scratch = [
        pltpu.VMEM((n_layers, D, TRI), BF), pltpu.VMEM((n_layers, HALF, D), BF),
        pltpu.VMEM((n_layers, D, HID), BF), pltpu.VMEM((n_layers, D, HID), BF),
        pltpu.VMEM((n_layers, 2, packed, 128), BF), pltpu.VMEM((n_layers, 2, packed, 128), BF),
        pltpu.VMEM((2, zs, SEQ, 8, 128), F32),
        pltpu.VMEM((n_layers, 4, D), F32), pltpu.VMEM((n_layers, 2, t, D), BF),
        pltpu.VMEM((n_layers, 2, t, HALF), BF), pltpu.VMEM((n_layers, 2, 2 * t, HALF), BF),
        pltpu.VMEM((n_layers, 2, 2 * t, HALF), BF), pltpu.VMEM((HALF, t), F32),
        pltpu.VMEM((n_layers, 2, t, HALF), BF), pltpu.VMEM((n_layers, HALF, 2 * t), BF),
        pltpu.VMEM((n_layers, 2, 8, t), F32), pltpu.VMEM((n_layers, 2, t, D), BF),
        pltpu.VMEM((n_layers, D, 2 * t), BF), pltpu.VMEM((n_layers, D, 2 * t), BF),
        pltpu.VMEM((n_layers, 2, t, HID), BF),
        pltpu.VMEM((n_layers, 2, t, HID), BF), pltpu.VMEM((2 * n_layers, t, D), BF),
        pltpu.VMEM((2 * n_layers, t, D), BF), pltpu.VMEM((n_layers + 1, t, D), F32),
        pltpu.VMEM((n_layers, t, D), F32),
        pltpu.SemaphoreType.DMA((n_layers, len(KINDS), 2, zs)),
        pltpu.SemaphoreType.DMA((n_layers, len(KINDS), 2, zs)),
        pltpu.SemaphoreType.DMA((n_layers, len(KINDS), 2)), pltpu.SemaphoreType.DMA((n_layers, len(KINDS), 4)),
        pltpu.SemaphoreType.DMA((zs * SEQ + 1,)), pltpu.SemaphoreType.DMA((zs * SEQ + 1,)),
        pltpu.SemaphoreType.DMA((24,)), pltpu.SemaphoreType.DMA((24,)), pltpu.SemaphoreType.DMA((32,)),
    ]
    results = pl.pallas_call(
        functools.partial(fwd_kernel, dp),
        name="forward",
        out_shape=outs,
        in_specs=[vmem(), vmem(), vmem(), pl.BlockSpec(memory_space=pltpu.SMEM), *([hbm()] * 5)],
        out_specs=specs,
        scratch_shapes=scratch,
        cost_estimate=pl.CostEstimate(flops=22 << 30, bytes_accessed=32 << 20, transcendentals=0),
        compiler_params=pltpu.CompilerParams(
            collective_id=4, has_side_effects=True, vmem_limit_bytes=VMEM_BYTES
        ),
    )(h, sc_own, tables, bias, *pieces)
    return split(results, ForwardHead, Saved, Saved)


def pack_rows(low, c):
    half = low.shape[1] // 2
    even = [low[:, :, :128], jnp.concatenate([low[:, :half, 128:], low[:, half:, 128:]], axis=2)]
    odd = [low[:, :, 64:], jnp.concatenate([low[:, half:, :64], low[:, :half, :64]], axis=2)]
    return jnp.where(c == 0, jnp.concatenate(even, axis=1), jnp.concatenate(odd, axis=1))


def unpack_rows(packed, c):
    rows = 2 * packed.shape[1] // 3
    wide, rest = packed[:, :rows], packed[:, rows:]
    even = jnp.concatenate([wide, jnp.concatenate([rest[:, :, :64], rest[:, :, 64:]], axis=1)], axis=2)
    odd = jnp.concatenate([jnp.concatenate([rest[:, :, 64:], rest[:, :, :64]], axis=1), wide], axis=2)
    return jnp.where(c == 0, even, odd)


def pieces_of(triple_weight, output_weight, expand_weight, shrink_weight, c):
    tri = triple_weight.astype(BF)
    whole = jnp.where(c == 0, tri[:, :, :HALF], tri[:, :, 192:])
    half = jnp.where(c == 0, tri[:, :, HALF:], tri[:, :, :192])
    shr = jnp.swapaxes(shrink_weight.astype(BF), 1, 2)
    return whole, pack_rows(half, c), pack_rows(output_weight.astype(BF), c), expand_weight.astype(BF), shr


class Sums(Spot):
    def __init__(self, n, rows):
        super().__init__()
        self.n = n
        self.rows = rows
        self.landed = {TRIPLE: n.y_tri, OUTPUT: n.y_out, EXPAND: n.y_exp, SHRINK: n.y_shr}
        self.owned = {TRIPLE: n.z_tri, OUTPUT: n.z_out, EXPAND: n.z_exp, SHRINK: n.z_shr}
        self.final = {TRIPLE: (n.f_whole, n.f_half), OUTPUT: (n.f_out,), EXPAND: (n.f_exp,), SHRINK: (n.f_shr,)}

    def view(self, kind, layer, y, z):
        n, r = self.n, self.rows
        if kind == EXPAND:
            return n.ge.at[layer, rows_of(2 * z + y, r), :]
        if kind == SHRINK:
            return n.gs.at[layer, :, rows_of(2 * lax.div(z, 2) + y, 4 * r)]
        return (n.gt if kind == TRIPLE else n.go).at[layer, rows_of(2 * lax.rem(z, 2) + y, r), :]

    def remote(self, src, dst, kind, layer, stage, sent, slot, to):
        return pltpu.make_async_remote_copy(
            src_ref=src,
            dst_ref=dst,
            send_sem=self.n.ssem.at[layer, kind, stage, sent],
            recv_sem=self.n.rsem.at[layer, kind, stage, slot],
            device_id=to,
            device_id_type=MESH,
        )

    def across_copy(self, kind, layer, j):
        return self.remote(
            self.view(kind, layer, 1 - self.y, self.origin(kind, j)), self.landed[kind].at[layer, j],
            kind, layer, 0, j, j, (self.across, self.s),
        )

    def across_all(self, kind, layer):
        for j in range(self.count(kind)):
            self.across_copy(kind, layer, j).start()

    def along_copy(self, kind, layer, j):
        z = self.origin(kind, j)
        slot = lax.rem(self.z - z + ZS - 1, ZS)
        mine = self.view(kind, layer, self.y, z)
        return self.remote(mine, self.owned[kind].at[layer, slot], kind, layer, 1, j, slot, (2 * z + self.y, self.s))

    def along(self, kind, layer, j):
        z = self.origin(kind, j)
        self.across_copy(kind, layer, j).wait_recv()
        mine = self.view(kind, layer, self.y, z)
        mine[...] = (mine[...].astype(F32) + self.landed[kind][layer, j].astype(F32)).astype(BF)
        pl.when(z != self.z)(lambda: self.along_copy(kind, layer, j).start())

    def along_all(self, kind, layer):
        for j in range(self.count(kind)):
            self.along(kind, layer, j)

    def parts(self, kind, layer):
        n = self.n
        mine = self.view(kind, layer, self.y, self.z)
        if kind == TRIPLE:
            return (
                mine.at[:, rows_of(self.x, HALF)], mine.at[:, rows_of(self.x + 1, HALF)],
                n.half_out.at[layer, 0], n.half_out.at[layer, 1],
            )
        if kind == OUTPUT:
            return n.out_out.at[layer, 0], n.out_out.at[layer, 1]
        return (mine,) if kind == EXPAND else (mine.at[pl.ds(0, 192), :], mine.at[pl.ds(192, 192), :])

    def home_copy(self, kind, layer, number, to, here=False):
        src = self.parts(kind, layer)[number]
        part = 1 if kind == TRIPLE and number >= 2 else 0
        dst = self.final[kind][part].at[layer]
        sem = self.n.home_rsem.at[layer, kind, part]
        if here:
            return pltpu.make_async_copy(src, dst, sem)
        return pltpu.make_async_remote_copy(
            src_ref=src, dst_ref=dst, send_sem=self.n.home_ssem.at[layer, kind, number], recv_sem=sem,
            device_id=(self.d, to), device_id_type=MESH,
        )

    def total(self, kind, layer):
        n = self.n

        def act():
            for slot in range(ZS - 1):
                ref = self.owned[kind].at[layer, slot]
                self.remote(ref, ref, kind, layer, 1, 0, slot, (self.across, self.s)).wait_recv()
            mine = self.view(kind, layer, self.y, self.z)
            value = mine[...].astype(F32)
            for slot in range(ZS - 1):
                value = value + self.owned[kind][layer, slot].astype(F32)
            n.squares[...] = n.squares[...] + squared(value)
            mine[...] = value.astype(BF)
            if kind == OUTPUT:
                first, second = pack_wide(value)
                n.out_out[layer, 0] = first.astype(BF)
                n.out_out[layer, 1] = second.astype(BF)
            if kind == TRIPLE:
                cut = mine[:, rows_of(2 * (1 - self.x), HALF)].astype(F32)
                first, second = pack_wide(cut)
                n.half_out[layer, 0] = first.astype(BF)
                n.half_out[layer, 1] = second.astype(BF)
            for number, to in self.naturals(kind):
                away = to != self.s
                place = (kind, layer, number, to)
                pl.when(away)(lambda place=place: self.home_copy(*place).start())
                pl.when(jnp.logical_not(away))(lambda place=place: self.home_copy(*place, True).start())

        self.if_owner(kind, act)

    def home(self, kind, layer):
        for part, final in enumerate(self.final[kind]):
            ref = final.at[layer]
            pltpu.make_async_remote_copy(
                src_ref=ref, dst_ref=ref, send_sem=self.n.home_ssem.at[layer, kind, 0],
                recv_sem=self.n.home_rsem.at[layer, kind, part], device_id=(self.d, self.peer), device_id_type=MESH,
            ).wait_recv()

    def finish(self, kind, layer):
        for j in range(self.count(kind)):
            self.across_copy(kind, layer, j).wait_send()
            pl.when(self.origin(kind, j) != self.z)(
                lambda j=j: self.along_copy(kind, layer, j).wait_send()
            )

        def act():
            for number, to in self.naturals(kind):
                place = (kind, layer, number, to)
                pl.when(to != self.s)(lambda place=place: self.home_copy(*place).wait_send())

        self.if_owner(kind, act)


def squared(value):
    return jnp.sum(jnp.sum(value * value, axis=1, keepdims=True), axis=0, keepdims=True)


def everywhere_start(w, use, buf):
    n = w.n
    mine = buf.at[w.y, w.z, w.s]

    def one(i, carry):
        z, s = lax.div(i, SEQ), lax.rem(i, SEQ)

        @pl.when(jnp.logical_or(z != w.z, s != w.s))
        def _():
            pltpu.make_async_remote_copy(
                src_ref=mine, dst_ref=mine, send_sem=n.ev_ssem.at[use, i],
                recv_sem=n.ev_rsem.at[use, w.z * SEQ + w.s], device_id=(2 * z + w.y, s), device_id_type=MESH,
            ).start()

        return carry

    lax.fori_loop(0, w.zs * SEQ, one, 0)


def everywhere_end(w, use, buf, pair):
    n = w.n

    def one(i, carry):
        z, s = lax.div(i, SEQ), lax.rem(i, SEQ)

        @pl.when(jnp.logical_or(z != w.z, s != w.s))
        def _():
            slot = buf.at[w.y, z, s]
            copy = pltpu.make_async_remote_copy(
                src_ref=slot, dst_ref=slot, send_sem=n.ev_ssem.at[use, i], recv_sem=n.ev_rsem.at[use, i],
                device_id=(2 * z + w.y, s), device_id_type=MESH,
            )
            copy.wait_recv()
            copy.wait_send()

        return carry

    lax.fori_loop(0, w.zs * SEQ, one, 0)

    def add(i, total):
        return total + buf[w.y, lax.div(i, SEQ), lax.rem(i, SEQ)]

    pair[w.y] = lax.fori_loop(1, w.zs * SEQ, add, buf[w.y, 0, 0])
    count = w.zs * SEQ
    copy = pltpu.make_async_remote_copy(
        src_ref=pair.at[w.y], dst_ref=pair.at[w.y], send_sem=n.ev_ssem.at[use, count],
        recv_sem=n.ev_rsem.at[use, count], device_id=(w.across, w.s), device_id_type=MESH,
    )
    copy.start()
    copy.wait()
    return pair[0] + pair[1]


class Loaded(NamedTuple):
    na: Any
    q: Any
    k: Any
    v: Any
    ctx: Any
    ctx_t: Any
    lse: Any
    nb: Any
    act: Any
    slope: Any
    wt: Any
    wo: Any
    we: Any
    ws: Any
    h: Any
    mid: Any


class BackwardIn(NamedTuple):
    g0: Any
    sc: Any
    cs: Any
    bias: Any


class BackwardOut(NamedTuple):
    g_out: Any
    scale_o: Any
    norm_o: Any
    whole_g: Any
    half_g: Any
    out_g: Any
    exp_g: Any
    shr_g: Any


class BackwardScratch(NamedTuple):
    gl: Any
    gl_t: Any
    hg: Any
    ml: Any
    cg: Any
    delta: Any
    dqt: Any
    dk: Any
    dv: Any
    kvsend: Any
    kvrecv: Any
    pg: Any
    part: Any
    psend: Any
    precv: Any
    gs_exp: Any
    gr_exp: Any
    gs_shr: Any
    gr_shr: Any
    gr_att: Any
    gt: Any
    go: Any
    ge: Any
    gs: Any
    y_tri: Any
    y_out: Any
    y_exp: Any
    y_shr: Any
    z_tri: Any
    z_out: Any
    z_exp: Any
    z_shr: Any
    half_out: Any
    out_out: Any
    f_whole: Any
    f_half: Any
    f_out: Any
    f_exp: Any
    f_shr: Any
    squares: Any
    early: Any
    early_pair: Any
    late: Any
    late_pair: Any
    sq: Any
    sq_pair: Any
    ssem: Any
    rsem: Any
    home_ssem: Any
    home_rsem: Any
    ev_ssem: Any
    ev_rsem: Any
    xs: Any
    xr: Any
    lsem: Any


def bwd_kernel(dp, *refs):
    ins, saved0, saved1, outs, loaded, scratch = split(
        refs, BackwardIn, Loaded, Loaded, BackwardOut, Loaded, BackwardScratch
    )
    n = Refs(ins, outs, loaded, scratch)
    saved = (saved0, saved1)
    t = n.g0.shape[0]
    w = Sums(n, D // dp)
    x, c, peer, sib = w.x, w.c, w.peer, w.sib
    y = 1 - x
    copies = Copies(n.lsem, n.xs, n.xr, w.d)
    loading = {}

    def load(layer, *wanted):
        for place in wanted:
            loading[place] = copies.local(saved[layer][place], loaded[place])

    def ready(*wanted):
        for place in wanted:
            loading[place].wait()

    na, q, k, v, ctx, ctx_t, lse, nb, act, slope, wt, wo, we, ws, h, mid = range(len(Loaded._fields))
    feed_places = (ws, slope, we, act, nb, mid)
    attend_places = (wo, ctx, q, k, v, lse, wt, na, ctx_t, h)
    load(LAYERS - 1, *feed_places, *attend_places)
    greet_all(w)
    n.g_out[...] = n.g0[...]

    for layer in reversed(range(LAYERS)):
        top = layer == LAYERS - 1

        n.gl[layer, x] = n.g_out[...].astype(BF)
        g_sent = copies.push(n.gl.at[layer, x], n.gl.at[layer, x], peer)
        ready(ws, slope, we)

        def back(block, pump):
            def step(i, carry):
                pump(i)
                lanes = pl.ds(pl.multiple_of(i * 256, 256), 256)
                pulled = nn(n.gl[layer, block], n.ws[:, lanes])
                n.hg[block, :, lanes] = (pulled * n.slope[block, :, lanes].astype(F32)).astype(BF)
                return carry

            lax.fori_loop(0, HID // 256, step, 0)
            return nt(n.hg[block], n.we[...])

        def pump_tri(i):
            if not top:

                @pl.when(i < 2)
                def _():
                    w.along(TRIPLE, layer + 1, i)
                    w.along(OUTPUT, layer + 1, i)

        n.part[...] = back(x, lambda i: None)
        g_sent.wait()
        use = 2 * layer
        n.psend[...] = back(y, lambda i: None).astype(BF)
        part_sent = copies.push(n.psend, n.precv.at[use], peer)
        ready(act, nb, mid)
        for block in range(2):
            n.gl_t[:, block * t : block * t + t] = n.gl[layer, block].T

        def exp_tile(which, i):
            off = pl.ds(pl.multiple_of(which * D + i * 256, 256), 256)
            return nn(n.nb[...], n.hg[:, :, off].reshape(2 * t, 256))

        def shr_tile(which, i):
            off = pl.ds(pl.multiple_of(i * 256, 256), 256)
            return nn(n.gl_t[rows_of(which, HALF), :], n.act[:, :, off].reshape(2 * t, 256))

        def send_exp(i, carry):
            at = pl.ds(pl.multiple_of(i * 256, 256), 256)
            n.gs_exp[:, at] = exp_tile(1 - c, i).astype(BF)
            return carry

        def send_shr(i, carry):
            at = pl.ds(pl.multiple_of(i * 256, 256), 256)
            n.gs_shr[:, at] = shr_tile(1 - c, i).astype(BF)
            return carry

        lax.fori_loop(0, D // 256, send_exp, 0)
        exp_sent = copies.push(n.gs_exp, n.gr_exp, sib)
        lax.fori_loop(0, HID // 256, send_shr, 0)
        shr_sent = copies.push(n.gs_shr, n.gr_shr, sib)

        def keep_exp(i, carry):
            at = pl.ds(pl.multiple_of(i * 256, 256), 256)
            n.ge[layer, :, at] = (exp_tile(c, i) + n.gr_exp[:, at].astype(F32)).astype(BF)
            return carry

        def keep_shr(i, carry):
            pump_tri(i)
            at = pl.ds(pl.multiple_of(i * 256, 256), 256)
            n.gs[layer, :, at] = (shr_tile(c, i) + n.gr_shr[:, at].astype(F32)).astype(BF)
            return carry

        exp_sent.wait()
        lax.fori_loop(0, D // 256, keep_exp, 0)
        w.across_all(EXPAND, layer)
        shr_sent.wait()
        lax.fori_loop(0, HID // 256, keep_shr, 0)
        w.across_all(SHRINK, layer)
        part_sent.wait()
        dy = n.part[...] + n.precv[use].astype(F32)
        back_mid, rows_b = norm_back(n.mid[...], n.sc[layer, 2:3, :], dy)
        n.g_out[...] = n.g_out[...] + back_mid

        n.ml[layer, x] = n.g_out[...].astype(BF)
        ml_sent = copies.push(n.ml.at[layer, x], n.ml.at[layer, x], peer)
        if layer:
            load(layer - 1, *feed_places)
        n.dk[...] = jnp.zeros_like(n.dk)
        n.dv[...] = jnp.zeros_like(n.dv)
        ready(wo, ctx, q, k, v, lse)

        def attend(block, pump):
            other = 1 - block
            n.cg[block] = nt(n.ml[layer, block], n.wo[...]).astype(BF)
            weighed = (n.cg[block].astype(F32) * n.ctx[block].astype(F32)).T
            for head in range(HALF // HD):
                n.delta[head : head + 1, :] = jnp.sum(
                    weighed[head * HD : head * HD + HD, :], axis=0, keepdims=True
                )

            def pair_step(p, carry):
                pump(p)
                lanes = pl.ds(pl.multiple_of(p * 128, 128), 128)
                q_pair, cg_pair = n.q[block, :, lanes], n.cg[block, :, lanes]
                for which in range(2):
                    q_head, cg_head = half_of(q_pair, which), half_of(cg_pair, which)
                    row = pl.ds(2 * p + which, 1)
                    total, dots = n.lse[block, row, :], n.delta[row, :]
                    turned = None
                    for side in (block, other):
                        k_pair, v_pair = n.k[side, :, lanes], n.v[side, :, lanes]
                        scores = nt(k_pair, q_head)
                        if side is other:
                            scores = scores + n.bias[0]
                        probs = jnp.exp(scores - total)
                        score_grad = (probs * (nt(v_pair, cg_head) - dots)).astype(BF)
                        n.dv[side, :, lanes] += nn(probs.astype(BF), cg_head)
                        n.dk[side, :, lanes] += nn(score_grad, q_head)
                        piece = tn(k_pair, score_grad)
                        turned = piece if turned is None else turned + piece
                    head = pl.ds(pl.multiple_of(p * 128 + which * HD, HD), HD)
                    n.dqt[block, head, :] = turned[which * HD : which * HD + HD, :] * HD**-0.5
                return carry

            lax.fori_loop(0, HALF // 128, pair_step, 0)

        attend(x, lambda p: None)
        ml_sent.wait()
        attend(y, lambda p: w.along(EXPAND, layer, p))
        theirs, mine = rows_of(1 - c, t), rows_of(c, t)
        for side in range(2):
            n.kvsend[side, :, pl.ds(0, HALF)] = n.dk[side, theirs, :].astype(BF)
            n.kvsend[side, :, pl.ds(HALF, HALF)] = n.dv[side, theirs, :].astype(BF)
        kv_sent = copies.push(n.kvsend, n.kvrecv.at[layer], sib)
        w.along(EXPAND, layer, 3)

        def unturn(block, j, value):
            cosine, sine = n.cs[block, :, 0:128], n.cs[block, :, 128:256]
            rounded = value.astype(BF).astype(F32)
            n.pg[block, :, pl.ds(128 * j, 128)] = turn(rounded, cosine, -sine).astype(BF)

        for side in range(2):
            for j in range(3):
                unturn(side, j, n.dqt[side, 128 * j : 128 * j + 128, :].T)
        kv_sent.wait()
        for side in range(2):
            for j in range(3):
                at = pl.ds(128 * j, 128)
                unturn(side, 3 + j, n.dk[side, mine, at] + n.kvrecv[layer, side, :, at].astype(F32))
                n.pg[side, :, pl.ds(D + 128 * j, 128)] = (
                    n.dv[side, mine, at] + n.kvrecv[layer, side, :, pl.ds(HALF + 128 * j, 128)].astype(F32)
                ).astype(BF)
        ready(wt, na, ctx_t, h)
        use = 2 * layer + 1
        n.psend[...] = nt(n.pg[y], n.wt[...]).astype(BF)
        part_sent = copies.push(n.psend, n.precv.at[use], peer)
        rows = D // dp

        def send_tri(i, carry):
            pl.when(i < 2)(lambda: w.along(SHRINK, layer, i))
            off = pl.ds(pl.multiple_of((1 - c) * HALF + i * rows, rows), rows)
            n.gs_shr[rows_of(i, rows), pl.ds(0, TRI)] = nn(n.na[off, :], n.pg[...].reshape(2 * t, TRI)).astype(BF)
            return carry

        lax.fori_loop(0, w.zs, send_tri, 0)
        tri_cols, out_cols = pl.ds(0, TRI), pl.ds(TRI, HALF)
        tri_sent = copies.push(n.gs_shr.at[:, tri_cols], n.gr_att.at[:, tri_cols], sib)
        theirs_too = n.ml[layer, :, :, rows_of(1 - c, HALF)].reshape(2 * t, HALF)
        n.gs_shr[:, out_cols] = nn(n.ctx_t[...], theirs_too).astype(BF)
        out_sent = copies.push(n.gs_shr.at[:, out_cols], n.gr_att.at[:, out_cols], sib)
        n.part[...] = nt(n.pg[x], n.wt[...])
        tri_sent.wait()

        def keep_tri(i, carry):
            at = rows_of(i, rows)
            row_block = n.na[pl.ds(pl.multiple_of(c * HALF + i * rows, rows), rows), :]
            value = nn(row_block, n.pg[...].reshape(2 * t, TRI)) + n.gr_att[at, tri_cols].astype(F32)
            n.gt[layer, at, :] = value.astype(BF)
            return carry

        lax.fori_loop(0, w.zs, keep_tri, 0)
        w.across_all(TRIPLE, layer)
        out_sent.wait()
        mine_too = n.ml[layer, :, :, rows_of(c, HALF)].reshape(2 * t, HALF)
        value = nn(n.ctx_t[...], mine_too) + n.gr_att[:, out_cols].astype(F32)
        n.go[layer] = value.astype(BF)
        w.across_all(OUTPUT, layer)
        part_sent.wait()
        dy = n.part[...] + n.precv[use].astype(F32)
        back_h, rows_a = norm_back(n.h[...], n.sc[layer, 0:1, :], dy)
        n.g_out[...] = n.g_out[...] + back_h
        mine_at = (w.y, w.z, w.s)
        if layer:
            load(layer - 1, *attend_places)
            n.early[(*mine_at, pl.ds(0, 2))] = rows_a
            n.early[(*mine_at, pl.ds(2, 2))] = rows_b
        else:
            n.early[(*mine_at, pl.ds(4, 2))] = rows_b
            n.late[mine_at] = rows_a

    everywhere_start(w, 0, n.early)
    everywhere_start(w, 1, n.late)
    n.squares[...] = jnp.zeros_like(n.squares)
    for kind in (EXPAND, SHRINK, TRIPLE, OUTPUT):
        w.total(kind, 1)
    w.along_all(TRIPLE, 0)
    w.along_all(OUTPUT, 0)
    for kind in (EXPAND, SHRINK):
        w.total(kind, 0)
    first = everywhere_end(w, 0, n.early, n.early_pair)
    second = everywhere_end(w, 1, n.late, n.late_pair)
    n.scale_o[1, pl.ds(0, 2)] = first[0:2]
    n.scale_o[1, pl.ds(2, 2)] = first[2:4]
    n.scale_o[0, pl.ds(0, 2)] = second
    n.scale_o[0, pl.ds(2, 2)] = first[4:6]
    for kind in (TRIPLE, OUTPUT):
        w.total(kind, 0)
    n.sq[w.y, w.z, w.s] = jnp.broadcast_to(n.squares[...], (8, 128))
    everywhere_start(w, 2, n.sq)
    for layer in range(LAYERS):
        for kind in KINDS:
            w.home(kind, layer)
    outputs = [
        copies.local(a, b)
        for a, b in (
            (n.f_whole, n.whole_g), (n.f_half, n.half_g), (n.f_out, n.out_g), (n.f_exp, n.exp_g), (n.f_shr, n.shr_g)
        )
    ]
    total = everywhere_end(w, 2, n.sq, n.sq_pair)
    n.norm_o[...] = total + squared(first[0:6]) + squared(second)
    for copy in outputs:
        copy.wait()
    for layer in range(LAYERS):
        for kind in KINDS:
            w.finish(kind, layer)


def backward_all(dp, g, f, residual, tables, bias):
    t = g.shape[0]
    zs = dp // 2
    r = D // dp
    packed = 3 * r // 2
    head, saved0, saved1 = f
    saved = (*saved0, residual, head.mid_o0, *saved1, head.h_mid, head.mid_o1)
    outs = [
        sds((t, D), F32), sds((LAYERS, 4, D), F32), sds((8, 128), F32), sds((LAYERS, r, HALF), BF),
        sds((LAYERS, packed, 128), BF), sds((LAYERS, packed, 128), BF), sds((LAYERS, r, D), BF),
        sds((LAYERS, 192, 4 * r), BF),
    ]
    v = pltpu.VMEM
    ll = LAYERS
    scratch = [
        *(v(array.shape, array.dtype) for array in saved[: len(Loaded._fields)]),
        v((ll, 2, t, D), BF), v((D, 2 * t), BF), v((2, t, HID), BF), v((ll, 2, t, D), BF), v((2, t, HALF), BF), v((8, t), F32),
        v((2, HALF, t), F32), v((2, 2 * t, HALF), F32), v((2, 2 * t, HALF), F32), v((2, t, D), BF),
        v((ll, 2, t, D), BF), v((2, t, TRI), BF), v((t, D), F32), v((t, D), BF), v((2 * ll, t, D), BF),
        v((D, D), BF), v((D, D), BF), v((HALF, HID), BF), v((HALF, HID), BF), v((HALF, HID), BF),
        v((ll, HALF, TRI), BF), v((ll, HALF, HALF), BF), v((ll, D, D), BF), v((ll, HALF, HID), BF),
        v((ll, 2, r, TRI), BF), v((ll, 2, r, HALF), BF), v((ll, 4, r, D), BF), v((ll, 2, HALF, 4 * r), BF),
        v((ll, 3, r, TRI), BF), v((ll, 3, r, HALF), BF), v((ll, 3, r, D), BF), v((ll, 3, HALF, 4 * r), BF),
        v((ll, 2, packed, 128), BF), v((ll, 2, packed, 128), BF),
        v((ll, r, HALF), BF), v((ll, packed, 128), BF), v((ll, packed, 128), BF), v((ll, r, D), BF),
        v((ll, 192, 4 * r), BF), v((1, 1), F32),
        v((2, zs, SEQ, 8, D), F32), v((2, 8, D), F32), v((2, zs, SEQ, 2, D), F32), v((2, 2, D), F32),
        v((2, zs, SEQ, 8, 128), F32), v((2, 8, 128), F32),
        pltpu.SemaphoreType.DMA((ll, len(KINDS), 2, zs)), pltpu.SemaphoreType.DMA((ll, len(KINDS), 2, zs)),
        pltpu.SemaphoreType.DMA((ll, len(KINDS), 4)), pltpu.SemaphoreType.DMA((ll, len(KINDS), 2)),
        pltpu.SemaphoreType.DMA((3, zs * SEQ + 1)), pltpu.SemaphoreType.DMA((3, zs * SEQ + 1)),
        pltpu.SemaphoreType.DMA((20,)), pltpu.SemaphoreType.DMA((20,)), pltpu.SemaphoreType.DMA((40,)),
    ]
    results = pl.pallas_call(
        functools.partial(bwd_kernel, dp),
        name="backward",
        out_shape=outs,
        in_specs=[vmem(), vmem(), vmem(), pl.BlockSpec(memory_space=pltpu.SMEM), *([hbm()] * len(saved))],
        out_specs=[vmem()] * 3 + [hbm()] * 5,
        scratch_shapes=scratch,
        cost_estimate=pl.CostEstimate(flops=44 << 30, bytes_accessed=48 << 20, transcendentals=0),
        compiler_params=pltpu.CompilerParams(
            collective_id=5, has_side_effects=True, vmem_limit_bytes=VMEM_BYTES
        ),
    )(g, head.sc_o, tables, bias, *saved)
    return BackwardOut(*results)


class Moves:
    def __init__(self, dp):
        self.dp = dp
        self.d = lax.axis_index("dp")
        s = lax.axis_index("seq")
        self.s, self.x, self.c = s, s // 2, s % 2
        half = dp // 2
        ids = [(d, s) for d in range(dp) for s in range(SEQ)]
        self.tri = []
        for r in range(2):
            for j in range(3):
                perm = []
                for d, s in ids:
                    b = (3 * s + j) % 4
                    to = (2 * (d % half) + (r ^ (b % 2)), 2 * (b // 2) + d // half)
                    perm.append((d * SEQ + s, to[0] * SEQ + to[1]))
                self.tri.append(perm)
        self.out = []
        for r in range(2):
            perm = []
            for d, s in ids:
                to = (2 * (d % half) + (r ^ (s % 2)), 2 * (d // half) + s // 2)
                perm.append((d * SEQ + s, to[0] * SEQ + to[1]))
            self.out.append(perm)
        self.shr = []
        for k in range(4):
            perm = []
            for d, s in ids:
                to = (4 * (d % (dp // 4)) + (k + s) % 4, d // (dp // 4))
                perm.append((d * SEQ + s, to[0] * SEQ + to[1]))
            self.shr.append(perm)

    def send(self, piece, perm, back):
        if back:
            perm = [(b, a) for a, b in perm]
        return lax.ppermute(piece, ("dp", "seq"), perm)

    @staticmethod
    def pick(pieces, index):
        return lax.dynamic_index_in_dim(jnp.stack(pieces), index, 0, keepdims=False)

    def tri_out(self, low):
        n, rows, _ = low.shape
        halves = low.reshape(n, 2, rows // 2, 3, 192)
        got = []
        for r in range(2):
            for j in range(3):
                which = r ^ (((3 * self.s + j) % 4) % 2)
                piece = lax.dynamic_index_in_dim(halves[:, :, :, j], which, 1, keepdims=False)
                got.append(self.send(piece, self.tri[3 * r + j], False))
        parts = []
        for t in range(3):
            for bb in range(2):
                r, j = bb ^ (self.d % 2), (t + 2 * self.x + bb) % 3
                parts.append(self.pick(got, 3 * r + j))
        return jnp.concatenate(parts, axis=-1)

    def tri_back(self, grad):
        n, rows, _ = grad.shape
        got = []
        for r in range(2):
            for j in range(3):
                bb = (self.d % 2) ^ r
                t = (j - (2 * self.x + bb)) % 3
                piece = lax.dynamic_slice_in_dim(grad, (2 * t + bb) * 192, 192, 2)
                got.append(self.send(piece, self.tri[3 * r + j], True))
        cols = []
        for j in range(3):
            two = []
            for hh in range(2):
                r = hh ^ (((3 * self.s + j) % 4) % 2)
                two.append(self.pick([got[j], got[3 + j]], r))
            cols.append(jnp.concatenate(two, axis=1))
        return jnp.concatenate(cols, axis=-1)

    def out_out(self, low):
        n, rows, _ = low.shape
        halves = low.reshape(n, 2, rows // 2, 192)
        got = [
            self.send(
                lax.dynamic_index_in_dim(halves, r ^ (self.s % 2), 1, keepdims=False), self.out[r], False
            )
            for r in range(2)
        ]
        return jnp.concatenate([self.pick(got, u ^ (self.d % 2)) for u in range(2)], axis=-1)

    def out_back(self, grad):
        got = []
        for r in range(2):
            u = r ^ (self.d % 2)
            got.append(self.send(lax.dynamic_slice_in_dim(grad, u * 192, 192, 2), self.out[r], True))
        return jnp.concatenate([self.pick(got, hh ^ (self.s % 2)) for hh in range(2)], axis=1)

    def shr_out(self, low):
        n, rows, _ = low.shape
        subs = low.reshape(n, 4, rows // 4, 192)
        got = [
            self.send(
                lax.dynamic_index_in_dim(subs, (k + self.s) % 4, 1, keepdims=False), self.shr[k], False
            )
            for k in range(4)
        ]
        return jnp.concatenate([self.pick(got, (self.d - s) % 4) for s in range(4)], axis=-1)

    def shr_back(self, grad):
        got = []
        for k in range(4):
            piece = lax.dynamic_slice_in_dim(grad, ((self.d - k) % 4) * 192, 192, 2)
            got.append(self.send(piece, self.shr[k], True))
        return jnp.concatenate([self.pick(got, (sub - self.s) % 4) for sub in range(4)], axis=1)


def tables_here(segments, t, x, c):
    group = segments.shape[0]
    whole = segments[0] == segments[group - 1]
    place_in_half = c * t + jnp.arange(t, dtype=jnp.int32)
    second = jnp.where(whole, group // 2, 0).astype(jnp.int32)
    positions = jnp.stack([place_in_half, place_in_half + second]).astype(F32)
    lane = jnp.arange(128, dtype=jnp.int32)
    inverse = 1.0 / ROTARY_BASE ** ((lane % (HD // 2)).astype(F32) * (2.0 / HD))
    angles = positions[:, :, None] * inverse[None, None, :]
    sign = jnp.where(lane % HD < HD // 2, -1.0, 1.0).astype(F32)
    tables = jnp.concatenate([jnp.cos(angles), jnp.sin(angles) * sign], axis=-1)
    bias = jnp.where(whole, 0.0, MASKED).astype(F32).reshape(1)
    return tables, bias


def layers_narrow(
    dp, moves, residual, cotangent, scales_weight, tables, bias,
    triple_weight, output_weight, expand_weight, shrink_weight,
):
    d, s = lax.axis_index("dp"), lax.axis_index("seq")
    scales_all = lax.psum(
        lax.dynamic_update_slice(
            jnp.zeros((LAYERS, 4, D), F32), scales_weight.astype(BF).astype(F32), (0, s, d * (D // dp))
        ),
        ("dp", "seq"),
    )
    tri = moves.tri_out(triple_weight.astype(BF))
    out = moves.out_out(output_weight.astype(BF))
    shr = moves.shr_out(shrink_weight.astype(BF))
    attend_parts = jnp.concatenate([tri, out], axis=-1)
    feed_parts = jnp.concatenate([expand_weight.astype(BF), shr], axis=-1)
    gather = functools.partial(lax.all_gather, axis_name="dp", axis=0, tiled=True)
    wa, wf = [], []
    for layer in range(LAYERS):
        wa.append(gather(attend_parts[layer]))
        wf.append(gather(feed_parts[layer]))

    stream = residual
    kept = []
    for layer in range(LAYERS):
        scales = scales_all[layer]
        middle, *attend_saved = attend_fwd(stream, wa[layer], scales, tables, bias)
        following, *feed_saved = feed_fwd(middle, wf[layer], scales)
        kept.append((stream, middle, attend_saved, feed_saved))
        stream = following

    g = cotangent
    attend_grads, feed_grads, scale_grads = [None] * LAYERS, [None] * LAYERS, [None] * LAYERS
    scatter = functools.partial(lax.psum_scatter, axis_name="dp", scatter_dimension=0, tiled=True)
    for layer in reversed(range(LAYERS)):
        scales = scales_all[layer]
        h, middle, attend_saved, feed_saved = kept[layer]
        mg, feed_grad, rows_b = feed_bwd(g, middle, wf[layer], scales, *feed_saved)
        feed_grads[layer] = scatter(feed_grad).astype(F32)
        g, attend_grad, rows_a = attend_bwd(mg, h, wa[layer], scales, tables, bias, attend_saved)
        attend_grads[layer] = scatter(attend_grad).astype(F32)
        scale_grads[layer] = jnp.concatenate([rows_a, rows_b], axis=0)

    scale_grad = lax.psum(jnp.stack(scale_grads), ("dp", "seq"))
    own_scale = lax.dynamic_slice(scale_grad, (0, s, d * (D // dp)), (LAYERS, 1, D // dp))
    squares = jnp.sum(own_scale * own_scale)
    for part in (*attend_grads, *feed_grads):
        squares = squares + jnp.sum(part * part)
    grad_norm = jnp.sqrt(lax.psum(squares, ("dp", "seq")))

    attend_grad, feed_grad = jnp.stack(attend_grads).astype(BF), jnp.stack(feed_grads).astype(BF)
    triple_grad = moves.tri_back(attend_grad[:, :, :TRI]).astype(F32)
    output_grad = moves.out_back(attend_grad[:, :, TRI:]).astype(F32)
    expand_grad = feed_grad[:, :, :D].astype(F32)
    shrink_grad = moves.shr_back(feed_grad[:, :, D:]).astype(F32)
    return stream, g, grad_norm, (triple_grad, output_grad, expand_grad, shrink_grad, own_scale)


def layers_wide(
    dp, moves, residual, cotangent, scales_weight, tables, bias,
    triple_weight, output_weight, expand_weight, shrink_weight,
):
    d, s, c = lax.axis_index("dp"), lax.axis_index("seq"), moves.c
    sc_own = jnp.zeros((8, 128), F32)
    sc_own = sc_own.at[:LAYERS, : D // dp].set(scales_weight[:, 0].astype(BF).astype(F32))
    pieces = pieces_of(triple_weight, output_weight, expand_weight, shrink_weight, c)
    f = forward_all(dp, residual, sc_own, tables, bias, pieces)
    b = backward_all(dp, cotangent, f, residual, tables, bias)
    half_g, out_g = unpack_rows(b.half_g.astype(F32), c), unpack_rows(b.out_g.astype(F32), c)
    triple_grad = jnp.where(
        c == 0,
        jnp.concatenate([b.whole_g.astype(F32), half_g], axis=-1),
        jnp.concatenate([half_g, b.whole_g.astype(F32)], axis=-1),
    )
    own_scale = lax.dynamic_slice(b.scale_o, (0, s, d * (D // dp)), (LAYERS, 1, D // dp))
    grad_norm = jnp.sqrt(b.norm_o[0, 0])
    return f[0].h_out, b.g_out, grad_norm, (
        triple_grad, out_g, b.exp_g.astype(F32), jnp.swapaxes(b.shr_g, 1, 2).astype(F32), own_scale
    )


def local(dp, *args):
    (residual, cotangent, segments) = args[:3]
    (
        triple_weight, triple_moment, triple_square, triple_shadow,
        output_weight, output_moment, output_square, output_shadow,
        expand_weight, expand_moment, expand_square, expand_shadow,
        shrink_weight, shrink_moment, shrink_square, shrink_shadow,
        scales_weight, scales_moment, scales_square, scales_shadow,
    ) = args[3:]
    moves = Moves(dp)
    t = residual.shape[0]
    d, s = lax.axis_index("dp"), lax.axis_index("seq")
    tables, bias = tables_here(segments, t, moves.x, moves.c)

    if dp == 2 * ZS:
        stream, g, grad_norm, grads = layers_wide(
            dp, moves, residual, cotangent, scales_weight, tables, bias,
            triple_weight, output_weight, expand_weight, shrink_weight,
        )
    else:
        stream, g, grad_norm, grads = layers_narrow(
            dp, moves, residual, cotangent, scales_weight, tables, bias,
            triple_weight, output_weight, expand_weight, shrink_weight,
        )
    triple_grad, output_grad, expand_grad, shrink_grad, own_scale = grads
    limit = CLIP_RATIO * math.sqrt(float(LAYERS * (4 * D * D + 2 * D * FF + 4 * D)))
    factor = limit / (grad_norm + 1e-06)

    results = [stream, g, grad_norm]
    for weight, moment, square, shadow, grad, rate in (
        (triple_weight, triple_moment, triple_square, triple_shadow, triple_grad, RATE_FACTOR / math.sqrt(D)),
        (output_weight, output_moment, output_square, output_shadow, output_grad, RATE_FACTOR / math.sqrt(D // 16)),
        (expand_weight, expand_moment, expand_square, expand_shadow, expand_grad, RATE_FACTOR / math.sqrt(D)),
        (shrink_weight, shrink_moment, shrink_square, shrink_shadow, shrink_grad, RATE_FACTOR / math.sqrt(FF)),
        (scales_weight, scales_moment, scales_square, scales_shadow, own_scale, SCALES_RATE),
    ):
        results.extend(adam_step(weight, moment, square, shadow, grad * factor, rate))
    return tuple(results)


def solution(mesh):
    token = P(("dp", "seq"), None)
    weight = P(None, "dp", "seq")
    scale = P(None, "seq", "dp")
    return jax.shard_map(
        functools.partial(local, mesh.shape["dp"]),
        mesh=mesh,
        in_specs=(token, token, P("dp"), *([weight] * 16), *([scale] * 4)),
        out_specs=(token, token, P(), *([weight] * 16), *([scale] * 4)),
        check_vma=False,
    )
```

```python
import functools
import math
from typing import Any, NamedTuple

import jax
import jax.numpy as jnp
from jax import lax
from jax.experimental import pallas as pl
from jax.experimental.pallas import tpu as pltpu
from jax.sharding import PartitionSpec as P

D = 768
FF = 3072
HD = 64
LAYERS = 2
STEP = 2
SEQ = 4

EPSILON = 1e-05
ROTARY_BASE = 10000.0
BETA_ONE = 0.9
BETA_TWO = 0.999
ADAM_EPSILON = 1e-08
DECAY_RATE = 0.01
SHADOW_RATE = 0.99
CLIP_RATIO = 0.5
RATE_FACTOR = 1.5
SCALES_RATE = 0.6
MASKED = -1000000000.0

HALF = D // 2
TRI = 3 * HALF
HID = FF // 2
BF = jnp.bfloat16
F32 = jnp.float32
MESH = pl.DeviceIdType.MESH
VMEM_BYTES = 60 << 20


def adam_step(weight, moment, square, shadow, gradient, step_rate):
    shadow_decay = min(SHADOW_RATE, (1.0 + STEP) / (10.0 + STEP))
    momentum = BETA_ONE * moment + (1.0 - BETA_ONE) * gradient
    variance = BETA_TWO * square + (1.0 - BETA_TWO) * gradient * gradient
    corrected = (
        momentum
        / (1.0 - BETA_ONE**STEP)
        / (jnp.sqrt(variance / (1.0 - BETA_TWO**STEP)) + ADAM_EPSILON)
    )
    updated = weight - step_rate * (corrected + DECAY_RATE * weight)
    average = shadow_decay * shadow + (1.0 - shadow_decay) * updated
    return (updated, momentum, variance, average)


def nn(a, b):
    return lax.dot_general(a, b, (((1,), (0,)), ((), ())), preferred_element_type=F32)


def nt(a, b):
    return lax.dot_general(a, b, (((1,), (1,)), ((), ())), preferred_element_type=F32)


def tn(a, b):
    return lax.dot_general(a, b, (((0,), (0,)), ((), ())), preferred_element_type=F32)


def place():
    s = lax.axis_index("seq")
    x = lax.div(s, 2)
    c = lax.rem(s, 2)
    return lax.axis_index("dp"), x, c, lax.rem(s + 2, SEQ), s + 1 - 2 * c


def greet(d, peer, sib):
    barrier = pltpu.get_barrier_semaphore()
    for other in (peer, sib):
        pl.semaphore_signal(barrier, inc=1, device_id=(d, other), device_id_type=MESH)
    pl.semaphore_wait(barrier, 2)


def rows_of(c, n):
    return pl.ds(pl.multiple_of(c * n, n), n)


class Copies:
    def __init__(self, lsem, ssem, rsem, d):
        self.lsem, self.ssem, self.rsem, self.d = lsem, ssem, rsem, d
        self.n_local = 0
        self.n_remote = 0

    def local(self, src, dst):
        copy = pltpu.make_async_copy(src, dst, self.lsem.at[self.n_local])
        self.n_local += 1
        copy.start()
        return copy

    def push(self, src, dst, to):
        copy = pltpu.make_async_remote_copy(
            src_ref=src,
            dst_ref=dst,
            send_sem=self.ssem.at[self.n_remote],
            recv_sem=self.rsem.at[self.n_remote],
            device_id=(self.d, to),
            device_id_type=MESH,
        )
        self.n_remote += 1
        copy.start()
        return copy


def norm_stats(values):
    center = values - jnp.mean(values, axis=-1, keepdims=True)
    spread = jnp.mean(center * center, axis=-1, keepdims=True)
    scale = lax.rsqrt(spread + EPSILON)
    return center * scale, scale


def norm_back(values, gain, dy):
    xhat, scale = norm_stats(values)
    u = gain * dy
    du = u - jnp.mean(u, axis=-1, keepdims=True)
    back = scale * (du - xhat * jnp.mean(u * xhat, axis=-1, keepdims=True))
    rows = jnp.concatenate(
        [jnp.sum(xhat * dy, axis=0, keepdims=True), jnp.sum(dy, axis=0, keepdims=True)], axis=0
    )
    return back, rows


def turn(chunk, cosine, sine):
    lane = lax.broadcasted_iota(jnp.int32, chunk.shape, 1)
    swapped = jnp.where(
        lax.rem(lane, HD) < HD // 2, pltpu.roll(chunk, 128 - HD // 2, 1), pltpu.roll(chunk, HD // 2, 1)
    )
    return chunk * cosine + swapped * sine


def half_of(pair, which):
    lane = lax.broadcasted_iota(jnp.int32, pair.shape, 1)
    keep = (lane < HD) if which == 0 else (lane >= HD)
    return jnp.where(keep, pair, jnp.zeros_like(pair))


def attend_fwd_kernel(
    h, wa, sc, cs, bias, mid, na_o, q_o, k_o, v_o, ctx_o, lse_o,
    wt, wo, na, q, k, v, ctxt, ctx, lse, psend, precv, lsem, ssem, rsem,
):
    d, x, c, peer, sib = place()
    y = 1 - x
    rows = h.shape[0]
    copies = Copies(lsem, ssem, rsem, d)
    greet(d, peer, sib)
    wt_own, wo_own = wt.at[rows_of(c, HALF), :], wo.at[:, rows_of(c, HALF)]
    tri_part, out_part = wa.at[:, pl.ds(0, TRI)], wa.at[:, pl.ds(TRI, HALF)]
    tri_sent = copies.push(tri_part, wt_own, sib)
    tri_local = copies.local(tri_part, wt_own)
    out_sent = copies.push(out_part, wo_own, sib)
    out_local = copies.local(out_part, wo_own)
    xhat, _ = norm_stats(h[...])
    na[x] = (xhat * sc[0:1, :] + sc[1:2, :]).astype(BF)
    na_sent = copies.push(na.at[x], na.at[x], peer)
    tri_local.wait()
    tri_sent.wait()

    def project(block):
        cosine, sine = cs[block, :, 0:128], cs[block, :, 128:256]
        for j in range(9):
            part = nn(na[block], wt[:, 128 * j : 128 * j + 128])
            lanes = pl.ds(128 * (j % 3), 128)
            if j < 3:
                q[block, :, lanes] = (turn(part, cosine, sine) * HD**-0.5).astype(BF)
            elif j < 6:
                k[block, rows_of(c, rows), lanes] = turn(part, cosine, sine).astype(BF)
            else:
                v[block, rows_of(c, rows), lanes] = part.astype(BF)

    def share(block):
        mine = (block, rows_of(c, rows))
        return [copies.push(k.at[mine], k.at[mine], sib), copies.push(v.at[mine], v.at[mine], sib)]

    project(x)
    shared = share(x)
    na_sent.wait()
    project(y)
    shared += share(y)
    out_local.wait()
    out_sent.wait()
    for copy in shared:
        copy.wait()

    def attend(block):
        other = 1 - block

        def pair_step(p, carry):
            lanes = pl.ds(pl.multiple_of(p * 128, 128), 128)
            q_pair = q[block, :, lanes]
            k_same, k_cross = k[block, :, lanes], k[other, :, lanes]
            v_same, v_cross = v[block, :, lanes], v[other, :, lanes]
            for which in range(2):
                q_head = half_of(q_pair, which)
                s_same = nt(k_same, q_head)
                s_cross = nt(k_cross, q_head) + bias[0]
                top = jnp.maximum(
                    jnp.max(s_same, axis=0, keepdims=True), jnp.max(s_cross, axis=0, keepdims=True)
                )
                e_same = jnp.exp(s_same - top)
                e_cross = jnp.exp(s_cross - top)
                total = jnp.sum(e_same, axis=0, keepdims=True) + jnp.sum(
                    e_cross, axis=0, keepdims=True
                )
                mixed = tn(v_same, e_same.astype(BF)) + tn(v_cross, e_cross.astype(BF))
                head = pl.ds(pl.multiple_of(p * 128 + which * HD, HD), HD)
                ctxt[head, :] = mixed[which * HD : which * HD + HD, :] / total
                lse[block, pl.ds(2 * p + which, 1), :] = top + jnp.log(total)
            return carry

        lax.fori_loop(0, HALF // 128, pair_step, 0)
        ctx[block] = ctxt[...].T.astype(BF)
        return nn(ctx[block], wo[...])

    psend[...] = attend(y).astype(BF)
    part_sent = copies.push(psend, precv, peer)
    mid[...] = h[...] + attend(x)
    saves = [
        copies.local(a, b)
        for a, b in ((na, na_o), (q, q_o), (k, k_o), (v, v_o), (ctx, ctx_o), (lse, lse_o))
    ]
    part_sent.wait()
    mid[...] = mid[...] + precv[...].astype(F32)
    for copy in saves:
        copy.wait()


def hbm():
    return pl.BlockSpec(memory_space=pl.ANY)


def vmem():
    return pl.BlockSpec(memory_space=pltpu.VMEM)


def call(kernel, name, number, ins, outs, out_shape, scratch, n_local, n_remote, flops, args):
    return pl.pallas_call(
        kernel,
        name=name,
        out_shape=out_shape,
        in_specs=ins,
        out_specs=outs,
        scratch_shapes=[
            *scratch,
            pltpu.SemaphoreType.DMA((n_local,)),
            pltpu.SemaphoreType.DMA((n_remote,)),
            pltpu.SemaphoreType.DMA((n_remote,)),
        ],
        cost_estimate=pl.CostEstimate(flops=flops, bytes_accessed=16 << 20, transcendentals=0),
        compiler_params=pltpu.CompilerParams(
            collective_id=number, has_side_effects=True, vmem_limit_bytes=VMEM_BYTES
        ),
    )(*args)


def sds(shape, dtype):
    return jax.ShapeDtypeStruct(shape, dtype)


def attend_fwd(h, wa, scales, tables, bias):
    t = h.shape[0]
    return call(
        attend_fwd_kernel, "attend_fwd", 0,
        [vmem(), hbm(), vmem(), vmem(), pl.BlockSpec(memory_space=pltpu.SMEM)],
        [vmem()] + [hbm()] * 6,
        [
            sds((t, D), F32), sds((2, t, D), BF), sds((2, t, HALF), BF), sds((2, 2 * t, HALF), BF),
            sds((2, 2 * t, HALF), BF), sds((2, t, HALF), BF), sds((2, 8, t), F32),
        ],
        [
            pltpu.VMEM((D, TRI), BF), pltpu.VMEM((HALF, D), BF), pltpu.VMEM((2, t, D), BF),
            pltpu.VMEM((2, t, HALF), BF), pltpu.VMEM((2, 2 * t, HALF), BF),
            pltpu.VMEM((2, 2 * t, HALF), BF), pltpu.VMEM((HALF, t), F32),
            pltpu.VMEM((2, t, HALF), BF), pltpu.VMEM((2, 8, t), F32),
            pltpu.VMEM((t, D), BF), pltpu.VMEM((t, D), BF),
        ],
        8, 8, 6 << 30, (h, wa, scales, tables, bias),
    )


def gelu_parts(hidden):
    phi_cap = 0.5 * (1.0 + lax.erf(hidden * math.sqrt(0.5)))
    density = jnp.exp(-0.5 * hidden * hidden) * (1.0 / math.sqrt(2.0 * math.pi))
    return hidden * phi_cap, phi_cap + hidden * density


def feed_fwd_kernel(
    mid, wf, sc, h_next, nb_o, act_o, slope_o,
    we, ws, nb, act, slope, psend, precv, lsem, ssem, rsem,
):
    d, x, c, peer, sib = place()
    y = 1 - x
    copies = Copies(lsem, ssem, rsem, d)
    greet(d, peer, sib)
    xhat, _ = norm_stats(mid[...])
    nb[x] = (xhat * sc[2:3, :] + sc[3:4, :]).astype(BF)
    nb_sent = copies.push(nb.at[x], nb.at[x], peer)
    we_own, ws_own = we.at[:, rows_of(c, D)], ws.at[rows_of(c, D), :]
    exp_part, shr_part = wf.at[:, pl.ds(0, D)], wf.at[:, pl.ds(D, D)]
    weights = [
        copies.local(exp_part, we_own),
        copies.push(exp_part, we_own, sib),
        copies.local(shr_part, ws_own),
        copies.push(shr_part, ws_own, sib),
    ]
    for copy in weights:
        copy.wait()

    def feed(block):
        def step(i, carry):
            lanes = pl.ds(pl.multiple_of(i * 256, 256), 256)
            value, rate = gelu_parts(nn(nb[block], we[:, lanes]))
            act[block, :, lanes] = value.astype(BF)
            slope[block, :, lanes] = rate.astype(BF)
            return carry

        lax.fori_loop(0, HID // 256, step, 0)
        return nn(act[block], ws[...])

    h_next[...] = mid[...] + feed(x)
    nb_sent.wait()
    psend[...] = feed(y).astype(BF)
    part_sent = copies.push(psend, precv, peer)
    saves = [copies.local(a, b) for a, b in ((nb, nb_o), (act, act_o), (slope, slope_o))]
    part_sent.wait()
    h_next[...] = h_next[...] + precv[...].astype(F32)
    for copy in saves:
        copy.wait()


def feed_fwd(mid, wf, scales):
    t = mid.shape[0]
    return call(
        feed_fwd_kernel, "feed_fwd", 1,
        [vmem(), hbm(), vmem()],
        [vmem()] + [hbm()] * 3,
        [sds((t, D), F32), sds((2, t, D), BF), sds((2, t, HID), BF), sds((2, t, HID), BF)],
        [
            pltpu.VMEM((D, HID), BF), pltpu.VMEM((HID, D), BF), pltpu.VMEM((2, t, D), BF),
            pltpu.VMEM((2, t, HID), BF), pltpu.VMEM((2, t, HID), BF),
            pltpu.VMEM((t, D), BF), pltpu.VMEM((t, D), BF),
        ],
        5, 4, 5 << 30, (mid, wf, scales),
    )


def feed_bwd_kernel(
    g, mid, wf, sc, nb_h, act_h, slope_h, mid_grad, wg_o, rows_o,
    we, ws, nb, act, slope, gl, hg, part, psend, precv, gown, gsend, grecv, lsem, ssem, rsem,
):
    d, x, c, peer, sib = place()
    y = 1 - x
    t = g.shape[0]
    copies = Copies(lsem, ssem, rsem, d)
    greet(d, peer, sib)
    gl[x] = g[...].astype(BF)
    g_sent = copies.push(gl.at[x], gl.at[x], peer)
    we_own, ws_own = we.at[:, rows_of(c, D)], ws.at[rows_of(c, D), :]
    exp_part, shr_part = wf.at[:, pl.ds(0, D)], wf.at[:, pl.ds(D, D)]
    weights = [
        copies.local(shr_part, ws_own),
        copies.push(shr_part, ws_own, sib),
        copies.local(exp_part, we_own),
        copies.push(exp_part, we_own, sib),
        copies.local(slope_h, slope),
        copies.local(act_h, act),
        copies.local(nb_h, nb),
    ]
    for copy in weights:
        copy.wait()

    def back(block):
        def step(i, carry):
            lanes = pl.ds(pl.multiple_of(i * 256, 256), 256)
            pulled = nt(gl[block], ws[lanes, :])
            hg[block, :, lanes] = (pulled * slope[block, :, lanes].astype(F32)).astype(BF)
            return carry

        lax.fori_loop(0, HID // 256, step, 0)
        return nt(hg[block], we[...])

    part[...] = back(x)
    g_sent.wait()
    psend[...] = back(y).astype(BF)
    part_sent = copies.push(psend, precv, peer)

    gl_all = gl[...].reshape(2 * t, D)
    nb_all = nb[...].reshape(2 * t, D)

    def grads(which, store):
        def step(i, carry):
            at = pl.ds(pl.multiple_of(i * 256, 256), 256)
            off = pl.ds(pl.multiple_of(which * D + i * 256, 256), 256)
            hg_part = hg[:, :, off].reshape(2 * t, 256)
            act_part = act[:, :, off].reshape(2 * t, 256)
            store(0, at, tn(nb_all, hg_part))
            store(1, at, tn(act_part, gl_all))
            return carry

        lax.fori_loop(0, D // 256, step, 0)

    def to_send(kind, at, value):
        if kind == 0:
            gsend[:, at] = value.astype(BF)
        else:
            gsend[at, pl.ds(D, D)] = value.astype(BF)

    def to_keep(kind, at, value):
        if kind == 0:
            gown[:, at] = value
        else:
            gown[at, pl.ds(D, D)] = value

    grads(1 - c, to_send)
    grad_sent = copies.push(gsend, grecv, sib)
    grads(c, to_keep)
    part_sent.wait()
    dy = part[...] + precv[...].astype(F32)
    back_mid, rows = norm_back(mid[...], sc[2:3, :], dy)
    mid_grad[...] = g[...] + back_mid
    rows_o[...] = rows
    grad_sent.wait()
    gsend[...] = (gown[...] + grecv[...].astype(F32)).astype(BF)
    copies.local(gsend, wg_o).wait()


def feed_bwd(g, mid, wf, scales, nb, act, slope):
    t = g.shape[0]
    return call(
        feed_bwd_kernel, "feed_bwd", 2,
        [vmem(), vmem(), hbm(), vmem(), hbm(), hbm(), hbm()],
        [vmem(), hbm(), vmem()],
        [sds((t, D), F32), sds((D, 2 * D), BF), sds((2, D), F32)],
        [
            pltpu.VMEM((D, HID), BF), pltpu.VMEM((HID, D), BF), pltpu.VMEM((2, t, D), BF),
            pltpu.VMEM((2, t, HID), BF), pltpu.VMEM((2, t, HID), BF), pltpu.VMEM((2, t, D), BF),
            pltpu.VMEM((2, t, HID), BF), pltpu.VMEM((t, D), F32), pltpu.VMEM((t, D), BF),
            pltpu.VMEM((t, D), BF), pltpu.VMEM((D, 2 * D), F32), pltpu.VMEM((D, 2 * D), BF),
            pltpu.VMEM((D, 2 * D), BF),
        ],
        6, 5, 10 << 30, (g, mid, wf, scales, nb, act, slope),
    )


def attend_bwd_kernel(
    mg, h, wa, sc, cs, bias, na, q, k, v, ctx, lse, g_prev, wg_o, rows_o,
    wt, wo, ml, cg, delta, dqt, dk, dv, kvsend, kvrecv, pg, part, psend, precv,
    gown, gsend, grecv, lsem, ssem, rsem,
):
    d, x, c, peer, sib = place()
    y = 1 - x
    t = mg.shape[0]
    copies = Copies(lsem, ssem, rsem, d)
    greet(d, peer, sib)
    ml[x] = mg[...].astype(BF)
    ml_sent = copies.push(ml.at[x], ml.at[x], peer)
    wt_own, wo_own = wt.at[rows_of(c, HALF), :], wo.at[:, rows_of(c, HALF)]
    tri_part, out_part = wa.at[:, pl.ds(0, TRI)], wa.at[:, pl.ds(TRI, HALF)]
    out_moves = [copies.local(out_part, wo_own), copies.push(out_part, wo_own, sib)]
    tri_moves = [copies.local(tri_part, wt_own), copies.push(tri_part, wt_own, sib)]
    dk[...] = jnp.zeros_like(dk)
    dv[...] = jnp.zeros_like(dv)
    for copy in out_moves:
        copy.wait()

    def attend(block):
        other = 1 - block
        pulled = nt(ml[block], wo[...])
        cg[block] = pulled.astype(BF)
        weighed = (cg[block].astype(F32) * ctx[block].astype(F32)).T
        for head in range(HALF // HD):
            delta[head : head + 1, :] = jnp.sum(
                weighed[head * HD : head * HD + HD, :], axis=0, keepdims=True
            )

        def pair_step(p, carry):
            lanes = pl.ds(pl.multiple_of(p * 128, 128), 128)
            q_pair, cg_pair = q[block, :, lanes], cg[block, :, lanes]
            for which in range(2):
                q_head, cg_head = half_of(q_pair, which), half_of(cg_pair, which)
                row = pl.ds(2 * p + which, 1)
                total, dots = lse[block, row, :], delta[row, :]
                turned = None
                for side in (block, other):
                    k_pair, v_pair = k[side, :, lanes], v[side, :, lanes]
                    scores = nt(k_pair, q_head)
                    if side is other:
                        scores = scores + bias[0]
                    probs = jnp.exp(scores - total)
                    score_grad = (probs * (nt(v_pair, cg_head) - dots)).astype(BF)
                    dv[side, :, lanes] += nn(probs.astype(BF), cg_head)
                    dk[side, :, lanes] += nn(score_grad, q_head)
                    piece = tn(k_pair, score_grad)
                    turned = piece if turned is None else turned + piece
                head = pl.ds(pl.multiple_of(p * 128 + which * HD, HD), HD)
                dqt[block, head, :] = turned[which * HD : which * HD + HD, :] * HD**-0.5
            return carry

        lax.fori_loop(0, HALF // 128, pair_step, 0)

    attend(x)
    ml_sent.wait()
    attend(y)
    theirs, mine = rows_of(1 - c, t), rows_of(c, t)
    for side in range(2):
        kvsend[side, :, pl.ds(0, HALF)] = dk[side, theirs, :].astype(BF)
        kvsend[side, :, pl.ds(HALF, HALF)] = dv[side, theirs, :].astype(BF)
    kv_sent = copies.push(kvsend, kvrecv, sib)

    def unturn(block, j, value):
        cosine, sine = cs[block, :, 0:128], cs[block, :, 128:256]
        rounded = value.astype(BF).astype(F32)
        pg[block, :, pl.ds(128 * j, 128)] = turn(rounded, cosine, -sine).astype(BF)

    for side in range(2):
        for j in range(3):
            unturn(side, j, dqt[side, 128 * j : 128 * j + 128, :].T)
    kv_sent.wait()
    for side in range(2):
        for j in range(3):
            at = pl.ds(128 * j, 128)
            unturn(side, 3 + j, dk[side, mine, at] + kvrecv[side, :, at].astype(F32))
            pg[side, :, pl.ds(D + 128 * j, 128)] = (
                dv[side, mine, at] + kvrecv[side, :, pl.ds(HALF + 128 * j, 128)].astype(F32)
            ).astype(BF)
    for copy in tri_moves:
        copy.wait()
    psend[...] = nt(pg[y], wt[...]).astype(BF)
    part_sent = copies.push(psend, precv, peer)
    part[...] = nt(pg[x], wt[...])

    ml_all = ml[...].reshape(2 * t, D)
    na_all = na[...].reshape(2 * t, D)
    ctx_all = ctx[...].reshape(2 * t, HALF)

    def grads(which, store):
        def step(i, carry):
            off = pl.ds(pl.multiple_of(which * HALF + i * 128, 128), 128)
            at = pl.ds(pl.multiple_of(i * 128, 128), 128)
            store(0, at, tn(na[:, :, off].reshape(2 * t, 128), pg[...].reshape(2 * t, TRI)))
            store(1, at, tn(ctx_all, ml[:, :, off].reshape(2 * t, 128)))
            return carry

        lax.fori_loop(0, HALF // 128, step, 0)

    def to_send(kind, at, value):
        if kind == 0:
            gsend[at, pl.ds(0, TRI)] = value.astype(BF)
        else:
            gsend[:, pl.ds(pl.multiple_of(TRI + at.start, 128), 128)] = value.astype(BF)

    def to_keep(kind, at, value):
        if kind == 0:
            gown[at, pl.ds(0, TRI)] = value
        else:
            gown[:, pl.ds(pl.multiple_of(TRI + at.start, 128), 128)] = value

    grads(1 - c, to_send)
    grad_sent = copies.push(gsend, grecv, sib)
    grads(c, to_keep)
    part_sent.wait()
    dy = part[...] + precv[...].astype(F32)
    back, rows = norm_back(h[...], sc[0:1, :], dy)
    g_prev[...] = mg[...] + back
    rows_o[...] = rows
    grad_sent.wait()
    gsend[...] = (gown[...] + grecv[...].astype(F32)).astype(BF)
    copies.local(gsend, wg_o).wait()


def attend_bwd(mg, h, wa, scales, tables, bias, saved):
    t = mg.shape[0]
    return call(
        attend_bwd_kernel, "attend_bwd", 3,
        [vmem(), vmem(), hbm(), vmem(), vmem(), pl.BlockSpec(memory_space=pltpu.SMEM)] + [vmem()] * 6,
        [vmem(), hbm(), vmem()],
        [sds((t, D), F32), sds((HALF, 2 * D), BF), sds((2, D), F32)],
        [
            pltpu.VMEM((D, TRI), BF), pltpu.VMEM((HALF, D), BF), pltpu.VMEM((2, t, D), BF),
            pltpu.VMEM((2, t, HALF), BF), pltpu.VMEM((8, t), F32), pltpu.VMEM((2, HALF, t), F32),
            pltpu.VMEM((2, 2 * t, HALF), F32), pltpu.VMEM((2, 2 * t, HALF), F32),
            pltpu.VMEM((2, t, D), BF), pltpu.VMEM((2, t, D), BF), pltpu.VMEM((2, t, TRI), BF),
            pltpu.VMEM((t, D), F32), pltpu.VMEM((t, D), BF), pltpu.VMEM((t, D), BF),
            pltpu.VMEM((HALF, 2 * D), F32), pltpu.VMEM((HALF, 2 * D), BF),
            pltpu.VMEM((HALF, 2 * D), BF),
        ],
        3, 6, 10 << 30, (mg, h, wa, scales, tables, bias, *saved),
    )


TRIPLE, OUTPUT, EXPAND, SHRINK = range(4)
KINDS = (TRIPLE, OUTPUT, EXPAND, SHRINK)
ZS = 4


class Spot:
    def __init__(self):
        s = lax.axis_index("seq")
        self.s = s
        self.x, self.c = lax.div(s, 2), lax.rem(s, 2)
        self.d = lax.axis_index("dp")
        self.z, self.y = lax.div(self.d, 2), lax.rem(self.d, 2)
        self.upper, self.odd = lax.div(self.z, 2), lax.rem(self.z, 2)
        self.sib, self.peer = s + 1 - 2 * self.c, lax.rem(s + 2, SEQ)
        self.across = self.d + 1 - 2 * self.y
        self.zs = ZS

    def count(self, kind):
        return ZS if kind == EXPAND else ZS // 2

    def origin(self, kind, j):
        if kind == TRIPLE:
            return 2 * self.c + j
        if kind == OUTPUT:
            return 2 * self.x + j
        return j if kind == EXPAND else 2 * j + self.x

    def own_slot(self, kind):
        return {TRIPLE: self.odd, OUTPUT: self.odd, EXPAND: self.z, SHRINK: self.upper}[kind]

    def if_owner(self, kind, act):
        if kind == EXPAND:
            act()
        elif kind == TRIPLE:
            pl.when(self.c == self.upper)(act)
        elif kind == OUTPUT:
            pl.when(self.x == self.upper)(act)
        else:
            pl.when(self.x == self.odd)(act)

    def naturals(self, kind):
        x, c = self.x, self.c
        if kind == TRIPLE:
            return ((0, 2 * x), (1, 2 * x + 1), (2, 2 * (1 - x)), (3, 2 * (1 - x) + 1))
        if kind == EXPAND:
            return ((0, 2 * c + x),)
        return ((0, 2 * c), (1, 2 * c + 1))

    def targets(self, kind):
        x, c = self.x, self.c
        if kind == TRIPLE:
            return ((c, 0, 2 * x + self.upper), (2 + c, 1, 2 * (1 - x) + self.upper))
        if kind == OUTPUT:
            return ((c, 0, 2 * self.upper + x),)
        if kind == EXPAND:
            return ((0, 0, 2 * c + x),)
        return ((c, 0, 2 * self.odd + x),)


class Saved(NamedTuple):
    na: Any
    q: Any
    k: Any
    k_t: Any
    v: Any
    ctx: Any
    ctx_t: Any
    lse: Any
    nb: Any
    act: Any
    slope: Any
    wt: Any
    wo: Any
    we: Any
    ws: Any


class ForwardIn(NamedTuple):
    h0: Any
    g0: Any
    sc_w: Any
    cs: Any
    bias: Any
    tri_w: Any
    out_w: Any
    exp_w: Any
    shr_w: Any


class ForwardHead(NamedTuple):
    h_out: Any
    h_mid: Any
    mid_o0: Any
    mid_o1: Any
    sc_o: Any
    gl_o: Any


class ForwardScratch(NamedTuple):
    p_whole: Any
    p_half: Any
    p_out: Any
    p_exp: Any
    p_shr: Any
    gl: Any
    wt: Any
    wo: Any
    we: Any
    ws: Any
    hb: Any
    ob: Any
    scl: Any
    sc: Any
    na: Any
    q: Any
    k: Any
    v: Any
    ctxt: Any
    ctx: Any
    ctx_t: Any
    lse: Any
    nb: Any
    na_t: Any
    nb_t: Any
    k_t: Any
    v_t: Any
    act: Any
    slope: Any
    psend: Any
    precv: Any
    hs: Any
    mid: Any
    ssem: Any
    rsem: Any
    zero_ssem: Any
    zero_rsem: Any
    sc_ssem: Any
    sc_rsem: Any
    xs: Any
    xr: Any
    lsem: Any


class Refs:
    def __init__(self, *groups):
        for group in groups:
            for name, ref in zip(group._fields, group):
                setattr(self, name, ref)


def split(refs, *kinds):
    out, at = [], 0
    for kind in kinds:
        size = len(kind._fields)
        out.append(kind(*refs[at : at + size]))
        at += size
    return out


class Weights(Spot):
    def __init__(self, n, rows):
        super().__init__()
        self.n = n
        self.rows = rows
        self.source = {
            TRIPLE: (n.p_whole, n.p_half), OUTPUT: (n.p_out,), EXPAND: (n.p_exp,), SHRINK: (n.p_shr,)
        }

    def view(self, kind, layer, y, z, c):
        n, r = self.n, self.rows
        if kind == EXPAND:
            return n.we.at[layer, rows_of(2 * z + y, r), rows_of(c, D)]
        at = 2 * lax.rem(z, 2) + y
        if kind == TRIPLE:
            return n.wt.at[layer, pl.ds(pl.multiple_of(HALF * c + r * at, r), r), :]
        if kind == OUTPUT:
            return n.wo.at[layer, rows_of(at, r), rows_of(c, HALF)]
        return n.ws.at[layer, rows_of(c, HALF), rows_of(2 * lax.div(z, 2) + y, 4 * r)]

    def piece(self, kind, layer, number, to):
        n, r = self.n, self.rows
        x, c = lax.div(to, 2), lax.rem(to, 2)
        if kind == TRIPLE:
            start = pl.ds(pl.multiple_of(HALF * c + r * (2 * self.odd + self.y), r), r)
            return (n.wt.at[layer, start, rows_of(x + self.core_of(number), HALF)], n.hb.at[layer, self.core_of(number)])
        if kind == OUTPUT:
            return n.ob.at[layer, number]
        if kind == EXPAND:
            return self.view(kind, layer, self.y, self.z, c)
        rows = pl.ds(pl.multiple_of(HALF * c + 192 * number, 192), 192)
        return n.ws.at[layer, rows, rows_of(2 * self.upper + self.y, 4 * r)]

    @staticmethod
    def core_of(number):
        return lax.rem(number, 2)

    def landing(self, kind, layer, number, part, to):
        spot = self.piece(kind, layer, number, to)
        return spot[part] if kind == TRIPLE else spot

    def zero_copy(self, kind, layer, number, part, to):
        return pltpu.make_async_remote_copy(
            src_ref=self.source[kind][part].at[layer],
            dst_ref=self.landing(kind, layer, number, part, to),
            send_sem=self.n.zero_ssem.at[layer, kind, part],
            recv_sem=self.n.zero_rsem.at[layer, kind, number],
            device_id=(self.d, to),
            device_id_type=MESH,
        )

    def zero_here(self, kind, layer, number, part, to):
        return pltpu.make_async_copy(
            self.source[kind][part].at[layer], self.landing(kind, layer, number, part, to),
            self.n.zero_rsem.at[layer, kind, number],
        )

    def zero(self, kind, layer):
        for number, part, to in self.targets(kind):
            away = to != self.s
            place = (kind, layer, number, part, to)
            pl.when(away)(lambda place=place: self.zero_copy(*place).start())
            pl.when(jnp.logical_not(away))(lambda place=place: self.zero_here(*place).start())

    def remote(self, ref, kind, layer, stage, sent, slot, to):
        return pltpu.make_async_remote_copy(
            src_ref=ref,
            dst_ref=ref,
            send_sem=self.n.ssem.at[layer, kind, stage, sent],
            recv_sem=self.n.rsem.at[layer, kind, stage, slot],
            device_id=to,
            device_id_type=MESH,
        )

    def spread(self, kind, layer):
        def act():
            for number, _ in self.naturals(kind):
                part = 1 if kind == TRIPLE and number >= 2 else 0
                ref = self.landing(kind, layer, number, part, self.s)
                pltpu.make_async_remote_copy(
                    src_ref=ref, dst_ref=ref, send_sem=self.n.zero_ssem.at[layer, kind, part],
                    recv_sem=self.n.zero_rsem.at[layer, kind, number], device_id=(self.d, self.peer),
                    device_id_type=MESH,
                ).wait_recv()
            n, r = self.n, self.rows
            if kind == TRIPLE:
                start = HALF * self.c + r * (2 * self.odd + self.y)
                join(n.hb[layer, 0], n.hb[layer, 1], n.wt, layer, start, 2 * (1 - self.x) * HALF, r)
            elif kind == OUTPUT:
                join(n.ob[layer, 0], n.ob[layer, 1], n.wo, layer, r * (2 * self.odd + self.y), HALF * self.c, r)
            ref = self.view(kind, layer, self.y, self.z, self.c)
            slot = self.own_slot(kind)
            for k in range(1, ZS):
                other = lax.rem(self.z + k, ZS)
                self.remote(ref, kind, layer, 0, k, slot, (2 * other + self.y, self.s)).start()
            self.remote(ref, kind, layer, 1, slot, slot, (self.across, self.s)).start()

        self.if_owner(kind, act)

    def onward(self, kind, layer, j):
        z = self.origin(kind, j)

        @pl.when(z != self.z)
        def _():
            ref = self.view(kind, layer, self.y, z, self.c)
            self.remote(ref, kind, layer, 0, 0, j, (self.across, self.s)).wait_recv()
            self.remote(ref, kind, layer, 1, j, j, (self.across, self.s)).start()

    def onward_all(self, kind, layer):
        for j in range(self.count(kind)):
            self.onward(kind, layer, j)

    def arrive(self, kind, layer):
        for j in range(self.count(kind)):
            ref = self.view(kind, layer, 1 - self.y, self.origin(kind, j), self.c)
            self.remote(ref, kind, layer, 1, j, j, (self.across, self.s)).wait_recv()

    def finish(self, kind, layer):
        for number, part, to in self.targets(kind):
            place = (kind, layer, number, part, to)
            pl.when(to != self.s)(lambda place=place: self.zero_copy(*place).wait_send())

        def act():
            ref = self.view(kind, layer, self.y, self.z, self.c)
            for k in range(1, ZS):
                self.remote(ref, kind, layer, 0, k, 0, (self.across, self.s)).wait_send()

        self.if_owner(kind, act)
        for j in range(self.count(kind)):
            ref = self.view(kind, layer, self.y, self.origin(kind, j), self.c)
            self.remote(ref, kind, layer, 1, j, j, (self.across, self.s)).wait_send()


def join(first, second, into, layer, row, col, rows):
    half = rows // 2
    top, bottom = join_packed(first[rows:], second[rows:])
    all_rows = pl.ds(pl.multiple_of(row, half), rows)
    into[layer, all_rows, pl.ds(pl.multiple_of(col, 128), 128)] = first[:rows]
    middle = pl.ds(pl.multiple_of(col + 128, 128), 128)
    into[layer, pl.ds(pl.multiple_of(row, half), half), middle] = top
    into[layer, pl.ds(pl.multiple_of(row + half, half), half), middle] = bottom
    into[layer, all_rows, pl.ds(pl.multiple_of(col + 256, 128), 128)] = second[:rows]


def greet_all(w):
    barrier = pltpu.get_barrier_semaphore()

    def one(i, carry):
        z, s = lax.div(i, SEQ), lax.rem(i, SEQ)
        away = jnp.logical_or(z != w.z, s != w.s)

        @pl.when(away)
        def _():
            pl.semaphore_signal(barrier, inc=1, device_id=(2 * z + w.y, s), device_id_type=MESH)

        return carry

    lax.fori_loop(0, w.zs * SEQ, one, 0)
    pl.semaphore_signal(barrier, inc=1, device_id=(w.across, w.s), device_id_type=MESH)
    pl.semaphore_wait(barrier, w.zs * SEQ)


def left_half(shape):
    return lax.broadcasted_iota(jnp.int32, shape, 1) < HD


def join_packed(first, second):
    first, second = first.astype(F32), second.astype(F32)
    left = left_half(first.shape)
    top = jnp.where(left, first, second)
    bottom = pltpu.roll(jnp.where(left, second, first), HD, 1)
    return top.astype(BF), bottom.astype(BF)


def pack_wide(value):
    half = value.shape[0] // 2
    top, bottom = value[:half, 128:256], pltpu.roll(value[half:, 128:256], HD, 1)
    left = left_half(top.shape)
    first, second = jnp.where(left, top, bottom), jnp.where(left, bottom, top)
    return (
        jnp.concatenate([value[:, :128], first], axis=0),
        jnp.concatenate([value[:, 256:], second], axis=0),
    )


def gather_scales_start(w):
    n = w.n
    mine = n.scl.at[w.y, w.z, w.s]
    mine[...] = jnp.zeros_like(mine)
    wide = n.sc_w.shape[-1]
    for layer in range(LAYERS):
        mine[layer : layer + 1, 0:wide] = n.sc_w[layer].astype(BF).astype(F32)

    def one(i, carry):
        z, s = lax.div(i, SEQ), lax.rem(i, SEQ)

        @pl.when(jnp.logical_or(z != w.z, s != w.s))
        def _():
            pltpu.make_async_remote_copy(
                src_ref=mine, dst_ref=mine, send_sem=n.sc_ssem.at[i],
                recv_sem=n.sc_rsem.at[w.z * SEQ + w.s], device_id=(2 * z + w.y, s), device_id_type=MESH,
            ).start()

        return carry

    lax.fori_loop(0, w.zs * SEQ, one, 0)


def gather_scales_end(w):
    n = w.n

    def one(i, carry):
        z, s = lax.div(i, SEQ), lax.rem(i, SEQ)

        @pl.when(jnp.logical_or(z != w.z, s != w.s))
        def _():
            slot = n.scl.at[w.y, z, s]
            copy = pltpu.make_async_remote_copy(
                src_ref=slot, dst_ref=slot, send_sem=n.sc_ssem.at[i], recv_sem=n.sc_rsem.at[i],
                device_id=(2 * z + w.y, s), device_id_type=MESH,
            )
            copy.wait_recv()
            copy.wait_send()

        return carry

    lax.fori_loop(0, w.zs * SEQ, one, 0)
    count = w.zs * SEQ
    plane = n.scl.at[w.y]
    copy = pltpu.make_async_remote_copy(
        src_ref=plane, dst_ref=plane, send_sem=n.sc_ssem.at[count], recv_sem=n.sc_rsem.at[count],
        device_id=(w.across, w.s), device_id_type=MESH,
    )
    copy.start()
    copy.wait()
    wide = n.sc.shape[-1] // (2 * w.zs)
    for s in range(SEQ):
        both = [n.scl[d % 2, d // 2, s][:, :wide] for d in range(2 * w.zs)]
        rows = jnp.concatenate(both, axis=1)
        for layer in range(LAYERS):
            n.sc[layer, s : s + 1, :] = rows[layer : layer + 1, :]


def fwd_kernel(dp, *refs):
    ins, outs, saved0, saved1, scratch = split(refs, ForwardIn, ForwardHead, Saved, Saved, ForwardScratch)
    n = Refs(ins, outs, scratch)
    saved = (saved0, saved1)
    rows = n.exp_w.shape[1]
    t = n.h0.shape[0]
    w = Weights(n, rows)
    x, c, peer, sib = w.x, w.c, w.peer, w.sib
    y = 1 - x
    parts = (pl.ds(0, t // 2), pl.ds(t // 2, t // 2))
    copies = Copies(n.lsem, n.xs, n.xr, w.d)
    waits = []

    def save(src, dst):
        waits.append(copies.local(src, dst))

    half_rows = rows // 2

    def pack(low, into, layer, core):
        wide, rest = (low[:, :128], low[:, 128:]) if core == 0 else (low[:, 64:], low[:, :64])
        ends = [rest[:half_rows], rest[half_rows:]]
        into[layer, pl.ds(0, rows), :] = wide.astype(BF)
        into[layer, pl.ds(rows, half_rows), :] = jnp.concatenate(ends if core == 0 else ends[::-1], axis=1).astype(BF)

    def round_triple(layer):
        for core in range(2):

            @pl.when(c == core)
            def _():
                tri = n.tri_w[layer]
                n.p_whole[layer] = (tri[:, :HALF] if core == 0 else tri[:, 192:]).astype(BF)
                pack(tri[:, HALF:] if core == 0 else tri[:, :192], n.p_half, layer, core)

    def round_output(layer):
        for core in range(2):
            pl.when(c == core)(lambda: pack(n.out_w[layer], n.p_out, layer, core))

    round_triple(0)
    greet_all(w)
    w.zero(TRIPLE, 0)
    gather_scales_start(w)
    round_output(0)
    w.zero(OUTPUT, 0)
    n.p_exp[...] = n.exp_w[...].astype(BF)
    w.zero(EXPAND, 0)
    n.p_shr[...] = n.shr_w[...].astype(BF)
    w.zero(SHRINK, 0)
    round_triple(1)
    round_output(1)
    for kind in KINDS:
        w.zero(kind, 1)
    for layer in range(LAYERS):
        for kind in KINDS:
            w.spread(kind, layer)
    n.hs[0] = n.h0[...]
    xhat, _ = norm_stats(n.hs[0])
    gather_scales_end(w)

    def share_tri(layer):
        own = n.wt.at[layer, rows_of(c, HALF), :]
        return copies.push(own, own, sib)

    def share_out(layer):
        own = n.wo.at[layer, :, rows_of(c, HALF)]
        return copies.push(own, own, sib)

    def share_shr(layer):
        own = n.ws.at[layer, rows_of(c, HALF), :]
        return copies.push(own, own, sib)

    def share_exp(layer):
        own = n.we.at[layer, :, rows_of(c, D)]
        return copies.push(own, own, sib)

    for layer in range(LAYERS):
        last = layer == LAYERS - 1
        if layer:
            xhat, _ = norm_stats(n.hs[layer])
        n.na[layer, x] = (xhat * n.sc[layer, 0:1, :] + n.sc[layer, 1:2, :]).astype(BF)
        na_sent = copies.push(n.na.at[layer, x], n.na.at[layer, x], peer)
        if last:
            n.gl[x] = n.g0[...].astype(BF)
            gl_sent = copies.push(n.gl.at[x], n.gl.at[x], peer)
        if layer == 0:
            w.onward_all(TRIPLE, 0)
            w.onward_all(OUTPUT, 0)
            w.arrive(TRIPLE, 0)
            tri_sent = share_tri(0)
        tri_sent.wait()

        def project(block):
            cosine, sine = n.cs[block, :, 0:128], n.cs[block, :, 128:256]
            for j in range(9):
                part = nn(n.na[layer, block], n.wt[layer, :, 128 * j : 128 * j + 128])
                lanes = pl.ds(128 * (j % 3), 128)
                if j < 3:
                    n.q[layer, block, :, lanes] = (turn(part, cosine, sine) * HD**-0.5).astype(BF)
                elif j < 6:
                    n.k[layer, block, rows_of(c, t), lanes] = turn(part, cosine, sine).astype(BF)
                else:
                    n.v[layer, block, rows_of(c, t), lanes] = part.astype(BF)

        def share(block):
            at = (layer, block, rows_of(c, t))
            return [
                copies.push(n.k.at[at], n.k.at[at], sib),
                copies.push(n.v.at[at], n.v.at[at], sib),
            ]

        project(x)
        shared = share(x)
        na_sent.wait()
        project(y)
        shared += share(y)
        w.arrive(OUTPUT, layer)
        out_sent = share_out(layer)
        for copy in shared:
            copy.wait()
        for block in range(2):
            n.v_t[block] = n.v[layer, block].T
        save(n.q.at[layer], saved[layer].q)
        save(n.k.at[layer], saved[layer].k)
        save(n.v.at[layer], saved[layer].v)

        def attend(block, pump):
            other = 1 - block

            def pair_step(p, carry):
                pump(p)
                lanes = pl.ds(pl.multiple_of(p * 128, 128), 128)
                q_pair = n.q[layer, block, :, lanes]
                k_same, k_cross = n.k[layer, block, :, lanes], n.k[layer, other, :, lanes]
                for which in range(2):
                    q_head = half_of(q_pair, which)
                    s_same = nt(k_same, q_head)
                    s_cross = nt(k_cross, q_head) + n.bias[0]
                    top = jnp.maximum(
                        jnp.max(s_same, axis=0, keepdims=True), jnp.max(s_cross, axis=0, keepdims=True)
                    )
                    e_same = jnp.exp(s_same - top)
                    e_cross = jnp.exp(s_cross - top)
                    total = jnp.sum(e_same, axis=0, keepdims=True) + jnp.sum(
                        e_cross, axis=0, keepdims=True
                    )
                    head = pl.ds(pl.multiple_of(p * 128 + which * HD, HD), HD)
                    mixed = nn(n.v_t[block, head, :], e_same.astype(BF)) + nn(n.v_t[other, head, :], e_cross.astype(BF))
                    n.ctxt[head, :] = mixed / total
                    n.lse[layer, block, pl.ds(2 * p + which, 1), :] = top + jnp.log(total)
                return carry

            lax.fori_loop(0, HALF // 128, pair_step, 0)
            n.ctx_t[layer, :, rows_of(block, t)] = n.ctxt[...].astype(BF)
            n.ctx[layer, block] = n.ctxt[...].T.astype(BF)

        def early(p):
            kind = SHRINK if layer else EXPAND
            pl.when(p > 0)(lambda: w.onward(kind, layer, p - 1))

        attend(y, early)
        if last:
            gl_sent.wait()
            save(n.gl, n.gl_o)
        out_sent.wait()
        use = 2 * layer
        n.psend[use] = nn(n.ctx[layer, y], n.wo[layer]).astype(BF)
        part_sent = copies.push(n.psend.at[use], n.precv.at[use], peer)


        def late(p):
            if layer == 0:
                pl.when(p == 0)(lambda: w.onward(EXPAND, layer, 2))
                pl.when(p == 0)(lambda: w.onward(EXPAND, layer, 3))
                pl.when(p > 0)(lambda: w.onward(SHRINK, layer, p - 1))

        attend(x, late)
        n.mid[layer] = n.hs[layer] + nn(n.ctx[layer, x], n.wo[layer])
        save(n.ctx.at[layer], saved[layer].ctx)
        save(n.lse.at[layer], saved[layer].lse)
        save(n.wt.at[layer], saved[layer].wt)
        save(n.wo.at[layer], saved[layer].wo)
        save(n.ctx_t.at[layer], saved[layer].ctx_t)
        for block in range(2):
            n.na_t[layer, :, block * t : block * t + t] = n.na[layer, block].T
            n.k_t[layer, block] = n.k[layer, block].T
        save(n.na_t.at[layer], saved[layer].na)
        save(n.k_t.at[layer], saved[layer].k_t)
        part_sent.wait()
        n.mid[layer] = n.mid[layer] + n.precv[use].astype(F32)
        save(n.mid.at[layer], (n.mid_o0, n.mid_o1)[layer])

        xhat, _ = norm_stats(n.mid[layer])
        n.nb[layer, x] = (xhat * n.sc[layer, 2:3, :] + n.sc[layer, 3:4, :]).astype(BF)
        nb_sent = [copies.push(n.nb.at[layer, x, part], n.nb.at[layer, x, part], peer) for part in parts]
        w.arrive(EXPAND, layer)
        exp_sent = share_exp(layer)
        w.arrive(SHRINK, layer)
        shr_sent = share_shr(layer)
        exp_sent.wait()
        save(n.we.at[layer], saved[layer].we)

        def feed(block, part, pump):
            def step(i, carry):
                pump(i)
                lanes = pl.ds(pl.multiple_of(i * 256, 256), 256)
                value, rate = gelu_parts(nn(n.nb[layer, block, part, :], n.we[layer, :, lanes]))
                n.act[layer, block, part, lanes] = value.astype(BF)
                n.slope[layer, block, part, lanes] = rate.astype(BF)
                return carry

            lax.fori_loop(0, HID // 256, step, 0)

        def pump(i):
            if not last:

                @pl.when(i < 2)
                def _():
                    w.onward(TRIPLE, layer + 1, i)
                    w.onward(OUTPUT, layer + 1, i)

        feed(x, pl.ds(0, t), lambda i: None)
        shr_sent.wait()
        save(n.ws.at[layer], saved[layer].ws)
        n.hs[layer + 1] = n.mid[layer] + nt(n.act[layer, x], n.ws[layer])
        use = 2 * layer + 1
        part_sent = []
        for number, part in enumerate(parts):
            nb_sent[number].wait()
            feed(y, part, pump if number == 0 else lambda i: None)
            n.psend[use, part, :] = nt(n.act[layer, y, part, :], n.ws[layer]).astype(BF)
            part_sent.append(copies.push(n.psend.at[use, part], n.precv.at[use, part], peer))
        for block in range(2):
            n.nb_t[layer, :, block * t : block * t + t] = n.nb[layer, block].T
        save(n.nb_t.at[layer], saved[layer].nb)
        save(n.act.at[layer], saved[layer].act)
        save(n.slope.at[layer], saved[layer].slope)
        if not last:
            w.onward_all(EXPAND, layer + 1)
            w.arrive(TRIPLE, layer + 1)
            tri_sent = share_tri(layer + 1)
        for copy in part_sent:
            copy.wait()
        n.hs[layer + 1] = n.hs[layer + 1] + n.precv[use].astype(F32)

    n.h_out[...] = n.hs[LAYERS]
    n.sc_o[...] = n.sc[...]
    save(n.hs.at[1], n.h_mid)
    for copy in waits:
        copy.wait()
    for layer in range(LAYERS):
        for kind in KINDS:
            w.finish(kind, layer)


def forward_all(dp, h, g, scales_weight, tables, bias, shards):
    t = h.shape[0]
    zs, packed = dp // 2, 3 * (D // dp) // 2
    per_layer = [
        sds((D, 2 * t), BF), sds((2, t, HALF), BF), sds((2, 2 * t, HALF), BF), sds((2, HALF, 2 * t), BF), sds((2, 2 * t, HALF), BF),
        sds((2, t, HALF), BF), sds((HALF, 2 * t), BF), sds((2, 8, t), F32), sds((D, 2 * t), BF), sds((2, t, HID), BF),
        sds((2, t, HID), BF), sds((D, TRI), BF), sds((HALF, D), BF), sds((D, HID), BF), sds((D, HID), BF),
    ]
    token = sds((t, D), F32)
    outs = [token, token, token, token, sds((LAYERS, 4, D), F32), sds((2, t, D), BF), *per_layer, *per_layer]
    specs = [vmem(), hbm(), hbm(), hbm(), vmem(), hbm(), *([hbm()] * (2 * len(per_layer)))]
    n_layers = LAYERS
    rows = D // dp
    scratch = [
        pltpu.VMEM((n_layers, rows, HALF), BF), pltpu.VMEM((n_layers, packed, 128), BF),
        pltpu.VMEM((n_layers, packed, 128), BF), pltpu.VMEM((n_layers, rows, D), BF),
        pltpu.VMEM((n_layers, 192, 4 * rows), BF), pltpu.VMEM((2, t, D), BF),
        pltpu.VMEM((n_layers, D, TRI), BF), pltpu.VMEM((n_layers, HALF, D), BF),
        pltpu.VMEM((n_layers, D, HID), BF), pltpu.VMEM((n_layers, D, HID), BF),
        pltpu.VMEM((n_layers, 2, packed, 128), BF), pltpu.VMEM((n_layers, 2, packed, 128), BF),
        pltpu.VMEM((2, zs, SEQ, 8, 128), F32),
        pltpu.VMEM((n_layers, 4, D), F32), pltpu.VMEM((n_layers, 2, t, D), BF),
        pltpu.VMEM((n_layers, 2, t, HALF), BF), pltpu.VMEM((n_layers, 2, 2 * t, HALF), BF),
        pltpu.VMEM((n_layers, 2, 2 * t, HALF), BF), pltpu.VMEM((HALF, t), F32),
        pltpu.VMEM((n_layers, 2, t, HALF), BF), pltpu.VMEM((n_layers, HALF, 2 * t), BF),
        pltpu.VMEM((n_layers, 2, 8, t), F32), pltpu.VMEM((n_layers, 2, t, D), BF),
        pltpu.VMEM((n_layers, D, 2 * t), BF), pltpu.VMEM((n_layers, D, 2 * t), BF),
        pltpu.VMEM((n_layers, 2, HALF, 2 * t), BF), pltpu.VMEM((2, HALF, 2 * t), BF),
        pltpu.VMEM((n_layers, 2, t, HID), BF),
        pltpu.VMEM((n_layers, 2, t, HID), BF), pltpu.VMEM((2 * n_layers, t, D), BF),
        pltpu.VMEM((2 * n_layers, t, D), BF), pltpu.VMEM((n_layers + 1, t, D), F32),
        pltpu.VMEM((n_layers, t, D), F32),
        pltpu.SemaphoreType.DMA((n_layers, len(KINDS), 2, zs)),
        pltpu.SemaphoreType.DMA((n_layers, len(KINDS), 2, zs)),
        pltpu.SemaphoreType.DMA((n_layers, len(KINDS), 2)), pltpu.SemaphoreType.DMA((n_layers, len(KINDS), 4)),
        pltpu.SemaphoreType.DMA((zs * SEQ + 1,)), pltpu.SemaphoreType.DMA((zs * SEQ + 1,)),
        pltpu.SemaphoreType.DMA((32,)), pltpu.SemaphoreType.DMA((32,)), pltpu.SemaphoreType.DMA((40,)),
    ]
    results = pl.pallas_call(
        functools.partial(fwd_kernel, dp),
        name="forward",
        out_shape=outs,
        in_specs=[*([vmem()] * 4), pl.BlockSpec(memory_space=pltpu.SMEM), *([vmem()] * 4)],
        out_specs=specs,
        scratch_shapes=scratch,
        cost_estimate=pl.CostEstimate(flops=22 << 30, bytes_accessed=32 << 20, transcendentals=0),
        compiler_params=pltpu.CompilerParams(
            collective_id=4, has_side_effects=True, vmem_limit_bytes=VMEM_BYTES
        ),
    )(h, g, scales_weight, tables, bias, *shards)
    return split(results, ForwardHead, Saved, Saved)


class Sums(Spot):
    def __init__(self, n, rows):
        super().__init__()
        self.n = n
        self.rows = rows
        self.landed = {TRIPLE: n.y_tri, OUTPUT: n.y_out, EXPAND: n.y_exp, SHRINK: n.y_shr}
        self.owned = {TRIPLE: n.z_tri, OUTPUT: n.z_out, EXPAND: n.z_exp, SHRINK: n.z_shr}
        self.final = {TRIPLE: (n.f_whole, n.f_half), OUTPUT: (n.f_out,), EXPAND: (n.f_exp,), SHRINK: (n.f_shr,)}

    def view(self, kind, layer, y, z):
        n, r = self.n, self.rows
        if kind == EXPAND:
            return n.ge.at[layer, rows_of(2 * z + y, r), :]
        if kind == SHRINK:
            return n.gs.at[layer, :, rows_of(2 * lax.div(z, 2) + y, 4 * r)]
        return (n.gt if kind == TRIPLE else n.go).at[layer, rows_of(2 * lax.rem(z, 2) + y, r), :]

    def remote(self, src, dst, kind, layer, stage, sent, slot, to):
        return pltpu.make_async_remote_copy(
            src_ref=src,
            dst_ref=dst,
            send_sem=self.n.ssem.at[layer, kind, stage, sent],
            recv_sem=self.n.rsem.at[layer, kind, stage, slot],
            device_id=to,
            device_id_type=MESH,
        )

    def across_copy(self, kind, layer, j):
        return self.remote(
            self.view(kind, layer, 1 - self.y, self.origin(kind, j)), self.landed[kind].at[layer, j],
            kind, layer, 0, j, j, (self.across, self.s),
        )

    def across_all(self, kind, layer):
        for j in range(self.count(kind)):
            self.across_copy(kind, layer, j).start()

    def along_copy(self, kind, layer, j):
        z = self.origin(kind, j)
        slot = lax.rem(self.z - z + ZS - 1, ZS)
        mine = self.view(kind, layer, self.y, z)
        return self.remote(mine, self.owned[kind].at[layer, slot], kind, layer, 1, j, slot, (2 * z + self.y, self.s))

    def along(self, kind, layer, j):
        z = self.origin(kind, j)
        self.across_copy(kind, layer, j).wait_recv()
        mine = self.view(kind, layer, self.y, z)
        mine[...] = (mine[...].astype(F32) + self.landed[kind][layer, j].astype(F32)).astype(BF)
        pl.when(z != self.z)(lambda: self.along_copy(kind, layer, j).start())

    def along_all(self, kind, layer):
        for j in range(self.count(kind)):
            self.along(kind, layer, j)

    def parts(self, kind, layer):
        n = self.n
        mine = self.view(kind, layer, self.y, self.z)
        if kind == TRIPLE:
            return (
                mine.at[:, rows_of(self.x, HALF)], mine.at[:, rows_of(self.x + 1, HALF)],
                n.half_out.at[layer, 0], n.half_out.at[layer, 1],
            )
        if kind == OUTPUT:
            return n.out_out.at[layer, 0], n.out_out.at[layer, 1]
        return (mine,) if kind == EXPAND else (mine.at[pl.ds(0, 192), :], mine.at[pl.ds(192, 192), :])

    def home_copy(self, kind, layer, number, to, here=False):
        src = self.parts(kind, layer)[number]
        part = 1 if kind == TRIPLE and number >= 2 else 0
        dst = self.final[kind][part].at[layer]
        sem = self.n.home_rsem.at[layer, kind, part]
        if here:
            return pltpu.make_async_copy(src, dst, sem)
        return pltpu.make_async_remote_copy(
            src_ref=src, dst_ref=dst, send_sem=self.n.home_ssem.at[layer, kind, number], recv_sem=sem,
            device_id=(self.d, to), device_id_type=MESH,
        )

    def total(self, kind, layer):
        n = self.n

        def act():
            for slot in range(ZS - 1):
                ref = self.owned[kind].at[layer, slot]
                self.remote(ref, ref, kind, layer, 1, 0, slot, (self.across, self.s)).wait_recv()
            mine = self.view(kind, layer, self.y, self.z)
            value = mine[...].astype(F32)
            for slot in range(ZS - 1):
                value = value + self.owned[kind][layer, slot].astype(F32)
            n.squares[...] = n.squares[...] + squared(value)
            mine[...] = value.astype(BF)
            if kind == OUTPUT:
                first, second = pack_wide(value)
                n.out_out[layer, 0] = first.astype(BF)
                n.out_out[layer, 1] = second.astype(BF)
            if kind == TRIPLE:
                cut = mine[:, rows_of(2 * (1 - self.x), HALF)].astype(F32)
                first, second = pack_wide(cut)
                n.half_out[layer, 0] = first.astype(BF)
                n.half_out[layer, 1] = second.astype(BF)
            for number, to in self.naturals(kind):
                away = to != self.s
                place = (kind, layer, number, to)
                pl.when(away)(lambda place=place: self.home_copy(*place).start())
                pl.when(jnp.logical_not(away))(lambda place=place: self.home_copy(*place, True).start())

        self.if_owner(kind, act)

    def home(self, kind, layer):
        for part, final in enumerate(self.final[kind]):
            ref = final.at[layer]
            pltpu.make_async_remote_copy(
                src_ref=ref, dst_ref=ref, send_sem=self.n.home_ssem.at[layer, kind, 0],
                recv_sem=self.n.home_rsem.at[layer, kind, part], device_id=(self.d, self.peer), device_id_type=MESH,
            ).wait_recv()

    def finish(self, kind, layer):
        for j in range(self.count(kind)):
            self.across_copy(kind, layer, j).wait_send()
            pl.when(self.origin(kind, j) != self.z)(
                lambda j=j: self.along_copy(kind, layer, j).wait_send()
            )

        def act():
            for number, to in self.naturals(kind):
                place = (kind, layer, number, to)
                pl.when(to != self.s)(lambda place=place: self.home_copy(*place).wait_send())

        self.if_owner(kind, act)


def squared(value):
    return jnp.sum(jnp.sum(value * value, axis=1, keepdims=True), axis=0, keepdims=True)


def everywhere_start(w, use, buf):
    n = w.n
    mine = buf.at[w.y, w.z, w.s]

    def one(i, carry):
        z, s = lax.div(i, SEQ), lax.rem(i, SEQ)

        @pl.when(jnp.logical_or(z != w.z, s != w.s))
        def _():
            pltpu.make_async_remote_copy(
                src_ref=mine, dst_ref=mine, send_sem=n.ev_ssem.at[use, i],
                recv_sem=n.ev_rsem.at[use, w.z * SEQ + w.s], device_id=(2 * z + w.y, s), device_id_type=MESH,
            ).start()

        return carry

    lax.fori_loop(0, w.zs * SEQ, one, 0)


def everywhere_end(w, use, buf, pair):
    n = w.n

    def one(i, carry):
        z, s = lax.div(i, SEQ), lax.rem(i, SEQ)

        @pl.when(jnp.logical_or(z != w.z, s != w.s))
        def _():
            slot = buf.at[w.y, z, s]
            copy = pltpu.make_async_remote_copy(
                src_ref=slot, dst_ref=slot, send_sem=n.ev_ssem.at[use, i], recv_sem=n.ev_rsem.at[use, i],
                device_id=(2 * z + w.y, s), device_id_type=MESH,
            )
            copy.wait_recv()
            copy.wait_send()

        return carry

    lax.fori_loop(0, w.zs * SEQ, one, 0)

    def add(i, total):
        return total + buf[w.y, lax.div(i, SEQ), lax.rem(i, SEQ)]

    pair[w.y] = lax.fori_loop(1, w.zs * SEQ, add, buf[w.y, 0, 0])
    count = w.zs * SEQ
    copy = pltpu.make_async_remote_copy(
        src_ref=pair.at[w.y], dst_ref=pair.at[w.y], send_sem=n.ev_ssem.at[use, count],
        recv_sem=n.ev_rsem.at[use, count], device_id=(w.across, w.s), device_id_type=MESH,
    )
    copy.start()
    copy.wait()
    return pair[0] + pair[1]


class Loaded(NamedTuple):
    na: Any
    q: Any
    k: Any
    k_t: Any
    v: Any
    ctx: Any
    ctx_t: Any
    lse: Any
    nb: Any
    act: Any
    slope: Any
    wt: Any
    wo: Any
    we: Any
    ws: Any
    h: Any
    mid: Any


class BackwardIn(NamedTuple):
    g0: Any
    gl_h: Any
    sc: Any
    cs: Any
    bias: Any


class BackwardOut(NamedTuple):
    g_out: Any
    scale_o: Any
    norm_o: Any
    tri_g: Any
    out_g: Any
    exp_g: Any
    shr_g: Any


class BackwardScratch(NamedTuple):
    gl: Any
    gl_t: Any
    hg: Any
    ml: Any
    cg: Any
    delta: Any
    dqt: Any
    dk: Any
    dv: Any
    kvsend: Any
    kvrecv: Any
    pg: Any
    part: Any
    psend: Any
    precv: Any
    gs_exp: Any
    gr_exp: Any
    gs_shr: Any
    gr_shr: Any
    gr_att: Any
    gt: Any
    go: Any
    ge: Any
    gs: Any
    y_tri: Any
    y_out: Any
    y_exp: Any
    y_shr: Any
    z_tri: Any
    z_out: Any
    z_exp: Any
    z_shr: Any
    half_out: Any
    out_out: Any
    f_whole: Any
    f_half: Any
    f_out: Any
    f_exp: Any
    f_shr: Any
    squares: Any
    early: Any
    early_pair: Any
    late: Any
    late_pair: Any
    sq: Any
    sq_pair: Any
    ssem: Any
    rsem: Any
    home_ssem: Any
    home_rsem: Any
    ev_ssem: Any
    ev_rsem: Any
    xs: Any
    xr: Any
    lsem: Any


def bwd_kernel(dp, *refs):
    ins, saved0, saved1, outs, loaded, scratch = split(
        refs, BackwardIn, Loaded, Loaded, BackwardOut, Loaded, BackwardScratch
    )
    n = Refs(ins, outs, loaded, scratch)
    saved = (saved0, saved1)
    t = n.g0.shape[0]
    w = Sums(n, D // dp)
    x, c, peer, sib = w.x, w.c, w.peer, w.sib
    y = 1 - x
    parts = (pl.ds(0, t // 2), pl.ds(t // 2, t // 2))
    copies = Copies(n.lsem, n.xs, n.xr, w.d)
    loading = {}

    def load(layer, *wanted):
        for place in wanted:
            loading[place] = copies.local(saved[layer][place], loaded[place])

    def ready(*wanted):
        for place in wanted:
            loading[place].wait()

    na, q, k, k_t, v, ctx, ctx_t, lse, nb, act, slope, wt, wo, we, ws, h, mid = range(len(Loaded._fields))
    feed_places = (ws, slope, we, act, nb, mid)
    attend_places = (wo, ctx, q, k, v, lse, k_t, wt, na, ctx_t, h)
    top_gl = copies.local(n.gl_h, n.gl.at[LAYERS - 1])
    load(LAYERS - 1, *feed_places, *attend_places)
    greet_all(w)
    n.g_out[...] = n.g0[...]

    for layer in reversed(range(LAYERS)):
        top = layer == LAYERS - 1

        if top:
            top_gl.wait()
        else:
            n.gl[layer, x] = n.g_out[...].astype(BF)
            g_sent = [copies.push(n.gl.at[layer, x, part], n.gl.at[layer, x, part], peer) for part in parts]
        ready(ws, slope, we)

        def back(block, part):
            def step(i, carry):
                lanes = pl.ds(pl.multiple_of(i * 256, 256), 256)
                pulled = nn(n.gl[layer, block, part, :], n.ws[:, lanes])
                n.hg[block, part, lanes] = (pulled * n.slope[block, part, lanes].astype(F32)).astype(BF)
                return carry

            lax.fori_loop(0, HID // 256, step, 0)
            return nt(n.hg[block, part, :], n.we[...])

        def pump_tri(i):
            if not top:

                @pl.when(i < 2)
                def _():
                    w.along(TRIPLE, layer + 1, i)
                    w.along(OUTPUT, layer + 1, i)

        n.part[...] = back(x, pl.ds(0, t))
        use = 2 * layer
        part_sent = []
        for number, part in enumerate(parts):
            if not top:
                g_sent[number].wait()
            n.psend[part, :] = back(y, part).astype(BF)
            part_sent.append(copies.push(n.psend.at[part], n.precv.at[use, part], peer))
        ready(act, nb, mid)
        for block in range(2):
            n.gl_t[:, block * t : block * t + t] = n.gl[layer, block].T

        def exp_tile(which, i):
            off = pl.ds(pl.multiple_of(which * D + i * 256, 256), 256)
            return nn(n.nb[...], n.hg[:, :, off].reshape(2 * t, 256))

        def shr_tile(which, i):
            off = pl.ds(pl.multiple_of(i * 256, 256), 256)
            return nn(n.gl_t[rows_of(which, HALF), :], n.act[:, :, off].reshape(2 * t, 256))

        def send_exp(i, carry):
            at = pl.ds(pl.multiple_of(i * 256, 256), 256)
            n.gs_exp[:, at] = exp_tile(1 - c, i).astype(BF)
            return carry

        def send_shr(i, carry):
            at = pl.ds(pl.multiple_of(i * 256, 256), 256)
            n.gs_shr[:, at] = shr_tile(1 - c, i).astype(BF)
            return carry

        lax.fori_loop(0, D // 256, send_exp, 0)
        exp_sent = copies.push(n.gs_exp, n.gr_exp, sib)
        lax.fori_loop(0, HID // 256, send_shr, 0)
        shr_sent = copies.push(n.gs_shr, n.gr_shr, sib)

        def keep_exp(i, carry):
            at = pl.ds(pl.multiple_of(i * 256, 256), 256)
            n.ge[layer, :, at] = (exp_tile(c, i) + n.gr_exp[:, at].astype(F32)).astype(BF)
            return carry

        def keep_shr(i, carry):
            pump_tri(i)
            at = pl.ds(pl.multiple_of(i * 256, 256), 256)
            n.gs[layer, :, at] = (shr_tile(c, i) + n.gr_shr[:, at].astype(F32)).astype(BF)
            return carry

        exp_sent.wait()
        lax.fori_loop(0, D // 256, keep_exp, 0)
        w.across_all(EXPAND, layer)
        shr_sent.wait()
        lax.fori_loop(0, HID // 256, keep_shr, 0)
        w.across_all(SHRINK, layer)
        for copy in part_sent:
            copy.wait()
        dy = n.part[...] + n.precv[use].astype(F32)
        back_mid, rows_b = norm_back(n.mid[...], n.sc[layer, 2:3, :], dy)
        n.g_out[...] = n.g_out[...] + back_mid

        n.ml[layer, x] = n.g_out[...].astype(BF)
        ml_sent = copies.push(n.ml.at[layer, x], n.ml.at[layer, x], peer)
        if layer:
            load(layer - 1, *feed_places)
        n.dk[...] = jnp.zeros_like(n.dk)
        n.dv[...] = jnp.zeros_like(n.dv)
        ready(wo, ctx, q, k, v, lse, k_t)

        def attend(block, pump):
            other = 1 - block
            n.cg[block] = nt(n.ml[layer, block], n.wo[...]).astype(BF)
            weighed = (n.cg[block].astype(F32) * n.ctx[block].astype(F32)).T
            for head in range(HALF // HD):
                n.delta[head : head + 1, :] = jnp.sum(
                    weighed[head * HD : head * HD + HD, :], axis=0, keepdims=True
                )

            def pair_step(p, carry):
                pump(p)
                lanes = pl.ds(pl.multiple_of(p * 128, 128), 128)
                q_pair, cg_pair = n.q[block, :, lanes], n.cg[block, :, lanes]
                for which in range(2):
                    q_head, cg_head = half_of(q_pair, which), half_of(cg_pair, which)
                    row = pl.ds(2 * p + which, 1)
                    total, dots = n.lse[block, row, :], n.delta[row, :]
                    turned = None
                    head = pl.ds(pl.multiple_of(p * 128 + which * HD, HD), HD)
                    for side in (block, other):
                        k_pair, v_pair = n.k[side, :, lanes], n.v[side, :, lanes]
                        scores = nt(k_pair, q_head)
                        if side is other:
                            scores = scores + n.bias[0]
                        probs = jnp.exp(scores - total)
                        score_grad = (probs * (nt(v_pair, cg_head) - dots)).astype(BF)
                        n.dv[side, :, lanes] += nn(probs.astype(BF), cg_head)
                        n.dk[side, :, lanes] += nn(score_grad, q_head)
                        piece = nn(n.k_t[side, head, :], score_grad)
                        turned = piece if turned is None else turned + piece
                    n.dqt[block, head, :] = turned * HD**-0.5
                return carry

            lax.fori_loop(0, HALF // 128, pair_step, 0)

        attend(x, lambda p: None)
        ml_sent.wait()
        attend(y, lambda p: w.along(EXPAND, layer, p))
        theirs, mine = rows_of(1 - c, t), rows_of(c, t)
        for side in range(2):
            n.kvsend[side, :, pl.ds(0, HALF)] = n.dk[side, theirs, :].astype(BF)
            n.kvsend[side, :, pl.ds(HALF, HALF)] = n.dv[side, theirs, :].astype(BF)
        kv_sent = copies.push(n.kvsend, n.kvrecv.at[layer], sib)
        w.along(EXPAND, layer, 3)

        def unturn(block, j, value):
            cosine, sine = n.cs[block, :, 0:128], n.cs[block, :, 128:256]
            rounded = value.astype(BF).astype(F32)
            n.pg[block, :, pl.ds(128 * j, 128)] = turn(rounded, cosine, -sine).astype(BF)

        for side in range(2):
            for j in range(3):
                unturn(side, j, n.dqt[side, 128 * j : 128 * j + 128, :].T)
        kv_sent.wait()
        for side in range(2):
            for j in range(3):
                at = pl.ds(128 * j, 128)
                unturn(side, 3 + j, n.dk[side, mine, at] + n.kvrecv[layer, side, :, at].astype(F32))
                n.pg[side, :, pl.ds(D + 128 * j, 128)] = (
                    n.dv[side, mine, at] + n.kvrecv[layer, side, :, pl.ds(HALF + 128 * j, 128)].astype(F32)
                ).astype(BF)
        ready(wt, na, ctx_t, h)
        use = 2 * layer + 1
        n.psend[...] = nt(n.pg[y], n.wt[...]).astype(BF)
        part_sent = copies.push(n.psend, n.precv.at[use], peer)
        rows = D // dp

        def send_tri(i, carry):
            pl.when(i < 2)(lambda: w.along(SHRINK, layer, i))
            off = pl.ds(pl.multiple_of((1 - c) * HALF + i * rows, rows), rows)
            n.gs_shr[rows_of(i, rows), pl.ds(0, TRI)] = nn(n.na[off, :], n.pg[...].reshape(2 * t, TRI)).astype(BF)
            return carry

        lax.fori_loop(0, w.zs, send_tri, 0)
        tri_cols, out_cols = pl.ds(0, TRI), pl.ds(TRI, HALF)
        tri_sent = copies.push(n.gs_shr.at[:, tri_cols], n.gr_att.at[:, tri_cols], sib)
        theirs_too = n.ml[layer, :, :, rows_of(1 - c, HALF)].reshape(2 * t, HALF)
        n.gs_shr[:, out_cols] = nn(n.ctx_t[...], theirs_too).astype(BF)
        out_sent = copies.push(n.gs_shr.at[:, out_cols], n.gr_att.at[:, out_cols], sib)
        n.part[...] = nt(n.pg[x], n.wt[...])
        tri_sent.wait()

        def keep_tri(i, carry):
            at = rows_of(i, rows)
            row_block = n.na[pl.ds(pl.multiple_of(c * HALF + i * rows, rows), rows), :]
            value = nn(row_block, n.pg[...].reshape(2 * t, TRI)) + n.gr_att[at, tri_cols].astype(F32)
            n.gt[layer, at, :] = value.astype(BF)
            return carry

        lax.fori_loop(0, w.zs, keep_tri, 0)
        w.across_all(TRIPLE, layer)
        out_sent.wait()
        mine_too = n.ml[layer, :, :, rows_of(c, HALF)].reshape(2 * t, HALF)
        value = nn(n.ctx_t[...], mine_too) + n.gr_att[:, out_cols].astype(F32)
        n.go[layer] = value.astype(BF)
        w.across_all(OUTPUT, layer)
        part_sent.wait()
        dy = n.part[...] + n.precv[use].astype(F32)
        back_h, rows_a = norm_back(n.h[...], n.sc[layer, 0:1, :], dy)
        n.g_out[...] = n.g_out[...] + back_h
        mine_at = (w.y, w.z, w.s)
        if layer:
            load(layer - 1, *attend_places)
            n.early[(*mine_at, pl.ds(0, 2))] = rows_a
            n.early[(*mine_at, pl.ds(2, 2))] = rows_b
        else:
            n.early[(*mine_at, pl.ds(4, 2))] = rows_b
            n.late[mine_at] = rows_a

    everywhere_start(w, 0, n.early)
    everywhere_start(w, 1, n.late)
    n.squares[...] = jnp.zeros_like(n.squares)
    for kind in (EXPAND, SHRINK, TRIPLE, OUTPUT):
        w.total(kind, 1)
    w.along_all(TRIPLE, 0)
    w.along_all(OUTPUT, 0)
    for kind in (EXPAND, SHRINK):
        w.total(kind, 0)
    first = everywhere_end(w, 0, n.early, n.early_pair)
    second = everywhere_end(w, 1, n.late, n.late_pair)
    n.scale_o[1, pl.ds(0, 2)] = first[0:2]
    n.scale_o[1, pl.ds(2, 2)] = first[2:4]
    n.scale_o[0, pl.ds(0, 2)] = second
    n.scale_o[0, pl.ds(2, 2)] = first[4:6]
    for kind in (TRIPLE, OUTPUT):
        w.total(kind, 0)
    n.sq[w.y, w.z, w.s] = jnp.broadcast_to(n.squares[...], (8, 128))
    everywhere_start(w, 2, n.sq)
    for layer in range(LAYERS):
        for kind in KINDS:
            w.home(kind, layer)
    rows = D // dp

    def natural(packed):
        wide, rest = packed[:rows].astype(F32), packed[rows:].astype(F32)
        even = jnp.concatenate([rest[:, :HD], rest[:, HD:]], axis=0)
        odd = jnp.concatenate([rest[:, HD:], rest[:, :HD]], axis=0)
        return jnp.concatenate([wide, even], axis=1), jnp.concatenate([odd, wide], axis=1)

    for layer in range(LAYERS):
        halves, outs_here = natural(n.f_half[layer]), natural(n.f_out[layer])
        whole = n.f_whole[layer].astype(F32)

        @pl.when(c == 0)
        def _():
            n.tri_g[layer] = jnp.concatenate([whole, halves[0]], axis=1)
            n.out_g[layer] = outs_here[0]

        @pl.when(c == 1)
        def _():
            n.tri_g[layer] = jnp.concatenate([halves[1], whole], axis=1)
            n.out_g[layer] = outs_here[1]

    outputs = [
        copies.local(a, b)
        for a, b in ((n.f_exp, n.exp_g), (n.f_shr, n.shr_g))
    ]
    total = everywhere_end(w, 2, n.sq, n.sq_pair)
    n.norm_o[...] = total + squared(first[0:6]) + squared(second)
    for copy in outputs:
        copy.wait()
    for layer in range(LAYERS):
        for kind in KINDS:
            w.finish(kind, layer)


def backward_all(dp, g, f, residual, tables, bias):
    t = g.shape[0]
    zs = dp // 2
    r = D // dp
    packed = 3 * r // 2
    head, saved0, saved1 = f
    saved = (*saved0, residual, head.mid_o0, *saved1, head.h_mid, head.mid_o1)
    outs = [
        sds((t, D), F32), sds((LAYERS, 4, D), F32), sds((8, 128), F32), sds((LAYERS, r, TRI // 2), F32),
        sds((LAYERS, r, 192), F32), sds((LAYERS, r, D), BF),
        sds((LAYERS, 192, 4 * r), BF),
    ]
    v = pltpu.VMEM
    ll = LAYERS
    scratch = [
        *(v(array.shape, array.dtype) for array in saved[: len(Loaded._fields)]),
        v((ll, 2, t, D), BF), v((D, 2 * t), BF), v((2, t, HID), BF), v((ll, 2, t, D), BF), v((2, t, HALF), BF), v((8, t), F32),
        v((2, HALF, t), F32), v((2, 2 * t, HALF), F32), v((2, 2 * t, HALF), F32), v((2, t, D), BF),
        v((ll, 2, t, D), BF), v((2, t, TRI), BF), v((t, D), F32), v((t, D), BF), v((2 * ll, t, D), BF),
        v((D, D), BF), v((D, D), BF), v((HALF, HID), BF), v((HALF, HID), BF), v((HALF, HID), BF),
        v((ll, HALF, TRI), BF), v((ll, HALF, HALF), BF), v((ll, D, D), BF), v((ll, HALF, HID), BF),
        v((ll, 2, r, TRI), BF), v((ll, 2, r, HALF), BF), v((ll, 4, r, D), BF), v((ll, 2, HALF, 4 * r), BF),
        v((ll, 3, r, TRI), BF), v((ll, 3, r, HALF), BF), v((ll, 3, r, D), BF), v((ll, 3, HALF, 4 * r), BF),
        v((ll, 2, packed, 128), BF), v((ll, 2, packed, 128), BF),
        v((ll, r, HALF), BF), v((ll, packed, 128), BF), v((ll, packed, 128), BF), v((ll, r, D), BF),
        v((ll, 192, 4 * r), BF), v((1, 1), F32),
        v((2, zs, SEQ, 8, D), F32), v((2, 8, D), F32), v((2, zs, SEQ, 2, D), F32), v((2, 2, D), F32),
        v((2, zs, SEQ, 8, 128), F32), v((2, 8, 128), F32),
        pltpu.SemaphoreType.DMA((ll, len(KINDS), 2, zs)), pltpu.SemaphoreType.DMA((ll, len(KINDS), 2, zs)),
        pltpu.SemaphoreType.DMA((ll, len(KINDS), 4)), pltpu.SemaphoreType.DMA((ll, len(KINDS), 2)),
        pltpu.SemaphoreType.DMA((3, zs * SEQ + 1)), pltpu.SemaphoreType.DMA((3, zs * SEQ + 1)),
        pltpu.SemaphoreType.DMA((28,)), pltpu.SemaphoreType.DMA((28,)), pltpu.SemaphoreType.DMA((48,)),
    ]
    results = pl.pallas_call(
        functools.partial(bwd_kernel, dp),
        name="backward",
        out_shape=outs,
        in_specs=[vmem(), hbm(), vmem(), vmem(), pl.BlockSpec(memory_space=pltpu.SMEM), *([hbm()] * len(saved))],
        out_specs=[vmem()] * 5 + [hbm()] * 2,
        scratch_shapes=scratch,
        cost_estimate=pl.CostEstimate(flops=44 << 30, bytes_accessed=48 << 20, transcendentals=0),
        compiler_params=pltpu.CompilerParams(
            collective_id=5, has_side_effects=True, vmem_limit_bytes=VMEM_BYTES
        ),
    )(g, head.gl_o, head.sc_o, tables, bias, *saved)
    return BackwardOut(*results)


class Moves:
    def __init__(self, dp):
        self.dp = dp
        self.d = lax.axis_index("dp")
        s = lax.axis_index("seq")
        self.s, self.x, self.c = s, s // 2, s % 2
        half = dp // 2
        ids = [(d, s) for d in range(dp) for s in range(SEQ)]
        self.tri = []
        for r in range(2):
            for j in range(3):
                perm = []
                for d, s in ids:
                    b = (3 * s + j) % 4
                    to = (2 * (d % half) + (r ^ (b % 2)), 2 * (b // 2) + d // half)
                    perm.append((d * SEQ + s, to[0] * SEQ + to[1]))
                self.tri.append(perm)
        self.out = []
        for r in range(2):
            perm = []
            for d, s in ids:
                to = (2 * (d % half) + (r ^ (s % 2)), 2 * (d // half) + s // 2)
                perm.append((d * SEQ + s, to[0] * SEQ + to[1]))
            self.out.append(perm)
        self.shr = []
        for k in range(4):
            perm = []
            for d, s in ids:
                to = (4 * (d % (dp // 4)) + (k + s) % 4, d // (dp // 4))
                perm.append((d * SEQ + s, to[0] * SEQ + to[1]))
            self.shr.append(perm)

    def send(self, piece, perm, back):
        if back:
            perm = [(b, a) for a, b in perm]
        return lax.ppermute(piece, ("dp", "seq"), perm)

    @staticmethod
    def pick(pieces, index):
        return lax.dynamic_index_in_dim(jnp.stack(pieces), index, 0, keepdims=False)

    def tri_out(self, low):
        n, rows, _ = low.shape
        halves = low.reshape(n, 2, rows // 2, 3, 192)
        got = []
        for r in range(2):
            for j in range(3):
                which = r ^ (((3 * self.s + j) % 4) % 2)
                piece = lax.dynamic_index_in_dim(halves[:, :, :, j], which, 1, keepdims=False)
                got.append(self.send(piece, self.tri[3 * r + j], False))
        parts = []
        for t in range(3):
            for bb in range(2):
                r, j = bb ^ (self.d % 2), (t + 2 * self.x + bb) % 3
                parts.append(self.pick(got, 3 * r + j))
        return jnp.concatenate(parts, axis=-1)

    def tri_back(self, grad):
        n, rows, _ = grad.shape
        got = []
        for r in range(2):
            for j in range(3):
                bb = (self.d % 2) ^ r
                t = (j - (2 * self.x + bb)) % 3
                piece = lax.dynamic_slice_in_dim(grad, (2 * t + bb) * 192, 192, 2)
                got.append(self.send(piece, self.tri[3 * r + j], True))
        cols = []
        for j in range(3):
            two = []
            for hh in range(2):
                r = hh ^ (((3 * self.s + j) % 4) % 2)
                two.append(self.pick([got[j], got[3 + j]], r))
            cols.append(jnp.concatenate(two, axis=1))
        return jnp.concatenate(cols, axis=-1)

    def out_out(self, low):
        n, rows, _ = low.shape
        halves = low.reshape(n, 2, rows // 2, 192)
        got = [
            self.send(
                lax.dynamic_index_in_dim(halves, r ^ (self.s % 2), 1, keepdims=False), self.out[r], False
            )
            for r in range(2)
        ]
        return jnp.concatenate([self.pick(got, u ^ (self.d % 2)) for u in range(2)], axis=-1)

    def out_back(self, grad):
        got = []
        for r in range(2):
            u = r ^ (self.d % 2)
            got.append(self.send(lax.dynamic_slice_in_dim(grad, u * 192, 192, 2), self.out[r], True))
        return jnp.concatenate([self.pick(got, hh ^ (self.s % 2)) for hh in range(2)], axis=1)

    def shr_out(self, low):
        n, rows, _ = low.shape
        subs = low.reshape(n, 4, rows // 4, 192)
        got = [
            self.send(
                lax.dynamic_index_in_dim(subs, (k + self.s) % 4, 1, keepdims=False), self.shr[k], False
            )
            for k in range(4)
        ]
        return jnp.concatenate([self.pick(got, (self.d - s) % 4) for s in range(4)], axis=-1)

    def shr_back(self, grad):
        got = []
        for k in range(4):
            piece = lax.dynamic_slice_in_dim(grad, ((self.d - k) % 4) * 192, 192, 2)
            got.append(self.send(piece, self.shr[k], True))
        return jnp.concatenate([self.pick(got, (sub - self.s) % 4) for sub in range(4)], axis=1)


def tables_here(segments, t, x, c):
    group = segments.shape[0]
    whole = segments[0] == segments[group - 1]
    place_in_half = c * t + jnp.arange(t, dtype=jnp.int32)
    second = jnp.where(whole, group // 2, 0).astype(jnp.int32)
    positions = jnp.stack([place_in_half, place_in_half + second]).astype(F32)
    lane = jnp.arange(128, dtype=jnp.int32)
    inverse = 1.0 / ROTARY_BASE ** ((lane % (HD // 2)).astype(F32) * (2.0 / HD))
    angles = positions[:, :, None] * inverse[None, None, :]
    sign = jnp.where(lane % HD < HD // 2, -1.0, 1.0).astype(F32)
    tables = jnp.concatenate([jnp.cos(angles), jnp.sin(angles) * sign], axis=-1)
    bias = jnp.where(whole, 0.0, MASKED).astype(F32).reshape(1)
    return tables, bias


def layers_narrow(
    dp, moves, residual, cotangent, scales_weight, tables, bias,
    triple_weight, output_weight, expand_weight, shrink_weight,
):
    d, s = lax.axis_index("dp"), lax.axis_index("seq")
    scales_all = lax.psum(
        lax.dynamic_update_slice(
            jnp.zeros((LAYERS, 4, D), F32), scales_weight.astype(BF).astype(F32), (0, s, d * (D // dp))
        ),
        ("dp", "seq"),
    )
    tri = moves.tri_out(triple_weight.astype(BF))
    out = moves.out_out(output_weight.astype(BF))
    shr = moves.shr_out(shrink_weight.astype(BF))
    attend_parts = jnp.concatenate([tri, out], axis=-1)
    feed_parts = jnp.concatenate([expand_weight.astype(BF), shr], axis=-1)
    gather = functools.partial(lax.all_gather, axis_name="dp", axis=0, tiled=True)
    wa, wf = [], []
    for layer in range(LAYERS):
        wa.append(gather(attend_parts[layer]))
        wf.append(gather(feed_parts[layer]))

    stream = residual
    kept = []
    for layer in range(LAYERS):
        scales = scales_all[layer]
        middle, *attend_saved = attend_fwd(stream, wa[layer], scales, tables, bias)
        following, *feed_saved = feed_fwd(middle, wf[layer], scales)
        kept.append((stream, middle, attend_saved, feed_saved))
        stream = following

    g = cotangent
    attend_grads, feed_grads, scale_grads = [None] * LAYERS, [None] * LAYERS, [None] * LAYERS
    scatter = functools.partial(lax.psum_scatter, axis_name="dp", scatter_dimension=0, tiled=True)
    for layer in reversed(range(LAYERS)):
        scales = scales_all[layer]
        h, middle, attend_saved, feed_saved = kept[layer]
        mg, feed_grad, rows_b = feed_bwd(g, middle, wf[layer], scales, *feed_saved)
        feed_grads[layer] = scatter(feed_grad).astype(F32)
        g, attend_grad, rows_a = attend_bwd(mg, h, wa[layer], scales, tables, bias, attend_saved)
        attend_grads[layer] = scatter(attend_grad).astype(F32)
        scale_grads[layer] = jnp.concatenate([rows_a, rows_b], axis=0)

    scale_grad = lax.psum(jnp.stack(scale_grads), ("dp", "seq"))
    own_scale = lax.dynamic_slice(scale_grad, (0, s, d * (D // dp)), (LAYERS, 1, D // dp))
    squares = jnp.sum(own_scale * own_scale)
    for part in (*attend_grads, *feed_grads):
        squares = squares + jnp.sum(part * part)
    grad_norm = jnp.sqrt(lax.psum(squares, ("dp", "seq")))

    attend_grad, feed_grad = jnp.stack(attend_grads).astype(BF), jnp.stack(feed_grads).astype(BF)
    triple_grad = moves.tri_back(attend_grad[:, :, :TRI]).astype(F32)
    output_grad = moves.out_back(attend_grad[:, :, TRI:]).astype(F32)
    expand_grad = feed_grad[:, :, :D].astype(F32)
    shrink_grad = moves.shr_back(feed_grad[:, :, D:]).astype(F32)
    return stream, g, grad_norm, (triple_grad, output_grad, expand_grad, shrink_grad, own_scale)


def layers_wide(
    dp, moves, residual, cotangent, scales_weight, tables, bias,
    triple_weight, output_weight, expand_weight, shrink_weight,
):
    d, s = lax.axis_index("dp"), lax.axis_index("seq")
    shards = (triple_weight, output_weight, expand_weight, jnp.swapaxes(shrink_weight, 1, 2))
    f = forward_all(dp, residual, cotangent, scales_weight, tables, bias, shards)
    b = backward_all(dp, cotangent, f, residual, tables, bias)
    own_scale = lax.dynamic_slice(b.scale_o, (0, s, d * (D // dp)), (LAYERS, 1, D // dp))
    grad_norm = jnp.sqrt(b.norm_o[0, 0])
    return f[0].h_out, b.g_out, grad_norm, (
        b.tri_g, b.out_g, b.exp_g.astype(F32), jnp.swapaxes(b.shr_g, 1, 2).astype(F32), own_scale
    )


def local(dp, *args):
    (residual, cotangent, segments) = args[:3]
    (
        triple_weight, triple_moment, triple_square, triple_shadow,
        output_weight, output_moment, output_square, output_shadow,
        expand_weight, expand_moment, expand_square, expand_shadow,
        shrink_weight, shrink_moment, shrink_square, shrink_shadow,
        scales_weight, scales_moment, scales_square, scales_shadow,
    ) = args[3:]
    moves = Moves(dp)
    t = residual.shape[0]
    d, s = lax.axis_index("dp"), lax.axis_index("seq")
    tables, bias = tables_here(segments, t, moves.x, moves.c)

    if dp == 2 * ZS:
        stream, g, grad_norm, grads = layers_wide(
            dp, moves, residual, cotangent, scales_weight, tables, bias,
            triple_weight, output_weight, expand_weight, shrink_weight,
        )
    else:
        stream, g, grad_norm, grads = layers_narrow(
            dp, moves, residual, cotangent, scales_weight, tables, bias,
            triple_weight, output_weight, expand_weight, shrink_weight,
        )
    triple_grad, output_grad, expand_grad, shrink_grad, own_scale = grads
    limit = CLIP_RATIO * math.sqrt(float(LAYERS * (4 * D * D + 2 * D * FF + 4 * D)))
    factor = limit / (grad_norm + 1e-06)

    results = [stream, g, grad_norm]
    for weight, moment, square, shadow, grad, rate in (
        (triple_weight, triple_moment, triple_square, triple_shadow, triple_grad, RATE_FACTOR / math.sqrt(D)),
        (output_weight, output_moment, output_square, output_shadow, output_grad, RATE_FACTOR / math.sqrt(D // 16)),
        (expand_weight, expand_moment, expand_square, expand_shadow, expand_grad, RATE_FACTOR / math.sqrt(D)),
        (shrink_weight, shrink_moment, shrink_square, shrink_shadow, shrink_grad, RATE_FACTOR / math.sqrt(FF)),
        (scales_weight, scales_moment, scales_square, scales_shadow, own_scale, SCALES_RATE),
    ):
        results.extend(adam_step(weight, moment, square, shadow, grad * factor, rate))
    return tuple(results)


def solution(mesh):
    token = P(("dp", "seq"), None)
    weight = P(None, "dp", "seq")
    scale = P(None, "seq", "dp")
    return jax.shard_map(
        functools.partial(local, mesh.shape["dp"]),
        mesh=mesh,
        in_specs=(token, token, P("dp"), *([weight] * 16), *([scale] * 4)),
        out_specs=(token, token, P(), *([weight] * 16), *([scale] * 4)),
        check_vma=False,
    )
```

```python
import functools
import math
from typing import Any, NamedTuple

import jax
import jax.numpy as jnp
from jax import lax
from jax.experimental import pallas as pl
from jax.experimental.pallas import tpu as pltpu
from jax.sharding import PartitionSpec as P

D = 768
FF = 3072
HD = 64
LAYERS = 2
STEP = 2
SEQ = 4

EPSILON = 1e-05
ROTARY_BASE = 10000.0
BETA_ONE = 0.9
BETA_TWO = 0.999
ADAM_EPSILON = 1e-08
DECAY_RATE = 0.01
SHADOW_RATE = 0.99
CLIP_RATIO = 0.5
RATE_FACTOR = 1.5
SCALES_RATE = 0.6
MASKED = -1000000000.0

HALF = D // 2
TRI = 3 * HALF
HID = FF // 2
BF = jnp.bfloat16
F32 = jnp.float32
MESH = pl.DeviceIdType.MESH
VMEM_BYTES = 60 << 20


def adam_step(weight, moment, square, shadow, gradient, step_rate):
    shadow_decay = min(SHADOW_RATE, (1.0 + STEP) / (10.0 + STEP))
    momentum = BETA_ONE * moment + (1.0 - BETA_ONE) * gradient
    variance = BETA_TWO * square + (1.0 - BETA_TWO) * gradient * gradient
    corrected = (
        momentum
        / (1.0 - BETA_ONE**STEP)
        / (jnp.sqrt(variance / (1.0 - BETA_TWO**STEP)) + ADAM_EPSILON)
    )
    updated = weight - step_rate * (corrected + DECAY_RATE * weight)
    average = shadow_decay * shadow + (1.0 - shadow_decay) * updated
    return (updated, momentum, variance, average)


def nn(a, b):
    return lax.dot_general(a, b, (((1,), (0,)), ((), ())), preferred_element_type=F32)


def nt(a, b):
    return lax.dot_general(a, b, (((1,), (1,)), ((), ())), preferred_element_type=F32)


def tn(a, b):
    return lax.dot_general(a, b, (((0,), (0,)), ((), ())), preferred_element_type=F32)


def place():
    s = lax.axis_index("seq")
    x = lax.div(s, 2)
    c = lax.rem(s, 2)
    return lax.axis_index("dp"), x, c, lax.rem(s + 2, SEQ), s + 1 - 2 * c


def greet(d, peer, sib):
    barrier = pltpu.get_barrier_semaphore()
    for other in (peer, sib):
        pl.semaphore_signal(barrier, inc=1, device_id=(d, other), device_id_type=MESH)
    pl.semaphore_wait(barrier, 2)


def rows_of(c, n):
    return pl.ds(pl.multiple_of(c * n, n), n)


class Copies:
    def __init__(self, lsem, ssem, rsem, d):
        self.lsem, self.ssem, self.rsem, self.d = lsem, ssem, rsem, d
        self.n_local = 0
        self.n_remote = 0

    def local(self, src, dst):
        copy = pltpu.make_async_copy(src, dst, self.lsem.at[self.n_local])
        self.n_local += 1
        copy.start()
        return copy

    def push(self, src, dst, to):
        copy = pltpu.make_async_remote_copy(
            src_ref=src,
            dst_ref=dst,
            send_sem=self.ssem.at[self.n_remote],
            recv_sem=self.rsem.at[self.n_remote],
            device_id=(self.d, to),
            device_id_type=MESH,
        )
        self.n_remote += 1
        copy.start()
        return copy


def norm_stats(values):
    center = values - jnp.mean(values, axis=-1, keepdims=True)
    spread = jnp.mean(center * center, axis=-1, keepdims=True)
    scale = lax.rsqrt(spread + EPSILON)
    return center * scale, scale


def norm_back(values, gain, dy):
    xhat, scale = norm_stats(values)
    u = gain * dy
    du = u - jnp.mean(u, axis=-1, keepdims=True)
    back = scale * (du - xhat * jnp.mean(u * xhat, axis=-1, keepdims=True))
    rows = jnp.concatenate(
        [jnp.sum(xhat * dy, axis=0, keepdims=True), jnp.sum(dy, axis=0, keepdims=True)], axis=0
    )
    return back, rows


def turn(chunk, cosine, sine):
    lane = lax.broadcasted_iota(jnp.int32, chunk.shape, 1)
    swapped = jnp.where(
        lax.rem(lane, HD) < HD // 2, pltpu.roll(chunk, 128 - HD // 2, 1), pltpu.roll(chunk, HD // 2, 1)
    )
    return chunk * cosine + swapped * sine


def half_of(pair, which):
    lane = lax.broadcasted_iota(jnp.int32, pair.shape, 1)
    keep = (lane < HD) if which == 0 else (lane >= HD)
    return jnp.where(keep, pair, jnp.zeros_like(pair))


def attend_fwd_kernel(
    h, wa, sc, cs, bias, mid, na_o, q_o, k_o, v_o, ctx_o, lse_o,
    wt, wo, na, q, k, v, ctxt, ctx, lse, psend, precv, lsem, ssem, rsem,
):
    d, x, c, peer, sib = place()
    y = 1 - x
    rows = h.shape[0]
    copies = Copies(lsem, ssem, rsem, d)
    greet(d, peer, sib)
    wt_own, wo_own = wt.at[rows_of(c, HALF), :], wo.at[:, rows_of(c, HALF)]
    tri_part, out_part = wa.at[:, pl.ds(0, TRI)], wa.at[:, pl.ds(TRI, HALF)]
    tri_sent = copies.push(tri_part, wt_own, sib)
    tri_local = copies.local(tri_part, wt_own)
    out_sent = copies.push(out_part, wo_own, sib)
    out_local = copies.local(out_part, wo_own)
    xhat, _ = norm_stats(h[...])
    na[x] = (xhat * sc[0:1, :] + sc[1:2, :]).astype(BF)
    na_sent = copies.push(na.at[x], na.at[x], peer)
    tri_local.wait()
    tri_sent.wait()

    def project(block):
        cosine, sine = cs[block, :, 0:128], cs[block, :, 128:256]
        for j in range(9):
            part = nn(na[block], wt[:, 128 * j : 128 * j + 128])
            lanes = pl.ds(128 * (j % 3), 128)
            if j < 3:
                q[block, :, lanes] = (turn(part, cosine, sine) * HD**-0.5).astype(BF)
            elif j < 6:
                k[block, rows_of(c, rows), lanes] = turn(part, cosine, sine).astype(BF)
            else:
                v[block, rows_of(c, rows), lanes] = part.astype(BF)

    def share(block):
        mine = (block, rows_of(c, rows))
        return [copies.push(k.at[mine], k.at[mine], sib), copies.push(v.at[mine], v.at[mine], sib)]

    project(x)
    shared = share(x)
    na_sent.wait()
    project(y)
    shared += share(y)
    out_local.wait()
    out_sent.wait()
    for copy in shared:
        copy.wait()

    def attend(block):
        other = 1 - block

        def pair_step(p, carry):
            lanes = pl.ds(pl.multiple_of(p * 128, 128), 128)
            q_pair = q[block, :, lanes]
            k_same, k_cross = k[block, :, lanes], k[other, :, lanes]
            v_same, v_cross = v[block, :, lanes], v[other, :, lanes]
            for which in range(2):
                q_head = half_of(q_pair, which)
                s_same = nt(k_same, q_head)
                s_cross = nt(k_cross, q_head) + bias[0]
                top = jnp.maximum(
                    jnp.max(s_same, axis=0, keepdims=True), jnp.max(s_cross, axis=0, keepdims=True)
                )
                e_same = jnp.exp(s_same - top)
                e_cross = jnp.exp(s_cross - top)
                total = jnp.sum(e_same, axis=0, keepdims=True) + jnp.sum(
                    e_cross, axis=0, keepdims=True
                )
                mixed = tn(v_same, e_same.astype(BF)) + tn(v_cross, e_cross.astype(BF))
                head = pl.ds(pl.multiple_of(p * 128 + which * HD, HD), HD)
                ctxt[head, :] = mixed[which * HD : which * HD + HD, :] / total
                lse[block, pl.ds(2 * p + which, 1), :] = top + jnp.log(total)
            return carry

        lax.fori_loop(0, HALF // 128, pair_step, 0)
        ctx[block] = ctxt[...].T.astype(BF)
        return nn(ctx[block], wo[...])

    psend[...] = attend(y).astype(BF)
    part_sent = copies.push(psend, precv, peer)
    mid[...] = h[...] + attend(x)
    saves = [
        copies.local(a, b)
        for a, b in ((na, na_o), (q, q_o), (k, k_o), (v, v_o), (ctx, ctx_o), (lse, lse_o))
    ]
    part_sent.wait()
    mid[...] = mid[...] + precv[...].astype(F32)
    for copy in saves:
        copy.wait()


def hbm():
    return pl.BlockSpec(memory_space=pl.ANY)


def vmem():
    return pl.BlockSpec(memory_space=pltpu.VMEM)


def call(kernel, name, number, ins, outs, out_shape, scratch, n_local, n_remote, flops, args):
    return pl.pallas_call(
        kernel,
        name=name,
        out_shape=out_shape,
        in_specs=ins,
        out_specs=outs,
        scratch_shapes=[
            *scratch,
            pltpu.SemaphoreType.DMA((n_local,)),
            pltpu.SemaphoreType.DMA((n_remote,)),
            pltpu.SemaphoreType.DMA((n_remote,)),
        ],
        cost_estimate=pl.CostEstimate(flops=flops, bytes_accessed=16 << 20, transcendentals=0),
        compiler_params=pltpu.CompilerParams(
            collective_id=number, has_side_effects=True, vmem_limit_bytes=VMEM_BYTES
        ),
    )(*args)


def sds(shape, dtype):
    return jax.ShapeDtypeStruct(shape, dtype)


def attend_fwd(h, wa, scales, tables, bias):
    t = h.shape[0]
    return call(
        attend_fwd_kernel, "attend_fwd", 0,
        [vmem(), hbm(), vmem(), vmem(), pl.BlockSpec(memory_space=pltpu.SMEM)],
        [vmem()] + [hbm()] * 6,
        [
            sds((t, D), F32), sds((2, t, D), BF), sds((2, t, HALF), BF), sds((2, 2 * t, HALF), BF),
            sds((2, 2 * t, HALF), BF), sds((2, t, HALF), BF), sds((2, 8, t), F32),
        ],
        [
            pltpu.VMEM((D, TRI), BF), pltpu.VMEM((HALF, D), BF), pltpu.VMEM((2, t, D), BF),
            pltpu.VMEM((2, t, HALF), BF), pltpu.VMEM((2, 2 * t, HALF), BF),
            pltpu.VMEM((2, 2 * t, HALF), BF), pltpu.VMEM((HALF, t), F32),
            pltpu.VMEM((2, t, HALF), BF), pltpu.VMEM((2, 8, t), F32),
            pltpu.VMEM((t, D), BF), pltpu.VMEM((t, D), BF),
        ],
        8, 8, 6 << 30, (h, wa, scales, tables, bias),
    )


def gelu_parts(hidden):
    phi_cap = 0.5 * (1.0 + lax.erf(hidden * math.sqrt(0.5)))
    density = jnp.exp(-0.5 * hidden * hidden) * (1.0 / math.sqrt(2.0 * math.pi))
    return hidden * phi_cap, phi_cap + hidden * density


def feed_fwd_kernel(
    mid, wf, sc, h_next, nb_o, act_o, slope_o,
    we, ws, nb, act, slope, psend, precv, lsem, ssem, rsem,
):
    d, x, c, peer, sib = place()
    y = 1 - x
    copies = Copies(lsem, ssem, rsem, d)
    greet(d, peer, sib)
    xhat, _ = norm_stats(mid[...])
    nb[x] = (xhat * sc[2:3, :] + sc[3:4, :]).astype(BF)
    nb_sent = copies.push(nb.at[x], nb.at[x], peer)
    we_own, ws_own = we.at[:, rows_of(c, D)], ws.at[rows_of(c, D), :]
    exp_part, shr_part = wf.at[:, pl.ds(0, D)], wf.at[:, pl.ds(D, D)]
    weights = [
        copies.local(exp_part, we_own),
        copies.push(exp_part, we_own, sib),
        copies.local(shr_part, ws_own),
        copies.push(shr_part, ws_own, sib),
    ]
    for copy in weights:
        copy.wait()

    def feed(block):
        def step(i, carry):
            lanes = pl.ds(pl.multiple_of(i * 256, 256), 256)
            value, rate = gelu_parts(nn(nb[block], we[:, lanes]))
            act[block, :, lanes] = value.astype(BF)
            slope[block, :, lanes] = rate.astype(BF)
            return carry

        lax.fori_loop(0, HID // 256, step, 0)
        return nn(act[block], ws[...])

    h_next[...] = mid[...] + feed(x)
    nb_sent.wait()
    psend[...] = feed(y).astype(BF)
    part_sent = copies.push(psend, precv, peer)
    saves = [copies.local(a, b) for a, b in ((nb, nb_o), (act, act_o), (slope, slope_o))]
    part_sent.wait()
    h_next[...] = h_next[...] + precv[...].astype(F32)
    for copy in saves:
        copy.wait()


def feed_fwd(mid, wf, scales):
    t = mid.shape[0]
    return call(
        feed_fwd_kernel, "feed_fwd", 1,
        [vmem(), hbm(), vmem()],
        [vmem()] + [hbm()] * 3,
        [sds((t, D), F32), sds((2, t, D), BF), sds((2, t, HID), BF), sds((2, t, HID), BF)],
        [
            pltpu.VMEM((D, HID), BF), pltpu.VMEM((HID, D), BF), pltpu.VMEM((2, t, D), BF),
            pltpu.VMEM((2, t, HID), BF), pltpu.VMEM((2, t, HID), BF),
            pltpu.VMEM((t, D), BF), pltpu.VMEM((t, D), BF),
        ],
        5, 4, 5 << 30, (mid, wf, scales),
    )


def feed_bwd_kernel(
    g, mid, wf, sc, nb_h, act_h, slope_h, mid_grad, wg_o, rows_o,
    we, ws, nb, act, slope, gl, hg, part, psend, precv, gown, gsend, grecv, lsem, ssem, rsem,
):
    d, x, c, peer, sib = place()
    y = 1 - x
    t = g.shape[0]
    copies = Copies(lsem, ssem, rsem, d)
    greet(d, peer, sib)
    gl[x] = g[...].astype(BF)
    g_sent = copies.push(gl.at[x], gl.at[x], peer)
    we_own, ws_own = we.at[:, rows_of(c, D)], ws.at[rows_of(c, D), :]
    exp_part, shr_part = wf.at[:, pl.ds(0, D)], wf.at[:, pl.ds(D, D)]
    weights = [
        copies.local(shr_part, ws_own),
        copies.push(shr_part, ws_own, sib),
        copies.local(exp_part, we_own),
        copies.push(exp_part, we_own, sib),
        copies.local(slope_h, slope),
        copies.local(act_h, act),
        copies.local(nb_h, nb),
    ]
    for copy in weights:
        copy.wait()

    def back(block):
        def step(i, carry):
            lanes = pl.ds(pl.multiple_of(i * 256, 256), 256)
            pulled = nt(gl[block], ws[lanes, :])
            hg[block, :, lanes] = (pulled * slope[block, :, lanes].astype(F32)).astype(BF)
            return carry

        lax.fori_loop(0, HID // 256, step, 0)
        return nt(hg[block], we[...])

    part[...] = back(x)
    g_sent.wait()
    psend[...] = back(y).astype(BF)
    part_sent = copies.push(psend, precv, peer)

    gl_all = gl[...].reshape(2 * t, D)
    nb_all = nb[...].reshape(2 * t, D)

    def grads(which, store):
        def step(i, carry):
            at = pl.ds(pl.multiple_of(i * 256, 256), 256)
            off = pl.ds(pl.multiple_of(which * D + i * 256, 256), 256)
            hg_part = hg[:, :, off].reshape(2 * t, 256)
            act_part = act[:, :, off].reshape(2 * t, 256)
            store(0, at, tn(nb_all, hg_part))
            store(1, at, tn(act_part, gl_all))
            return carry

        lax.fori_loop(0, D // 256, step, 0)

    def to_send(kind, at, value):
        if kind == 0:
            gsend[:, at] = value.astype(BF)
        else:
            gsend[at, pl.ds(D, D)] = value.astype(BF)

    def to_keep(kind, at, value):
        if kind == 0:
            gown[:, at] = value
        else:
            gown[at, pl.ds(D, D)] = value

    grads(1 - c, to_send)
    grad_sent = copies.push(gsend, grecv, sib)
    grads(c, to_keep)
    part_sent.wait()
    dy = part[...] + precv[...].astype(F32)
    back_mid, rows = norm_back(mid[...], sc[2:3, :], dy)
    mid_grad[...] = g[...] + back_mid
    rows_o[...] = rows
    grad_sent.wait()
    gsend[...] = (gown[...] + grecv[...].astype(F32)).astype(BF)
    copies.local(gsend, wg_o).wait()


def feed_bwd(g, mid, wf, scales, nb, act, slope):
    t = g.shape[0]
    return call(
        feed_bwd_kernel, "feed_bwd", 2,
        [vmem(), vmem(), hbm(), vmem(), hbm(), hbm(), hbm()],
        [vmem(), hbm(), vmem()],
        [sds((t, D), F32), sds((D, 2 * D), BF), sds((2, D), F32)],
        [
            pltpu.VMEM((D, HID), BF), pltpu.VMEM((HID, D), BF), pltpu.VMEM((2, t, D), BF),
            pltpu.VMEM((2, t, HID), BF), pltpu.VMEM((2, t, HID), BF), pltpu.VMEM((2, t, D), BF),
            pltpu.VMEM((2, t, HID), BF), pltpu.VMEM((t, D), F32), pltpu.VMEM((t, D), BF),
            pltpu.VMEM((t, D), BF), pltpu.VMEM((D, 2 * D), F32), pltpu.VMEM((D, 2 * D), BF),
            pltpu.VMEM((D, 2 * D), BF),
        ],
        6, 5, 10 << 30, (g, mid, wf, scales, nb, act, slope),
    )


def attend_bwd_kernel(
    mg, h, wa, sc, cs, bias, na, q, k, v, ctx, lse, g_prev, wg_o, rows_o,
    wt, wo, ml, cg, delta, dqt, dk, dv, kvsend, kvrecv, pg, part, psend, precv,
    gown, gsend, grecv, lsem, ssem, rsem,
):
    d, x, c, peer, sib = place()
    y = 1 - x
    t = mg.shape[0]
    copies = Copies(lsem, ssem, rsem, d)
    greet(d, peer, sib)
    ml[x] = mg[...].astype(BF)
    ml_sent = copies.push(ml.at[x], ml.at[x], peer)
    wt_own, wo_own = wt.at[rows_of(c, HALF), :], wo.at[:, rows_of(c, HALF)]
    tri_part, out_part = wa.at[:, pl.ds(0, TRI)], wa.at[:, pl.ds(TRI, HALF)]
    out_moves = [copies.local(out_part, wo_own), copies.push(out_part, wo_own, sib)]
    tri_moves = [copies.local(tri_part, wt_own), copies.push(tri_part, wt_own, sib)]
    dk[...] = jnp.zeros_like(dk)
    dv[...] = jnp.zeros_like(dv)
    for copy in out_moves:
        copy.wait()

    def attend(block):
        other = 1 - block
        pulled = nt(ml[block], wo[...])
        cg[block] = pulled.astype(BF)
        weighed = (cg[block].astype(F32) * ctx[block].astype(F32)).T
        for head in range(HALF // HD):
            delta[head : head + 1, :] = jnp.sum(
                weighed[head * HD : head * HD + HD, :], axis=0, keepdims=True
            )

        def pair_step(p, carry):
            lanes = pl.ds(pl.multiple_of(p * 128, 128), 128)
            q_pair, cg_pair = q[block, :, lanes], cg[block, :, lanes]
            for which in range(2):
                q_head, cg_head = half_of(q_pair, which), half_of(cg_pair, which)
                row = pl.ds(2 * p + which, 1)
                total, dots = lse[block, row, :], delta[row, :]
                turned = None
                for side in (block, other):
                    k_pair, v_pair = k[side, :, lanes], v[side, :, lanes]
                    scores = nt(k_pair, q_head)
                    if side is other:
                        scores = scores + bias[0]
                    probs = jnp.exp(scores - total)
                    score_grad = (probs * (nt(v_pair, cg_head) - dots)).astype(BF)
                    dv[side, :, lanes] += nn(probs.astype(BF), cg_head)
                    dk[side, :, lanes] += nn(score_grad, q_head)
                    piece = tn(k_pair, score_grad)
                    turned = piece if turned is None else turned + piece
                head = pl.ds(pl.multiple_of(p * 128 + which * HD, HD), HD)
                dqt[block, head, :] = turned[which * HD : which * HD + HD, :] * HD**-0.5
            return carry

        lax.fori_loop(0, HALF // 128, pair_step, 0)

    attend(x)
    ml_sent.wait()
    attend(y)
    theirs, mine = rows_of(1 - c, t), rows_of(c, t)
    for side in range(2):
        kvsend[side, :, pl.ds(0, HALF)] = dk[side, theirs, :].astype(BF)
        kvsend[side, :, pl.ds(HALF, HALF)] = dv[side, theirs, :].astype(BF)
    kv_sent = copies.push(kvsend, kvrecv, sib)

    def unturn(block, j, value):
        cosine, sine = cs[block, :, 0:128], cs[block, :, 128:256]
        rounded = value.astype(BF).astype(F32)
        pg[block, :, pl.ds(128 * j, 128)] = turn(rounded, cosine, -sine).astype(BF)

    for side in range(2):
        for j in range(3):
            unturn(side, j, dqt[side, 128 * j : 128 * j + 128, :].T)
    kv_sent.wait()
    for side in range(2):
        for j in range(3):
            at = pl.ds(128 * j, 128)
            unturn(side, 3 + j, dk[side, mine, at] + kvrecv[side, :, at].astype(F32))
            pg[side, :, pl.ds(D + 128 * j, 128)] = (
                dv[side, mine, at] + kvrecv[side, :, pl.ds(HALF + 128 * j, 128)].astype(F32)
            ).astype(BF)
    for copy in tri_moves:
        copy.wait()
    psend[...] = nt(pg[y], wt[...]).astype(BF)
    part_sent = copies.push(psend, precv, peer)
    part[...] = nt(pg[x], wt[...])

    ml_all = ml[...].reshape(2 * t, D)
    na_all = na[...].reshape(2 * t, D)
    ctx_all = ctx[...].reshape(2 * t, HALF)

    def grads(which, store):
        def step(i, carry):
            off = pl.ds(pl.multiple_of(which * HALF + i * 128, 128), 128)
            at = pl.ds(pl.multiple_of(i * 128, 128), 128)
            store(0, at, tn(na[:, :, off].reshape(2 * t, 128), pg[...].reshape(2 * t, TRI)))
            store(1, at, tn(ctx_all, ml[:, :, off].reshape(2 * t, 128)))
            return carry

        lax.fori_loop(0, HALF // 128, step, 0)

    def to_send(kind, at, value):
        if kind == 0:
            gsend[at, pl.ds(0, TRI)] = value.astype(BF)
        else:
            gsend[:, pl.ds(pl.multiple_of(TRI + at.start, 128), 128)] = value.astype(BF)

    def to_keep(kind, at, value):
        if kind == 0:
            gown[at, pl.ds(0, TRI)] = value
        else:
            gown[:, pl.ds(pl.multiple_of(TRI + at.start, 128), 128)] = value

    grads(1 - c, to_send)
    grad_sent = copies.push(gsend, grecv, sib)
    grads(c, to_keep)
    part_sent.wait()
    dy = part[...] + precv[...].astype(F32)
    back, rows = norm_back(h[...], sc[0:1, :], dy)
    g_prev[...] = mg[...] + back
    rows_o[...] = rows
    grad_sent.wait()
    gsend[...] = (gown[...] + grecv[...].astype(F32)).astype(BF)
    copies.local(gsend, wg_o).wait()


def attend_bwd(mg, h, wa, scales, tables, bias, saved):
    t = mg.shape[0]
    return call(
        attend_bwd_kernel, "attend_bwd", 3,
        [vmem(), vmem(), hbm(), vmem(), vmem(), pl.BlockSpec(memory_space=pltpu.SMEM)] + [vmem()] * 6,
        [vmem(), hbm(), vmem()],
        [sds((t, D), F32), sds((HALF, 2 * D), BF), sds((2, D), F32)],
        [
            pltpu.VMEM((D, TRI), BF), pltpu.VMEM((HALF, D), BF), pltpu.VMEM((2, t, D), BF),
            pltpu.VMEM((2, t, HALF), BF), pltpu.VMEM((8, t), F32), pltpu.VMEM((2, HALF, t), F32),
            pltpu.VMEM((2, 2 * t, HALF), F32), pltpu.VMEM((2, 2 * t, HALF), F32),
            pltpu.VMEM((2, t, D), BF), pltpu.VMEM((2, t, D), BF), pltpu.VMEM((2, t, TRI), BF),
            pltpu.VMEM((t, D), F32), pltpu.VMEM((t, D), BF), pltpu.VMEM((t, D), BF),
            pltpu.VMEM((HALF, 2 * D), F32), pltpu.VMEM((HALF, 2 * D), BF),
            pltpu.VMEM((HALF, 2 * D), BF),
        ],
        3, 6, 10 << 30, (mg, h, wa, scales, tables, bias, *saved),
    )


TRIPLE, OUTPUT, EXPAND, SHRINK = range(4)
KINDS = (TRIPLE, OUTPUT, EXPAND, SHRINK)
ZS = 4


class Spot:
    def __init__(self):
        s = lax.axis_index("seq")
        self.s = s
        self.x, self.c = lax.div(s, 2), lax.rem(s, 2)
        self.d = lax.axis_index("dp")
        self.z, self.y = lax.div(self.d, 2), lax.rem(self.d, 2)
        self.upper, self.odd = lax.div(self.z, 2), lax.rem(self.z, 2)
        self.sib, self.peer = s + 1 - 2 * self.c, lax.rem(s + 2, SEQ)
        self.across = self.d + 1 - 2 * self.y
        self.zs = ZS

    def count(self, kind):
        return ZS if kind == EXPAND else ZS // 2

    def origin(self, kind, j):
        if kind == TRIPLE:
            return 2 * self.c + j
        if kind == OUTPUT:
            return 2 * self.x + j
        return j if kind == EXPAND else 2 * j + self.x

    def own_slot(self, kind):
        return {TRIPLE: self.odd, OUTPUT: self.odd, EXPAND: self.z, SHRINK: self.upper}[kind]

    def if_owner(self, kind, act):
        if kind == EXPAND:
            act()
        elif kind == TRIPLE:
            pl.when(self.c == self.upper)(act)
        elif kind == OUTPUT:
            pl.when(self.x == self.upper)(act)
        else:
            pl.when(self.x == self.odd)(act)

    def naturals(self, kind):
        x, c = self.x, self.c
        if kind == TRIPLE:
            return ((0, 2 * x), (1, 2 * x + 1), (2, 2 * (1 - x)), (3, 2 * (1 - x) + 1))
        if kind == EXPAND:
            return ((0, 2 * c + x),)
        return ((0, 2 * c), (1, 2 * c + 1))

    def targets(self, kind):
        x, c = self.x, self.c
        if kind == TRIPLE:
            return ((c, 0, 2 * x + self.upper), (2 + c, 1, 2 * (1 - x) + self.upper))
        if kind == OUTPUT:
            return ((c, 0, 2 * self.upper + x),)
        if kind == EXPAND:
            return ((0, 0, 2 * c + x),)
        return ((c, 0, 2 * self.odd + x),)


class Saved(NamedTuple):
    na: Any
    q: Any
    k: Any
    k_t: Any
    v: Any
    ctx: Any
    ctx_t: Any
    lse: Any
    nb: Any
    act: Any
    slope: Any
    wt: Any
    wo: Any
    we: Any
    ws: Any


class ForwardIn(NamedTuple):
    h0: Any
    g0: Any
    sc_w: Any
    segments: Any
    tri_w: Any
    out_w: Any
    exp_w: Any
    shr_w: Any


class ForwardHead(NamedTuple):
    h_out: Any
    h_mid: Any
    mid_o0: Any
    mid_o1: Any
    sc_o: Any
    gl_o: Any
    cs_o: Any


class ForwardScratch(NamedTuple):
    cs: Any
    p_whole: Any
    p_half: Any
    p_out: Any
    p_exp: Any
    p_shr: Any
    gl: Any
    wt: Any
    wo: Any
    we: Any
    ws: Any
    hb: Any
    ob: Any
    scl: Any
    sc: Any
    na: Any
    q: Any
    k: Any
    v: Any
    ctxt: Any
    ctx: Any
    ctx_t: Any
    lse: Any
    nb: Any
    na_t: Any
    nb_t: Any
    k_t: Any
    v_t: Any
    act: Any
    slope: Any
    psend: Any
    precv: Any
    hs: Any
    mid: Any
    ssem: Any
    rsem: Any
    zero_ssem: Any
    zero_rsem: Any
    sc_ssem: Any
    sc_rsem: Any
    xs: Any
    xr: Any
    lsem: Any


class Refs:
    def __init__(self, *groups):
        for group in groups:
            for name, ref in zip(group._fields, group):
                setattr(self, name, ref)


def split(refs, *kinds):
    out, at = [], 0
    for kind in kinds:
        size = len(kind._fields)
        out.append(kind(*refs[at : at + size]))
        at += size
    return out


class Weights(Spot):
    def __init__(self, n, rows):
        super().__init__()
        self.n = n
        self.rows = rows
        self.source = {
            TRIPLE: (n.p_whole, n.p_half), OUTPUT: (n.p_out,), EXPAND: (n.p_exp,), SHRINK: (n.p_shr,)
        }

    def view(self, kind, layer, y, z, c):
        n, r = self.n, self.rows
        if kind == EXPAND:
            return n.we.at[layer, rows_of(2 * z + y, r), rows_of(c, D)]
        at = 2 * lax.rem(z, 2) + y
        if kind == TRIPLE:
            return n.wt.at[layer, pl.ds(pl.multiple_of(HALF * c + r * at, r), r), :]
        if kind == OUTPUT:
            return n.wo.at[layer, rows_of(at, r), rows_of(c, HALF)]
        return n.ws.at[layer, rows_of(c, HALF), rows_of(2 * lax.div(z, 2) + y, 4 * r)]

    def piece(self, kind, layer, number, to):
        n, r = self.n, self.rows
        x, c = lax.div(to, 2), lax.rem(to, 2)
        if kind == TRIPLE:
            start = pl.ds(pl.multiple_of(HALF * c + r * (2 * self.odd + self.y), r), r)
            return (n.wt.at[layer, start, rows_of(x + self.core_of(number), HALF)], n.hb.at[layer, self.core_of(number)])
        if kind == OUTPUT:
            return n.ob.at[layer, number]
        if kind == EXPAND:
            return self.view(kind, layer, self.y, self.z, c)
        rows = pl.ds(pl.multiple_of(HALF * c + 192 * number, 192), 192)
        return n.ws.at[layer, rows, rows_of(2 * self.upper + self.y, 4 * r)]

    @staticmethod
    def core_of(number):
        return lax.rem(number, 2)

    def landing(self, kind, layer, number, part, to):
        spot = self.piece(kind, layer, number, to)
        return spot[part] if kind == TRIPLE else spot

    def zero_copy(self, kind, layer, number, part, to):
        return pltpu.make_async_remote_copy(
            src_ref=self.source[kind][part].at[layer],
            dst_ref=self.landing(kind, layer, number, part, to),
            send_sem=self.n.zero_ssem.at[layer, kind, part],
            recv_sem=self.n.zero_rsem.at[layer, kind, number],
            device_id=(self.d, to),
            device_id_type=MESH,
        )

    def zero_here(self, kind, layer, number, part, to):
        return pltpu.make_async_copy(
            self.source[kind][part].at[layer], self.landing(kind, layer, number, part, to),
            self.n.zero_rsem.at[layer, kind, number],
        )

    def zero(self, kind, layer):
        for number, part, to in self.targets(kind):
            away = to != self.s
            place = (kind, layer, number, part, to)
            pl.when(away)(lambda place=place: self.zero_copy(*place).start())
            pl.when(jnp.logical_not(away))(lambda place=place: self.zero_here(*place).start())

    def remote(self, ref, kind, layer, stage, sent, slot, to):
        return pltpu.make_async_remote_copy(
            src_ref=ref,
            dst_ref=ref,
            send_sem=self.n.ssem.at[layer, kind, stage, sent],
            recv_sem=self.n.rsem.at[layer, kind, stage, slot],
            device_id=to,
            device_id_type=MESH,
        )

    def spread(self, kind, layer):
        def act():
            for number, _ in self.naturals(kind):
                part = 1 if kind == TRIPLE and number >= 2 else 0
                ref = self.landing(kind, layer, number, part, self.s)
                pltpu.make_async_remote_copy(
                    src_ref=ref, dst_ref=ref, send_sem=self.n.zero_ssem.at[layer, kind, part],
                    recv_sem=self.n.zero_rsem.at[layer, kind, number], device_id=(self.d, self.peer),
                    device_id_type=MESH,
                ).wait_recv()
            n, r = self.n, self.rows
            if kind == TRIPLE:
                start = HALF * self.c + r * (2 * self.odd + self.y)
                join(n.hb[layer, 0], n.hb[layer, 1], n.wt, layer, start, 2 * (1 - self.x) * HALF, r)
            elif kind == OUTPUT:
                join(n.ob[layer, 0], n.ob[layer, 1], n.wo, layer, r * (2 * self.odd + self.y), HALF * self.c, r)
            ref = self.view(kind, layer, self.y, self.z, self.c)
            slot = self.own_slot(kind)
            for k in range(1, ZS):
                other = lax.rem(self.z + k, ZS)
                self.remote(ref, kind, layer, 0, k, slot, (2 * other + self.y, self.s)).start()
            self.remote(ref, kind, layer, 1, slot, slot, (self.across, self.s)).start()

        self.if_owner(kind, act)

    def onward(self, kind, layer, j):
        z = self.origin(kind, j)

        @pl.when(z != self.z)
        def _():
            ref = self.view(kind, layer, self.y, z, self.c)
            self.remote(ref, kind, layer, 0, 0, j, (self.across, self.s)).wait_recv()
            self.remote(ref, kind, layer, 1, j, j, (self.across, self.s)).start()

    def onward_all(self, kind, layer):
        for j in range(self.count(kind)):
            self.onward(kind, layer, j)

    def arrive(self, kind, layer):
        for j in range(self.count(kind)):
            ref = self.view(kind, layer, 1 - self.y, self.origin(kind, j), self.c)
            self.remote(ref, kind, layer, 1, j, j, (self.across, self.s)).wait_recv()

    def finish(self, kind, layer):
        for number, part, to in self.targets(kind):
            place = (kind, layer, number, part, to)
            pl.when(to != self.s)(lambda place=place: self.zero_copy(*place).wait_send())

        def act():
            ref = self.view(kind, layer, self.y, self.z, self.c)
            for k in range(1, ZS):
                self.remote(ref, kind, layer, 0, k, 0, (self.across, self.s)).wait_send()

        self.if_owner(kind, act)
        for j in range(self.count(kind)):
            ref = self.view(kind, layer, self.y, self.origin(kind, j), self.c)
            self.remote(ref, kind, layer, 1, j, j, (self.across, self.s)).wait_send()


def join(first, second, into, layer, row, col, rows):
    half = rows // 2
    top, bottom = join_packed(first[rows:], second[rows:])
    all_rows = pl.ds(pl.multiple_of(row, half), rows)
    into[layer, all_rows, pl.ds(pl.multiple_of(col, 128), 128)] = first[:rows]
    middle = pl.ds(pl.multiple_of(col + 128, 128), 128)
    into[layer, pl.ds(pl.multiple_of(row, half), half), middle] = top
    into[layer, pl.ds(pl.multiple_of(row + half, half), half), middle] = bottom
    into[layer, all_rows, pl.ds(pl.multiple_of(col + 256, 128), 128)] = second[:rows]


def greet_all(w):
    barrier = pltpu.get_barrier_semaphore()

    def one(i, carry):
        z, s = lax.div(i, SEQ), lax.rem(i, SEQ)
        away = jnp.logical_or(z != w.z, s != w.s)

        @pl.when(away)
        def _():
            pl.semaphore_signal(barrier, inc=1, device_id=(2 * z + w.y, s), device_id_type=MESH)

        return carry

    lax.fori_loop(0, w.zs * SEQ, one, 0)
    pl.semaphore_signal(barrier, inc=1, device_id=(w.across, w.s), device_id_type=MESH)
    pl.semaphore_wait(barrier, w.zs * SEQ)


def left_half(shape):
    return lax.broadcasted_iota(jnp.int32, shape, 1) < HD


def join_packed(first, second):
    first, second = first.astype(F32), second.astype(F32)
    left = left_half(first.shape)
    top = jnp.where(left, first, second)
    bottom = pltpu.roll(jnp.where(left, second, first), HD, 1)
    return top.astype(BF), bottom.astype(BF)


def pack_wide(value):
    half = value.shape[0] // 2
    top, bottom = value[:half, 128:256], pltpu.roll(value[half:, 128:256], HD, 1)
    left = left_half(top.shape)
    first, second = jnp.where(left, top, bottom), jnp.where(left, bottom, top)
    return (
        jnp.concatenate([value[:, :128], first], axis=0),
        jnp.concatenate([value[:, 256:], second], axis=0),
    )


def gather_scales_start(w):
    n = w.n
    mine = n.scl.at[w.y, w.z, w.s]
    mine[...] = jnp.zeros_like(mine)
    wide = n.sc_w.shape[-1]
    for layer in range(LAYERS):
        mine[layer : layer + 1, 0:wide] = n.sc_w[layer].astype(BF).astype(F32)

    def one(i, carry):
        z, s = lax.div(i, SEQ), lax.rem(i, SEQ)

        @pl.when(jnp.logical_or(z != w.z, s != w.s))
        def _():
            pltpu.make_async_remote_copy(
                src_ref=mine, dst_ref=mine, send_sem=n.sc_ssem.at[i],
                recv_sem=n.sc_rsem.at[w.z * SEQ + w.s], device_id=(2 * z + w.y, s), device_id_type=MESH,
            ).start()

        return carry

    lax.fori_loop(0, w.zs * SEQ, one, 0)


def gather_scales_end(w):
    n = w.n

    def one(i, carry):
        z, s = lax.div(i, SEQ), lax.rem(i, SEQ)

        @pl.when(jnp.logical_or(z != w.z, s != w.s))
        def _():
            slot = n.scl.at[w.y, z, s]
            copy = pltpu.make_async_remote_copy(
                src_ref=slot, dst_ref=slot, send_sem=n.sc_ssem.at[i], recv_sem=n.sc_rsem.at[i],
                device_id=(2 * z + w.y, s), device_id_type=MESH,
            )
            copy.wait_recv()
            copy.wait_send()

        return carry

    lax.fori_loop(0, w.zs * SEQ, one, 0)
    count = w.zs * SEQ
    plane = n.scl.at[w.y]
    copy = pltpu.make_async_remote_copy(
        src_ref=plane, dst_ref=plane, send_sem=n.sc_ssem.at[count], recv_sem=n.sc_rsem.at[count],
        device_id=(w.across, w.s), device_id_type=MESH,
    )
    copy.start()
    copy.wait()
    wide = n.sc.shape[-1] // (2 * w.zs)
    for s in range(SEQ):
        both = [n.scl[d % 2, d // 2, s][:, :wide] for d in range(2 * w.zs)]
        rows = jnp.concatenate(both, axis=1)
        for layer in range(LAYERS):
            n.sc[layer, s : s + 1, :] = rows[layer : layer + 1, :]


def fwd_kernel(dp, *refs):
    ins, outs, saved0, saved1, scratch = split(refs, ForwardIn, ForwardHead, Saved, Saved, ForwardScratch)
    n = Refs(ins, outs, scratch)
    saved = (saved0, saved1)
    rows = n.exp_w.shape[1]
    t = n.h0.shape[0]
    w = Weights(n, rows)
    x, c, peer, sib = w.x, w.c, w.peer, w.sib
    y = 1 - x
    parts = (pl.ds(0, t // 2), pl.ds(t // 2, t // 2))
    copies = Copies(n.lsem, n.xs, n.xr, w.d)
    waits = []

    def save(src, dst):
        waits.append(copies.local(src, dst))

    half_rows = rows // 2

    def pack(low, into, layer, core):
        wide, rest = (low[:, :128], low[:, 128:]) if core == 0 else (low[:, 64:], low[:, :64])
        ends = [rest[:half_rows], rest[half_rows:]]
        into[layer, pl.ds(0, rows), :] = wide.astype(BF)
        into[layer, pl.ds(rows, half_rows), :] = jnp.concatenate(ends if core == 0 else ends[::-1], axis=1).astype(BF)

    def round_triple(layer):
        for core in range(2):

            @pl.when(c == core)
            def _():
                tri = n.tri_w[layer]
                n.p_whole[layer] = (tri[:, :HALF] if core == 0 else tri[:, 192:]).astype(BF)
                pack(tri[:, HALF:] if core == 0 else tri[:, :192], n.p_half, layer, core)

    def round_output(layer):
        for core in range(2):
            pl.when(c == core)(lambda: pack(n.out_w[layer], n.p_out, layer, core))

    whole_group = n.segments[0] == n.segments[n.segments.shape[0] - 1]
    bias = jnp.where(whole_group, 0.0, MASKED)

    def make_tables():
        lane = lax.broadcasted_iota(jnp.int32, (t, 128), 1)
        token = lax.broadcasted_iota(jnp.int32, (t, 128), 0) + c * t
        step = lax.rem(lane, HD // 2).astype(F32)
        inverse = jnp.exp(step * (-2.0 / HD * math.log(ROTARY_BASE)))
        sign = jnp.where(lax.rem(lane, HD) < HD // 2, -1.0, 1.0)
        for block in range(2):
            offset = jnp.where(whole_group, block * 2 * t, 0)
            angle = (token + offset).astype(F32) * inverse
            n.cs[block, :, 0:128] = jnp.cos(angle)
            n.cs[block, :, 128:256] = jnp.sin(angle) * sign

    round_triple(0)
    greet_all(w)
    w.zero(TRIPLE, 0)
    gather_scales_start(w)
    round_output(0)
    w.zero(OUTPUT, 0)
    n.p_exp[...] = n.exp_w[...].astype(BF)
    w.zero(EXPAND, 0)
    n.p_shr[...] = n.shr_w[...].astype(BF)
    w.zero(SHRINK, 0)
    round_triple(1)
    round_output(1)
    for kind in KINDS:
        w.zero(kind, 1)
    for layer in range(LAYERS):
        for kind in KINDS:
            w.spread(kind, layer)
    n.hs[0] = n.h0[...]
    xhat, _ = norm_stats(n.hs[0])
    gather_scales_end(w)

    def share_tri(layer):
        own = n.wt.at[layer, rows_of(c, HALF), :]
        return copies.push(own, own, sib)

    def share_out(layer):
        own = n.wo.at[layer, :, rows_of(c, HALF)]
        return copies.push(own, own, sib)

    def share_shr(layer):
        own = n.ws.at[layer, rows_of(c, HALF), :]
        return copies.push(own, own, sib)

    def share_exp(layer):
        own = n.we.at[layer, :, rows_of(c, D)]
        return copies.push(own, own, sib)

    for layer in range(LAYERS):
        last = layer == LAYERS - 1
        if layer:
            xhat, _ = norm_stats(n.hs[layer])
        n.na[layer, x] = (xhat * n.sc[layer, 0:1, :] + n.sc[layer, 1:2, :]).astype(BF)
        na_sent = copies.push(n.na.at[layer, x], n.na.at[layer, x], peer)
        if last:
            n.gl[x] = n.g0[...].astype(BF)
            gl_sent = copies.push(n.gl.at[x], n.gl.at[x], peer)
        if layer == 0:
            make_tables()
            save(n.cs, n.cs_o)
            w.onward_all(TRIPLE, 0)
            w.onward_all(OUTPUT, 0)
            w.arrive(TRIPLE, 0)
            tri_sent = share_tri(0)
        tri_sent.wait()

        def project(block):
            cosine, sine = n.cs[block, :, 0:128], n.cs[block, :, 128:256]
            for j in range(9):
                part = nn(n.na[layer, block], n.wt[layer, :, 128 * j : 128 * j + 128])
                lanes = pl.ds(128 * (j % 3), 128)
                if j < 3:
                    n.q[layer, block, :, lanes] = (turn(part, cosine, sine) * HD**-0.5).astype(BF)
                elif j < 6:
                    n.k[layer, block, rows_of(c, t), lanes] = turn(part, cosine, sine).astype(BF)
                else:
                    n.v[layer, block, rows_of(c, t), lanes] = part.astype(BF)

        def share(block):
            at = (layer, block, rows_of(c, t))
            return [
                copies.push(n.k.at[at], n.k.at[at], sib),
                copies.push(n.v.at[at], n.v.at[at], sib),
            ]

        project(x)
        shared = share(x)
        na_sent.wait()
        project(y)
        shared += share(y)
        w.arrive(OUTPUT, layer)
        out_sent = share_out(layer)
        for copy in shared:
            copy.wait()
        for block in range(2):
            n.v_t[block] = n.v[layer, block].T
        save(n.q.at[layer], saved[layer].q)
        save(n.k.at[layer], saved[layer].k)
        save(n.v.at[layer], saved[layer].v)

        def attend(block, pump):
            other = 1 - block

            def pair_step(p, carry):
                pump(p)
                lanes = pl.ds(pl.multiple_of(p * 128, 128), 128)
                q_pair = n.q[layer, block, :, lanes]
                k_same, k_cross = n.k[layer, block, :, lanes], n.k[layer, other, :, lanes]
                for which in range(2):
                    q_head = half_of(q_pair, which)
                    s_same = nt(k_same, q_head)
                    s_cross = nt(k_cross, q_head) + bias
                    top = jnp.maximum(
                        jnp.max(s_same, axis=0, keepdims=True), jnp.max(s_cross, axis=0, keepdims=True)
                    )
                    e_same = jnp.exp(s_same - top)
                    e_cross = jnp.exp(s_cross - top)
                    total = jnp.sum(e_same, axis=0, keepdims=True) + jnp.sum(
                        e_cross, axis=0, keepdims=True
                    )
                    head = pl.ds(pl.multiple_of(p * 128 + which * HD, HD), HD)
                    mixed = nn(n.v_t[block, head, :], e_same.astype(BF)) + nn(n.v_t[other, head, :], e_cross.astype(BF))
                    n.ctxt[head, :] = mixed / total
                    n.lse[layer, block, pl.ds(2 * p + which, 1), :] = top + jnp.log(total)
                return carry

            lax.fori_loop(0, HALF // 128, pair_step, 0)
            n.ctx_t[layer, :, rows_of(block, t)] = n.ctxt[...].astype(BF)
            n.ctx[layer, block] = n.ctxt[...].T.astype(BF)

        def early(p):
            kind = SHRINK if layer else EXPAND
            pl.when(p > 0)(lambda: w.onward(kind, layer, p - 1))

        attend(y, early)
        if last:
            gl_sent.wait()
            save(n.gl, n.gl_o)
        out_sent.wait()
        use = 2 * layer
        n.psend[use] = nn(n.ctx[layer, y], n.wo[layer]).astype(BF)
        part_sent = copies.push(n.psend.at[use], n.precv.at[use], peer)


        def late(p):
            if layer == 0:
                pl.when(p == 0)(lambda: w.onward(EXPAND, layer, 2))
                pl.when(p == 0)(lambda: w.onward(EXPAND, layer, 3))
                pl.when(p > 0)(lambda: w.onward(SHRINK, layer, p - 1))

        attend(x, late)
        n.mid[layer] = n.hs[layer] + nn(n.ctx[layer, x], n.wo[layer])
        save(n.ctx.at[layer], saved[layer].ctx)
        save(n.lse.at[layer], saved[layer].lse)
        save(n.wt.at[layer], saved[layer].wt)
        save(n.wo.at[layer], saved[layer].wo)
        save(n.ctx_t.at[layer], saved[layer].ctx_t)
        for block in range(2):
            n.na_t[layer, :, block * t : block * t + t] = n.na[layer, block].T
            n.k_t[layer, block] = n.k[layer, block].T
        save(n.na_t.at[layer], saved[layer].na)
        save(n.k_t.at[layer], saved[layer].k_t)
        part_sent.wait()
        n.mid[layer] = n.mid[layer] + n.precv[use].astype(F32)
        save(n.mid.at[layer], (n.mid_o0, n.mid_o1)[layer])

        xhat, _ = norm_stats(n.mid[layer])
        n.nb[layer, x] = (xhat * n.sc[layer, 2:3, :] + n.sc[layer, 3:4, :]).astype(BF)
        nb_sent = [copies.push(n.nb.at[layer, x, part], n.nb.at[layer, x, part], peer) for part in parts]
        w.arrive(EXPAND, layer)
        exp_sent = share_exp(layer)
        w.arrive(SHRINK, layer)
        shr_sent = share_shr(layer)
        exp_sent.wait()
        save(n.we.at[layer], saved[layer].we)

        def feed(block, part, pump):
            def step(i, carry):
                pump(i)
                lanes = pl.ds(pl.multiple_of(i * 256, 256), 256)
                value, rate = gelu_parts(nn(n.nb[layer, block, part, :], n.we[layer, :, lanes]))
                n.act[layer, block, part, lanes] = value.astype(BF)
                n.slope[layer, block, part, lanes] = rate.astype(BF)
                return carry

            lax.fori_loop(0, HID // 256, step, 0)

        def pump(i):
            if not last:

                @pl.when(i < 2)
                def _():
                    w.onward(TRIPLE, layer + 1, i)
                    w.onward(OUTPUT, layer + 1, i)

        feed(x, pl.ds(0, t), lambda i: None)
        shr_sent.wait()
        save(n.ws.at[layer], saved[layer].ws)
        n.hs[layer + 1] = n.mid[layer] + nt(n.act[layer, x], n.ws[layer])
        use = 2 * layer + 1
        part_sent = []
        for number, part in enumerate(parts):
            nb_sent[number].wait()
            feed(y, part, pump if number == 0 else lambda i: None)
            n.psend[use, part, :] = nt(n.act[layer, y, part, :], n.ws[layer]).astype(BF)
            part_sent.append(copies.push(n.psend.at[use, part], n.precv.at[use, part], peer))
        for block in range(2):
            n.nb_t[layer, :, block * t : block * t + t] = n.nb[layer, block].T
        save(n.nb_t.at[layer], saved[layer].nb)
        save(n.act.at[layer], saved[layer].act)
        save(n.slope.at[layer], saved[layer].slope)
        if not last:
            w.onward_all(EXPAND, layer + 1)
            w.arrive(TRIPLE, layer + 1)
            tri_sent = share_tri(layer + 1)
        for copy in part_sent:
            copy.wait()
        n.hs[layer + 1] = n.hs[layer + 1] + n.precv[use].astype(F32)

    n.h_out[...] = n.hs[LAYERS]
    n.sc_o[...] = n.sc[...]
    save(n.hs.at[1], n.h_mid)
    for copy in waits:
        copy.wait()
    for layer in range(LAYERS):
        for kind in KINDS:
            w.finish(kind, layer)


def forward_all(dp, h, g, scales_weight, segments, shards):
    t = h.shape[0]
    zs, packed = dp // 2, 3 * (D // dp) // 2
    per_layer = [
        sds((D, 2 * t), BF), sds((2, t, HALF), BF), sds((2, 2 * t, HALF), BF), sds((2, HALF, 2 * t), BF), sds((2, 2 * t, HALF), BF),
        sds((2, t, HALF), BF), sds((HALF, 2 * t), BF), sds((2, 8, t), F32), sds((D, 2 * t), BF), sds((2, t, HID), BF),
        sds((2, t, HID), BF), sds((D, TRI), BF), sds((HALF, D), BF), sds((D, HID), BF), sds((D, HID), BF),
    ]
    token = sds((t, D), F32)
    outs = [token, token, token, token, sds((LAYERS, 4, D), F32), sds((2, t, D), BF), sds((2, t, 256), F32), *per_layer, *per_layer]
    specs = [vmem(), hbm(), hbm(), hbm(), vmem(), hbm(), hbm(), *([hbm()] * (2 * len(per_layer)))]
    n_layers = LAYERS
    rows = D // dp
    scratch = [
        pltpu.VMEM((2, t, 256), F32), pltpu.VMEM((n_layers, rows, HALF), BF), pltpu.VMEM((n_layers, packed, 128), BF),
        pltpu.VMEM((n_layers, packed, 128), BF), pltpu.VMEM((n_layers, rows, D), BF),
        pltpu.VMEM((n_layers, 192, 4 * rows), BF), pltpu.VMEM((2, t, D), BF),
        pltpu.VMEM((n_layers, D, TRI), BF), pltpu.VMEM((n_layers, HALF, D), BF),
        pltpu.VMEM((n_layers, D, HID), BF), pltpu.VMEM((n_layers, D, HID), BF),
        pltpu.VMEM((n_layers, 2, packed, 128), BF), pltpu.VMEM((n_layers, 2, packed, 128), BF),
        pltpu.VMEM((2, zs, SEQ, 8, 128), F32),
        pltpu.VMEM((n_layers, 4, D), F32), pltpu.VMEM((n_layers, 2, t, D), BF),
        pltpu.VMEM((n_layers, 2, t, HALF), BF), pltpu.VMEM((n_layers, 2, 2 * t, HALF), BF),
        pltpu.VMEM((n_layers, 2, 2 * t, HALF), BF), pltpu.VMEM((HALF, t), F32),
        pltpu.VMEM((n_layers, 2, t, HALF), BF), pltpu.VMEM((n_layers, HALF, 2 * t), BF),
        pltpu.VMEM((n_layers, 2, 8, t), F32), pltpu.VMEM((n_layers, 2, t, D), BF),
        pltpu.VMEM((n_layers, D, 2 * t), BF), pltpu.VMEM((n_layers, D, 2 * t), BF),
        pltpu.VMEM((n_layers, 2, HALF, 2 * t), BF), pltpu.VMEM((2, HALF, 2 * t), BF),
        pltpu.VMEM((n_layers, 2, t, HID), BF),
        pltpu.VMEM((n_layers, 2, t, HID), BF), pltpu.VMEM((2 * n_layers, t, D), BF),
        pltpu.VMEM((2 * n_layers, t, D), BF), pltpu.VMEM((n_layers + 1, t, D), F32),
        pltpu.VMEM((n_layers, t, D), F32),
        pltpu.SemaphoreType.DMA((n_layers, len(KINDS), 2, zs)),
        pltpu.SemaphoreType.DMA((n_layers, len(KINDS), 2, zs)),
        pltpu.SemaphoreType.DMA((n_layers, len(KINDS), 2)), pltpu.SemaphoreType.DMA((n_layers, len(KINDS), 4)),
        pltpu.SemaphoreType.DMA((zs * SEQ + 1,)), pltpu.SemaphoreType.DMA((zs * SEQ + 1,)),
        pltpu.SemaphoreType.DMA((32,)), pltpu.SemaphoreType.DMA((32,)), pltpu.SemaphoreType.DMA((40,)),
    ]
    results = pl.pallas_call(
        functools.partial(fwd_kernel, dp),
        name="forward",
        out_shape=outs,
        in_specs=[*([vmem()] * 3), pl.BlockSpec(memory_space=pltpu.SMEM), *([vmem()] * 4)],
        out_specs=specs,
        scratch_shapes=scratch,
        cost_estimate=pl.CostEstimate(flops=22 << 30, bytes_accessed=32 << 20, transcendentals=0),
        compiler_params=pltpu.CompilerParams(
            collective_id=4, has_side_effects=True, vmem_limit_bytes=VMEM_BYTES
        ),
    )(h, g, scales_weight, segments, *shards)
    return split(results, ForwardHead, Saved, Saved)


class Sums(Spot):
    def __init__(self, n, rows):
        super().__init__()
        self.n = n
        self.rows = rows
        self.landed = {TRIPLE: n.y_tri, OUTPUT: n.y_out, EXPAND: n.y_exp, SHRINK: n.y_shr}
        self.owned = {TRIPLE: n.z_tri, OUTPUT: n.z_out, EXPAND: n.z_exp, SHRINK: n.z_shr}
        self.final = {TRIPLE: (n.f_whole, n.f_half), OUTPUT: (n.f_out,), EXPAND: (n.f_exp,), SHRINK: (n.f_shr,)}

    def view(self, kind, layer, y, z):
        n, r = self.n, self.rows
        if kind == EXPAND:
            return n.ge.at[layer, rows_of(2 * z + y, r), :]
        if kind == SHRINK:
            return n.gs.at[layer, :, rows_of(2 * lax.div(z, 2) + y, 4 * r)]
        return (n.gt if kind == TRIPLE else n.go).at[layer, rows_of(2 * lax.rem(z, 2) + y, r), :]

    def remote(self, src, dst, kind, layer, stage, sent, slot, to):
        return pltpu.make_async_remote_copy(
            src_ref=src,
            dst_ref=dst,
            send_sem=self.n.ssem.at[layer, kind, stage, sent],
            recv_sem=self.n.rsem.at[layer, kind, stage, slot],
            device_id=to,
            device_id_type=MESH,
        )

    def across_copy(self, kind, layer, j):
        return self.remote(
            self.view(kind, layer, 1 - self.y, self.origin(kind, j)), self.landed[kind].at[layer, j],
            kind, layer, 0, j, j, (self.across, self.s),
        )

    def across_all(self, kind, layer):
        for j in range(self.count(kind)):
            self.across_copy(kind, layer, j).start()

    def along_copy(self, kind, layer, j):
        z = self.origin(kind, j)
        slot = lax.rem(self.z - z + ZS - 1, ZS)
        mine = self.view(kind, layer, self.y, z)
        return self.remote(mine, self.owned[kind].at[layer, slot], kind, layer, 1, j, slot, (2 * z + self.y, self.s))

    def along(self, kind, layer, j):
        z = self.origin(kind, j)
        self.across_copy(kind, layer, j).wait_recv()
        mine = self.view(kind, layer, self.y, z)
        mine[...] = (mine[...].astype(F32) + self.landed[kind][layer, j].astype(F32)).astype(BF)
        pl.when(z != self.z)(lambda: self.along_copy(kind, layer, j).start())

    def along_all(self, kind, layer):
        for j in range(self.count(kind)):
            self.along(kind, layer, j)

    def parts(self, kind, layer):
        n = self.n
        mine = self.view(kind, layer, self.y, self.z)
        if kind == TRIPLE:
            return (
                mine.at[:, rows_of(self.x, HALF)], mine.at[:, rows_of(self.x + 1, HALF)],
                n.half_out.at[layer, 0], n.half_out.at[layer, 1],
            )
        if kind == OUTPUT:
            return n.out_out.at[layer, 0], n.out_out.at[layer, 1]
        return (mine,) if kind == EXPAND else (mine.at[pl.ds(0, 192), :], mine.at[pl.ds(192, 192), :])

    def home_copy(self, kind, layer, number, to, here=False):
        src = self.parts(kind, layer)[number]
        part = 1 if kind == TRIPLE and number >= 2 else 0
        dst = self.final[kind][part].at[layer]
        sem = self.n.home_rsem.at[layer, kind, part]
        if here:
            return pltpu.make_async_copy(src, dst, sem)
        return pltpu.make_async_remote_copy(
            src_ref=src, dst_ref=dst, send_sem=self.n.home_ssem.at[layer, kind, number], recv_sem=sem,
            device_id=(self.d, to), device_id_type=MESH,
        )

    def total(self, kind, layer):
        n = self.n

        def act():
            for slot in range(ZS - 1):
                ref = self.owned[kind].at[layer, slot]
                self.remote(ref, ref, kind, layer, 1, 0, slot, (self.across, self.s)).wait_recv()
            mine = self.view(kind, layer, self.y, self.z)
            value = mine[...].astype(F32)
            for slot in range(ZS - 1):
                value = value + self.owned[kind][layer, slot].astype(F32)
            n.squares[...] = n.squares[...] + squared(value)
            mine[...] = value.astype(BF)
            if kind == OUTPUT:
                first, second = pack_wide(value)
                n.out_out[layer, 0] = first.astype(BF)
                n.out_out[layer, 1] = second.astype(BF)
            if kind == TRIPLE:
                cut = mine[:, rows_of(2 * (1 - self.x), HALF)].astype(F32)
                first, second = pack_wide(cut)
                n.half_out[layer, 0] = first.astype(BF)
                n.half_out[layer, 1] = second.astype(BF)
            for number, to in self.naturals(kind):
                away = to != self.s
                place = (kind, layer, number, to)
                pl.when(away)(lambda place=place: self.home_copy(*place).start())
                pl.when(jnp.logical_not(away))(lambda place=place: self.home_copy(*place, True).start())

        self.if_owner(kind, act)

    def home(self, kind, layer):
        for part, final in enumerate(self.final[kind]):
            ref = final.at[layer]
            pltpu.make_async_remote_copy(
                src_ref=ref, dst_ref=ref, send_sem=self.n.home_ssem.at[layer, kind, 0],
                recv_sem=self.n.home_rsem.at[layer, kind, part], device_id=(self.d, self.peer), device_id_type=MESH,
            ).wait_recv()

    def finish(self, kind, layer):
        for j in range(self.count(kind)):
            self.across_copy(kind, layer, j).wait_send()
            pl.when(self.origin(kind, j) != self.z)(
                lambda j=j: self.along_copy(kind, layer, j).wait_send()
            )

        def act():
            for number, to in self.naturals(kind):
                place = (kind, layer, number, to)
                pl.when(to != self.s)(lambda place=place: self.home_copy(*place).wait_send())

        self.if_owner(kind, act)


def squared(value):
    return jnp.sum(jnp.sum(value * value, axis=1, keepdims=True), axis=0, keepdims=True)


def everywhere_start(w, use, buf):
    n = w.n
    mine = buf.at[w.y, w.z, w.s]

    def one(i, carry):
        z, s = lax.div(i, SEQ), lax.rem(i, SEQ)

        @pl.when(jnp.logical_or(z != w.z, s != w.s))
        def _():
            pltpu.make_async_remote_copy(
                src_ref=mine, dst_ref=mine, send_sem=n.ev_ssem.at[use, i],
                recv_sem=n.ev_rsem.at[use, w.z * SEQ + w.s], device_id=(2 * z + w.y, s), device_id_type=MESH,
            ).start()

        return carry

    lax.fori_loop(0, w.zs * SEQ, one, 0)


def everywhere_end(w, use, buf, pair):
    n = w.n

    def one(i, carry):
        z, s = lax.div(i, SEQ), lax.rem(i, SEQ)

        @pl.when(jnp.logical_or(z != w.z, s != w.s))
        def _():
            slot = buf.at[w.y, z, s]
            copy = pltpu.make_async_remote_copy(
                src_ref=slot, dst_ref=slot, send_sem=n.ev_ssem.at[use, i], recv_sem=n.ev_rsem.at[use, i],
                device_id=(2 * z + w.y, s), device_id_type=MESH,
            )
            copy.wait_recv()
            copy.wait_send()

        return carry

    lax.fori_loop(0, w.zs * SEQ, one, 0)

    def add(i, total):
        return total + buf[w.y, lax.div(i, SEQ), lax.rem(i, SEQ)]

    pair[w.y] = lax.fori_loop(1, w.zs * SEQ, add, buf[w.y, 0, 0])
    count = w.zs * SEQ
    copy = pltpu.make_async_remote_copy(
        src_ref=pair.at[w.y], dst_ref=pair.at[w.y], send_sem=n.ev_ssem.at[use, count],
        recv_sem=n.ev_rsem.at[use, count], device_id=(w.across, w.s), device_id_type=MESH,
    )
    copy.start()
    copy.wait()
    return pair[0] + pair[1]


class Loaded(NamedTuple):
    na: Any
    q: Any
    k: Any
    k_t: Any
    v: Any
    ctx: Any
    ctx_t: Any
    lse: Any
    nb: Any
    act: Any
    slope: Any
    wt: Any
    wo: Any
    we: Any
    ws: Any
    h: Any
    mid: Any


class BackwardIn(NamedTuple):
    g0: Any
    gl_h: Any
    sc: Any
    cs: Any
    segments: Any


class BackwardOut(NamedTuple):
    g_out: Any
    scale_o: Any
    norm_o: Any
    tri_g: Any
    out_g: Any
    exp_g: Any
    shr_g: Any


class BackwardScratch(NamedTuple):
    gl: Any
    gl_t: Any
    hg: Any
    ml: Any
    cg: Any
    delta: Any
    dqt: Any
    dk: Any
    dv: Any
    kvsend: Any
    kvrecv: Any
    pg: Any
    part: Any
    psend: Any
    precv: Any
    gs_exp: Any
    gr_exp: Any
    gs_shr: Any
    gr_shr: Any
    gr_att: Any
    gt: Any
    go: Any
    ge: Any
    gs: Any
    y_tri: Any
    y_out: Any
    y_exp: Any
    y_shr: Any
    z_tri: Any
    z_out: Any
    z_exp: Any
    z_shr: Any
    half_out: Any
    out_out: Any
    f_whole: Any
    f_half: Any
    f_out: Any
    f_exp: Any
    f_shr: Any
    squares: Any
    early: Any
    early_pair: Any
    late: Any
    late_pair: Any
    sq: Any
    sq_pair: Any
    ssem: Any
    rsem: Any
    home_ssem: Any
    home_rsem: Any
    ev_ssem: Any
    ev_rsem: Any
    xs: Any
    xr: Any
    lsem: Any


def bwd_kernel(dp, *refs):
    ins, saved0, saved1, outs, loaded, scratch = split(
        refs, BackwardIn, Loaded, Loaded, BackwardOut, Loaded, BackwardScratch
    )
    n = Refs(ins, outs, loaded, scratch)
    saved = (saved0, saved1)
    t = n.g0.shape[0]
    w = Sums(n, D // dp)
    x, c, peer, sib = w.x, w.c, w.peer, w.sib
    y = 1 - x
    bias = jnp.where(n.segments[0] == n.segments[n.segments.shape[0] - 1], 0.0, MASKED)
    parts = (pl.ds(0, t // 2), pl.ds(t // 2, t // 2))
    copies = Copies(n.lsem, n.xs, n.xr, w.d)
    loading = {}

    def load(layer, *wanted):
        for place in wanted:
            loading[place] = copies.local(saved[layer][place], loaded[place])

    def ready(*wanted):
        for place in wanted:
            loading[place].wait()

    na, q, k, k_t, v, ctx, ctx_t, lse, nb, act, slope, wt, wo, we, ws, h, mid = range(len(Loaded._fields))
    feed_places = (ws, slope, we, act, nb, mid)
    attend_places = (wo, ctx, q, k, v, lse, k_t, wt, na, ctx_t, h)
    top_gl = copies.local(n.gl_h, n.gl.at[LAYERS - 1])
    load(LAYERS - 1, *feed_places, *attend_places)
    greet_all(w)
    n.g_out[...] = n.g0[...]

    for layer in reversed(range(LAYERS)):
        top = layer == LAYERS - 1

        if top:
            top_gl.wait()
        else:
            n.gl[layer, x] = n.g_out[...].astype(BF)
            g_sent = [copies.push(n.gl.at[layer, x, part], n.gl.at[layer, x, part], peer) for part in parts]
        ready(ws, slope, we)

        def back(block, part):
            def step(i, carry):
                lanes = pl.ds(pl.multiple_of(i * 256, 256), 256)
                pulled = nn(n.gl[layer, block, part, :], n.ws[:, lanes])
                n.hg[block, part, lanes] = (pulled * n.slope[block, part, lanes].astype(F32)).astype(BF)
                return carry

            lax.fori_loop(0, HID // 256, step, 0)
            return nt(n.hg[block, part, :], n.we[...])

        def pump_tri(i):
            if not top:

                @pl.when(i < 2)
                def _():
                    w.along(TRIPLE, layer + 1, i)
                    w.along(OUTPUT, layer + 1, i)

        n.part[...] = back(x, pl.ds(0, t))
        use = 2 * layer
        part_sent = []
        for number, part in enumerate(parts):
            if not top:
                g_sent[number].wait()
            n.psend[part, :] = back(y, part).astype(BF)
            part_sent.append(copies.push(n.psend.at[part], n.precv.at[use, part], peer))
        ready(act, nb, mid)
        for block in range(2):
            n.gl_t[:, block * t : block * t + t] = n.gl[layer, block].T

        def exp_tile(which, i):
            off = pl.ds(pl.multiple_of(which * D + i * 256, 256), 256)
            return nn(n.nb[...], n.hg[:, :, off].reshape(2 * t, 256))

        def shr_tile(which, i):
            off = pl.ds(pl.multiple_of(i * 256, 256), 256)
            return nn(n.gl_t[rows_of(which, HALF), :], n.act[:, :, off].reshape(2 * t, 256))

        def send_exp(i, carry):
            at = pl.ds(pl.multiple_of(i * 256, 256), 256)
            n.gs_exp[:, at] = exp_tile(1 - c, i).astype(BF)
            return carry

        def send_shr(i, carry):
            at = pl.ds(pl.multiple_of(i * 256, 256), 256)
            n.gs_shr[:, at] = shr_tile(1 - c, i).astype(BF)
            return carry

        lax.fori_loop(0, D // 256, send_exp, 0)
        exp_sent = copies.push(n.gs_exp, n.gr_exp, sib)
        lax.fori_loop(0, HID // 256, send_shr, 0)
        shr_sent = copies.push(n.gs_shr, n.gr_shr, sib)

        def keep_exp(i, carry):
            at = pl.ds(pl.multiple_of(i * 256, 256), 256)
            n.ge[layer, :, at] = (exp_tile(c, i) + n.gr_exp[:, at].astype(F32)).astype(BF)
            return carry

        def keep_shr(i, carry):
            pump_tri(i)
            at = pl.ds(pl.multiple_of(i * 256, 256), 256)
            n.gs[layer, :, at] = (shr_tile(c, i) + n.gr_shr[:, at].astype(F32)).astype(BF)
            return carry

        exp_sent.wait()
        lax.fori_loop(0, D // 256, keep_exp, 0)
        w.across_all(EXPAND, layer)
        shr_sent.wait()
        lax.fori_loop(0, HID // 256, keep_shr, 0)
        w.across_all(SHRINK, layer)
        for copy in part_sent:
            copy.wait()
        dy = n.part[...] + n.precv[use].astype(F32)
        back_mid, rows_b = norm_back(n.mid[...], n.sc[layer, 2:3, :], dy)
        n.g_out[...] = n.g_out[...] + back_mid

        n.ml[layer, x] = n.g_out[...].astype(BF)
        ml_sent = copies.push(n.ml.at[layer, x], n.ml.at[layer, x], peer)
        if layer:
            load(layer - 1, *feed_places)
        n.dk[...] = jnp.zeros_like(n.dk)
        n.dv[...] = jnp.zeros_like(n.dv)
        ready(wo, ctx, q, k, v, lse, k_t)

        def attend(block, pump):
            other = 1 - block
            n.cg[block] = nt(n.ml[layer, block], n.wo[...]).astype(BF)
            weighed = (n.cg[block].astype(F32) * n.ctx[block].astype(F32)).T
            for head in range(HALF // HD):
                n.delta[head : head + 1, :] = jnp.sum(
                    weighed[head * HD : head * HD + HD, :], axis=0, keepdims=True
                )

            def pair_step(p, carry):
                pump(p)
                lanes = pl.ds(pl.multiple_of(p * 128, 128), 128)
                q_pair, cg_pair = n.q[block, :, lanes], n.cg[block, :, lanes]
                for which in range(2):
                    q_head, cg_head = half_of(q_pair, which), half_of(cg_pair, which)
                    row = pl.ds(2 * p + which, 1)
                    total, dots = n.lse[block, row, :], n.delta[row, :]
                    turned = None
                    head = pl.ds(pl.multiple_of(p * 128 + which * HD, HD), HD)
                    for side in (block, other):
                        k_pair, v_pair = n.k[side, :, lanes], n.v[side, :, lanes]
                        scores = nt(k_pair, q_head)
                        if side is other:
                            scores = scores + bias
                        probs = jnp.exp(scores - total)
                        score_grad = (probs * (nt(v_pair, cg_head) - dots)).astype(BF)
                        n.dv[side, :, lanes] += nn(probs.astype(BF), cg_head)
                        n.dk[side, :, lanes] += nn(score_grad, q_head)
                        piece = nn(n.k_t[side, head, :], score_grad)
                        turned = piece if turned is None else turned + piece
                    n.dqt[block, head, :] = turned * HD**-0.5
                return carry

            lax.fori_loop(0, HALF // 128, pair_step, 0)

        attend(x, lambda p: None)
        ml_sent.wait()
        attend(y, lambda p: w.along(EXPAND, layer, p))
        theirs, mine = rows_of(1 - c, t), rows_of(c, t)
        for side in range(2):
            n.kvsend[side, :, pl.ds(0, HALF)] = n.dk[side, theirs, :].astype(BF)
            n.kvsend[side, :, pl.ds(HALF, HALF)] = n.dv[side, theirs, :].astype(BF)
        kv_sent = copies.push(n.kvsend, n.kvrecv.at[layer], sib)
        w.along(EXPAND, layer, 3)

        def unturn(block, j, value):
            cosine, sine = n.cs[block, :, 0:128], n.cs[block, :, 128:256]
            rounded = value.astype(BF).astype(F32)
            n.pg[block, :, pl.ds(128 * j, 128)] = turn(rounded, cosine, -sine).astype(BF)

        for side in range(2):
            for j in range(3):
                unturn(side, j, n.dqt[side, 128 * j : 128 * j + 128, :].T)
        kv_sent.wait()
        for side in range(2):
            for j in range(3):
                at = pl.ds(128 * j, 128)
                unturn(side, 3 + j, n.dk[side, mine, at] + n.kvrecv[layer, side, :, at].astype(F32))
                n.pg[side, :, pl.ds(D + 128 * j, 128)] = (
                    n.dv[side, mine, at] + n.kvrecv[layer, side, :, pl.ds(HALF + 128 * j, 128)].astype(F32)
                ).astype(BF)
        ready(wt, na, ctx_t, h)
        use = 2 * layer + 1
        n.psend[...] = nt(n.pg[y], n.wt[...]).astype(BF)
        part_sent = copies.push(n.psend, n.precv.at[use], peer)
        rows = D // dp

        def send_tri(i, carry):
            pl.when(i < 2)(lambda: w.along(SHRINK, layer, i))
            off = pl.ds(pl.multiple_of((1 - c) * HALF + i * rows, rows), rows)
            n.gs_shr[rows_of(i, rows), pl.ds(0, TRI)] = nn(n.na[off, :], n.pg[...].reshape(2 * t, TRI)).astype(BF)
            return carry

        lax.fori_loop(0, w.zs, send_tri, 0)
        tri_cols, out_cols = pl.ds(0, TRI), pl.ds(TRI, HALF)
        tri_sent = copies.push(n.gs_shr.at[:, tri_cols], n.gr_att.at[:, tri_cols], sib)
        theirs_too = n.ml[layer, :, :, rows_of(1 - c, HALF)].reshape(2 * t, HALF)
        n.gs_shr[:, out_cols] = nn(n.ctx_t[...], theirs_too).astype(BF)
        out_sent = copies.push(n.gs_shr.at[:, out_cols], n.gr_att.at[:, out_cols], sib)
        n.part[...] = nt(n.pg[x], n.wt[...])
        tri_sent.wait()

        def keep_tri(i, carry):
            at = rows_of(i, rows)
            row_block = n.na[pl.ds(pl.multiple_of(c * HALF + i * rows, rows), rows), :]
            value = nn(row_block, n.pg[...].reshape(2 * t, TRI)) + n.gr_att[at, tri_cols].astype(F32)
            n.gt[layer, at, :] = value.astype(BF)
            return carry

        lax.fori_loop(0, w.zs, keep_tri, 0)
        w.across_all(TRIPLE, layer)
        out_sent.wait()
        mine_too = n.ml[layer, :, :, rows_of(c, HALF)].reshape(2 * t, HALF)
        value = nn(n.ctx_t[...], mine_too) + n.gr_att[:, out_cols].astype(F32)
        n.go[layer] = value.astype(BF)
        w.across_all(OUTPUT, layer)
        part_sent.wait()
        dy = n.part[...] + n.precv[use].astype(F32)
        back_h, rows_a = norm_back(n.h[...], n.sc[layer, 0:1, :], dy)
        n.g_out[...] = n.g_out[...] + back_h
        mine_at = (w.y, w.z, w.s)
        if layer:
            load(layer - 1, *attend_places)
            n.early[(*mine_at, pl.ds(0, 2))] = rows_a
            n.early[(*mine_at, pl.ds(2, 2))] = rows_b
        else:
            n.early[(*mine_at, pl.ds(4, 2))] = rows_b
            n.late[mine_at] = rows_a

    everywhere_start(w, 0, n.early)
    everywhere_start(w, 1, n.late)
    n.squares[...] = jnp.zeros_like(n.squares)
    for kind in (EXPAND, SHRINK, TRIPLE, OUTPUT):
        w.total(kind, 1)
    w.along_all(TRIPLE, 0)
    w.along_all(OUTPUT, 0)
    for kind in (EXPAND, SHRINK):
        w.total(kind, 0)
    first = everywhere_end(w, 0, n.early, n.early_pair)
    second = everywhere_end(w, 1, n.late, n.late_pair)
    n.scale_o[1, pl.ds(0, 2)] = first[0:2]
    n.scale_o[1, pl.ds(2, 2)] = first[2:4]
    n.scale_o[0, pl.ds(0, 2)] = second
    n.scale_o[0, pl.ds(2, 2)] = first[4:6]
    for kind in (TRIPLE, OUTPUT):
        w.total(kind, 0)
    n.sq[w.y, w.z, w.s] = jnp.broadcast_to(n.squares[...], (8, 128))
    everywhere_start(w, 2, n.sq)
    for layer in range(LAYERS):
        for kind in KINDS:
            w.home(kind, layer)
    rows = D // dp

    def natural(packed):
        wide, rest = packed[:rows].astype(F32), packed[rows:].astype(F32)
        even = jnp.concatenate([rest[:, :HD], rest[:, HD:]], axis=0)
        odd = jnp.concatenate([rest[:, HD:], rest[:, :HD]], axis=0)
        return jnp.concatenate([wide, even], axis=1), jnp.concatenate([odd, wide], axis=1)

    for layer in range(LAYERS):
        halves, outs_here = natural(n.f_half[layer]), natural(n.f_out[layer])
        whole = n.f_whole[layer].astype(F32)

        @pl.when(c == 0)
        def _():
            n.tri_g[layer] = jnp.concatenate([whole, halves[0]], axis=1)
            n.out_g[layer] = outs_here[0]

        @pl.when(c == 1)
        def _():
            n.tri_g[layer] = jnp.concatenate([halves[1], whole], axis=1)
            n.out_g[layer] = outs_here[1]

    outputs = [
        copies.local(a, b)
        for a, b in ((n.f_exp, n.exp_g), (n.f_shr, n.shr_g))
    ]
    total = everywhere_end(w, 2, n.sq, n.sq_pair)
    n.norm_o[...] = total + squared(first[0:6]) + squared(second)
    for copy in outputs:
        copy.wait()
    for layer in range(LAYERS):
        for kind in KINDS:
            w.finish(kind, layer)


def backward_all(dp, g, f, residual, segments):
    t = g.shape[0]
    zs = dp // 2
    r = D // dp
    packed = 3 * r // 2
    head, saved0, saved1 = f
    saved = (*saved0, residual, head.mid_o0, *saved1, head.h_mid, head.mid_o1)
    outs = [
        sds((t, D), F32), sds((LAYERS, 4, D), F32), sds((8, 128), F32), sds((LAYERS, r, TRI // 2), F32),
        sds((LAYERS, r, 192), F32), sds((LAYERS, r, D), BF),
        sds((LAYERS, 192, 4 * r), BF),
    ]
    v = pltpu.VMEM
    ll = LAYERS
    scratch = [
        *(v(array.shape, array.dtype) for array in saved[: len(Loaded._fields)]),
        v((ll, 2, t, D), BF), v((D, 2 * t), BF), v((2, t, HID), BF), v((ll, 2, t, D), BF), v((2, t, HALF), BF), v((8, t), F32),
        v((2, HALF, t), F32), v((2, 2 * t, HALF), F32), v((2, 2 * t, HALF), F32), v((2, t, D), BF),
        v((ll, 2, t, D), BF), v((2, t, TRI), BF), v((t, D), F32), v((t, D), BF), v((2 * ll, t, D), BF),
        v((D, D), BF), v((D, D), BF), v((HALF, HID), BF), v((HALF, HID), BF), v((HALF, HID), BF),
        v((ll, HALF, TRI), BF), v((ll, HALF, HALF), BF), v((ll, D, D), BF), v((ll, HALF, HID), BF),
        v((ll, 2, r, TRI), BF), v((ll, 2, r, HALF), BF), v((ll, 4, r, D), BF), v((ll, 2, HALF, 4 * r), BF),
        v((ll, 3, r, TRI), BF), v((ll, 3, r, HALF), BF), v((ll, 3, r, D), BF), v((ll, 3, HALF, 4 * r), BF),
        v((ll, 2, packed, 128), BF), v((ll, 2, packed, 128), BF),
        v((ll, r, HALF), BF), v((ll, packed, 128), BF), v((ll, packed, 128), BF), v((ll, r, D), BF),
        v((ll, 192, 4 * r), BF), v((1, 1), F32),
        v((2, zs, SEQ, 8, D), F32), v((2, 8, D), F32), v((2, zs, SEQ, 2, D), F32), v((2, 2, D), F32),
        v((2, zs, SEQ, 8, 128), F32), v((2, 8, 128), F32),
        pltpu.SemaphoreType.DMA((ll, len(KINDS), 2, zs)), pltpu.SemaphoreType.DMA((ll, len(KINDS), 2, zs)),
        pltpu.SemaphoreType.DMA((ll, len(KINDS), 4)), pltpu.SemaphoreType.DMA((ll, len(KINDS), 2)),
        pltpu.SemaphoreType.DMA((3, zs * SEQ + 1)), pltpu.SemaphoreType.DMA((3, zs * SEQ + 1)),
        pltpu.SemaphoreType.DMA((28,)), pltpu.SemaphoreType.DMA((28,)), pltpu.SemaphoreType.DMA((48,)),
    ]
    results = pl.pallas_call(
        functools.partial(bwd_kernel, dp),
        name="backward",
        out_shape=outs,
        in_specs=[vmem(), hbm(), vmem(), vmem(), pl.BlockSpec(memory_space=pltpu.SMEM), *([hbm()] * len(saved))],
        out_specs=[vmem()] * 5 + [hbm()] * 2,
        scratch_shapes=scratch,
        cost_estimate=pl.CostEstimate(flops=44 << 30, bytes_accessed=48 << 20, transcendentals=0),
        compiler_params=pltpu.CompilerParams(
            collective_id=5, has_side_effects=True, vmem_limit_bytes=VMEM_BYTES
        ),
    )(g, head.gl_o, head.sc_o, head.cs_o, segments, *saved)
    return BackwardOut(*results)


class Moves:
    def __init__(self, dp):
        self.dp = dp
        self.d = lax.axis_index("dp")
        s = lax.axis_index("seq")
        self.s, self.x, self.c = s, s // 2, s % 2
        half = dp // 2
        ids = [(d, s) for d in range(dp) for s in range(SEQ)]
        self.tri = []
        for r in range(2):
            for j in range(3):
                perm = []
                for d, s in ids:
                    b = (3 * s + j) % 4
                    to = (2 * (d % half) + (r ^ (b % 2)), 2 * (b // 2) + d // half)
                    perm.append((d * SEQ + s, to[0] * SEQ + to[1]))
                self.tri.append(perm)
        self.out = []
        for r in range(2):
            perm = []
            for d, s in ids:
                to = (2 * (d % half) + (r ^ (s % 2)), 2 * (d // half) + s // 2)
                perm.append((d * SEQ + s, to[0] * SEQ + to[1]))
            self.out.append(perm)
        self.shr = []
        for k in range(4):
            perm = []
            for d, s in ids:
                to = (4 * (d % (dp // 4)) + (k + s) % 4, d // (dp // 4))
                perm.append((d * SEQ + s, to[0] * SEQ + to[1]))
            self.shr.append(perm)

    def send(self, piece, perm, back):
        if back:
            perm = [(b, a) for a, b in perm]
        return lax.ppermute(piece, ("dp", "seq"), perm)

    @staticmethod
    def pick(pieces, index):
        return lax.dynamic_index_in_dim(jnp.stack(pieces), index, 0, keepdims=False)

    def tri_out(self, low):
        n, rows, _ = low.shape
        halves = low.reshape(n, 2, rows // 2, 3, 192)
        got = []
        for r in range(2):
            for j in range(3):
                which = r ^ (((3 * self.s + j) % 4) % 2)
                piece = lax.dynamic_index_in_dim(halves[:, :, :, j], which, 1, keepdims=False)
                got.append(self.send(piece, self.tri[3 * r + j], False))
        parts = []
        for t in range(3):
            for bb in range(2):
                r, j = bb ^ (self.d % 2), (t + 2 * self.x + bb) % 3
                parts.append(self.pick(got, 3 * r + j))
        return jnp.concatenate(parts, axis=-1)

    def tri_back(self, grad):
        n, rows, _ = grad.shape
        got = []
        for r in range(2):
            for j in range(3):
                bb = (self.d % 2) ^ r
                t = (j - (2 * self.x + bb)) % 3
                piece = lax.dynamic_slice_in_dim(grad, (2 * t + bb) * 192, 192, 2)
                got.append(self.send(piece, self.tri[3 * r + j], True))
        cols = []
        for j in range(3):
            two = []
            for hh in range(2):
                r = hh ^ (((3 * self.s + j) % 4) % 2)
                two.append(self.pick([got[j], got[3 + j]], r))
            cols.append(jnp.concatenate(two, axis=1))
        return jnp.concatenate(cols, axis=-1)

    def out_out(self, low):
        n, rows, _ = low.shape
        halves = low.reshape(n, 2, rows // 2, 192)
        got = [
            self.send(
                lax.dynamic_index_in_dim(halves, r ^ (self.s % 2), 1, keepdims=False), self.out[r], False
            )
            for r in range(2)
        ]
        return jnp.concatenate([self.pick(got, u ^ (self.d % 2)) for u in range(2)], axis=-1)

    def out_back(self, grad):
        got = []
        for r in range(2):
            u = r ^ (self.d % 2)
            got.append(self.send(lax.dynamic_slice_in_dim(grad, u * 192, 192, 2), self.out[r], True))
        return jnp.concatenate([self.pick(got, hh ^ (self.s % 2)) for hh in range(2)], axis=1)

    def shr_out(self, low):
        n, rows, _ = low.shape
        subs = low.reshape(n, 4, rows // 4, 192)
        got = [
            self.send(
                lax.dynamic_index_in_dim(subs, (k + self.s) % 4, 1, keepdims=False), self.shr[k], False
            )
            for k in range(4)
        ]
        return jnp.concatenate([self.pick(got, (self.d - s) % 4) for s in range(4)], axis=-1)

    def shr_back(self, grad):
        got = []
        for k in range(4):
            piece = lax.dynamic_slice_in_dim(grad, ((self.d - k) % 4) * 192, 192, 2)
            got.append(self.send(piece, self.shr[k], True))
        return jnp.concatenate([self.pick(got, (sub - self.s) % 4) for sub in range(4)], axis=1)


def tables_here(segments, t, x, c):
    group = segments.shape[0]
    whole = segments[0] == segments[group - 1]
    place_in_half = c * t + jnp.arange(t, dtype=jnp.int32)
    second = jnp.where(whole, group // 2, 0).astype(jnp.int32)
    positions = jnp.stack([place_in_half, place_in_half + second]).astype(F32)
    lane = jnp.arange(128, dtype=jnp.int32)
    inverse = 1.0 / ROTARY_BASE ** ((lane % (HD // 2)).astype(F32) * (2.0 / HD))
    angles = positions[:, :, None] * inverse[None, None, :]
    sign = jnp.where(lane % HD < HD // 2, -1.0, 1.0).astype(F32)
    tables = jnp.concatenate([jnp.cos(angles), jnp.sin(angles) * sign], axis=-1)
    bias = jnp.where(whole, 0.0, MASKED).astype(F32).reshape(1)
    return tables, bias


def layers_narrow(
    dp, moves, residual, cotangent, segments, scales_weight,
    triple_weight, output_weight, expand_weight, shrink_weight,
):
    tables, bias = tables_here(segments, residual.shape[0], moves.x, moves.c)
    d, s = lax.axis_index("dp"), lax.axis_index("seq")
    scales_all = lax.psum(
        lax.dynamic_update_slice(
            jnp.zeros((LAYERS, 4, D), F32), scales_weight.astype(BF).astype(F32), (0, s, d * (D // dp))
        ),
        ("dp", "seq"),
    )
    tri = moves.tri_out(triple_weight.astype(BF))
    out = moves.out_out(output_weight.astype(BF))
    shr = moves.shr_out(shrink_weight.astype(BF))
    attend_parts = jnp.concatenate([tri, out], axis=-1)
    feed_parts = jnp.concatenate([expand_weight.astype(BF), shr], axis=-1)
    gather = functools.partial(lax.all_gather, axis_name="dp", axis=0, tiled=True)
    wa, wf = [], []
    for layer in range(LAYERS):
        wa.append(gather(attend_parts[layer]))
        wf.append(gather(feed_parts[layer]))

    stream = residual
    kept = []
    for layer in range(LAYERS):
        scales = scales_all[layer]
        middle, *attend_saved = attend_fwd(stream, wa[layer], scales, tables, bias)
        following, *feed_saved = feed_fwd(middle, wf[layer], scales)
        kept.append((stream, middle, attend_saved, feed_saved))
        stream = following

    g = cotangent
    attend_grads, feed_grads, scale_grads = [None] * LAYERS, [None] * LAYERS, [None] * LAYERS
    scatter = functools.partial(lax.psum_scatter, axis_name="dp", scatter_dimension=0, tiled=True)
    for layer in reversed(range(LAYERS)):
        scales = scales_all[layer]
        h, middle, attend_saved, feed_saved = kept[layer]
        mg, feed_grad, rows_b = feed_bwd(g, middle, wf[layer], scales, *feed_saved)
        feed_grads[layer] = scatter(feed_grad).astype(F32)
        g, attend_grad, rows_a = attend_bwd(mg, h, wa[layer], scales, tables, bias, attend_saved)
        attend_grads[layer] = scatter(attend_grad).astype(F32)
        scale_grads[layer] = jnp.concatenate([rows_a, rows_b], axis=0)

    scale_grad = lax.psum(jnp.stack(scale_grads), ("dp", "seq"))
    own_scale = lax.dynamic_slice(scale_grad, (0, s, d * (D // dp)), (LAYERS, 1, D // dp))
    squares = jnp.sum(own_scale * own_scale)
    for part in (*attend_grads, *feed_grads):
        squares = squares + jnp.sum(part * part)
    grad_norm = jnp.sqrt(lax.psum(squares, ("dp", "seq")))

    attend_grad, feed_grad = jnp.stack(attend_grads).astype(BF), jnp.stack(feed_grads).astype(BF)
    triple_grad = moves.tri_back(attend_grad[:, :, :TRI]).astype(F32)
    output_grad = moves.out_back(attend_grad[:, :, TRI:]).astype(F32)
    expand_grad = feed_grad[:, :, :D].astype(F32)
    shrink_grad = moves.shr_back(feed_grad[:, :, D:]).astype(F32)
    return stream, g, grad_norm, (triple_grad, output_grad, expand_grad, shrink_grad, own_scale)


def layers_wide(
    dp, moves, residual, cotangent, segments, scales_weight,
    triple_weight, output_weight, expand_weight, shrink_weight,
):
    d, s = lax.axis_index("dp"), lax.axis_index("seq")
    shards = (triple_weight, output_weight, expand_weight, jnp.swapaxes(shrink_weight, 1, 2))
    f = forward_all(dp, residual, cotangent, scales_weight, segments, shards)
    b = backward_all(dp, cotangent, f, residual, segments)
    own_scale = lax.dynamic_slice(b.scale_o, (0, s, d * (D // dp)), (LAYERS, 1, D // dp))
    grad_norm = jnp.sqrt(b.norm_o[0, 0])
    return f[0].h_out, b.g_out, grad_norm, (
        b.tri_g, b.out_g, b.exp_g.astype(F32), jnp.swapaxes(b.shr_g, 1, 2).astype(F32), own_scale
    )


def local(dp, *args):
    (residual, cotangent, segments) = args[:3]
    (
        triple_weight, triple_moment, triple_square, triple_shadow,
        output_weight, output_moment, output_square, output_shadow,
        expand_weight, expand_moment, expand_square, expand_shadow,
        shrink_weight, shrink_moment, shrink_square, shrink_shadow,
        scales_weight, scales_moment, scales_square, scales_shadow,
    ) = args[3:]
    moves = Moves(dp)
    t = residual.shape[0]
    d, s = lax.axis_index("dp"), lax.axis_index("seq")

    if dp == 2 * ZS:
        stream, g, grad_norm, grads = layers_wide(
            dp, moves, residual, cotangent, segments, scales_weight,
            triple_weight, output_weight, expand_weight, shrink_weight,
        )
    else:
        stream, g, grad_norm, grads = layers_narrow(
            dp, moves, residual, cotangent, segments, scales_weight,
            triple_weight, output_weight, expand_weight, shrink_weight,
        )
    triple_grad, output_grad, expand_grad, shrink_grad, own_scale = grads
    limit = CLIP_RATIO * math.sqrt(float(LAYERS * (4 * D * D + 2 * D * FF + 4 * D)))
    factor = limit / (grad_norm + 1e-06)

    results = [stream, g, grad_norm]
    for weight, moment, square, shadow, grad, rate in (
        (triple_weight, triple_moment, triple_square, triple_shadow, triple_grad, RATE_FACTOR / math.sqrt(D)),
        (output_weight, output_moment, output_square, output_shadow, output_grad, RATE_FACTOR / math.sqrt(D // 16)),
        (expand_weight, expand_moment, expand_square, expand_shadow, expand_grad, RATE_FACTOR / math.sqrt(D)),
        (shrink_weight, shrink_moment, shrink_square, shrink_shadow, shrink_grad, RATE_FACTOR / math.sqrt(FF)),
        (scales_weight, scales_moment, scales_square, scales_shadow, own_scale, SCALES_RATE),
    ):
        results.extend(adam_step(weight, moment, square, shadow, grad * factor, rate))
    return tuple(results)


def solution(mesh):
    token = P(("dp", "seq"), None)
    weight = P(None, "dp", "seq")
    scale = P(None, "seq", "dp")
    return jax.shard_map(
        functools.partial(local, mesh.shape["dp"]),
        mesh=mesh,
        in_specs=(token, token, P("dp"), *([weight] * 16), *([scale] * 4)),
        out_specs=(token, token, P(), *([weight] * 16), *([scale] * 4)),
        check_vma=False,
    )
```

```python
import functools
import math
from typing import Any, NamedTuple

import jax
import jax.numpy as jnp
from jax import lax
from jax.experimental import pallas as pl
from jax.experimental.pallas import tpu as pltpu
from jax.sharding import PartitionSpec as P

D = 768
FF = 3072
HD = 64
LAYERS = 2
STEP = 2
SEQ = 4

EPSILON = 1e-05
ROTARY_BASE = 10000.0
BETA_ONE = 0.9
BETA_TWO = 0.999
ADAM_EPSILON = 1e-08
DECAY_RATE = 0.01
SHADOW_RATE = 0.99
CLIP_RATIO = 0.5
RATE_FACTOR = 1.5
SCALES_RATE = 0.6
MASKED = -1000000000.0

HALF = D // 2
TRI = 3 * HALF
HID = FF // 2
BF = jnp.bfloat16
F32 = jnp.float32
MESH = pl.DeviceIdType.MESH
VMEM_BYTES = 60 << 20


def adam_step(weight, moment, square, shadow, gradient, step_rate):
    shadow_decay = min(SHADOW_RATE, (1.0 + STEP) / (10.0 + STEP))
    momentum = BETA_ONE * moment + (1.0 - BETA_ONE) * gradient
    variance = BETA_TWO * square + (1.0 - BETA_TWO) * gradient * gradient
    corrected = (
        momentum
        / (1.0 - BETA_ONE**STEP)
        / (jnp.sqrt(variance / (1.0 - BETA_TWO**STEP)) + ADAM_EPSILON)
    )
    updated = weight - step_rate * (corrected + DECAY_RATE * weight)
    average = shadow_decay * shadow + (1.0 - shadow_decay) * updated
    return (updated, momentum, variance, average)


def nn(a, b):
    return lax.dot_general(a, b, (((1,), (0,)), ((), ())), preferred_element_type=F32)


def nt(a, b):
    return lax.dot_general(a, b, (((1,), (1,)), ((), ())), preferred_element_type=F32)


def tn(a, b):
    return lax.dot_general(a, b, (((0,), (0,)), ((), ())), preferred_element_type=F32)


def place():
    s = lax.axis_index("seq")
    x = lax.div(s, 2)
    c = lax.rem(s, 2)
    return lax.axis_index("dp"), x, c, lax.rem(s + 2, SEQ), s + 1 - 2 * c


def greet(d, peer, sib):
    barrier = pltpu.get_barrier_semaphore()
    for other in (peer, sib):
        pl.semaphore_signal(barrier, inc=1, device_id=(d, other), device_id_type=MESH)
    pl.semaphore_wait(barrier, 2)


def rows_of(c, n):
    return pl.ds(pl.multiple_of(c * n, n), n)


class Copies:
    def __init__(self, lsem, ssem, rsem, d):
        self.lsem, self.ssem, self.rsem, self.d = lsem, ssem, rsem, d
        self.n_local = 0
        self.n_remote = 0

    def local(self, src, dst):
        copy = pltpu.make_async_copy(src, dst, self.lsem.at[self.n_local])
        self.n_local += 1
        copy.start()
        return copy

    def push(self, src, dst, to):
        copy = pltpu.make_async_remote_copy(
            src_ref=src,
            dst_ref=dst,
            send_sem=self.ssem.at[self.n_remote],
            recv_sem=self.rsem.at[self.n_remote],
            device_id=(self.d, to),
            device_id_type=MESH,
        )
        self.n_remote += 1
        copy.start()
        return copy


def norm_stats(values):
    center = values - jnp.mean(values, axis=-1, keepdims=True)
    spread = jnp.mean(center * center, axis=-1, keepdims=True)
    scale = lax.rsqrt(spread + EPSILON)
    return center * scale, scale


def norm_back(values, gain, dy):
    xhat, scale = norm_stats(values)
    u = gain * dy
    du = u - jnp.mean(u, axis=-1, keepdims=True)
    back = scale * (du - xhat * jnp.mean(u * xhat, axis=-1, keepdims=True))
    rows = jnp.concatenate(
        [jnp.sum(xhat * dy, axis=0, keepdims=True), jnp.sum(dy, axis=0, keepdims=True)], axis=0
    )
    return back, rows


def turn(chunk, cosine, sine):
    lane = lax.broadcasted_iota(jnp.int32, chunk.shape, 1)
    swapped = jnp.where(
        lax.rem(lane, HD) < HD // 2, pltpu.roll(chunk, 128 - HD // 2, 1), pltpu.roll(chunk, HD // 2, 1)
    )
    return chunk * cosine + swapped * sine


def half_of(pair, which):
    lane = lax.broadcasted_iota(jnp.int32, pair.shape, 1)
    keep = (lane < HD) if which == 0 else (lane >= HD)
    return jnp.where(keep, pair, jnp.zeros_like(pair))


def attend_fwd_kernel(
    h, wa, sc, cs, bias, mid, na_o, q_o, k_o, v_o, ctx_o, lse_o,
    wt, wo, na, q, k, v, ctxt, ctx, lse, psend, precv, lsem, ssem, rsem,
):
    d, x, c, peer, sib = place()
    y = 1 - x
    rows = h.shape[0]
    copies = Copies(lsem, ssem, rsem, d)
    greet(d, peer, sib)
    wt_own, wo_own = wt.at[rows_of(c, HALF), :], wo.at[:, rows_of(c, HALF)]
    tri_part, out_part = wa.at[:, pl.ds(0, TRI)], wa.at[:, pl.ds(TRI, HALF)]
    tri_sent = copies.push(tri_part, wt_own, sib)
    tri_local = copies.local(tri_part, wt_own)
    out_sent = copies.push(out_part, wo_own, sib)
    out_local = copies.local(out_part, wo_own)
    xhat, _ = norm_stats(h[...])
    na[x] = (xhat * sc[0:1, :] + sc[1:2, :]).astype(BF)
    na_sent = copies.push(na.at[x], na.at[x], peer)
    tri_local.wait()
    tri_sent.wait()

    def project(block):
        cosine, sine = cs[block, :, 0:128], cs[block, :, 128:256]
        for j in range(9):
            part = nn(na[block], wt[:, 128 * j : 128 * j + 128])
            lanes = pl.ds(128 * (j % 3), 128)
            if j < 3:
                q[block, :, lanes] = (turn(part, cosine, sine) * HD**-0.5).astype(BF)
            elif j < 6:
                k[block, rows_of(c, rows), lanes] = turn(part, cosine, sine).astype(BF)
            else:
                v[block, rows_of(c, rows), lanes] = part.astype(BF)

    def share(block):
        mine = (block, rows_of(c, rows))
        return [copies.push(k.at[mine], k.at[mine], sib), copies.push(v.at[mine], v.at[mine], sib)]

    project(x)
    shared = share(x)
    na_sent.wait()
    project(y)
    shared += share(y)
    out_local.wait()
    out_sent.wait()
    for copy in shared:
        copy.wait()

    def attend(block):
        other = 1 - block

        def pair_step(p, carry):
            lanes = pl.ds(pl.multiple_of(p * 128, 128), 128)
            q_pair = q[block, :, lanes]
            k_same, k_cross = k[block, :, lanes], k[other, :, lanes]
            v_same, v_cross = v[block, :, lanes], v[other, :, lanes]
            for which in range(2):
                q_head = half_of(q_pair, which)
                s_same = nt(k_same, q_head)
                s_cross = nt(k_cross, q_head) + bias[0]
                top = jnp.maximum(
                    jnp.max(s_same, axis=0, keepdims=True), jnp.max(s_cross, axis=0, keepdims=True)
                )
                e_same = jnp.exp(s_same - top)
                e_cross = jnp.exp(s_cross - top)
                total = jnp.sum(e_same, axis=0, keepdims=True) + jnp.sum(
                    e_cross, axis=0, keepdims=True
                )
                mixed = tn(v_same, e_same.astype(BF)) + tn(v_cross, e_cross.astype(BF))
                head = pl.ds(pl.multiple_of(p * 128 + which * HD, HD), HD)
                ctxt[head, :] = mixed[which * HD : which * HD + HD, :] / total
                lse[block, pl.ds(2 * p + which, 1), :] = top + jnp.log(total)
            return carry

        lax.fori_loop(0, HALF // 128, pair_step, 0)
        ctx[block] = ctxt[...].T.astype(BF)
        return nn(ctx[block], wo[...])

    psend[...] = attend(y).astype(BF)
    part_sent = copies.push(psend, precv, peer)
    mid[...] = h[...] + attend(x)
    saves = [
        copies.local(a, b)
        for a, b in ((na, na_o), (q, q_o), (k, k_o), (v, v_o), (ctx, ctx_o), (lse, lse_o))
    ]
    part_sent.wait()
    mid[...] = mid[...] + precv[...].astype(F32)
    for copy in saves:
        copy.wait()


def hbm():
    return pl.BlockSpec(memory_space=pl.ANY)


def vmem():
    return pl.BlockSpec(memory_space=pltpu.VMEM)


def call(kernel, name, number, ins, outs, out_shape, scratch, n_local, n_remote, flops, args):
    return pl.pallas_call(
        kernel,
        name=name,
        out_shape=out_shape,
        in_specs=ins,
        out_specs=outs,
        scratch_shapes=[
            *scratch,
            pltpu.SemaphoreType.DMA((n_local,)),
            pltpu.SemaphoreType.DMA((n_remote,)),
            pltpu.SemaphoreType.DMA((n_remote,)),
        ],
        cost_estimate=pl.CostEstimate(flops=flops, bytes_accessed=16 << 20, transcendentals=0),
        compiler_params=pltpu.CompilerParams(
            collective_id=number, has_side_effects=True, vmem_limit_bytes=VMEM_BYTES
        ),
    )(*args)


def sds(shape, dtype):
    return jax.ShapeDtypeStruct(shape, dtype)


def attend_fwd(h, wa, scales, tables, bias):
    t = h.shape[0]
    return call(
        attend_fwd_kernel, "attend_fwd", 0,
        [vmem(), hbm(), vmem(), vmem(), pl.BlockSpec(memory_space=pltpu.SMEM)],
        [vmem()] + [hbm()] * 6,
        [
            sds((t, D), F32), sds((2, t, D), BF), sds((2, t, HALF), BF), sds((2, 2 * t, HALF), BF),
            sds((2, 2 * t, HALF), BF), sds((2, t, HALF), BF), sds((2, 8, t), F32),
        ],
        [
            pltpu.VMEM((D, TRI), BF), pltpu.VMEM((HALF, D), BF), pltpu.VMEM((2, t, D), BF),
            pltpu.VMEM((2, t, HALF), BF), pltpu.VMEM((2, 2 * t, HALF), BF),
            pltpu.VMEM((2, 2 * t, HALF), BF), pltpu.VMEM((HALF, t), F32),
            pltpu.VMEM((2, t, HALF), BF), pltpu.VMEM((2, 8, t), F32),
            pltpu.VMEM((t, D), BF), pltpu.VMEM((t, D), BF),
        ],
        8, 8, 6 << 30, (h, wa, scales, tables, bias),
    )


def gelu_parts(hidden):
    phi_cap = 0.5 * (1.0 + lax.erf(hidden * math.sqrt(0.5)))
    density = jnp.exp(-0.5 * hidden * hidden) * (1.0 / math.sqrt(2.0 * math.pi))
    return hidden * phi_cap, phi_cap + hidden * density


def feed_fwd_kernel(
    mid, wf, sc, h_next, nb_o, act_o, slope_o,
    we, ws, nb, act, slope, psend, precv, lsem, ssem, rsem,
):
    d, x, c, peer, sib = place()
    y = 1 - x
    copies = Copies(lsem, ssem, rsem, d)
    greet(d, peer, sib)
    xhat, _ = norm_stats(mid[...])
    nb[x] = (xhat * sc[2:3, :] + sc[3:4, :]).astype(BF)
    nb_sent = copies.push(nb.at[x], nb.at[x], peer)
    we_own, ws_own = we.at[:, rows_of(c, D)], ws.at[rows_of(c, D), :]
    exp_part, shr_part = wf.at[:, pl.ds(0, D)], wf.at[:, pl.ds(D, D)]
    weights = [
        copies.local(exp_part, we_own),
        copies.push(exp_part, we_own, sib),
        copies.local(shr_part, ws_own),
        copies.push(shr_part, ws_own, sib),
    ]
    for copy in weights:
        copy.wait()

    def feed(block):
        def step(i, carry):
            lanes = pl.ds(pl.multiple_of(i * 256, 256), 256)
            value, rate = gelu_parts(nn(nb[block], we[:, lanes]))
            act[block, :, lanes] = value.astype(BF)
            slope[block, :, lanes] = rate.astype(BF)
            return carry

        lax.fori_loop(0, HID // 256, step, 0)
        return nn(act[block], ws[...])

    h_next[...] = mid[...] + feed(x)
    nb_sent.wait()
    psend[...] = feed(y).astype(BF)
    part_sent = copies.push(psend, precv, peer)
    saves = [copies.local(a, b) for a, b in ((nb, nb_o), (act, act_o), (slope, slope_o))]
    part_sent.wait()
    h_next[...] = h_next[...] + precv[...].astype(F32)
    for copy in saves:
        copy.wait()


def feed_fwd(mid, wf, scales):
    t = mid.shape[0]
    return call(
        feed_fwd_kernel, "feed_fwd", 1,
        [vmem(), hbm(), vmem()],
        [vmem()] + [hbm()] * 3,
        [sds((t, D), F32), sds((2, t, D), BF), sds((2, t, HID), BF), sds((2, t, HID), BF)],
        [
            pltpu.VMEM((D, HID), BF), pltpu.VMEM((HID, D), BF), pltpu.VMEM((2, t, D), BF),
            pltpu.VMEM((2, t, HID), BF), pltpu.VMEM((2, t, HID), BF),
            pltpu.VMEM((t, D), BF), pltpu.VMEM((t, D), BF),
        ],
        5, 4, 5 << 30, (mid, wf, scales),
    )


def feed_bwd_kernel(
    g, mid, wf, sc, nb_h, act_h, slope_h, mid_grad, wg_o, rows_o,
    we, ws, nb, act, slope, gl, hg, part, psend, precv, gown, gsend, grecv, lsem, ssem, rsem,
):
    d, x, c, peer, sib = place()
    y = 1 - x
    t = g.shape[0]
    copies = Copies(lsem, ssem, rsem, d)
    greet(d, peer, sib)
    gl[x] = g[...].astype(BF)
    g_sent = copies.push(gl.at[x], gl.at[x], peer)
    we_own, ws_own = we.at[:, rows_of(c, D)], ws.at[rows_of(c, D), :]
    exp_part, shr_part = wf.at[:, pl.ds(0, D)], wf.at[:, pl.ds(D, D)]
    weights = [
        copies.local(shr_part, ws_own),
        copies.push(shr_part, ws_own, sib),
        copies.local(exp_part, we_own),
        copies.push(exp_part, we_own, sib),
        copies.local(slope_h, slope),
        copies.local(act_h, act),
        copies.local(nb_h, nb),
    ]
    for copy in weights:
        copy.wait()

    def back(block):
        def step(i, carry):
            lanes = pl.ds(pl.multiple_of(i * 256, 256), 256)
            pulled = nt(gl[block], ws[lanes, :])
            hg[block, :, lanes] = (pulled * slope[block, :, lanes].astype(F32)).astype(BF)
            return carry

        lax.fori_loop(0, HID // 256, step, 0)
        return nt(hg[block], we[...])

    part[...] = back(x)
    g_sent.wait()
    psend[...] = back(y).astype(BF)
    part_sent = copies.push(psend, precv, peer)

    gl_all = gl[...].reshape(2 * t, D)
    nb_all = nb[...].reshape(2 * t, D)

    def grads(which, store):
        def step(i, carry):
            at = pl.ds(pl.multiple_of(i * 256, 256), 256)
            off = pl.ds(pl.multiple_of(which * D + i * 256, 256), 256)
            hg_part = hg[:, :, off].reshape(2 * t, 256)
            act_part = act[:, :, off].reshape(2 * t, 256)
            store(0, at, tn(nb_all, hg_part))
            store(1, at, tn(act_part, gl_all))
            return carry

        lax.fori_loop(0, D // 256, step, 0)

    def to_send(kind, at, value):
        if kind == 0:
            gsend[:, at] = value.astype(BF)
        else:
            gsend[at, pl.ds(D, D)] = value.astype(BF)

    def to_keep(kind, at, value):
        if kind == 0:
            gown[:, at] = value
        else:
            gown[at, pl.ds(D, D)] = value

    grads(1 - c, to_send)
    grad_sent = copies.push(gsend, grecv, sib)
    grads(c, to_keep)
    part_sent.wait()
    dy = part[...] + precv[...].astype(F32)
    back_mid, rows = norm_back(mid[...], sc[2:3, :], dy)
    mid_grad[...] = g[...] + back_mid
    rows_o[...] = rows
    grad_sent.wait()
    gsend[...] = (gown[...] + grecv[...].astype(F32)).astype(BF)
    copies.local(gsend, wg_o).wait()


def feed_bwd(g, mid, wf, scales, nb, act, slope):
    t = g.shape[0]
    return call(
        feed_bwd_kernel, "feed_bwd", 2,
        [vmem(), vmem(), hbm(), vmem(), hbm(), hbm(), hbm()],
        [vmem(), hbm(), vmem()],
        [sds((t, D), F32), sds((D, 2 * D), BF), sds((2, D), F32)],
        [
            pltpu.VMEM((D, HID), BF), pltpu.VMEM((HID, D), BF), pltpu.VMEM((2, t, D), BF),
            pltpu.VMEM((2, t, HID), BF), pltpu.VMEM((2, t, HID), BF), pltpu.VMEM((2, t, D), BF),
            pltpu.VMEM((2, t, HID), BF), pltpu.VMEM((t, D), F32), pltpu.VMEM((t, D), BF),
            pltpu.VMEM((t, D), BF), pltpu.VMEM((D, 2 * D), F32), pltpu.VMEM((D, 2 * D), BF),
            pltpu.VMEM((D, 2 * D), BF),
        ],
        6, 5, 10 << 30, (g, mid, wf, scales, nb, act, slope),
    )


def attend_bwd_kernel(
    mg, h, wa, sc, cs, bias, na, q, k, v, ctx, lse, g_prev, wg_o, rows_o,
    wt, wo, ml, cg, delta, dqt, dk, dv, kvsend, kvrecv, pg, part, psend, precv,
    gown, gsend, grecv, lsem, ssem, rsem,
):
    d, x, c, peer, sib = place()
    y = 1 - x
    t = mg.shape[0]
    copies = Copies(lsem, ssem, rsem, d)
    greet(d, peer, sib)
    ml[x] = mg[...].astype(BF)
    ml_sent = copies.push(ml.at[x], ml.at[x], peer)
    wt_own, wo_own = wt.at[rows_of(c, HALF), :], wo.at[:, rows_of(c, HALF)]
    tri_part, out_part = wa.at[:, pl.ds(0, TRI)], wa.at[:, pl.ds(TRI, HALF)]
    out_moves = [copies.local(out_part, wo_own), copies.push(out_part, wo_own, sib)]
    tri_moves = [copies.local(tri_part, wt_own), copies.push(tri_part, wt_own, sib)]
    dk[...] = jnp.zeros_like(dk)
    dv[...] = jnp.zeros_like(dv)
    for copy in out_moves:
        copy.wait()

    def attend(block):
        other = 1 - block
        pulled = nt(ml[block], wo[...])
        cg[block] = pulled.astype(BF)
        weighed = (cg[block].astype(F32) * ctx[block].astype(F32)).T
        for head in range(HALF // HD):
            delta[head : head + 1, :] = jnp.sum(
                weighed[head * HD : head * HD + HD, :], axis=0, keepdims=True
            )

        def pair_step(p, carry):
            lanes = pl.ds(pl.multiple_of(p * 128, 128), 128)
            q_pair, cg_pair = q[block, :, lanes], cg[block, :, lanes]
            for which in range(2):
                q_head, cg_head = half_of(q_pair, which), half_of(cg_pair, which)
                row = pl.ds(2 * p + which, 1)
                total, dots = lse[block, row, :], delta[row, :]
                turned = None
                for side in (block, other):
                    k_pair, v_pair = k[side, :, lanes], v[side, :, lanes]
                    scores = nt(k_pair, q_head)
                    if side is other:
                        scores = scores + bias[0]
                    probs = jnp.exp(scores - total)
                    score_grad = (probs * (nt(v_pair, cg_head) - dots)).astype(BF)
                    dv[side, :, lanes] += nn(probs.astype(BF), cg_head)
                    dk[side, :, lanes] += nn(score_grad, q_head)
                    piece = tn(k_pair, score_grad)
                    turned = piece if turned is None else turned + piece
                head = pl.ds(pl.multiple_of(p * 128 + which * HD, HD), HD)
                dqt[block, head, :] = turned[which * HD : which * HD + HD, :] * HD**-0.5
            return carry

        lax.fori_loop(0, HALF // 128, pair_step, 0)

    attend(x)
    ml_sent.wait()
    attend(y)
    theirs, mine = rows_of(1 - c, t), rows_of(c, t)
    for side in range(2):
        kvsend[side, :, pl.ds(0, HALF)] = dk[side, theirs, :].astype(BF)
        kvsend[side, :, pl.ds(HALF, HALF)] = dv[side, theirs, :].astype(BF)
    kv_sent = copies.push(kvsend, kvrecv, sib)

    def unturn(block, j, value):
        cosine, sine = cs[block, :, 0:128], cs[block, :, 128:256]
        rounded = value.astype(BF).astype(F32)
        pg[block, :, pl.ds(128 * j, 128)] = turn(rounded, cosine, -sine).astype(BF)

    for side in range(2):
        for j in range(3):
            unturn(side, j, dqt[side, 128 * j : 128 * j + 128, :].T)
    kv_sent.wait()
    for side in range(2):
        for j in range(3):
            at = pl.ds(128 * j, 128)
            unturn(side, 3 + j, dk[side, mine, at] + kvrecv[side, :, at].astype(F32))
            pg[side, :, pl.ds(D + 128 * j, 128)] = (
                dv[side, mine, at] + kvrecv[side, :, pl.ds(HALF + 128 * j, 128)].astype(F32)
            ).astype(BF)
    for copy in tri_moves:
        copy.wait()
    psend[...] = nt(pg[y], wt[...]).astype(BF)
    part_sent = copies.push(psend, precv, peer)
    part[...] = nt(pg[x], wt[...])

    ml_all = ml[...].reshape(2 * t, D)
    na_all = na[...].reshape(2 * t, D)
    ctx_all = ctx[...].reshape(2 * t, HALF)

    def grads(which, store):
        def step(i, carry):
            off = pl.ds(pl.multiple_of(which * HALF + i * 128, 128), 128)
            at = pl.ds(pl.multiple_of(i * 128, 128), 128)
            store(0, at, tn(na[:, :, off].reshape(2 * t, 128), pg[...].reshape(2 * t, TRI)))
            store(1, at, tn(ctx_all, ml[:, :, off].reshape(2 * t, 128)))
            return carry

        lax.fori_loop(0, HALF // 128, step, 0)

    def to_send(kind, at, value):
        if kind == 0:
            gsend[at, pl.ds(0, TRI)] = value.astype(BF)
        else:
            gsend[:, pl.ds(pl.multiple_of(TRI + at.start, 128), 128)] = value.astype(BF)

    def to_keep(kind, at, value):
        if kind == 0:
            gown[at, pl.ds(0, TRI)] = value
        else:
            gown[:, pl.ds(pl.multiple_of(TRI + at.start, 128), 128)] = value

    grads(1 - c, to_send)
    grad_sent = copies.push(gsend, grecv, sib)
    grads(c, to_keep)
    part_sent.wait()
    dy = part[...] + precv[...].astype(F32)
    back, rows = norm_back(h[...], sc[0:1, :], dy)
    g_prev[...] = mg[...] + back
    rows_o[...] = rows
    grad_sent.wait()
    gsend[...] = (gown[...] + grecv[...].astype(F32)).astype(BF)
    copies.local(gsend, wg_o).wait()


def attend_bwd(mg, h, wa, scales, tables, bias, saved):
    t = mg.shape[0]
    return call(
        attend_bwd_kernel, "attend_bwd", 3,
        [vmem(), vmem(), hbm(), vmem(), vmem(), pl.BlockSpec(memory_space=pltpu.SMEM)] + [vmem()] * 6,
        [vmem(), hbm(), vmem()],
        [sds((t, D), F32), sds((HALF, 2 * D), BF), sds((2, D), F32)],
        [
            pltpu.VMEM((D, TRI), BF), pltpu.VMEM((HALF, D), BF), pltpu.VMEM((2, t, D), BF),
            pltpu.VMEM((2, t, HALF), BF), pltpu.VMEM((8, t), F32), pltpu.VMEM((2, HALF, t), F32),
            pltpu.VMEM((2, 2 * t, HALF), F32), pltpu.VMEM((2, 2 * t, HALF), F32),
            pltpu.VMEM((2, t, D), BF), pltpu.VMEM((2, t, D), BF), pltpu.VMEM((2, t, TRI), BF),
            pltpu.VMEM((t, D), F32), pltpu.VMEM((t, D), BF), pltpu.VMEM((t, D), BF),
            pltpu.VMEM((HALF, 2 * D), F32), pltpu.VMEM((HALF, 2 * D), BF),
            pltpu.VMEM((HALF, 2 * D), BF),
        ],
        3, 6, 10 << 30, (mg, h, wa, scales, tables, bias, *saved),
    )


TRIPLE, OUTPUT, EXPAND, SHRINK = range(4)
KINDS = (TRIPLE, OUTPUT, EXPAND, SHRINK)
ZS = 4


class Spot:
    def __init__(self):
        s = lax.axis_index("seq")
        self.s = s
        self.x, self.c = lax.div(s, 2), lax.rem(s, 2)
        self.d = lax.axis_index("dp")
        self.z, self.y = lax.div(self.d, 2), lax.rem(self.d, 2)
        self.upper, self.odd = lax.div(self.z, 2), lax.rem(self.z, 2)
        self.sib, self.peer = s + 1 - 2 * self.c, lax.rem(s + 2, SEQ)
        self.across = self.d + 1 - 2 * self.y
        self.zs = ZS

    def count(self, kind):
        return ZS if kind == EXPAND else ZS // 2

    def origin(self, kind, j):
        if kind == TRIPLE:
            return 2 * self.c + j
        if kind == OUTPUT:
            return 2 * self.x + j
        return j if kind == EXPAND else 2 * j + self.x

    def own_slot(self, kind):
        return {TRIPLE: self.odd, OUTPUT: self.odd, EXPAND: self.z, SHRINK: self.upper}[kind]

    def if_owner(self, kind, act):
        if kind == EXPAND:
            act()
        elif kind == TRIPLE:
            pl.when(self.c == self.upper)(act)
        elif kind == OUTPUT:
            pl.when(self.x == self.upper)(act)
        else:
            pl.when(self.x == self.odd)(act)

    def naturals(self, kind):
        x, c = self.x, self.c
        if kind == TRIPLE:
            return ((0, 2 * x), (1, 2 * x + 1), (2, 2 * (1 - x)), (3, 2 * (1 - x) + 1))
        if kind == EXPAND:
            return ((0, 2 * c + x),)
        return ((0, 2 * c), (1, 2 * c + 1))

    def targets(self, kind):
        x, c = self.x, self.c
        if kind == TRIPLE:
            return ((c, 0, 2 * x + self.upper), (2 + c, 1, 2 * (1 - x) + self.upper))
        if kind == OUTPUT:
            return ((c, 0, 2 * self.upper + x),)
        if kind == EXPAND:
            return ((0, 0, 2 * c + x),)
        return ((c, 0, 2 * self.odd + x),)


class Saved(NamedTuple):
    na: Any
    q: Any
    k: Any
    k_t: Any
    v: Any
    ctx: Any
    ctx_t: Any
    lse: Any
    nb: Any
    act: Any
    slope: Any
    wt: Any
    wo: Any
    we: Any
    ws: Any


class ForwardIn(NamedTuple):
    h0: Any
    g0: Any
    sc_w: Any
    cs: Any
    bias: Any
    tri_w: Any
    out_w: Any
    exp_w: Any
    shr_w: Any


class ForwardHead(NamedTuple):
    h_out: Any
    h_mid: Any
    mid_o0: Any
    mid_o1: Any
    sc_o: Any
    gl_o: Any


class ForwardScratch(NamedTuple):
    p_whole: Any
    p_half: Any
    p_out: Any
    p_exp: Any
    p_shr: Any
    gl: Any
    wt: Any
    wo: Any
    we: Any
    ws: Any
    hb: Any
    ob: Any
    scl: Any
    sc: Any
    na: Any
    q: Any
    k: Any
    v: Any
    ctxt: Any
    ctx: Any
    ctx_t: Any
    lse: Any
    nb: Any
    na_t: Any
    nb_t: Any
    k_t: Any
    v_t: Any
    act: Any
    slope: Any
    psend: Any
    precv: Any
    hs: Any
    mid: Any
    ssem: Any
    rsem: Any
    zero_ssem: Any
    zero_rsem: Any
    sc_ssem: Any
    sc_rsem: Any
    xs: Any
    xr: Any
    lsem: Any


class Refs:
    def __init__(self, *groups):
        for group in groups:
            for name, ref in zip(group._fields, group):
                setattr(self, name, ref)


def split(refs, *kinds):
    out, at = [], 0
    for kind in kinds:
        size = len(kind._fields)
        out.append(kind(*refs[at : at + size]))
        at += size
    return out


class Weights(Spot):
    def __init__(self, n, rows):
        super().__init__()
        self.n = n
        self.rows = rows
        self.source = {
            TRIPLE: (n.p_whole, n.p_half), OUTPUT: (n.p_out,), EXPAND: (n.p_exp,), SHRINK: (n.p_shr,)
        }

    def view(self, kind, layer, y, z, c):
        n, r = self.n, self.rows
        if kind == EXPAND:
            return n.we.at[layer, rows_of(2 * z + y, r), rows_of(c, D)]
        at = 2 * lax.rem(z, 2) + y
        if kind == TRIPLE:
            return n.wt.at[layer, pl.ds(pl.multiple_of(HALF * c + r * at, r), r), :]
        if kind == OUTPUT:
            return n.wo.at[layer, rows_of(at, r), rows_of(c, HALF)]
        return n.ws.at[layer, rows_of(c, HALF), rows_of(2 * lax.div(z, 2) + y, 4 * r)]

    def piece(self, kind, layer, number, to):
        n, r = self.n, self.rows
        x, c = lax.div(to, 2), lax.rem(to, 2)
        if kind == TRIPLE:
            start = pl.ds(pl.multiple_of(HALF * c + r * (2 * self.odd + self.y), r), r)
            return (n.wt.at[layer, start, rows_of(x + self.core_of(number), HALF)], n.hb.at[layer, self.core_of(number)])
        if kind == OUTPUT:
            return n.ob.at[layer, number]
        if kind == EXPAND:
            return self.view(kind, layer, self.y, self.z, c)
        rows = pl.ds(pl.multiple_of(HALF * c + 192 * number, 192), 192)
        return n.ws.at[layer, rows, rows_of(2 * self.upper + self.y, 4 * r)]

    @staticmethod
    def core_of(number):
        return lax.rem(number, 2)

    def landing(self, kind, layer, number, part, to):
        spot = self.piece(kind, layer, number, to)
        return spot[part] if kind == TRIPLE else spot

    def zero_copy(self, kind, layer, number, part, to):
        return pltpu.make_async_remote_copy(
            src_ref=self.source[kind][part].at[layer],
            dst_ref=self.landing(kind, layer, number, part, to),
            send_sem=self.n.zero_ssem.at[layer, kind, part],
            recv_sem=self.n.zero_rsem.at[layer, kind, number],
            device_id=(self.d, to),
            device_id_type=MESH,
        )

    def zero_here(self, kind, layer, number, part, to):
        return pltpu.make_async_copy(
            self.source[kind][part].at[layer], self.landing(kind, layer, number, part, to),
            self.n.zero_rsem.at[layer, kind, number],
        )

    def zero(self, kind, layer):
        for number, part, to in self.targets(kind):
            away = to != self.s
            place = (kind, layer, number, part, to)
            pl.when(away)(lambda place=place: self.zero_copy(*place).start())
            pl.when(jnp.logical_not(away))(lambda place=place: self.zero_here(*place).start())

    def remote(self, ref, kind, layer, stage, sent, slot, to):
        return pltpu.make_async_remote_copy(
            src_ref=ref,
            dst_ref=ref,
            send_sem=self.n.ssem.at[layer, kind, stage, sent],
            recv_sem=self.n.rsem.at[layer, kind, stage, slot],
            device_id=to,
            device_id_type=MESH,
        )

    def spread(self, kind, layer):
        def act():
            for number, _ in self.naturals(kind):
                part = 1 if kind == TRIPLE and number >= 2 else 0
                ref = self.landing(kind, layer, number, part, self.s)
                pltpu.make_async_remote_copy(
                    src_ref=ref, dst_ref=ref, send_sem=self.n.zero_ssem.at[layer, kind, part],
                    recv_sem=self.n.zero_rsem.at[layer, kind, number], device_id=(self.d, self.peer),
                    device_id_type=MESH,
                ).wait_recv()
            n, r = self.n, self.rows
            if kind == TRIPLE:
                start = HALF * self.c + r * (2 * self.odd + self.y)
                join(n.hb[layer, 0], n.hb[layer, 1], n.wt, layer, start, 2 * (1 - self.x) * HALF, r)
            elif kind == OUTPUT:
                join(n.ob[layer, 0], n.ob[layer, 1], n.wo, layer, r * (2 * self.odd + self.y), HALF * self.c, r)
            ref = self.view(kind, layer, self.y, self.z, self.c)
            slot = self.own_slot(kind)
            for k in range(1, ZS):
                other = lax.rem(self.z + k, ZS)
                self.remote(ref, kind, layer, 0, k, slot, (2 * other + self.y, self.s)).start()
            self.remote(ref, kind, layer, 1, slot, slot, (self.across, self.s)).start()

        self.if_owner(kind, act)

    def onward(self, kind, layer, j):
        z = self.origin(kind, j)

        @pl.when(z != self.z)
        def _():
            ref = self.view(kind, layer, self.y, z, self.c)
            self.remote(ref, kind, layer, 0, 0, j, (self.across, self.s)).wait_recv()
            self.remote(ref, kind, layer, 1, j, j, (self.across, self.s)).start()

    def onward_all(self, kind, layer):
        for j in range(self.count(kind)):
            self.onward(kind, layer, j)

    def arrive(self, kind, layer):
        for j in range(self.count(kind)):
            ref = self.view(kind, layer, 1 - self.y, self.origin(kind, j), self.c)
            self.remote(ref, kind, layer, 1, j, j, (self.across, self.s)).wait_recv()

    def finish(self, kind, layer):
        for number, part, to in self.targets(kind):
            place = (kind, layer, number, part, to)
            pl.when(to != self.s)(lambda place=place: self.zero_copy(*place).wait_send())

        def act():
            ref = self.view(kind, layer, self.y, self.z, self.c)
            for k in range(1, ZS):
                self.remote(ref, kind, layer, 0, k, 0, (self.across, self.s)).wait_send()

        self.if_owner(kind, act)
        for j in range(self.count(kind)):
            ref = self.view(kind, layer, self.y, self.origin(kind, j), self.c)
            self.remote(ref, kind, layer, 1, j, j, (self.across, self.s)).wait_send()


def join(first, second, into, layer, row, col, rows):
    half = rows // 2
    top, bottom = join_packed(first[rows:], second[rows:])
    all_rows = pl.ds(pl.multiple_of(row, half), rows)
    into[layer, all_rows, pl.ds(pl.multiple_of(col, 128), 128)] = first[:rows]
    middle = pl.ds(pl.multiple_of(col + 128, 128), 128)
    into[layer, pl.ds(pl.multiple_of(row, half), half), middle] = top
    into[layer, pl.ds(pl.multiple_of(row + half, half), half), middle] = bottom
    into[layer, all_rows, pl.ds(pl.multiple_of(col + 256, 128), 128)] = second[:rows]


def greet_all(w):
    barrier = pltpu.get_barrier_semaphore()

    def one(i, carry):
        z, s = lax.div(i, SEQ), lax.rem(i, SEQ)
        away = jnp.logical_or(z != w.z, s != w.s)

        @pl.when(away)
        def _():
            pl.semaphore_signal(barrier, inc=1, device_id=(2 * z + w.y, s), device_id_type=MESH)

        return carry

    lax.fori_loop(0, w.zs * SEQ, one, 0)
    pl.semaphore_signal(barrier, inc=1, device_id=(w.across, w.s), device_id_type=MESH)
    pl.semaphore_wait(barrier, w.zs * SEQ)


def left_half(shape):
    return lax.broadcasted_iota(jnp.int32, shape, 1) < HD


def join_packed(first, second):
    first, second = first.astype(F32), second.astype(F32)
    left = left_half(first.shape)
    top = jnp.where(left, first, second)
    bottom = pltpu.roll(jnp.where(left, second, first), HD, 1)
    return top.astype(BF), bottom.astype(BF)


def pack_wide(value):
    half = value.shape[0] // 2
    top, bottom = value[:half, 128:256], pltpu.roll(value[half:, 128:256], HD, 1)
    left = left_half(top.shape)
    first, second = jnp.where(left, top, bottom), jnp.where(left, bottom, top)
    return (
        jnp.concatenate([value[:, :128], first], axis=0),
        jnp.concatenate([value[:, 256:], second], axis=0),
    )


def gather_scales_start(w):
    n = w.n
    mine = n.scl.at[w.y, w.z, w.s]
    mine[...] = jnp.zeros_like(mine)
    wide = n.sc_w.shape[-1]
    for layer in range(LAYERS):
        mine[layer : layer + 1, 0:wide] = n.sc_w[layer].astype(BF).astype(F32)

    def one(i, carry):
        z, s = lax.div(i, SEQ), lax.rem(i, SEQ)

        @pl.when(jnp.logical_or(z != w.z, s != w.s))
        def _():
            pltpu.make_async_remote_copy(
                src_ref=mine, dst_ref=mine, send_sem=n.sc_ssem.at[i],
                recv_sem=n.sc_rsem.at[w.z * SEQ + w.s], device_id=(2 * z + w.y, s), device_id_type=MESH,
            ).start()

        return carry

    lax.fori_loop(0, w.zs * SEQ, one, 0)


def gather_scales_end(w):
    n = w.n

    def one(i, carry):
        z, s = lax.div(i, SEQ), lax.rem(i, SEQ)

        @pl.when(jnp.logical_or(z != w.z, s != w.s))
        def _():
            slot = n.scl.at[w.y, z, s]
            copy = pltpu.make_async_remote_copy(
                src_ref=slot, dst_ref=slot, send_sem=n.sc_ssem.at[i], recv_sem=n.sc_rsem.at[i],
                device_id=(2 * z + w.y, s), device_id_type=MESH,
            )
            copy.wait_recv()
            copy.wait_send()

        return carry

    lax.fori_loop(0, w.zs * SEQ, one, 0)
    count = w.zs * SEQ
    plane = n.scl.at[w.y]
    copy = pltpu.make_async_remote_copy(
        src_ref=plane, dst_ref=plane, send_sem=n.sc_ssem.at[count], recv_sem=n.sc_rsem.at[count],
        device_id=(w.across, w.s), device_id_type=MESH,
    )
    copy.start()
    copy.wait()
    wide = n.sc.shape[-1] // (2 * w.zs)
    for s in range(SEQ):
        both = [n.scl[d % 2, d // 2, s][:, :wide] for d in range(2 * w.zs)]
        rows = jnp.concatenate(both, axis=1)
        for layer in range(LAYERS):
            n.sc[layer, s : s + 1, :] = rows[layer : layer + 1, :]


def fwd_kernel(dp, *refs):
    ins, outs, saved0, saved1, scratch = split(refs, ForwardIn, ForwardHead, Saved, Saved, ForwardScratch)
    n = Refs(ins, outs, scratch)
    saved = (saved0, saved1)
    rows = n.exp_w.shape[1]
    t = n.h0.shape[0]
    w = Weights(n, rows)
    x, c, peer, sib = w.x, w.c, w.peer, w.sib
    y = 1 - x
    parts = (pl.ds(0, t // 2), pl.ds(t // 2, t // 2))
    copies = Copies(n.lsem, n.xs, n.xr, w.d)
    waits = []

    def save(src, dst):
        waits.append(copies.local(src, dst))

    half_rows = rows // 2

    def pack(low, into, layer, core):
        wide, rest = (low[:, :128], low[:, 128:]) if core == 0 else (low[:, 64:], low[:, :64])
        ends = [rest[:half_rows], rest[half_rows:]]
        into[layer, pl.ds(0, rows), :] = wide.astype(BF)
        into[layer, pl.ds(rows, half_rows), :] = jnp.concatenate(ends if core == 0 else ends[::-1], axis=1).astype(BF)

    def round_triple(layer):
        for core in range(2):

            @pl.when(c == core)
            def _():
                tri = n.tri_w[layer]
                n.p_whole[layer] = (tri[:, :HALF] if core == 0 else tri[:, 192:]).astype(BF)
                pack(tri[:, HALF:] if core == 0 else tri[:, :192], n.p_half, layer, core)

    def round_output(layer):
        for core in range(2):
            pl.when(c == core)(lambda: pack(n.out_w[layer], n.p_out, layer, core))

    round_triple(0)
    greet_all(w)
    w.zero(TRIPLE, 0)
    gather_scales_start(w)
    round_output(0)
    w.zero(OUTPUT, 0)
    n.p_exp[...] = n.exp_w[...].astype(BF)
    w.zero(EXPAND, 0)
    n.p_shr[...] = n.shr_w[...].astype(BF)
    w.zero(SHRINK, 0)
    round_triple(1)
    round_output(1)
    for kind in KINDS:
        w.zero(kind, 1)
    for layer in range(LAYERS):
        for kind in KINDS:
            w.spread(kind, layer)
    n.hs[0] = n.h0[...]
    xhat, _ = norm_stats(n.hs[0])
    gather_scales_end(w)

    def share_tri(layer):
        own = n.wt.at[layer, rows_of(c, HALF), :]
        return copies.push(own, own, sib)

    def share_out(layer):
        own = n.wo.at[layer, :, rows_of(c, HALF)]
        return copies.push(own, own, sib)

    def share_shr(layer):
        own = n.ws.at[layer, rows_of(c, HALF), :]
        return copies.push(own, own, sib)

    def share_exp(layer):
        own = n.we.at[layer, :, rows_of(c, D)]
        return copies.push(own, own, sib)

    for layer in range(LAYERS):
        last = layer == LAYERS - 1
        if layer:
            xhat, _ = norm_stats(n.hs[layer])
        n.na[layer, x] = (xhat * n.sc[layer, 0:1, :] + n.sc[layer, 1:2, :]).astype(BF)
        na_sent = copies.push(n.na.at[layer, x], n.na.at[layer, x], peer)
        if last:
            n.gl[x] = n.g0[...].astype(BF)
            gl_sent = copies.push(n.gl.at[x], n.gl.at[x], peer)
        if layer == 0:
            w.onward_all(TRIPLE, 0)
            w.onward_all(OUTPUT, 0)
            w.arrive(TRIPLE, 0)
            tri_sent = share_tri(0)
        tri_sent.wait()

        def project(block):
            cosine, sine = n.cs[block, :, 0:128], n.cs[block, :, 128:256]
            for j in range(9):
                part = nn(n.na[layer, block], n.wt[layer, :, 128 * j : 128 * j + 128])
                lanes = pl.ds(128 * (j % 3), 128)
                if j < 3:
                    n.q[layer, block, :, lanes] = (turn(part, cosine, sine) * HD**-0.5).astype(BF)
                elif j < 6:
                    n.k[layer, block, rows_of(c, t), lanes] = turn(part, cosine, sine).astype(BF)
                else:
                    n.v[layer, block, rows_of(c, t), lanes] = part.astype(BF)

        def share(block):
            at = (layer, block, rows_of(c, t))
            return [
                copies.push(n.k.at[at], n.k.at[at], sib),
                copies.push(n.v.at[at], n.v.at[at], sib),
            ]

        project(x)
        shared = share(x)
        na_sent.wait()
        project(y)
        shared += share(y)
        w.arrive(OUTPUT, layer)
        out_sent = share_out(layer)
        for copy in shared:
            copy.wait()
        for block in range(2):
            n.v_t[block] = n.v[layer, block].T
        save(n.q.at[layer], saved[layer].q)
        save(n.k.at[layer], saved[layer].k)
        save(n.v.at[layer], saved[layer].v)

        def attend(block, pump):
            other = 1 - block

            def pair_step(p, carry):
                pump(p)
                lanes = pl.ds(pl.multiple_of(p * 128, 128), 128)
                q_pair = n.q[layer, block, :, lanes]
                k_same, k_cross = n.k[layer, block, :, lanes], n.k[layer, other, :, lanes]
                for which in range(2):
                    q_head = half_of(q_pair, which)
                    s_same = nt(k_same, q_head)
                    s_cross = nt(k_cross, q_head) + n.bias[0]
                    top = jnp.maximum(
                        jnp.max(s_same, axis=0, keepdims=True), jnp.max(s_cross, axis=0, keepdims=True)
                    )
                    e_same = jnp.exp(s_same - top)
                    e_cross = jnp.exp(s_cross - top)
                    total = jnp.sum(e_same, axis=0, keepdims=True) + jnp.sum(
                        e_cross, axis=0, keepdims=True
                    )
                    head = pl.ds(pl.multiple_of(p * 128 + which * HD, HD), HD)
                    mixed = nn(n.v_t[block, head, :], e_same.astype(BF)) + nn(n.v_t[other, head, :], e_cross.astype(BF))
                    n.ctxt[head, :] = mixed / total
                    n.lse[layer, block, pl.ds(2 * p + which, 1), :] = top + jnp.log(total)
                return carry

            lax.fori_loop(0, HALF // 128, pair_step, 0)
            n.ctx_t[layer, :, rows_of(block, t)] = n.ctxt[...].astype(BF)
            n.ctx[layer, block] = n.ctxt[...].T.astype(BF)

        def early(p):
            kind = SHRINK if layer else EXPAND
            pl.when(p > 0)(lambda: w.onward(kind, layer, p - 1))

        attend(y, early)
        if last:
            gl_sent.wait()
            save(n.gl, n.gl_o)
        out_sent.wait()
        use = 2 * layer
        n.psend[use] = nn(n.ctx[layer, y], n.wo[layer]).astype(BF)
        part_sent = copies.push(n.psend.at[use], n.precv.at[use], peer)


        def late(p):
            if layer == 0:
                pl.when(p == 0)(lambda: w.onward(EXPAND, layer, 2))
                pl.when(p == 0)(lambda: w.onward(EXPAND, layer, 3))
                pl.when(p > 0)(lambda: w.onward(SHRINK, layer, p - 1))

        attend(x, late)
        n.mid[layer] = n.hs[layer] + nn(n.ctx[layer, x], n.wo[layer])
        save(n.ctx.at[layer], saved[layer].ctx)
        save(n.lse.at[layer], saved[layer].lse)
        save(n.wt.at[layer], saved[layer].wt)
        save(n.wo.at[layer], saved[layer].wo)
        save(n.ctx_t.at[layer], saved[layer].ctx_t)
        for block in range(2):
            n.na_t[layer, :, block * t : block * t + t] = n.na[layer, block].T
            n.k_t[layer, block] = n.k[layer, block].T
        save(n.na_t.at[layer], saved[layer].na)
        save(n.k_t.at[layer], saved[layer].k_t)
        part_sent.wait()
        n.mid[layer] = n.mid[layer] + n.precv[use].astype(F32)
        save(n.mid.at[layer], (n.mid_o0, n.mid_o1)[layer])

        xhat, _ = norm_stats(n.mid[layer])
        n.nb[layer, x] = (xhat * n.sc[layer, 2:3, :] + n.sc[layer, 3:4, :]).astype(BF)
        nb_sent = [copies.push(n.nb.at[layer, x, part], n.nb.at[layer, x, part], peer) for part in parts]
        w.arrive(EXPAND, layer)
        exp_sent = share_exp(layer)
        w.arrive(SHRINK, layer)
        shr_sent = share_shr(layer)
        exp_sent.wait()
        save(n.we.at[layer], saved[layer].we)

        def feed(block, part, pump):
            def step(i, carry):
                pump(i)
                lanes = pl.ds(pl.multiple_of(i * 256, 256), 256)
                value, rate = gelu_parts(nn(n.nb[layer, block, part, :], n.we[layer, :, lanes]))
                n.act[layer, block, part, lanes] = value.astype(BF)
                n.slope[layer, block, part, lanes] = rate.astype(BF)
                return carry

            lax.fori_loop(0, HID // 256, step, 0)

        def pump(i):
            if not last:

                @pl.when(i < 2)
                def _():
                    w.onward(TRIPLE, layer + 1, i)
                    w.onward(OUTPUT, layer + 1, i)

        feed(x, pl.ds(0, t), lambda i: None)
        use = 2 * layer + 1
        part_sent = []
        for number, part in enumerate(parts):
            nb_sent[number].wait()
            feed(y, part, pump if number == 0 else lambda i: None)
            if number == 0:
                shr_sent.wait()
            n.psend[use, part, :] = nt(n.act[layer, y, part, :], n.ws[layer]).astype(BF)
            part_sent.append(copies.push(n.psend.at[use, part], n.precv.at[use, part], peer))
        n.hs[layer + 1] = n.mid[layer] + nt(n.act[layer, x], n.ws[layer])
        save(n.ws.at[layer], saved[layer].ws)
        for block in range(2):
            n.nb_t[layer, :, block * t : block * t + t] = n.nb[layer, block].T
        save(n.nb_t.at[layer], saved[layer].nb)
        save(n.act.at[layer], saved[layer].act)
        save(n.slope.at[layer], saved[layer].slope)
        if not last:
            w.onward_all(EXPAND, layer + 1)
            w.arrive(TRIPLE, layer + 1)
            tri_sent = share_tri(layer + 1)
        for copy in part_sent:
            copy.wait()
        n.hs[layer + 1] = n.hs[layer + 1] + n.precv[use].astype(F32)

    n.h_out[...] = n.hs[LAYERS]
    n.sc_o[...] = n.sc[...]
    save(n.hs.at[1], n.h_mid)
    for copy in waits:
        copy.wait()
    for layer in range(LAYERS):
        for kind in KINDS:
            w.finish(kind, layer)


def forward_all(dp, h, g, scales_weight, tables, bias, shards):
    t = h.shape[0]
    zs, packed = dp // 2, 3 * (D // dp) // 2
    per_layer = [
        sds((D, 2 * t), BF), sds((2, t, HALF), BF), sds((2, 2 * t, HALF), BF), sds((2, HALF, 2 * t), BF), sds((2, 2 * t, HALF), BF),
        sds((2, t, HALF), BF), sds((HALF, 2 * t), BF), sds((2, 8, t), F32), sds((D, 2 * t), BF), sds((2, t, HID), BF),
        sds((2, t, HID), BF), sds((D, TRI), BF), sds((HALF, D), BF), sds((D, HID), BF), sds((D, HID), BF),
    ]
    token = sds((t, D), F32)
    outs = [token, token, token, token, sds((LAYERS, 4, D), F32), sds((2, t, D), BF), *per_layer, *per_layer]
    specs = [vmem(), hbm(), hbm(), hbm(), vmem(), hbm(), *([hbm()] * (2 * len(per_layer)))]
    n_layers = LAYERS
    rows = D // dp
    scratch = [
        pltpu.VMEM((n_layers, rows, HALF), BF), pltpu.VMEM((n_layers, packed, 128), BF),
        pltpu.VMEM((n_layers, packed, 128), BF), pltpu.VMEM((n_layers, rows, D), BF),
        pltpu.VMEM((n_layers, 192, 4 * rows), BF), pltpu.VMEM((2, t, D), BF),
        pltpu.VMEM((n_layers, D, TRI), BF), pltpu.VMEM((n_layers, HALF, D), BF),
        pltpu.VMEM((n_layers, D, HID), BF), pltpu.VMEM((n_layers, D, HID), BF),
        pltpu.VMEM((n_layers, 2, packed, 128), BF), pltpu.VMEM((n_layers, 2, packed, 128), BF),
        pltpu.VMEM((2, zs, SEQ, 8, 128), F32),
        pltpu.VMEM((n_layers, 4, D), F32), pltpu.VMEM((n_layers, 2, t, D), BF),
        pltpu.VMEM((n_layers, 2, t, HALF), BF), pltpu.VMEM((n_layers, 2, 2 * t, HALF), BF),
        pltpu.VMEM((n_layers, 2, 2 * t, HALF), BF), pltpu.VMEM((HALF, t), F32),
        pltpu.VMEM((n_layers, 2, t, HALF), BF), pltpu.VMEM((n_layers, HALF, 2 * t), BF),
        pltpu.VMEM((n_layers, 2, 8, t), F32), pltpu.VMEM((n_layers, 2, t, D), BF),
        pltpu.VMEM((n_layers, D, 2 * t), BF), pltpu.VMEM((n_layers, D, 2 * t), BF),
        pltpu.VMEM((n_layers, 2, HALF, 2 * t), BF), pltpu.VMEM((2, HALF, 2 * t), BF),
        pltpu.VMEM((n_layers, 2, t, HID), BF),
        pltpu.VMEM((n_layers, 2, t, HID), BF), pltpu.VMEM((2 * n_layers, t, D), BF),
        pltpu.VMEM((2 * n_layers, t, D), BF), pltpu.VMEM((n_layers + 1, t, D), F32),
        pltpu.VMEM((n_layers, t, D), F32),
        pltpu.SemaphoreType.DMA((n_layers, len(KINDS), 2, zs)),
        pltpu.SemaphoreType.DMA((n_layers, len(KINDS), 2, zs)),
        pltpu.SemaphoreType.DMA((n_layers, len(KINDS), 2)), pltpu.SemaphoreType.DMA((n_layers, len(KINDS), 4)),
        pltpu.SemaphoreType.DMA((zs * SEQ + 1,)), pltpu.SemaphoreType.DMA((zs * SEQ + 1,)),
        pltpu.SemaphoreType.DMA((32,)), pltpu.SemaphoreType.DMA((32,)), pltpu.SemaphoreType.DMA((40,)),
    ]
    results = pl.pallas_call(
        functools.partial(fwd_kernel, dp),
        name="forward",
        out_shape=outs,
        in_specs=[*([vmem()] * 4), pl.BlockSpec(memory_space=pltpu.SMEM), *([vmem()] * 4)],
        out_specs=specs,
        scratch_shapes=scratch,
        cost_estimate=pl.CostEstimate(flops=22 << 30, bytes_accessed=32 << 20, transcendentals=0),
        compiler_params=pltpu.CompilerParams(
            collective_id=4, has_side_effects=True, vmem_limit_bytes=VMEM_BYTES
        ),
    )(h, g, scales_weight, tables, bias, *shards)
    return split(results, ForwardHead, Saved, Saved)


class Sums(Spot):
    def __init__(self, n, rows):
        super().__init__()
        self.n = n
        self.rows = rows
        self.landed = {TRIPLE: n.y_tri, OUTPUT: n.y_out, EXPAND: n.y_exp, SHRINK: n.y_shr}
        self.owned = {TRIPLE: n.z_tri, OUTPUT: n.z_out, EXPAND: n.z_exp, SHRINK: n.z_shr}
        self.final = {TRIPLE: (n.f_whole, n.f_half), OUTPUT: (n.f_out,), EXPAND: (n.f_exp,), SHRINK: (n.f_shr,)}

    def view(self, kind, layer, y, z):
        n, r = self.n, self.rows
        if kind == EXPAND:
            return n.ge.at[layer, rows_of(2 * z + y, r), :]
        if kind == SHRINK:
            return n.gs.at[layer, :, rows_of(2 * lax.div(z, 2) + y, 4 * r)]
        return (n.gt if kind == TRIPLE else n.go).at[layer, rows_of(2 * lax.rem(z, 2) + y, r), :]

    def remote(self, src, dst, kind, layer, stage, sent, slot, to):
        return pltpu.make_async_remote_copy(
            src_ref=src,
            dst_ref=dst,
            send_sem=self.n.ssem.at[layer, kind, stage, sent],
            recv_sem=self.n.rsem.at[layer, kind, stage, slot],
            device_id=to,
            device_id_type=MESH,
        )

    def across_copy(self, kind, layer, j):
        return self.remote(
            self.view(kind, layer, 1 - self.y, self.origin(kind, j)), self.landed[kind].at[layer, j],
            kind, layer, 0, j, j, (self.across, self.s),
        )

    def across_all(self, kind, layer):
        for j in range(self.count(kind)):
            self.across_copy(kind, layer, j).start()

    def along_copy(self, kind, layer, j):
        z = self.origin(kind, j)
        slot = lax.rem(self.z - z + ZS - 1, ZS)
        mine = self.view(kind, layer, self.y, z)
        return self.remote(mine, self.owned[kind].at[layer, slot], kind, layer, 1, j, slot, (2 * z + self.y, self.s))

    def along(self, kind, layer, j):
        z = self.origin(kind, j)
        self.across_copy(kind, layer, j).wait_recv()
        mine = self.view(kind, layer, self.y, z)
        mine[...] = (mine[...].astype(F32) + self.landed[kind][layer, j].astype(F32)).astype(BF)
        pl.when(z != self.z)(lambda: self.along_copy(kind, layer, j).start())

    def along_all(self, kind, layer):
        for j in range(self.count(kind)):
            self.along(kind, layer, j)

    def parts(self, kind, layer):
        n = self.n
        mine = self.view(kind, layer, self.y, self.z)
        if kind == TRIPLE:
            return (
                mine.at[:, rows_of(self.x, HALF)], mine.at[:, rows_of(self.x + 1, HALF)],
                n.half_out.at[layer, 0], n.half_out.at[layer, 1],
            )
        if kind == OUTPUT:
            return n.out_out.at[layer, 0], n.out_out.at[layer, 1]
        return (mine,) if kind == EXPAND else (mine.at[pl.ds(0, 192), :], mine.at[pl.ds(192, 192), :])

    def home_copy(self, kind, layer, number, to, here=False):
        src = self.parts(kind, layer)[number]
        part = 1 if kind == TRIPLE and number >= 2 else 0
        dst = self.final[kind][part].at[layer]
        sem = self.n.home_rsem.at[layer, kind, part]
        if here:
            return pltpu.make_async_copy(src, dst, sem)
        return pltpu.make_async_remote_copy(
            src_ref=src, dst_ref=dst, send_sem=self.n.home_ssem.at[layer, kind, number], recv_sem=sem,
            device_id=(self.d, to), device_id_type=MESH,
        )

    def total(self, kind, layer):
        n = self.n

        def act():
            for slot in range(ZS - 1):
                ref = self.owned[kind].at[layer, slot]
                self.remote(ref, ref, kind, layer, 1, 0, slot, (self.across, self.s)).wait_recv()
            mine = self.view(kind, layer, self.y, self.z)
            value = mine[...].astype(F32)
            for slot in range(ZS - 1):
                value = value + self.owned[kind][layer, slot].astype(F32)
            n.squares[...] = n.squares[...] + squared(value)
            mine[...] = value.astype(BF)
            if kind == OUTPUT:
                first, second = pack_wide(value)
                n.out_out[layer, 0] = first.astype(BF)
                n.out_out[layer, 1] = second.astype(BF)
            if kind == TRIPLE:
                cut = mine[:, rows_of(2 * (1 - self.x), HALF)].astype(F32)
                first, second = pack_wide(cut)
                n.half_out[layer, 0] = first.astype(BF)
                n.half_out[layer, 1] = second.astype(BF)
            for number, to in self.naturals(kind):
                away = to != self.s
                place = (kind, layer, number, to)
                pl.when(away)(lambda place=place: self.home_copy(*place).start())
                pl.when(jnp.logical_not(away))(lambda place=place: self.home_copy(*place, True).start())

        self.if_owner(kind, act)

    def home(self, kind, layer):
        for part, final in enumerate(self.final[kind]):
            ref = final.at[layer]
            pltpu.make_async_remote_copy(
                src_ref=ref, dst_ref=ref, send_sem=self.n.home_ssem.at[layer, kind, 0],
                recv_sem=self.n.home_rsem.at[layer, kind, part], device_id=(self.d, self.peer), device_id_type=MESH,
            ).wait_recv()

    def finish(self, kind, layer):
        for j in range(self.count(kind)):
            self.across_copy(kind, layer, j).wait_send()
            pl.when(self.origin(kind, j) != self.z)(
                lambda j=j: self.along_copy(kind, layer, j).wait_send()
            )

        def act():
            for number, to in self.naturals(kind):
                place = (kind, layer, number, to)
                pl.when(to != self.s)(lambda place=place: self.home_copy(*place).wait_send())

        self.if_owner(kind, act)


def squared(value):
    return jnp.sum(jnp.sum(value * value, axis=1, keepdims=True), axis=0, keepdims=True)


def everywhere_start(w, use, buf):
    n = w.n
    mine = buf.at[w.y, w.z, w.s]

    def one(i, carry):
        z, s = lax.div(i, SEQ), lax.rem(i, SEQ)

        @pl.when(jnp.logical_or(z != w.z, s != w.s))
        def _():
            pltpu.make_async_remote_copy(
                src_ref=mine, dst_ref=mine, send_sem=n.ev_ssem.at[use, i],
                recv_sem=n.ev_rsem.at[use, w.z * SEQ + w.s], device_id=(2 * z + w.y, s), device_id_type=MESH,
            ).start()

        return carry

    lax.fori_loop(0, w.zs * SEQ, one, 0)


def everywhere_end(w, use, buf, pair):
    n = w.n

    def one(i, carry):
        z, s = lax.div(i, SEQ), lax.rem(i, SEQ)

        @pl.when(jnp.logical_or(z != w.z, s != w.s))
        def _():
            slot = buf.at[w.y, z, s]
            copy = pltpu.make_async_remote_copy(
                src_ref=slot, dst_ref=slot, send_sem=n.ev_ssem.at[use, i], recv_sem=n.ev_rsem.at[use, i],
                device_id=(2 * z + w.y, s), device_id_type=MESH,
            )
            copy.wait_recv()
            copy.wait_send()

        return carry

    lax.fori_loop(0, w.zs * SEQ, one, 0)

    def add(i, total):
        return total + buf[w.y, lax.div(i, SEQ), lax.rem(i, SEQ)]

    pair[w.y] = lax.fori_loop(1, w.zs * SEQ, add, buf[w.y, 0, 0])
    count = w.zs * SEQ
    copy = pltpu.make_async_remote_copy(
        src_ref=pair.at[w.y], dst_ref=pair.at[w.y], send_sem=n.ev_ssem.at[use, count],
        recv_sem=n.ev_rsem.at[use, count], device_id=(w.across, w.s), device_id_type=MESH,
    )
    copy.start()
    copy.wait()
    return pair[0] + pair[1]


class Loaded(NamedTuple):
    na: Any
    q: Any
    k: Any
    k_t: Any
    v: Any
    ctx: Any
    ctx_t: Any
    lse: Any
    nb: Any
    act: Any
    slope: Any
    wt: Any
    wo: Any
    we: Any
    ws: Any
    h: Any
    mid: Any


class BackwardIn(NamedTuple):
    g0: Any
    gl_h: Any
    sc: Any
    cs: Any
    bias: Any


class BackwardOut(NamedTuple):
    g_out: Any
    scale_o: Any
    norm_o: Any
    tri_g: Any
    out_g: Any
    exp_g: Any
    shr_g: Any


class BackwardScratch(NamedTuple):
    gl: Any
    gl_t: Any
    hg: Any
    ml: Any
    cg: Any
    delta: Any
    dqt: Any
    dk: Any
    dv: Any
    kvsend: Any
    kvrecv: Any
    pg: Any
    part: Any
    psend: Any
    precv: Any
    gs_exp: Any
    gr_exp: Any
    gs_shr: Any
    gr_shr: Any
    gr_att: Any
    gt: Any
    go: Any
    ge: Any
    gs: Any
    y_tri: Any
    y_out: Any
    y_exp: Any
    y_shr: Any
    z_tri: Any
    z_out: Any
    z_exp: Any
    z_shr: Any
    half_out: Any
    out_out: Any
    f_whole: Any
    f_half: Any
    f_out: Any
    f_exp: Any
    f_shr: Any
    squares: Any
    early: Any
    early_pair: Any
    late: Any
    late_pair: Any
    sq: Any
    sq_pair: Any
    ssem: Any
    rsem: Any
    home_ssem: Any
    home_rsem: Any
    ev_ssem: Any
    ev_rsem: Any
    xs: Any
    xr: Any
    lsem: Any


def bwd_kernel(dp, *refs):
    ins, saved0, saved1, outs, loaded, scratch = split(
        refs, BackwardIn, Loaded, Loaded, BackwardOut, Loaded, BackwardScratch
    )
    n = Refs(ins, outs, loaded, scratch)
    saved = (saved0, saved1)
    t = n.g0.shape[0]
    w = Sums(n, D // dp)
    x, c, peer, sib = w.x, w.c, w.peer, w.sib
    y = 1 - x
    parts = (pl.ds(0, t // 2), pl.ds(t // 2, t // 2))
    copies = Copies(n.lsem, n.xs, n.xr, w.d)
    loading = {}

    def load(layer, *wanted):
        for place in wanted:
            loading[place] = copies.local(saved[layer][place], loaded[place])

    def ready(*wanted):
        for place in wanted:
            loading[place].wait()

    na, q, k, k_t, v, ctx, ctx_t, lse, nb, act, slope, wt, wo, we, ws, h, mid = range(len(Loaded._fields))
    feed_places = (ws, slope, we, act, nb, mid)
    attend_places = (wo, ctx, q, k, v, lse, k_t, wt, na, ctx_t, h)
    top_gl = copies.local(n.gl_h, n.gl.at[LAYERS - 1])
    load(LAYERS - 1, *feed_places, *attend_places)
    n.squares[...] = jnp.zeros_like(n.squares)
    mine_at = (w.y, w.z, w.s)
    greet_all(w)
    n.g_out[...] = n.g0[...]

    for layer in reversed(range(LAYERS)):
        top = layer == LAYERS - 1

        if top:
            top_gl.wait()
        else:
            n.gl[layer, x] = n.g_out[...].astype(BF)
            g_sent = [copies.push(n.gl.at[layer, x, part], n.gl.at[layer, x, part], peer) for part in parts]
        ready(ws, slope, we)

        def back(block, part):
            def step(i, carry):
                lanes = pl.ds(pl.multiple_of(i * 256, 256), 256)
                pulled = nn(n.gl[layer, block, part, :], n.ws[:, lanes])
                n.hg[block, part, lanes] = (pulled * n.slope[block, part, lanes].astype(F32)).astype(BF)
                return carry

            lax.fori_loop(0, HID // 256, step, 0)
            return nt(n.hg[block, part, :], n.we[...])

        def pump_tri(i):
            if not top:

                @pl.when(i < 2)
                def _():
                    w.along(TRIPLE, layer + 1, i)
                    w.along(OUTPUT, layer + 1, i)

        n.part[...] = back(x, pl.ds(0, t))
        use = 2 * layer
        part_sent = []
        for number, part in enumerate(parts):
            if not top:
                g_sent[number].wait()
            n.psend[part, :] = back(y, part).astype(BF)
            part_sent.append(copies.push(n.psend.at[part], n.precv.at[use, part], peer))
        ready(act, nb, mid)
        for block in range(2):
            n.gl_t[:, block * t : block * t + t] = n.gl[layer, block].T

        def exp_tile(which, i):
            off = pl.ds(pl.multiple_of(which * D + i * 256, 256), 256)
            return nn(n.nb[...], n.hg[:, :, off].reshape(2 * t, 256))

        def shr_tile(which, i):
            off = pl.ds(pl.multiple_of(i * 256, 256), 256)
            return nn(n.gl_t[rows_of(which, HALF), :], n.act[:, :, off].reshape(2 * t, 256))

        def send_exp(i, carry):
            at = pl.ds(pl.multiple_of(i * 256, 256), 256)
            n.gs_exp[:, at] = exp_tile(1 - c, i).astype(BF)
            return carry

        def send_shr(i, carry):
            at = pl.ds(pl.multiple_of(i * 256, 256), 256)
            n.gs_shr[:, at] = shr_tile(1 - c, i).astype(BF)
            return carry

        lax.fori_loop(0, D // 256, send_exp, 0)
        exp_sent = copies.push(n.gs_exp, n.gr_exp, sib)
        lax.fori_loop(0, HID // 256, send_shr, 0)
        shr_sent = copies.push(n.gs_shr, n.gr_shr, sib)

        def keep_exp(i, carry):
            at = pl.ds(pl.multiple_of(i * 256, 256), 256)
            n.ge[layer, :, at] = (exp_tile(c, i) + n.gr_exp[:, at].astype(F32)).astype(BF)
            return carry

        def keep_shr(i, carry):
            pump_tri(i)
            at = pl.ds(pl.multiple_of(i * 256, 256), 256)
            n.gs[layer, :, at] = (shr_tile(c, i) + n.gr_shr[:, at].astype(F32)).astype(BF)
            return carry

        exp_sent.wait()
        lax.fori_loop(0, D // 256, keep_exp, 0)
        w.across_all(EXPAND, layer)
        shr_sent.wait()
        lax.fori_loop(0, HID // 256, keep_shr, 0)
        w.across_all(SHRINK, layer)
        for copy in part_sent:
            copy.wait()
        dy = n.part[...] + n.precv[use].astype(F32)
        back_mid, rows_b = norm_back(n.mid[...], n.sc[layer, 2:3, :], dy)
        n.g_out[...] = n.g_out[...] + back_mid

        n.ml[layer, x] = n.g_out[...].astype(BF)
        ml_sent = copies.push(n.ml.at[layer, x], n.ml.at[layer, x], peer)
        if layer:
            load(layer - 1, *feed_places)
        else:
            n.early[(*mine_at, pl.ds(4, 2))] = rows_b
            everywhere_start(w, 0, n.early)
            w.total(EXPAND, 1)
            w.total(SHRINK, 1)
        n.dk[...] = jnp.zeros_like(n.dk)
        n.dv[...] = jnp.zeros_like(n.dv)
        ready(wo, ctx, q, k, v, lse, k_t)

        def attend(block, pump):
            other = 1 - block
            n.cg[block] = nt(n.ml[layer, block], n.wo[...]).astype(BF)
            weighed = (n.cg[block].astype(F32) * n.ctx[block].astype(F32)).T
            for head in range(HALF // HD):
                n.delta[head : head + 1, :] = jnp.sum(
                    weighed[head * HD : head * HD + HD, :], axis=0, keepdims=True
                )

            def pair_step(p, carry):
                pump(p)
                lanes = pl.ds(pl.multiple_of(p * 128, 128), 128)
                q_pair, cg_pair = n.q[block, :, lanes], n.cg[block, :, lanes]
                for which in range(2):
                    q_head, cg_head = half_of(q_pair, which), half_of(cg_pair, which)
                    row = pl.ds(2 * p + which, 1)
                    total, dots = n.lse[block, row, :], n.delta[row, :]
                    turned = None
                    head = pl.ds(pl.multiple_of(p * 128 + which * HD, HD), HD)
                    for side in (block, other):
                        k_pair, v_pair = n.k[side, :, lanes], n.v[side, :, lanes]
                        scores = nt(k_pair, q_head)
                        if side is other:
                            scores = scores + n.bias[0]
                        probs = jnp.exp(scores - total)
                        score_grad = (probs * (nt(v_pair, cg_head) - dots)).astype(BF)
                        n.dv[side, :, lanes] += nn(probs.astype(BF), cg_head)
                        n.dk[side, :, lanes] += nn(score_grad, q_head)
                        piece = nn(n.k_t[side, head, :], score_grad)
                        turned = piece if turned is None else turned + piece
                    n.dqt[block, head, :] = turned * HD**-0.5
                return carry

            lax.fori_loop(0, HALF // 128, pair_step, 0)

        attend(x, lambda p: None)
        ml_sent.wait()
        attend(y, lambda p: None)
        theirs, mine = rows_of(1 - c, t), rows_of(c, t)
        for side in range(2):
            n.kvsend[side, :, pl.ds(0, HALF)] = n.dk[side, theirs, :].astype(BF)
            n.kvsend[side, :, pl.ds(HALF, HALF)] = n.dv[side, theirs, :].astype(BF)
        kv_sent = copies.push(n.kvsend, n.kvrecv.at[layer], sib)
        tri_cols, out_cols = pl.ds(0, TRI), pl.ds(TRI, HALF)
        theirs_too = n.ml[layer, :, :, rows_of(1 - c, HALF)].reshape(2 * t, HALF)
        ready(ctx_t)
        n.gs_shr[:, out_cols] = nn(n.ctx_t[...], theirs_too).astype(BF)
        out_sent = copies.push(n.gs_shr.at[:, out_cols], n.gr_att.at[:, out_cols], sib)
        w.along_all(EXPAND, layer)

        def unturn(block, j, value):
            cosine, sine = n.cs[block, :, 0:128], n.cs[block, :, 128:256]
            rounded = value.astype(BF).astype(F32)
            n.pg[block, :, pl.ds(128 * j, 128)] = turn(rounded, cosine, -sine).astype(BF)

        for side in range(2):
            for j in range(3):
                unturn(side, j, n.dqt[side, 128 * j : 128 * j + 128, :].T)
        kv_sent.wait()
        for side in range(2):
            for j in range(3):
                at = pl.ds(128 * j, 128)
                unturn(side, 3 + j, n.dk[side, mine, at] + n.kvrecv[layer, side, :, at].astype(F32))
                n.pg[side, :, pl.ds(D + 128 * j, 128)] = (
                    n.dv[side, mine, at] + n.kvrecv[layer, side, :, pl.ds(HALF + 128 * j, 128)].astype(F32)
                ).astype(BF)
        ready(wt, na, h)
        use = 2 * layer + 1
        n.psend[...] = nt(n.pg[y], n.wt[...]).astype(BF)
        part_sent = copies.push(n.psend, n.precv.at[use], peer)
        rows = D // dp
        out_sent.wait()
        mine_too = n.ml[layer, :, :, rows_of(c, HALF)].reshape(2 * t, HALF)
        value = nn(n.ctx_t[...], mine_too) + n.gr_att[:, out_cols].astype(F32)
        n.go[layer] = value.astype(BF)
        w.across_all(OUTPUT, layer)

        def send_tri(i, carry):
            off = pl.ds(pl.multiple_of((1 - c) * HALF + i * rows, rows), rows)
            n.gs_shr[rows_of(i, rows), pl.ds(0, TRI)] = nn(n.na[off, :], n.pg[...].reshape(2 * t, TRI)).astype(BF)
            return carry

        lax.fori_loop(0, w.zs, send_tri, 0)
        tri_sent = copies.push(n.gs_shr.at[:, tri_cols], n.gr_att.at[:, tri_cols], sib)
        n.part[...] = nt(n.pg[x], n.wt[...])
        tri_sent.wait()

        def keep_tri(i, carry):
            block = 2 * lax.rem(i, 2) + jnp.where(i < 2, 1 - w.y, w.y)
            at = rows_of(block, rows)
            row_block = n.na[pl.ds(pl.multiple_of(c * HALF + block * rows, rows), rows), :]
            value = nn(row_block, n.pg[...].reshape(2 * t, TRI)) + n.gr_att[at, tri_cols].astype(F32)
            n.gt[layer, at, :] = value.astype(BF)
            return carry

        lax.fori_loop(0, 2, keep_tri, 0)
        w.across_all(TRIPLE, layer)
        w.along_all(SHRINK, layer)
        lax.fori_loop(2, w.zs, keep_tri, 0)
        part_sent.wait()
        dy = n.part[...] + n.precv[use].astype(F32)
        back_h, rows_a = norm_back(n.h[...], n.sc[layer, 0:1, :], dy)
        n.g_out[...] = n.g_out[...] + back_h
        if layer:
            load(layer - 1, *attend_places)
            n.early[(*mine_at, pl.ds(0, 2))] = rows_a
            n.early[(*mine_at, pl.ds(2, 2))] = rows_b
        else:
            n.late[mine_at] = rows_a

    w.along_all(OUTPUT, 0)
    w.along(TRIPLE, 0, 0)
    everywhere_start(w, 1, n.late)
    w.along(TRIPLE, 0, 1)
    for kind in (TRIPLE, OUTPUT):
        w.total(kind, 1)
    for kind in (EXPAND, SHRINK):
        w.total(kind, 0)
    first = everywhere_end(w, 0, n.early, n.early_pair)
    second = everywhere_end(w, 1, n.late, n.late_pair)
    n.scale_o[1, pl.ds(0, 2)] = first[0:2]
    n.scale_o[1, pl.ds(2, 2)] = first[2:4]
    n.scale_o[0, pl.ds(0, 2)] = second
    n.scale_o[0, pl.ds(2, 2)] = first[4:6]
    for kind in (TRIPLE, OUTPUT):
        w.total(kind, 0)
    n.sq[w.y, w.z, w.s] = jnp.broadcast_to(n.squares[...], (8, 128))
    everywhere_start(w, 2, n.sq)
    for layer in range(LAYERS):
        for kind in KINDS:
            w.home(kind, layer)
    rows = D // dp

    def natural(packed):
        wide, rest = packed[:rows].astype(F32), packed[rows:].astype(F32)
        even = jnp.concatenate([rest[:, :HD], rest[:, HD:]], axis=0)
        odd = jnp.concatenate([rest[:, HD:], rest[:, :HD]], axis=0)
        return jnp.concatenate([wide, even], axis=1), jnp.concatenate([odd, wide], axis=1)

    for layer in range(LAYERS):
        halves, outs_here = natural(n.f_half[layer]), natural(n.f_out[layer])
        whole = n.f_whole[layer].astype(F32)

        @pl.when(c == 0)
        def _():
            n.tri_g[layer] = jnp.concatenate([whole, halves[0]], axis=1)
            n.out_g[layer] = outs_here[0]

        @pl.when(c == 1)
        def _():
            n.tri_g[layer] = jnp.concatenate([halves[1], whole], axis=1)
            n.out_g[layer] = outs_here[1]

    outputs = [
        copies.local(a, b)
        for a, b in ((n.f_exp, n.exp_g), (n.f_shr, n.shr_g))
    ]
    total = everywhere_end(w, 2, n.sq, n.sq_pair)
    n.norm_o[...] = total + squared(first[0:6]) + squared(second)
    for copy in outputs:
        copy.wait()
    for layer in range(LAYERS):
        for kind in KINDS:
            w.finish(kind, layer)


def backward_all(dp, g, f, residual, tables, bias):
    t = g.shape[0]
    zs = dp // 2
    r = D // dp
    packed = 3 * r // 2
    head, saved0, saved1 = f
    saved = (*saved0, residual, head.mid_o0, *saved1, head.h_mid, head.mid_o1)
    outs = [
        sds((t, D), F32), sds((LAYERS, 4, D), F32), sds((8, 128), F32), sds((LAYERS, r, TRI // 2), F32),
        sds((LAYERS, r, 192), F32), sds((LAYERS, r, D), BF),
        sds((LAYERS, 192, 4 * r), BF),
    ]
    v = pltpu.VMEM
    ll = LAYERS
    scratch = [
        *(v(array.shape, array.dtype) for array in saved[: len(Loaded._fields)]),
        v((ll, 2, t, D), BF), v((D, 2 * t), BF), v((2, t, HID), BF), v((ll, 2, t, D), BF), v((2, t, HALF), BF), v((8, t), F32),
        v((2, HALF, t), F32), v((2, 2 * t, HALF), F32), v((2, 2 * t, HALF), F32), v((2, t, D), BF),
        v((ll, 2, t, D), BF), v((2, t, TRI), BF), v((t, D), F32), v((t, D), BF), v((2 * ll, t, D), BF),
        v((D, D), BF), v((D, D), BF), v((HALF, HID), BF), v((HALF, HID), BF), v((HALF, HID), BF),
        v((ll, HALF, TRI), BF), v((ll, HALF, HALF), BF), v((ll, D, D), BF), v((ll, HALF, HID), BF),
        v((ll, 2, r, TRI), BF), v((ll, 2, r, HALF), BF), v((ll, 4, r, D), BF), v((ll, 2, HALF, 4 * r), BF),
        v((ll, 3, r, TRI), BF), v((ll, 3, r, HALF), BF), v((ll, 3, r, D), BF), v((ll, 3, HALF, 4 * r), BF),
        v((ll, 2, packed, 128), BF), v((ll, 2, packed, 128), BF),
        v((ll, r, HALF), BF), v((ll, packed, 128), BF), v((ll, packed, 128), BF), v((ll, r, D), BF),
        v((ll, 192, 4 * r), BF), v((1, 1), F32),
        v((2, zs, SEQ, 8, D), F32), v((2, 8, D), F32), v((2, zs, SEQ, 2, D), F32), v((2, 2, D), F32),
        v((2, zs, SEQ, 8, 128), F32), v((2, 8, 128), F32),
        pltpu.SemaphoreType.DMA((ll, len(KINDS), 2, zs)), pltpu.SemaphoreType.DMA((ll, len(KINDS), 2, zs)),
        pltpu.SemaphoreType.DMA((ll, len(KINDS), 4)), pltpu.SemaphoreType.DMA((ll, len(KINDS), 2)),
        pltpu.SemaphoreType.DMA((3, zs * SEQ + 1)), pltpu.SemaphoreType.DMA((3, zs * SEQ + 1)),
        pltpu.SemaphoreType.DMA((28,)), pltpu.SemaphoreType.DMA((28,)), pltpu.SemaphoreType.DMA((48,)),
    ]
    results = pl.pallas_call(
        functools.partial(bwd_kernel, dp),
        name="backward",
        out_shape=outs,
        in_specs=[vmem(), hbm(), vmem(), vmem(), pl.BlockSpec(memory_space=pltpu.SMEM), *([hbm()] * len(saved))],
        out_specs=[vmem()] * 5 + [hbm()] * 2,
        scratch_shapes=scratch,
        cost_estimate=pl.CostEstimate(flops=44 << 30, bytes_accessed=48 << 20, transcendentals=0),
        compiler_params=pltpu.CompilerParams(
            collective_id=5, has_side_effects=True, vmem_limit_bytes=VMEM_BYTES
        ),
    )(g, head.gl_o, head.sc_o, tables, bias, *saved)
    return BackwardOut(*results)


class Moves:
    def __init__(self, dp):
        self.dp = dp
        self.d = lax.axis_index("dp")
        s = lax.axis_index("seq")
        self.s, self.x, self.c = s, s // 2, s % 2
        half = dp // 2
        ids = [(d, s) for d in range(dp) for s in range(SEQ)]
        self.tri = []
        for r in range(2):
            for j in range(3):
                perm = []
                for d, s in ids:
                    b = (3 * s + j) % 4
                    to = (2 * (d % half) + (r ^ (b % 2)), 2 * (b // 2) + d // half)
                    perm.append((d * SEQ + s, to[0] * SEQ + to[1]))
                self.tri.append(perm)
        self.out = []
        for r in range(2):
            perm = []
            for d, s in ids:
                to = (2 * (d % half) + (r ^ (s % 2)), 2 * (d // half) + s // 2)
                perm.append((d * SEQ + s, to[0] * SEQ + to[1]))
            self.out.append(perm)
        self.shr = []
        for k in range(4):
            perm = []
            for d, s in ids:
                to = (4 * (d % (dp // 4)) + (k + s) % 4, d // (dp // 4))
                perm.append((d * SEQ + s, to[0] * SEQ + to[1]))
            self.shr.append(perm)

    def send(self, piece, perm, back):
        if back:
            perm = [(b, a) for a, b in perm]
        return lax.ppermute(piece, ("dp", "seq"), perm)

    @staticmethod
    def pick(pieces, index):
        return lax.dynamic_index_in_dim(jnp.stack(pieces), index, 0, keepdims=False)

    def tri_out(self, low):
        n, rows, _ = low.shape
        halves = low.reshape(n, 2, rows // 2, 3, 192)
        got = []
        for r in range(2):
            for j in range(3):
                which = r ^ (((3 * self.s + j) % 4) % 2)
                piece = lax.dynamic_index_in_dim(halves[:, :, :, j], which, 1, keepdims=False)
                got.append(self.send(piece, self.tri[3 * r + j], False))
        parts = []
        for t in range(3):
            for bb in range(2):
                r, j = bb ^ (self.d % 2), (t + 2 * self.x + bb) % 3
                parts.append(self.pick(got, 3 * r + j))
        return jnp.concatenate(parts, axis=-1)

    def tri_back(self, grad):
        n, rows, _ = grad.shape
        got = []
        for r in range(2):
            for j in range(3):
                bb = (self.d % 2) ^ r
                t = (j - (2 * self.x + bb)) % 3
                piece = lax.dynamic_slice_in_dim(grad, (2 * t + bb) * 192, 192, 2)
                got.append(self.send(piece, self.tri[3 * r + j], True))
        cols = []
        for j in range(3):
            two = []
            for hh in range(2):
                r = hh ^ (((3 * self.s + j) % 4) % 2)
                two.append(self.pick([got[j], got[3 + j]], r))
            cols.append(jnp.concatenate(two, axis=1))
        return jnp.concatenate(cols, axis=-1)

    def out_out(self, low):
        n, rows, _ = low.shape
        halves = low.reshape(n, 2, rows // 2, 192)
        got = [
            self.send(
                lax.dynamic_index_in_dim(halves, r ^ (self.s % 2), 1, keepdims=False), self.out[r], False
            )
            for r in range(2)
        ]
        return jnp.concatenate([self.pick(got, u ^ (self.d % 2)) for u in range(2)], axis=-1)

    def out_back(self, grad):
        got = []
        for r in range(2):
            u = r ^ (self.d % 2)
            got.append(self.send(lax.dynamic_slice_in_dim(grad, u * 192, 192, 2), self.out[r], True))
        return jnp.concatenate([self.pick(got, hh ^ (self.s % 2)) for hh in range(2)], axis=1)

    def shr_out(self, low):
        n, rows, _ = low.shape
        subs = low.reshape(n, 4, rows // 4, 192)
        got = [
            self.send(
                lax.dynamic_index_in_dim(subs, (k + self.s) % 4, 1, keepdims=False), self.shr[k], False
            )
            for k in range(4)
        ]
        return jnp.concatenate([self.pick(got, (self.d - s) % 4) for s in range(4)], axis=-1)

    def shr_back(self, grad):
        got = []
        for k in range(4):
            piece = lax.dynamic_slice_in_dim(grad, ((self.d - k) % 4) * 192, 192, 2)
            got.append(self.send(piece, self.shr[k], True))
        return jnp.concatenate([self.pick(got, (sub - self.s) % 4) for sub in range(4)], axis=1)


def tables_here(segments, t, x, c):
    group = segments.shape[0]
    whole = segments[0] == segments[group - 1]
    place_in_half = c * t + jnp.arange(t, dtype=jnp.int32)
    second = jnp.where(whole, group // 2, 0).astype(jnp.int32)
    positions = jnp.stack([place_in_half, place_in_half + second]).astype(F32)
    lane = jnp.arange(128, dtype=jnp.int32)
    inverse = 1.0 / ROTARY_BASE ** ((lane % (HD // 2)).astype(F32) * (2.0 / HD))
    angles = positions[:, :, None] * inverse[None, None, :]
    sign = jnp.where(lane % HD < HD // 2, -1.0, 1.0).astype(F32)
    tables = jnp.concatenate([jnp.cos(angles), jnp.sin(angles) * sign], axis=-1)
    bias = jnp.where(whole, 0.0, MASKED).astype(F32).reshape(1)
    return tables, bias


def layers_narrow(
    dp, moves, residual, cotangent, scales_weight, tables, bias,
    triple_weight, output_weight, expand_weight, shrink_weight,
):
    d, s = lax.axis_index("dp"), lax.axis_index("seq")
    scales_all = lax.psum(
        lax.dynamic_update_slice(
            jnp.zeros((LAYERS, 4, D), F32), scales_weight.astype(BF).astype(F32), (0, s, d * (D // dp))
        ),
        ("dp", "seq"),
    )
    tri = moves.tri_out(triple_weight.astype(BF))
    out = moves.out_out(output_weight.astype(BF))
    shr = moves.shr_out(shrink_weight.astype(BF))
    attend_parts = jnp.concatenate([tri, out], axis=-1)
    feed_parts = jnp.concatenate([expand_weight.astype(BF), shr], axis=-1)
    gather = functools.partial(lax.all_gather, axis_name="dp", axis=0, tiled=True)
    wa, wf = [], []
    for layer in range(LAYERS):
        wa.append(gather(attend_parts[layer]))
        wf.append(gather(feed_parts[layer]))

    stream = residual
    kept = []
    for layer in range(LAYERS):
        scales = scales_all[layer]
        middle, *attend_saved = attend_fwd(stream, wa[layer], scales, tables, bias)
        following, *feed_saved = feed_fwd(middle, wf[layer], scales)
        kept.append((stream, middle, attend_saved, feed_saved))
        stream = following

    g = cotangent
    attend_grads, feed_grads, scale_grads = [None] * LAYERS, [None] * LAYERS, [None] * LAYERS
    scatter = functools.partial(lax.psum_scatter, axis_name="dp", scatter_dimension=0, tiled=True)
    for layer in reversed(range(LAYERS)):
        scales = scales_all[layer]
        h, middle, attend_saved, feed_saved = kept[layer]
        mg, feed_grad, rows_b = feed_bwd(g, middle, wf[layer], scales, *feed_saved)
        feed_grads[layer] = scatter(feed_grad).astype(F32)
        g, attend_grad, rows_a = attend_bwd(mg, h, wa[layer], scales, tables, bias, attend_saved)
        attend_grads[layer] = scatter(attend_grad).astype(F32)
        scale_grads[layer] = jnp.concatenate([rows_a, rows_b], axis=0)

    scale_grad = lax.psum(jnp.stack(scale_grads), ("dp", "seq"))
    own_scale = lax.dynamic_slice(scale_grad, (0, s, d * (D // dp)), (LAYERS, 1, D // dp))
    squares = jnp.sum(own_scale * own_scale)
    for part in (*attend_grads, *feed_grads):
        squares = squares + jnp.sum(part * part)
    grad_norm = jnp.sqrt(lax.psum(squares, ("dp", "seq")))

    attend_grad, feed_grad = jnp.stack(attend_grads).astype(BF), jnp.stack(feed_grads).astype(BF)
    triple_grad = moves.tri_back(attend_grad[:, :, :TRI]).astype(F32)
    output_grad = moves.out_back(attend_grad[:, :, TRI:]).astype(F32)
    expand_grad = feed_grad[:, :, :D].astype(F32)
    shrink_grad = moves.shr_back(feed_grad[:, :, D:]).astype(F32)
    return stream, g, grad_norm, (triple_grad, output_grad, expand_grad, shrink_grad, own_scale)


def layers_wide(
    dp, moves, residual, cotangent, scales_weight, tables, bias,
    triple_weight, output_weight, expand_weight, shrink_weight,
):
    d, s = lax.axis_index("dp"), lax.axis_index("seq")
    shards = (triple_weight, output_weight, expand_weight, jnp.swapaxes(shrink_weight, 1, 2))
    f = forward_all(dp, residual, cotangent, scales_weight, tables, bias, shards)
    b = backward_all(dp, cotangent, f, residual, tables, bias)
    own_scale = lax.dynamic_slice(b.scale_o, (0, s, d * (D // dp)), (LAYERS, 1, D // dp))
    grad_norm = jnp.sqrt(b.norm_o[0, 0])
    return f[0].h_out, b.g_out, grad_norm, (
        b.tri_g, b.out_g, b.exp_g.astype(F32), jnp.swapaxes(b.shr_g, 1, 2).astype(F32), own_scale
    )


def local(dp, *args):
    (residual, cotangent, segments) = args[:3]
    (
        triple_weight, triple_moment, triple_square, triple_shadow,
        output_weight, output_moment, output_square, output_shadow,
        expand_weight, expand_moment, expand_square, expand_shadow,
        shrink_weight, shrink_moment, shrink_square, shrink_shadow,
        scales_weight, scales_moment, scales_square, scales_shadow,
    ) = args[3:]
    moves = Moves(dp)
    t = residual.shape[0]
    d, s = lax.axis_index("dp"), lax.axis_index("seq")
    tables, bias = tables_here(segments, t, moves.x, moves.c)

    if dp == 2 * ZS:
        stream, g, grad_norm, grads = layers_wide(
            dp, moves, residual, cotangent, scales_weight, tables, bias,
            triple_weight, output_weight, expand_weight, shrink_weight,
        )
    else:
        stream, g, grad_norm, grads = layers_narrow(
            dp, moves, residual, cotangent, scales_weight, tables, bias,
            triple_weight, output_weight, expand_weight, shrink_weight,
        )
    triple_grad, output_grad, expand_grad, shrink_grad, own_scale = grads
    limit = CLIP_RATIO * math.sqrt(float(LAYERS * (4 * D * D + 2 * D * FF + 4 * D)))
    factor = limit / (grad_norm + 1e-06)

    results = [stream, g, grad_norm]
    for weight, moment, square, shadow, grad, rate in (
        (triple_weight, triple_moment, triple_square, triple_shadow, triple_grad, RATE_FACTOR / math.sqrt(D)),
        (output_weight, output_moment, output_square, output_shadow, output_grad, RATE_FACTOR / math.sqrt(D // 16)),
        (expand_weight, expand_moment, expand_square, expand_shadow, expand_grad, RATE_FACTOR / math.sqrt(D)),
        (shrink_weight, shrink_moment, shrink_square, shrink_shadow, shrink_grad, RATE_FACTOR / math.sqrt(FF)),
        (scales_weight, scales_moment, scales_square, scales_shadow, own_scale, SCALES_RATE),
    ):
        results.extend(adam_step(weight, moment, square, shadow, grad * factor, rate))
    return tuple(results)


def solution(mesh):
    token = P(("dp", "seq"), None)
    weight = P(None, "dp", "seq")
    scale = P(None, "seq", "dp")
    return jax.shard_map(
        functools.partial(local, mesh.shape["dp"]),
        mesh=mesh,
        in_specs=(token, token, P("dp"), *([weight] * 16), *([scale] * 4)),
        out_specs=(token, token, P(), *([weight] * 16), *([scale] * 4)),
        check_vma=False,
    )
```
